32 devices in a mesh: tensor: 4 (over y, x), sub: 2 (over core), group: 4 (over z).
Axes of the slice: x: 2, y: 2, z: 4, core: 2. Of those that a mesh axis runs over, the one named last changes fastest.
Arguments:
- frames: bfloat16 [8, 1024, 1536], P(('sub', 'group'), 'tensor'), may hold values from -6 to 6
- text_states: bfloat16 [8, 64, 1536], P(('sub', 'group')), may hold values from -6 to 6
- selfgain: float32 [1536], replicated, may hold values from 0.5 to 1.5
- selfbias: float32 [1536], replicated, may hold values from -1.5 to 1.5
- selfqkv: bfloat16 [1536, 3, 1536], P(None, None, 'tensor'), may hold values from -0.15625 to 0.15625
- selfout: bfloat16 [1536, 1536], P('tensor'), may hold values from -0.625 to 0.625
- crossgain: float32 [1536], replicated, may hold values from 0.5 to 1.5
- crossbias: float32 [1536], replicated, may hold values from -1.5 to 1.5
- crossquery: bfloat16 [1536, 1536], P(None, 'tensor'), may hold values from -0.15625 to 0.15625
- crosskv: bfloat16 [1536, 2, 1536], P(None, None, 'tensor'), may hold values from -0.15625 to 0.15625
- crossout: bfloat16 [1536, 1536], P('tensor'), may hold values from -0.4375 to 0.4375
- feedgain: float32 [1536], replicated, may hold values from 0.5 to 1.5
- feedbias: float32 [1536], replicated, may hold values from -1.5 to 1.5
- feedup: bfloat16 [1536, 6144], P(None, 'tensor'), may hold values from -0.15625 to 0.15625
- feeddown: bfloat16 [6144, 1536], P('tensor'), may hold values from -0.078125 to 0.078125
- cotangent: float32 [8, 1024, 1536], P(('sub', 'group'), 'tensor'), may hold values from -6 to 6
Outputs:
- layer_output: float32 [8, 1024, 1536], P(('sub', 'group'), 'tensor')
- frame_grad: float32 [8, 1024, 1536], P(('sub', 'group'), 'tensor')
- text_grad: float32 [8, 64, 1536], P(('sub', 'group'))
- selfgain_grad: float32 [1536], P('sub')
- selfbias_grad: float32 [1536], P('sub')
- selfqkv_grad: float32 [1536, 3, 1536], P('sub', None, 'tensor')
- selfout_grad: float32 [1536, 1536], P(('tensor', 'sub'))
- crossgain_grad: float32 [1536], P('sub')
- crossbias_grad: float32 [1536], P('sub')
- crossquery_grad: float32 [1536, 1536], P('sub', 'tensor')
- crosskv_grad: float32 [1536, 2, 1536], P('sub', None, 'tensor')
- crossout_grad: float32 [1536, 1536], P(('tensor', 'sub'))
- feedgain_grad: float32 [1536], P('sub')
- feedbias_grad: float32 [1536], P('sub')
- feedup_grad: float32 [1536, 6144], P('sub', 'tensor')
- feeddown_grad: float32 [6144, 1536], P(('tensor', 'sub'))
The draws below stay inside these ranges and needn't reach their ends.
All inputs are finite; a program needn't handle non-finite values.
Results may differ from the reference program's by a relative error of at most 0.035.
Values may be sent and summed in bfloat16 or wider, within the bound.
A program may use at most 256 MiB of HBM per device.

```python
import jax
import jax.numpy as jnp
from jax import lax

D = 1536
HEADS = 24
HEAD = 64
FF = 6144
FRAMES = 1024
TEXT = 64
CLIPS = 8


def steps_of(key, extent, cuts, least, top_value):
    loudness, own = 1.0, jax.random.fold_in(key, 6)
    for position, blocks in cuts:
        steps = jnp.exp(jax.random.uniform(jax.random.fold_in(own, position), (blocks,), jnp.float32, least / len(cuts), top_value / len(cuts)))
        loudness = loudness * jnp.repeat(steps, extent[position] // blocks).reshape([-1 if axis == position else 1 for axis in range(len(extent))])
    return loudness


def centred(key, extent, width, most, cuts=(), kind=jnp.bfloat16):
    values = width * jax.random.normal(key, extent, jnp.float32)
    if cuts:
        values = values * steps_of(key, extent, cuts, -0.22, 0.18)
    return jnp.clip(values, -most, most).astype(kind)


def setup_inputs(seed: int = 0) -> dict:
    streams_of = jax.random.split(jax.random.key(seed), 17)
    frames = centred(streams_of[0], (CLIPS, FRAMES, D), 1.0, 6.0, ((0, 8), (1, 4)))
    text_states = centred(streams_of[1], (CLIPS, TEXT, D), 1.0, 6.0, ((0, 8),))
    selfgain = jnp.clip(1.0 + 0.1 * jax.random.normal(streams_of[2], (D,), jnp.float32), 0.5, 1.5)
    selfbias = centred(streams_of[3], (D,), 0.3, 1.5, (), jnp.float32)
    selfqkv = centred(streams_of[4], (D, 3, D), D ** -0.5, 0.15625, ((2, 4),))
    selfout = centred(streams_of[5], (D, D), (D // 16) ** -0.5, 0.625, ((0, 4),))
    crossgain = jnp.clip(1.0 + 0.1 * jax.random.normal(streams_of[6], (D,), jnp.float32), 0.5, 1.5)
    crossbias = centred(streams_of[7], (D,), 0.3, 1.5, (), jnp.float32)
    crossquery = centred(streams_of[8], (D, D), D ** -0.5, 0.15625, ((1, 4),))
    crosskv = centred(streams_of[9], (D, 2, D), D ** -0.5, 0.15625, ((2, 4),))
    crossout = centred(streams_of[10], (D, D), (D // 8) ** -0.5, 0.4375, ((0, 4),))
    feedgain = jnp.clip(1.0 + 0.1 * jax.random.normal(streams_of[11], (D,), jnp.float32), 0.5, 1.5)
    feedbias = centred(streams_of[12], (D,), 0.3, 1.5, (), jnp.float32)
    feedup = centred(streams_of[13], (D, FF), D ** -0.5, 0.15625, ((1, 4),))
    feeddown = centred(streams_of[14], (FF, D), FF ** -0.5, 0.078125, ((0, 4),))
    cotangent = centred(streams_of[15], (CLIPS, FRAMES, D), 1.0, 6.0, ((0, 8), (1, 4)), jnp.float32)
    return dict(frames=frames, text_states=text_states, selfgain=selfgain, selfbias=selfbias, selfqkv=selfqkv, selfout=selfout, crossgain=crossgain, crossbias=crossbias, crossquery=crossquery, crosskv=crosskv, crossout=crossout, feedgain=feedgain, feedbias=feedbias, feedup=feedup, feeddown=feeddown, cotangent=cotangent)


EPSILON = 1e-05
PRECISE = lax.Precision.HIGHEST

@jax.custom_vjp
def low(v):
    return lax.optimization_barrier(v.astype(jnp.bfloat16)).astype(jnp.float32)

@jax.custom_vjp
def low_back(v):
    return v

def low_keep(v):
    return (low(v), None)

def low_pass(kept, grad):
    return (grad,)

def back_keep(v):
    return (v, None)

def back_low(kept, grad):
    return (low(grad),)
low.defvjp(low_keep, low_pass)
low_back.defvjp(back_keep, back_low)

def layer_norm(values, gain_row, bias_row):
    centre = values - lax.optimization_barrier(jnp.mean(values, -1, keepdims=True))
    variance = lax.optimization_barrier(jnp.mean(centre * centre, -1, keepdims=True))
    return centre * lax.rsqrt(variance + EPSILON) * gain_row + bias_row

def matmul(left_side, right_side):
    return jnp.dot(left_side, right_side, precision=PRECISE)

def attend(queries, key_vals, value_vals, causal):
    total_rows = queries.shape[0]
    block_rows = min(512, total_rows)
    scaling = queries.shape[-1] ** (-0.5)
    key_pos = jnp.arange(key_vals.shape[0]).astype(jnp.int32)

    def one_block(offset):
        query_block = lax.dynamic_slice_in_dim(queries, offset, block_rows, 0)
        scores = jnp.einsum('qhd,khd->hqk', query_block, key_vals, precision=PRECISE) * scaling
        scores = low_back(scores)
        if causal:
            row_pos = offset + jnp.arange(block_rows).astype(jnp.int32)
            scores = jnp.where(key_pos[None, None, :] <= row_pos[None, :, None], scores, -1e+30)
        weights = jax.nn.softmax(scores, axis=-1)
        return jnp.einsum('hqk,khd->qhd', low(weights), value_vals, precision=PRECISE)
    offsets = (jnp.arange(total_rows // block_rows) * block_rows).astype(jnp.int32)
    result = lax.map(jax.checkpoint(one_block), offsets)
    return result.reshape(queries.shape)

def forward_clip(frame_vals, text_vals, params):
    selfgain, selfbias, selfqkv, selfout, crossgain, crossbias, crossquery, crosskv, crossout, feedgain, feedbias, feedup, feeddown = params
    length = frame_vals.shape[0]
    text_len = text_vals.shape[0]
    self_rows = low(layer_norm(frame_vals, selfgain, selfbias))
    triple = low_back(low(matmul(self_rows, selfqkv.reshape(D, 3 * D)))).reshape(length, 3, HEADS, HEAD)
    self_heads = low_back(low(attend(triple[:, 0], triple[:, 1], triple[:, 2], True))).reshape(length, D)
    after_self = frame_vals + low_back(matmul(self_heads, selfout))
    cross_rows = low(layer_norm(after_self, crossgain, crossbias))
    cross_queries = low_back(low(matmul(cross_rows, crossquery))).reshape(length, HEADS, HEAD)
    memory = low_back(low(matmul(text_vals, crosskv.reshape(D, 2 * D)))).reshape(text_len, 2, HEADS, HEAD)
    cross_heads = low_back(low(attend(cross_queries, memory[:, 0], memory[:, 1], False))).reshape(length, D)
    after_cross = after_self + low_back(matmul(cross_heads, crossout))
    feed_rows = low(layer_norm(after_cross, feedgain, feedbias))
    hidden_pre = low_back(matmul(feed_rows, feedup))
    hidden_act = low(jax.nn.gelu(hidden_pre, approximate=False))
    return after_cross + low_back(matmul(hidden_act, feeddown))

def reference(frames, text_states, selfgain, selfbias, selfqkv, selfout, crossgain, crossbias, crossquery, crosskv, crossout, feedgain, feedbias, feedup, feeddown, cotangent):
    frame_vals = frames.astype(jnp.float32)
    text_vals = text_states.astype(jnp.float32)
    params = tuple((array.astype(jnp.float32) for array in (selfgain, selfbias, selfqkv, selfout, crossgain, crossbias, crossquery, crosskv, crossout, feedgain, feedbias, feedup, feeddown)))

    def whole(frame_in, text_in, weights):

        def per_clip(pair):
            return forward_clip(pair[0], pair[1], weights)
        return lax.map(per_clip, (frame_in, text_in))
    outputs, pullback = jax.vjp(whole, frame_vals, text_vals, params)
    frame_grad, text_grad, grads = pullback(cotangent.astype(jnp.float32))
    return (outputs, frame_grad, text_grad, grads[0], grads[1], grads[2], grads[3], grads[4], grads[5], grads[6], grads[7], grads[8], grads[9], grads[10], grads[11], grads[12])
```

```python
from functools import partial

import jax
import jax.numpy as jnp
from jax import lax
from jax.experimental import pallas as pl
from jax.experimental.pallas import tpu as pltpu
from jax.sharding import PartitionSpec as P

HEAD = 64
EPSILON = 1e-05
NEG_BIG = -1e30
LOG2E = 1.4426950408889634
MESH = pl.DeviceIdType.MESH
F32 = jnp.float32
BF = jnp.bfloat16
ANY = pl.BlockSpec(memory_space=pl.ANY)
VMEM_LIMIT = 63 << 20


def neighbours():
    t = lax.axis_index("tensor")
    return t, t + 1 - 2 * (t % 2), (t + 2) % 4, 3 - t


def greet(targets):
    barrier = pltpu.get_barrier_semaphore()
    for target in targets:
        pl.semaphore_signal(barrier, inc=1, device_id=target, device_id_type=MESH)
    pl.semaphore_wait(barrier, len(targets))


def dot(a, b):
    return lax.dot_general(a, b, (((1,), (0,)), ((), ())), preferred_element_type=F32)


def dot_t(a, b):
    return lax.dot_general(a, b, (((1,), (1,)), ((), ())), preferred_element_type=F32)


def dot_c(a, b):
    return lax.dot_general(a, b, (((0,), (0,)), ((), ())), preferred_element_type=F32)


def cols(j, width):
    return pl.ds(pl.multiple_of(j * width, width), width)


def rows_at(j, height):
    return pl.ds(pl.multiple_of(j * height, height), height)


def split(count):
    first = (count // 2 + 15) // 16 * 16
    return pl.ds(0, first), pl.ds(first, count - first)


class Gather:
    def __init__(self, own, dst, send, recv, base, halves=None):
        self.own, self.dst, self.send, self.recv, self.base = own, dst, send, recv, base
        self.halves = halves or split(own.shape[0])

    def copy(self, k):
        t, x, y, _ = neighbours()
        first, second = self.halves
        half = (first, second, second, first, first, second)[k]
        place = (t, t, t, t, x, y)[k]
        target = (x, y, x, y, y, x)[k]
        source = self.own.at[half] if k < 4 else self.dst.at[place, half]
        return pltpu.make_async_remote_copy(
            source,
            self.dst.at[place, half],
            self.send.at[self.base + k],
            self.recv.at[self.base + k],
            device_id={"tensor": target},
            device_id_type=MESH,
        )

    def start(self):
        for k in range(4):
            self.copy(k).start()

    def relay_x(self):
        self.copy(0).wait_recv()
        self.copy(4).start()

    def relay_y(self):
        self.copy(1).wait_recv()
        self.copy(5).start()

    def have_x(self):
        self.copy(2).wait_recv()

    def have_y(self):
        self.copy(3).wait_recv()

    def have_d(self):
        self.copy(4).wait_recv()
        self.copy(5).wait_recv()

    def drain(self):
        for k in range(6):
            self.copy(k).wait_send()


class Scatter:
    def __init__(self, part, land, stage, send, recv, base):
        self.part, self.land, self.stage = part, land, stage
        self.send, self.recv, self.base = send, recv, base
        self.half = part.shape[1] // 2

    def copy(self, k):
        t, x, y, d = neighbours()
        low, high = pl.ds(0, self.half), pl.ds(self.half, self.half)
        source = (
            self.part.at[d, low],
            self.part.at[d, high],
            self.part.at[x, low],
            self.stage.at[1],
            self.part.at[y, high],
            self.stage.at[0],
        )[k]
        target = (x, y, x, x, y, y)[k]
        return pltpu.make_async_remote_copy(
            source,
            self.land.at[k],
            self.send.at[self.base + k],
            self.recv.at[self.base + k],
            device_id={"tensor": target},
            device_id_type=MESH,
        )

    def diagonal(self):
        self.copy(0).start()
        self.copy(1).start()

    def along_x(self):
        self.copy(2).start()

    def along_y(self):
        self.copy(4).start()

    def relay(self):
        t, x, y, d = neighbours()
        low, high = pl.ds(0, self.half), pl.ds(self.half, self.half)
        self.copy(0).wait_recv()
        self.stage[0] = (self.part[y, low].astype(F32) + self.land[0].astype(F32)).astype(BF)
        self.copy(5).start()
        self.copy(1).wait_recv()
        self.stage[1] = (self.part[x, high].astype(F32) + self.land[1].astype(F32)).astype(BF)
        self.copy(3).start()

    def finish(self, take, step):
        t, x, y, d = neighbours()
        for k in (2, 4, 5, 3):
            self.copy(k).wait_recv()
        for base, a, b in ((0, 2, 5), (self.half, 4, 3)):

            def block(i, carry, base=base, a=a, b=b):
                here = rows_at(i, step)
                rows = pl.ds(pl.multiple_of(base + i * step, step), step)
                take(
                    rows,
                    self.part[t, rows].astype(F32)
                    + self.land[a, here].astype(F32)
                    + self.land[b, here].astype(F32),
                )
                return carry

            lax.fori_loop(0, self.half // step, block, 0)

    def drain(self):
        for k in range(6):
            self.copy(k).wait_send()


def normed_rows(values):
    centre = values - jnp.mean(values, -1, keepdims=True)
    inverse = lax.rsqrt(jnp.mean(centre * centre, -1, keepdims=True) + EPSILON)
    return centre * inverse, inverse


def params(cid, **more):
    return pltpu.CompilerParams(
        collective_id=cid, has_side_effects=True, vmem_limit_bytes=VMEM_LIMIT, **more
    )


def dma(count):
    return pltpu.SemaphoreType.DMA((count,))


def shape(*dims, kind=BF):
    return jax.ShapeDtypeStruct(dims, kind)


def enter_kernel(
    frames, gain, bias, qkv, text, kv, o_rows, o_triple, o_memory,
    v_frames, v_gain, v_bias, v_qkv, v_text, v_kv, rows, triple, memory, load, store, send, recv,
):
    t, x, y, d = neighbours()
    loads = [
        pltpu.make_async_copy(a, b, load.at[i])
        for i, (a, b) in enumerate(
            ((frames, v_frames), (gain, v_gain), (bias, v_bias), (qkv, v_qkv), (text, v_text), (kv, v_kv))
        )
    ]
    for copy in loads:
        copy.start()
    greet([{"tensor": x}, {"tensor": y}])
    for copy in loads[:3]:
        copy.wait()
    count, width = v_qkv.shape
    block = 384

    def norm_block(i, carry):
        here = rows_at(i, 64)
        hat, _ = normed_rows(v_frames[here].astype(F32))
        rows[t, here] = (hat * v_gain[...] + v_bias[...]).astype(BF)
        return carry

    lax.fori_loop(0, v_frames.shape[0] // 64, norm_block, 0)
    gather = Gather(rows.at[t], rows, send, recv, 0)
    gather.start()
    texts = Gather(memory.at[t], memory, send, recv, 6)

    def project(place):
        def step(j, carry):
            triple[place, :, cols(j, block)] = dot(rows[place], v_qkv[:, cols(j, block)]).astype(BF)
            return carry

        lax.fori_loop(0, width // block, step, 0)

    def put(k, place):
        a = pltpu.make_async_copy(rows.at[place], o_rows.at[place], store.at[2 * k])
        b = pltpu.make_async_copy(triple.at[place], o_triple.at[place], store.at[2 * k + 1])
        a.start()
        b.start()
        return [a, b]

    loads[4].wait()
    loads[5].wait()

    def texts_step(j, carry):
        memory[t, :, cols(j, block)] = dot(v_text[...], v_kv[:, cols(j, block)]).astype(BF)
        return carry

    lax.fori_loop(0, v_kv.shape[1] // block, texts_step, 0)
    texts.start()
    loads[3].wait()
    project(t)
    stores = put(0, t)
    gather.relay_x()
    gather.relay_y()
    gather.have_x()
    project(x)
    stores += put(1, x)
    gather.have_y()
    project(y)
    stores += put(2, y)
    texts.relay_x()
    texts.relay_y()
    texts.have_x()
    texts.have_y()
    gather.have_d()
    project(d)
    stores += put(3, d)
    texts.have_d()
    last = pltpu.make_async_copy(memory, o_memory, store.at[8])
    last.start()
    gather.drain()
    texts.drain()
    for copy in stores:
        copy.wait()
    last.wait()


def enter(frames, gain, bias, qkv, text, kv):
    n, m = frames.shape
    width, texts, kvw = qkv.shape[1], text.shape[0], kv.shape[1]
    return pl.pallas_call(
        enter_kernel,
        name="enter",
        out_shape=[shape(4, n, m), shape(4, n, width), shape(4, texts, kvw)],
        in_specs=[ANY] * 6,
        out_specs=[ANY] * 3,
        scratch_shapes=[
            pltpu.VMEM((n, m), frames.dtype), pltpu.VMEM((1, m), F32), pltpu.VMEM((1, m), F32),
            pltpu.VMEM(qkv.shape, BF), pltpu.VMEM(text.shape, BF), pltpu.VMEM(kv.shape, BF),
            pltpu.VMEM((4, n, m), BF), pltpu.VMEM((4, n, width), BF), pltpu.VMEM((4, texts, kvw), BF),
            dma(6), dma(9), dma(12), dma(12),
        ],
        compiler_params=params(1),
    )(frames, gain, bias, qkv, text, kv)


def head_lanes(rows):
    return lax.broadcasted_iota(jnp.int32, (rows, 128), 1)


def attend_rows(triple, place, blocks, heads, flat, sums):
    n = triple.shape[1]
    width = heads * HEAD
    scale = HEAD ** (-0.5) * LOG2E
    lanes = head_lanes(n)

    def pair(p, stats):
        here = pl.ds(pl.multiple_of(p * 128, 128), 128)
        key_cols = pl.ds(pl.multiple_of(width + p * 128, 128), 128)
        value_cols = pl.ds(pl.multiple_of(2 * width + p * 128, 128), 128)
        query = triple[place, :, here]
        keys = triple[0:blocks, :, key_cols].reshape(blocks * n, 128)
        values = triple[0:blocks, :, value_cols].reshape(blocks * n, 128)
        outs = []
        for h in range(2):
            mine = (lanes < HEAD) if h == 0 else (lanes >= HEAD)
            scores = dot_t(jnp.where(mine, query, jnp.zeros_like(query)), keys)
            row = lax.broadcasted_iota(jnp.int32, scores.shape, 0)
            col = lax.broadcasted_iota(jnp.int32, scores.shape, 1)
            scores = jnp.where(col <= row + (blocks - 1) * n, scores, NEG_BIG)
            peak = jnp.max(scores, -1, keepdims=True) * scale
            exponent = jnp.exp2(scores * scale - peak)
            total = jnp.sum(exponent, -1, keepdims=True)
            outs.append(dot(exponent.astype(BF), values) / total)
            stats = jnp.where(lanes == 2 * p + h, peak + jnp.log2(total), stats)
        flat[place, :, here] = jnp.where(lanes < HEAD, outs[0], outs[1]).astype(BF)
        return stats

    sums[place] = lax.fori_loop(0, heads // 2, pair, jnp.zeros((n, 128), F32))


def attend_kernel(
    triple_in, out_in, frames_in, wq, wo, o_flat, o_sums, o_after, o_wq, o_wo,
    triple, v_out, v_frames, flat, sums, after, part, land, stage, v_wq, v_wo, load, store, send, recv, side,
):
    t, x, y, d = neighbours()
    s = lax.axis_index("sub")
    subs = lax.axis_size("sub")
    n = triple.shape[1]
    m = v_out.shape[1]
    heads = v_out.shape[0] // HEAD
    loads = [
        pltpu.make_async_copy(a, b, load.at[i])
        for i, (a, b) in enumerate(
            ((triple_in, triple), (out_in, v_out), (frames_in, v_frames), (wq, v_wq), (wo, v_wo))
        )
    ]
    for copy in loads:
        copy.start()
    greet(
        [{"tensor": x}, {"tensor": y}]
        + [{"sub": (s + k) % subs} for k in range(1, subs)]
    )
    scatter = Scatter(part, land, stage, send, recv, 0)
    gathers = []
    for i, (weight, full) in enumerate(((wq, o_wq), (wo, o_wo))):
        piece = weight.shape[0] // subs
        first, second = split(piece)
        offset = pl.multiple_of(s * piece, piece)
        halves = (
            pl.ds(offset, first.size),
            pl.ds(pl.multiple_of(offset + first.size, 16), second.size),
        )
        gathers.append((Gather(weight, full, send, recv, 6 + 6 * i, halves), full, pl.ds(offset, piece)))

    def shared(i, j, k):
        _, full, piece = gathers[i]
        place = (x, y, d)[j]
        slot = (i * 3 + j) * (subs - 1) + k - 1
        return pltpu.make_async_remote_copy(
            full.at[place, piece], full.at[place, piece],
            send.at[18 + slot], recv.at[18 + slot],
            device_id={"sub": (s + k) % subs}, device_id_type=MESH,
        )

    for gather, _, _ in gathers:
        gather.start()
    for copy in loads[:2]:
        copy.wait()

    def one(i, carry):
        far_y = 1 - i // 2
        far_x = 1 - i % 2
        place = (t // 2 + far_y - 2 * (t // 2) * far_y) * 2 + (t % 2 + far_x - 2 * (t % 2) * far_x)
        for blocks in range(1, 5):

            @pl.when(place == blocks - 1)
            def _(blocks=blocks):
                attend_rows(triple, blocks - 1, blocks, heads, flat, sums)

        def out_step(j, carry):
            part[place, :, cols(j, 512)] = dot(flat[place], v_out[:, cols(j, 512)]).astype(BF)
            return carry

        lax.fori_loop(0, m // 512, out_step, 0)

        @pl.when(i == 0)
        def _():
            scatter.diagonal()

        @pl.when(i == 1)
        def _():
            scatter.along_y()

        @pl.when(i == 2)
        def _():
            scatter.along_x()

        return carry

    lax.fori_loop(0, 4, one, 0)
    for gather, _, _ in gathers:
        gather.relay_x()
        gather.relay_y()
    stores = [
        pltpu.make_async_copy(flat, o_flat, store.at[0]),
        pltpu.make_async_copy(sums, o_sums, store.at[1]),
    ]
    loads[3].wait()
    loads[4].wait()
    stores += [
        pltpu.make_async_copy(v_wq, o_wq.at[t], store.at[2]),
        pltpu.make_async_copy(v_wo, o_wo.at[t], store.at[3]),
    ]
    for copy in stores:
        copy.start()
    scatter.relay()
    for i, (gather, _, _) in enumerate(gathers):
        gather.have_x()
        gather.have_y()
        gather.have_d()
        for j in range(3):
            for k in range(1, subs):
                shared(i, j, k).start()
    loads[2].wait()

    def take(rows, total):
        after[rows] = v_frames[rows].astype(F32) + total

    scatter.finish(take, 64)
    last = pltpu.make_async_copy(after, o_after, store.at[4])
    last.start()
    scatter.drain()
    for i, (gather, _, _) in enumerate(gathers):
        gather.drain()
        for j in range(3):
            for k in range(1, subs):
                shared(i, j, k).wait()
    for copy in stores:
        copy.wait()
    last.wait()


def attend(triple, out, frames, wq, wo, subs):
    _, n, width = triple.shape
    local, m = out.shape
    extra = 18 + 6 * (subs - 1)
    return pl.pallas_call(
        attend_kernel,
        name="attend",
        out_shape=[
            shape(4, n, local), shape(4, n, 128, kind=F32), shape(n, m, kind=F32),
            shape(4, *wq.shape), shape(4, *wo.shape),
        ],
        in_specs=[ANY] * 5,
        out_specs=[ANY] * 5,
        scratch_shapes=[
            pltpu.VMEM((4, n, width), BF), pltpu.VMEM((local, m), BF), pltpu.VMEM((n, m), frames.dtype),
            pltpu.VMEM((4, n, local), BF), pltpu.VMEM((4, n, 128), F32), pltpu.VMEM((n, m), F32),
            pltpu.VMEM((4, n, m), BF), pltpu.VMEM((6, n // 2, m), BF), pltpu.VMEM((2, n // 2, m), BF),
            pltpu.VMEM(wq.shape, BF), pltpu.VMEM(wo.shape, BF),
            dma(5), dma(5), dma(extra), dma(extra), dma(1),
        ],
        compiler_params=params(2),
    )(triple, out, frames, wq, wo)


def stack_pair(block, rows):
    lanes = head_lanes(rows)
    zero = jnp.zeros_like(block)
    return jnp.concatenate([jnp.where(lanes < HEAD, block, zero), jnp.where(lanes >= HEAD, block, zero)], 0)


def pair_softmax(query, keys):
    scale = HEAD ** (-0.5) * LOG2E
    scores = dot_t(query, keys)
    left = head_lanes(scores.shape[0]) < HEAD
    low = jnp.max(jnp.where(left, scores, -jnp.inf), -1, keepdims=True)
    high = jnp.max(jnp.where(left, -jnp.inf, scores), -1, keepdims=True)
    exponent = jnp.exp2((scores - jnp.where(left, low, high)) * scale)
    total = pair_sum(exponent, left)
    return exponent / total, left


def pair_sum(values, left):
    low = jnp.sum(jnp.where(left, values, 0.0), -1, keepdims=True)
    high = jnp.sum(jnp.where(left, 0.0, values), -1, keepdims=True)
    return jnp.where(left, low, high)


def cross_kernel(
    after_in, gains_in, wq_in, wo_in, memory_in, cot_in,
    o_query, o_flat, o_after, o_rows, o_grads,
    after, gains, wq, wo, memory, cot, rows, query, flat, result, feed, grads, load, store, send, recv,
):
    t, x, y, d = neighbours()
    loads = [
        pltpu.make_async_copy(a, b, load.at[i])
        for i, (a, b) in enumerate(
            ((cot_in, cot), (after_in, after), (gains_in, gains), (wq_in, wq), (memory_in, memory), (wo_in, wo))
        )
    ]
    for copy in loads:
        copy.start()
    greet([{"tensor": x}, {"tensor": y}])
    n, m = after.shape
    width = wq.shape[2]
    texts = memory.shape[1]
    loads[0].wait()

    def round_block(i, carry):
        here = rows_at(i, 64)
        grads[t, here] = cot[here].astype(BF)
        return carry

    lax.fori_loop(0, n // 64, round_block, 0)
    gather = Gather(grads.at[t], grads, send, recv, 0)
    gather.start()
    loads[1].wait()
    loads[2].wait()

    def norm_block(i, carry):
        here = rows_at(i, 64)
        hat, _ = normed_rows(after[here])
        rows[here] = (hat * gains[0:1] + gains[1:2]).astype(BF)
        return carry

    lax.fori_loop(0, n // 64, norm_block, 0)
    loads[3].wait()
    loads[4].wait()

    def quarter(q, carry):
        query[:, cols(q, width)] = dot(rows[...], wq[q]).astype(BF)

        def pair(p, carry):
            keys = stack_pair(memory[q, :, cols(p, 128)], texts)
            values = stack_pair(memory[q, :, pl.ds(pl.multiple_of(width + p * 128, 128), 128)], texts)
            here = pl.ds(pl.multiple_of(q * width + p * 128, 128), 128)
            probs, _ = pair_softmax(query[:, here], keys)
            flat[:, here] = dot(probs.astype(BF), values).astype(BF)
            return carry

        lax.fori_loop(0, width // 128, pair, 0)
        return carry

    lax.fori_loop(0, 4, quarter, 0)
    gather.relay_x()
    gather.relay_y()
    stores = [pltpu.make_async_copy(query, o_query, store.at[0]), pltpu.make_async_copy(flat, o_flat, store.at[1])]
    loads[5].wait()

    def out_step(j, carry):
        result[:, cols(j, 512)] = after[:, cols(j, 512)] + dot(flat[...], wo[:, cols(j, 512)])
        return carry

    lax.fori_loop(0, m // 512, out_step, 0)

    def feed_block(i, carry):
        here = rows_at(i, 64)
        hat, _ = normed_rows(result[here])
        feed[here] = (hat * gains[2:3] + gains[3:4]).astype(BF)
        return carry

    lax.fori_loop(0, n // 64, feed_block, 0)
    stores += [pltpu.make_async_copy(result, o_after, store.at[2]), pltpu.make_async_copy(feed, o_rows, store.at[3])]
    for copy in stores:
        copy.start()
    gather.have_x()
    gather.have_y()
    gather.have_d()
    last = pltpu.make_async_copy(grads, o_grads, store.at[4])
    last.start()
    gather.drain()
    for copy in stores:
        copy.wait()
    last.wait()


def cross(after, gains, wq, wo, memory, cot):
    n, m = after.shape
    return pl.pallas_call(
        cross_kernel,
        name="cross",
        out_shape=[shape(n, m), shape(n, m), shape(n, m, kind=F32), shape(n, m), shape(4, n, m)],
        in_specs=[ANY] * 6,
        out_specs=[ANY] * 5,
        scratch_shapes=[
            pltpu.VMEM((n, m), F32), pltpu.VMEM(gains.shape, F32), pltpu.VMEM(wq.shape, BF), pltpu.VMEM(wo.shape, BF),
            pltpu.VMEM(memory.shape, BF), pltpu.VMEM((n, m), F32), pltpu.VMEM((n, m), BF), pltpu.VMEM((n, m), BF),
            pltpu.VMEM((n, m), BF), pltpu.VMEM((n, m), F32), pltpu.VMEM((n, m), BF), pltpu.VMEM((4, n, m), BF),
            dma(6), dma(5), dma(6), dma(6),
        ],
        compiler_params=params(3),
    )(after, gains, wq, wo, memory, cot)


def gelu_both(pre):
    size = jnp.abs(pre) * 0.7071067811865476
    rate = 1.0 / (1.0 + 0.3275911 * size)
    bell = jnp.exp2(pre * pre * (-0.5 * LOG2E))
    series = rate * (
        0.254829592
        + rate * (-0.284496736 + rate * (1.421413741 + rate * (-1.453152027 + rate * 1.061405429)))
    )
    tail = 0.5 * series * bell
    gate = jnp.where(pre >= 0, 1.0 - tail, tail)
    return pre * gate, gate + pre * (0.3989422804014327 * bell)


class Halves:
    def __init__(self, whole, land, send, recv, base):
        self.whole, self.land, self.send, self.recv, self.base = whole, land, send, recv, base
        self.subs = lax.axis_size("sub")
        self.piece = whole.shape[1] // self.subs

    def copies(self, w):
        s = lax.axis_index("sub")
        made = []
        for k in range(1, self.subs):
            target = (s + k) % self.subs
            slot = w * (self.subs - 1) + k - 1
            made.append(
                pltpu.make_async_remote_copy(
                    self.whole.at[w, rows_at(target, self.piece)],
                    self.land.at[w, k - 1],
                    self.send.at[self.base + slot],
                    self.recv.at[self.base + slot],
                    device_id={"sub": target},
                    device_id_type=MESH,
                )
            )
        return made

    def start(self, w):
        for copy in self.copies(w):
            copy.start()

    def total(self, w, take, step):
        s = lax.axis_index("sub")
        for copy in self.copies(w):
            copy.wait_recv()

        def block(i, carry):
            here = rows_at(i, step)
            value = self.whole[w, pl.ds(pl.multiple_of(s * self.piece + i * step, step), step)].astype(F32)
            for k in range(1, self.subs):
                value = value + self.land[w, k - 1, here].astype(F32)
            take(here, value)
            return carry

        lax.fori_loop(0, self.piece // step, block, 0)

    def drain(self, w):
        for copy in self.copies(w):
            copy.wait_send()


def weight_grad(left, right, whole, w, halves, block):
    s = lax.axis_index("sub")
    subs = lax.axis_size("sub")
    total_rows = left.shape[0] * left.shape[1]
    count = whole.shape[1] // block
    begin = ((s + 1) % subs) * halves.piece // block

    def one(j, carry):
        b = (begin + j) % count
        turned = left[:, :, cols(b, block)].reshape(total_rows, block)

        def inner(i, carry):
            other = right[:, :, cols(i, 512)].reshape(total_rows, 512)
            whole[w, rows_at(b, block), cols(i, 512)] = dot_c(turned, other).astype(BF)
            return carry

        lax.fori_loop(0, whole.shape[2] // 512, inner, 0)
        return carry

    if subs == 2:
        lax.fori_loop(0, count // 2, one, 0)
        halves.start(w)
        lax.fori_loop(count // 2, count, one, 0)
    else:
        lax.fori_loop(0, count, one, 0)
        halves.start(w)


def feed_kernel(
    rows_in, grads_in, up_in, down_in, after_in, o_layer, o_norm, o_pieces,
    rows, grads, up, down, result, act, pre_grad, part_out, part_norm, land_out, land_norm, stage_out, stage_norm,
    whole, land_whole, load, store, send, recv,
):
    t, x, y, d = neighbours()
    s = lax.axis_index("sub")
    subs = lax.axis_size("sub")
    loads = [
        pltpu.make_async_copy(a, b, load.at[i])
        for i, (a, b) in enumerate(
            ((rows_in, rows.at[t]), (up_in, up), (grads_in, grads), (down_in, down), (after_in, result))
        )
    ]
    for copy in loads:
        copy.start()
    greet([{"tensor": x}, {"tensor": y}] + [{"sub": (s + k) % subs} for k in range(1, subs)])
    n, m = result.shape
    hidden = up.shape[1]
    loads[0].wait()
    gather = Gather(rows.at[t], rows, send, recv, 0)
    gather.start()
    back = Scatter(part_norm, land_norm, stage_norm, send, recv, 6)
    fore = Scatter(part_out, land_out, stage_out, send, recv, 12)
    halves = Halves(whole, land_whole, send, recv, 18)
    for copy in loads[1:4]:
        copy.wait()

    def work(place):
        def step(j, carry):
            here = cols(j, 256)
            value, slope = gelu_both(dot(rows[place], up[:, here]))
            act[place, :, here] = value.astype(BF)
            pre_grad[place, :, here] = (dot_t(grads[place], down[here]) * slope).astype(BF)
            return carry

        lax.fori_loop(0, hidden // 256, step, 0)

        def out_step(j, carry):
            part_norm[place, :, cols(j, 512)] = dot_t(pre_grad[place], up[rows_at(j, 512)]).astype(BF)
            part_out[place, :, cols(j, 512)] = dot(act[place], down[:, cols(j, 512)]).astype(BF)
            return carry

        lax.fori_loop(0, m // 512, out_step, 0)

    def turn(i, carry):
        far_y = i // 2
        far_x = i % 2
        place = (t // 2 + far_y - 2 * (t // 2) * far_y) * 2 + (t % 2 + far_x - 2 * (t % 2) * far_x)

        @pl.when(i == 1)
        def _():
            gather.relay_x()
            gather.relay_y()
            gather.have_x()

        @pl.when(i == 2)
        def _():
            gather.have_y()

        @pl.when(i == 3)
        def _():
            gather.have_d()

        work(place)

        @pl.when(i == 1)
        def _():
            back.along_x()

        @pl.when(i == 2)
        def _():
            back.along_y()

        @pl.when(i == 3)
        def _():
            back.diagonal()

        return carry

    lax.fori_loop(0, 4, turn, 0)
    fore.diagonal()
    fore.along_x()
    fore.along_y()
    weight_grad(act, grads, whole, 0, halves, 256)
    back.relay()
    weight_grad(rows, pre_grad, whole, 1, halves, 256)
    fore.relay()
    loads[4].wait()
    pieces = land_whole
    for w in range(2):

        def take(here, value, w=w):
            pieces[w, 0, here] = value.astype(BF)

        halves.total(w, take, 64)
    stores = [pltpu.make_async_copy(pieces.at[:, 0], o_pieces, store.at[0])]
    stores[0].start()

    def take_out(here, total):
        result[here] = result[here] + total

    norm_total = part_norm

    fore.finish(take_out, 64)
    stores.append(pltpu.make_async_copy(result, o_layer, store.at[1]))
    stores[1].start()

    def take_norm(here, total):
        norm_total[t, here] = total.astype(BF)

    back.finish(take_norm, 64)
    stores.append(pltpu.make_async_copy(norm_total.at[t], o_norm, store.at[2]))
    stores[2].start()
    gather.drain()
    back.drain()
    fore.drain()
    for w in range(2):
        halves.drain(w)
    for copy in stores:
        copy.wait()


def feed(rows, grads, up, down, after, subs):
    n, m = rows.shape
    hidden = up.shape[1]
    count = 18 + 2 * (subs - 1)
    return pl.pallas_call(
        feed_kernel,
        name="feed",
        out_shape=[shape(n, m, kind=F32), shape(n, m), shape(2, m // subs, hidden)],
        in_specs=[ANY] * 5,
        out_specs=[ANY] * 3,
        scratch_shapes=[
            pltpu.VMEM((4, n, m), BF), pltpu.VMEM((4, n, m), BF), pltpu.VMEM((m, hidden), BF), pltpu.VMEM((hidden, m), BF),
            pltpu.VMEM((n, m), F32), pltpu.VMEM((4, n, hidden), BF), pltpu.VMEM((4, n, hidden), BF),
            pltpu.VMEM((4, n, m), BF), pltpu.VMEM((4, n, m), BF),
            pltpu.VMEM((6, n // 2, m), BF), pltpu.VMEM((6, n // 2, m), BF),
            pltpu.VMEM((2, n // 2, m), BF), pltpu.VMEM((2, n // 2, m), BF),
            pltpu.VMEM((2, m, hidden), BF), pltpu.VMEM((2, subs - 1, m // subs, hidden), BF),
            dma(5), dma(3), dma(count), dma(count),
        ],
        compiler_params=params(4),
    )(rows, grads, up, down, after)


def norm_back_block(grad, source, gain):
    hat, inverse = normed_rows(source)
    scaled = grad * gain
    inner = scaled - jnp.mean(scaled, -1, keepdims=True) - hat * jnp.mean(scaled * hat, -1, keepdims=True)
    return inverse * inner, grad * hat


def fold(block):
    total = block[0:8]
    for i in range(1, block.shape[0] // 8):
        total = total + block[8 * i : 8 * i + 8]
    return total


def unstack(block):
    lanes = head_lanes(block.shape[0] // 2)
    return jnp.where(lanes < HEAD, block[: block.shape[0] // 2], block[block.shape[0] // 2 :])


def cross_back_kernel(
    cot_in, norm_in, cross_in, self_in, gains_in, query_in, flat_in, memory_in, wq_in, wo_in,
    o_out, o_branch, o_sums, o_memory, o_wq, o_wo,
    cot, norm, after_cross, after_self, gains, query, flat, memory, wq, wo,
    branch, rows, query_grad, memory_grad, sums, whole_q, whole_o, land_q, land_o, piece_q, piece_o,
    load, store, send, recv,
):
    s = lax.axis_index("sub")
    subs = lax.axis_size("sub")
    loads = [
        pltpu.make_async_copy(a, b, load.at[i])
        for i, (a, b) in enumerate(
            (
                (cot_in, cot), (norm_in, norm), (cross_in, after_cross), (gains_in, gains), (wo_in, wo),
                (query_in, query), (flat_in, flat), (memory_in, memory), (self_in, after_self), (wq_in, wq),
            )
        )
    ]
    for copy in loads:
        copy.start()
    greet([{"sub": (s + k) % subs} for k in range(1, subs)])
    n, m = cot.shape
    width = wq.shape[2]
    texts = memory.shape[1]
    for copy in loads[:4]:
        copy.wait()
    scale = HEAD ** (-0.5)

    def feed_block(i, carry):
        here = rows_at(i, 64)
        grad = norm[here].astype(F32)
        inner, terms = norm_back_block(grad, after_cross[here], gains[2:3])
        total = cot[here] + inner
        cot[here] = total
        branch[here] = total.astype(BF)
        return carry[0] + fold(terms), carry[1] + fold(grad)

    zero = jnp.zeros((8, m), F32)
    gain_sum, bias_sum = lax.fori_loop(0, n // 64, feed_block, (zero, zero))
    sums[0:8] = gain_sum
    sums[8:16] = bias_sum
    loads[8].wait()

    def norm_block(i, carry):
        here = rows_at(i, 64)
        hat, _ = normed_rows(after_self[here])
        rows[here] = (hat * gains[0:1] + gains[1:2]).astype(BF)
        return carry

    lax.fori_loop(0, n // 64, norm_block, 0)
    for copy in loads[4:8]:
        copy.wait()

    def quarter(q, carry):
        grad_heads = dot_t(branch[...], wo[rows_at(q, width)]).astype(BF)
        whole_q_cols = cols(q, width)
        query_grad_block = []
        for p in range(width // 128):
            lane = slice(p * 128, p * 128 + 128)
            keys = stack_pair(memory[q, :, lane], texts)
            values = stack_pair(memory[q, :, width + p * 128 : width + p * 128 + 128], texts)
            here = pl.ds(pl.multiple_of(q * width + p * 128, 128), 128)
            grad = grad_heads[:, lane]
            ask = query[:, here]
            probs, left = pair_softmax(ask, keys)
            grad_probs = dot_t(grad, values)
            centred = pair_sum(grad_probs * probs, left)
            grad_scores = (probs * (grad_probs - centred)).astype(BF)
            query_grad[:, here] = (dot(grad_scores, keys) * scale).astype(BF)
            memory_grad[q, :, lane] = unstack(dot_c(grad_scores, ask) * scale).astype(BF)
            memory_grad[q, :, width + p * 128 : width + p * 128 + 128] = unstack(
                dot_c(probs.astype(BF), grad)
            ).astype(BF)
        return carry

    lax.fori_loop(0, 4, quarter, 0)
    stores = [pltpu.make_async_copy(memory_grad, o_memory, store.at[0])]
    stores[0].start()
    halves_q = Halves(whole_q, land_q, send, recv, 0)
    halves_o = Halves(whole_o, land_o, send, recv, 4 * (subs - 1))

    def weights(q, carry):
        def grad_o(j, carry):
            whole_o[q, :, cols(j, 512)] = dot_c(flat[:, cols(q, width)], branch[:, cols(j, 512)]).astype(BF)
            return carry

        lax.fori_loop(0, m // 512, grad_o, 0)

        def grad_q(j, carry):
            whole_q[q, rows_at(j, 256)] = dot_c(rows[:, cols(j, 256)], query_grad[:, cols(q, width)]).astype(BF)
            return carry

        lax.fori_loop(0, m // 256, grad_q, 0)
        return carry

    lax.fori_loop(0, 4, weights, 0)
    for q in range(4):
        halves_q.start(q)
        halves_o.start(q)
    loads[9].wait()

    def norm_grad(j, carry):
        here = rows_at(j, 256)
        total = jnp.zeros((n, 256), F32)
        for q in range(4):
            total = total + dot_t(query_grad[:, q * width : (q + 1) * width], wq[q, here])
        after_cross[:, cols(j, 256)] = total
        return carry

    lax.fori_loop(0, m // 256, norm_grad, 0)

    def self_block(i, carry):
        here = rows_at(i, 64)
        grad = after_cross[here]
        inner, terms = norm_back_block(grad, after_self[here], gains[0:1])
        total = cot[here] + inner
        cot[here] = total
        branch[here] = total.astype(BF)
        return carry[0] + fold(terms), carry[1] + fold(grad)

    gain_sum, bias_sum = lax.fori_loop(0, n // 64, self_block, (zero, zero))
    sums[16:24] = gain_sum
    sums[24:32] = bias_sum
    stores += [
        pltpu.make_async_copy(cot, o_out, store.at[1]),
        pltpu.make_async_copy(branch, o_branch, store.at[2]),
        pltpu.make_async_copy(sums, o_sums, store.at[3]),
    ]
    for copy in stores[1:]:
        copy.start()
    for halves, piece in ((halves_q, piece_q), (halves_o, piece_o)):
        for q in range(4):

            def take(here, value, q=q, piece=piece):
                piece[q, here] = value.astype(BF)

            halves.total(q, take, 16)
    stores += [pltpu.make_async_copy(piece_q, o_wq, store.at[4]), pltpu.make_async_copy(piece_o, o_wo, store.at[5])]
    for copy in stores[4:]:
        copy.start()
    for q in range(4):
        halves_q.drain(q)
        halves_o.drain(q)
    for copy in stores:
        copy.wait()


def cross_back(cot, norm, after_cross, after_self, gains, query, flat, memory, wq, wo, subs):
    n, m = cot.shape
    width = wq.shape[2]
    count = 8 * (subs - 1)
    part_q, part_o = (4, m // subs, width), (4, width // subs, m)
    return pl.pallas_call(
        cross_back_kernel,
        name="cross_back",
        out_shape=[
            shape(n, m, kind=F32), shape(n, m), shape(32, m, kind=F32), shape(*memory.shape), shape(*part_q), shape(*part_o),
        ],
        in_specs=[ANY] * 10,
        out_specs=[ANY] * 6,
        scratch_shapes=[
            pltpu.VMEM((n, m), F32), pltpu.VMEM((n, m), BF), pltpu.VMEM((n, m), F32), pltpu.VMEM((n, m), F32),
            pltpu.VMEM(gains.shape, F32), pltpu.VMEM((n, m), BF), pltpu.VMEM((n, m), BF), pltpu.VMEM(memory.shape, BF),
            pltpu.VMEM(wq.shape, BF), pltpu.VMEM(wo.shape, BF),
            pltpu.VMEM((n, m), BF), pltpu.VMEM((n, m), BF), pltpu.VMEM((n, m), BF), pltpu.VMEM(memory.shape, BF),
            pltpu.VMEM((32, m), F32), pltpu.VMEM((4, m, width), BF), pltpu.VMEM((4, width, m), BF),
            pltpu.VMEM((4, subs - 1, m // subs, width), BF), pltpu.VMEM((4, subs - 1, width // subs, m), BF),
            pltpu.VMEM(part_q, BF), pltpu.VMEM(part_o, BF),
            dma(10), dma(6), dma(count), dma(count),
        ],
        compiler_params=params(5),
    )(cot, norm, after_cross, after_self, gains, query, flat, memory, wq, wo)


def attend_rows_back(triple, place, blocks, heads, grad_heads, deltas, sums, grads, grad_keys, grad_values):
    n = triple.shape[1]
    width = heads * HEAD
    scale = HEAD ** (-0.5)
    lanes = head_lanes(n)
    key_lanes = head_lanes(blocks * n)

    def pair(p, carry):
        here = pl.ds(pl.multiple_of(p * 128, 128), 128)
        key_cols = pl.ds(pl.multiple_of(width + p * 128, 128), 128)
        value_cols = pl.ds(pl.multiple_of(2 * width + p * 128, 128), 128)
        query = triple[place, :, here]
        grad = grad_heads[place, :, here]
        keys = triple[0:blocks, :, key_cols].reshape(blocks * n, 128)
        values = triple[0:blocks, :, value_cols].reshape(blocks * n, 128)
        stats = sums[place]
        means = deltas[place]
        found = []
        for h in range(2):
            mine = (lanes < HEAD) if h == 0 else (lanes >= HEAD)
            log_sum = jnp.sum(jnp.where(lanes == 2 * p + h, stats, 0.0), -1, keepdims=True)
            delta = jnp.sum(jnp.where(lanes == 2 * p + h, means, 0.0), -1, keepdims=True)
            scores = dot_t(jnp.where(mine, query, jnp.zeros_like(query)), keys)
            row = lax.broadcasted_iota(jnp.int32, scores.shape, 0)
            col = lax.broadcasted_iota(jnp.int32, scores.shape, 1)
            probs = jnp.where(
                col <= row + (blocks - 1) * n, jnp.exp2(scores * (scale * LOG2E) - log_sum), 0.0
            )
            grad_probs = dot_t(jnp.where(mine, grad, jnp.zeros_like(grad)), values)
            grad_scores = (probs * (grad_probs - delta)).astype(BF)
            found.append((dot(grad_scores, keys), dot_c(grad_scores, query), dot_c(probs.astype(BF), grad)))
        grads[place, :, here] = (jnp.where(lanes < HEAD, found[0][0], found[1][0]) * scale).astype(BF)
        grad_keys[0 : blocks * n, here] += jnp.where(key_lanes < HEAD, found[0][1], found[1][1]) * scale
        grad_values[0 : blocks * n, here] += jnp.where(key_lanes < HEAD, found[0][2], found[1][2])
        return carry

    lax.fori_loop(0, heads // 2, pair, 0)


def attend_back_kernel(
    branch_in, triple_in, flat_in, sums_in, out_in, qkv_in, rows_in, frames_in, gains_in, grad_in, memory_in, text_in, kv_in,
    cross_q_in, cross_o_in,
    o_frames, o_sums, o_text, o_qkv, o_out, o_kv, o_cq, o_co,
    branch, triple, flat, sums, out, qkv, rows, frames, gains, grad_out, memory, text, kv,
    cross_q, cross_o, land_q, land_o, land_m, stage_q, stage_o, stage_m,
    grad_heads, deltas, grads, grad_keys, grad_values, part, land, stage, whole_qkv, land_qkv, whole_out, land_out,
    whole_kv, land_kv, text_grad, sums_out, sum_m,
    load, store, send, recv,
):
    t, x, y, d = neighbours()
    s = lax.axis_index("sub")
    subs = lax.axis_size("sub")
    names = (
        (branch_in, branch.at[t]), (out_in, out), (flat_in, flat), (triple_in, triple), (sums_in, sums),
        (memory_in, memory), (cross_q_in, cross_q), (cross_o_in, cross_o), (qkv_in, qkv), (rows_in, rows),
        (text_in, text), (kv_in, kv), (frames_in, frames), (gains_in, gains), (grad_in, grad_out),
    )
    loads = [pltpu.make_async_copy(a, b, load.at[i]) for i, (a, b) in enumerate(names)]
    for copy in loads:
        copy.start()
    greet([{"tensor": x}, {"tensor": y}] + [{"sub": (s + k) % subs} for k in range(1, subs)])
    n, m = grad_out.shape
    width = triple.shape[2]
    local = out.shape[0]
    heads = local // HEAD
    gather = Gather(branch.at[t], branch, send, recv, 0)
    scatter = Scatter(part, land, stage, send, recv, 6)
    scatter_m = Scatter(memory, land_m, stage_m, send, recv, 12)
    scatter_q = Scatter(cross_q, land_q, stage_q, send, recv, 18)
    scatter_o = Scatter(cross_o, land_o, stage_o, send, recv, 24)
    halves_qkv = Halves(whole_qkv, land_qkv, send, recv, 30)
    halves_out = Halves(whole_out, land_out, send, recv, 30 + subs - 1)
    halves_kv = Halves(whole_kv, land_kv, send, recv, 30 + 2 * (subs - 1))
    loads[0].wait()
    gather.start()
    for copy in loads[5:8]:
        copy.wait()
    for each in (scatter_m, scatter_q, scatter_o):
        each.diagonal()
        each.along_x()
        each.along_y()
    for copy in loads[1:5]:
        copy.wait()
    grad_keys[...] = jnp.zeros_like(grad_keys)
    grad_values[...] = jnp.zeros_like(grad_values)
    lanes = head_lanes(n)

    def turn(i, carry):
        far_y = i // 2
        far_x = i % 2
        place = (t // 2 + far_y - 2 * (t // 2) * far_y) * 2 + (t % 2 + far_x - 2 * (t % 2) * far_x)

        @pl.when(i == 1)
        def _():
            gather.relay_x()
            gather.relay_y()
            gather.have_x()

        @pl.when(i == 2)
        def _():
            gather.have_y()

        @pl.when(i == 3)
        def _():
            gather.have_d()

        grad_heads[place] = dot_t(branch[place], out[...]).astype(BF)

        def delta(p, stats):
            here = pl.ds(pl.multiple_of(p * 128, 128), 128)
            product = grad_heads[place, :, here].astype(F32) * flat[place, :, here].astype(F32)
            low = jnp.sum(jnp.where(lanes < HEAD, product, 0.0), -1, keepdims=True)
            high = jnp.sum(jnp.where(lanes < HEAD, 0.0, product), -1, keepdims=True)
            return jnp.where(lanes == 2 * p, low, jnp.where(lanes == 2 * p + 1, high, stats))

        deltas[place] = lax.fori_loop(0, heads // 2, delta, jnp.zeros((n, 128), F32))
        for blocks in range(1, 5):

            @pl.when(place == blocks - 1)
            def _(blocks=blocks):
                attend_rows_back(
                    triple, blocks - 1, blocks, heads, grad_heads, deltas, sums, grads, grad_keys, grad_values
                )

        return carry

    lax.fori_loop(0, 4, turn, 0)
    for copy in loads[8:12]:
        copy.wait()

    def finish_grads(i, carry):
        grads[i, :, local : 2 * local] = grad_keys[rows_at(i, n)].astype(BF)
        grads[i, :, 2 * local :] = grad_values[rows_at(i, n)].astype(BF)
        return carry

    lax.fori_loop(0, 4, finish_grads, 0)

    def back(i, carry):
        far_y = 1 - i // 2
        far_x = 1 - i % 2
        place = (t // 2 + far_y - 2 * (t // 2) * far_y) * 2 + (t % 2 + far_x - 2 * (t % 2) * far_x)

        def step(j, carry):
            part[place, :, cols(j, 512)] = dot_t(grads[place], qkv[rows_at(j, 512)]).astype(BF)
            return carry

        lax.fori_loop(0, m // 512, step, 0)

        @pl.when(i == 0)
        def _():
            scatter.diagonal()

        @pl.when(i == 1)
        def _():
            scatter.along_y()

        @pl.when(i == 2)
        def _():
            scatter.along_x()

        return carry

    lax.fori_loop(0, 4, back, 0)
    for each in (scatter_m, scatter_q, scatter_o):
        each.relay()

    def take_m(here, total):
        sum_m[here] = total.astype(BF)

    scatter_m.finish(take_m, 16)
    text_grad[...] = dot_t(sum_m[...], kv[...])
    stores = [pltpu.make_async_copy(text_grad, o_text, store.at[0])]
    stores[0].start()

    def grad_kv(j, carry):
        whole_kv[0, rows_at(j, 384)] = dot_c(text[:, cols(j, 384)], sum_m[...]).astype(BF)
        return carry

    lax.fori_loop(0, m // 384, grad_kv, 0)
    halves_kv.start(0)

    def grad_wout(j, carry):
        whole_out[0, :, cols(j, 512)] = dot_c(
            flat[...].reshape(4 * n, local), branch[:, :, cols(j, 512)].reshape(4 * n, 512)
        ).astype(BF)
        return carry

    lax.fori_loop(0, m // 512, grad_wout, 0)
    halves_out.start(0)
    scatter.relay()

    def grad_wqkv(j, carry):
        turned = rows[:, :, cols(j, 256)].reshape(4 * n, 256)

        def inner(i, carry):
            whole_qkv[0, rows_at(j, 256), cols(i, 384)] = dot_c(
                turned, grads[:, :, cols(i, 384)].reshape(4 * n, 384)
            ).astype(BF)
            return carry

        lax.fori_loop(0, width // 384, inner, 0)
        return carry

    lax.fori_loop(0, m // 256, grad_wqkv, 0)
    halves_qkv.start(0)
    for each, landed, output, slot in ((scatter_q, land_q, o_cq, 1), (scatter_o, land_o, o_co, 2)):
        half = each.half

        def take(here, total, each=each):
            each.part[t, here] = total.astype(BF)

        each.finish(take, 16)
        stores.append(pltpu.make_async_copy(each.part.at[t], output, store.at[slot]))
        stores[-1].start()
    for each, output, slot in ((halves_kv, o_kv, 3), (halves_out, o_out, 4), (halves_qkv, o_qkv, 5)):

        def take(here, total, each=each):
            each.land[0, 0, here] = total.astype(BF)

        each.total(0, take, 16)
        stores.append(pltpu.make_async_copy(each.land.at[0, 0], output, store.at[slot]))
        stores[-1].start()
    for copy in loads[12:]:
        copy.wait()

    def take_norm(here, total):
        part[t, here] = total.astype(BF)

    scatter.finish(take_norm, 64)

    def frame_block(i, carry):
        here = rows_at(i, 64)
        grad = part[t, here].astype(F32)
        inner, terms = norm_back_block(grad, frames[here].astype(F32), gains[0:1])
        grad_out[here] = grad_out[here] + inner
        return carry[0] + fold(terms), carry[1] + fold(grad)

    zero = jnp.zeros((8, m), F32)
    gain_sum, bias_sum = lax.fori_loop(0, n // 64, frame_block, (zero, zero))
    sums_out[0:8] = gain_sum
    sums_out[8:16] = bias_sum
    stores += [pltpu.make_async_copy(grad_out, o_frames, store.at[6]), pltpu.make_async_copy(sums_out, o_sums, store.at[7])]
    for copy in stores[-2:]:
        copy.start()
    gather.drain()
    for each in (scatter, scatter_m, scatter_q, scatter_o):
        each.drain()
    for each in (halves_qkv, halves_out, halves_kv):
        each.drain(0)
    for copy in stores:
        copy.wait()


def attend_back(branch, triple, flat, sums, out, qkv, rows, frames, gains, grad, memory, text, kv, cross_q, cross_o, subs):
    n, m = grad.shape
    width = triple.shape[2]
    local = out.shape[0]
    texts, kvw = text.shape[0], kv.shape[1]
    count = 30 + 3 * (subs - 1)
    piece_q, piece_o = cross_q.shape[1:], cross_o.shape[1:]
    v = pltpu.VMEM
    return pl.pallas_call(
        attend_back_kernel,
        name="attend_back",
        out_shape=[
            shape(n, m, kind=F32), shape(16, m, kind=F32), shape(texts, m, kind=F32), shape(m // subs, width),
            shape(local // subs, m), shape(m // subs, kvw), shape(*piece_q), shape(*piece_o),
        ],
        in_specs=[ANY] * 15,
        out_specs=[ANY] * 8,
        scratch_shapes=[
            v((4, n, m), BF), v(triple.shape, BF), v(flat.shape, BF), v(sums.shape, F32), v(out.shape, BF), v(qkv.shape, BF),
            v(rows.shape, BF), v(frames.shape, frames.dtype), v(gains.shape, F32), v((n, m), F32), v(memory.shape, BF),
            v(text.shape, BF), v(kv.shape, BF),
            v(cross_q.shape, BF), v(cross_o.shape, BF),
            v((6, piece_q[0] // 2, piece_q[1]), BF), v((6, piece_o[0] // 2, piece_o[1]), BF), v((6, texts // 2, kvw), BF),
            v((2, piece_q[0] // 2, piece_q[1]), BF), v((2, piece_o[0] // 2, piece_o[1]), BF), v((2, texts // 2, kvw), BF),
            v((4, n, local), BF), v((4, n, 128), F32), v((4, n, width), BF), v((4 * n, local), F32), v((4 * n, local), F32),
            v((4, n, m), BF), v((6, n // 2, m), BF), v((2, n // 2, m), BF),
            v((1, m, width), BF), v((1, subs - 1, m // subs, width), BF),
            v((1, local, m), BF), v((1, subs - 1, local // subs, m), BF),
            v((1, m, kvw), BF), v((1, subs - 1, m // subs, kvw), BF),
            v((texts, m), F32), v((16, m), F32), v((texts, kvw), BF),
            dma(15), dma(8), dma(count), dma(count),
        ],
        compiler_params=params(6),
    )(branch, triple, flat, sums, out, qkv, rows, frames, gains, grad, memory, text, kv, cross_q, cross_o)


def total_kernel(
    feed_in, qkv_in, cq_in, kv_in, out_in, co_in, sums_a_in, sums_b_in, text_in,
    o_up, o_down, o_qkv, o_cq, o_kv, o_out, o_co, o_text, o_vectors,
    own, from_left, from_right, to_right, to_left, result, sums_a, sums_b, text, text_land, text_full, vectors, vectors_land, share,
    share_land, load, store, send_right, recv_right, send_left, recv_left, send, recv,
):
    t, x, y, d = neighbours()
    s, subs = lax.axis_index("sub"), lax.axis_size("sub")
    g, groups = lax.axis_index("group"), lax.axis_size("group")
    chunk = result.shape[1]
    m = own.shape[1]
    width, cq_width, kv_width = qkv_in.shape[1], cq_in.shape[1], kv_in.shape[1]
    piece, kv_rows, out_rows = feed_in.shape[1], kv_in.shape[0] // 2, out_in.shape[0]
    start_qkv = 2 * piece
    start_kv = start_qkv + qkv_in.shape[0]
    start_out = start_kv + kv_rows
    start_co = start_out + out_rows
    count = own.shape[0] // chunk
    loads = [
        pltpu.make_async_copy(a, b, load.at[i])
        for i, (a, b) in enumerate(
            (
                (feed_in.at[0], own.at[pl.ds(0, piece)]),
                (feed_in.at[1], own.at[pl.ds(piece, piece)]),
                (qkv_in, own.at[pl.ds(start_qkv, piece), pl.ds(0, width)]),
                (cq_in, own.at[pl.ds(start_qkv, piece), pl.ds(width, cq_width)]),
                (kv_in.at[pl.ds(0, kv_rows)], own.at[pl.ds(start_kv, kv_rows), pl.ds(0, kv_width)]),
                (kv_in.at[pl.ds(kv_rows, kv_rows)], own.at[pl.ds(start_kv, kv_rows), pl.ds(kv_width, kv_width)]),
                (out_in, own.at[pl.ds(start_out, out_rows)]),
                (co_in, own.at[pl.ds(start_co, out_rows)]),
                (sums_a_in, sums_a),
                (sums_b_in, sums_b),
                (text_in, text),
            )
        )
    ]
    for copy in loads:
        copy.start()
    greet(
        [{"tensor": x}, {"tensor": y}, {"tensor": d}]
        + [{"sub": (s + k) % subs} for k in range(1, subs)]
        + [{"group": (g + k) % groups} for k in range(1, groups)]
    )
    for copy in loads:
        copy.wait()
    share_width = m // subs
    for i in range(6):
        source, at = (sums_a, i) if i < 4 else (sums_b, i - 4)
        row = jnp.sum(source[8 * at : 8 * at + 8], 0, keepdims=True)
        for j in range(subs):
            vectors[j, i : i + 1] = row[:, j * share_width : (j + 1) * share_width]
    strip = text.shape[0] // 4

    def remote(source, target, k, device):
        return pltpu.make_async_remote_copy(
            source, target, send.at[k], recv.at[k], device_id=device, device_id_type=MESH
        )

    square = (x, y, d)
    first = [remote(vectors, vectors_land.at[k], k, {"tensor": square[k]}) for k in range(3)]
    first += [
        remote(text.at[rows_at(square[k], strip)], text_land.at[k], 3 + k, {"tensor": square[k]}) for k in range(3)
    ]
    second = [
        remote(share.at[0, (s + k) % subs], share_land.at[k - 1], 5 + k, {"sub": (s + k) % subs}) for k in range(1, subs)
    ]
    base = 5 + subs
    second += [
        remote(text_full.at[rows_at(t, strip)], text_full.at[rows_at(t, strip)], base + k, {"tensor": square[k]}) for k in range(3)
    ]
    base += 3
    third = [
        remote(share.at[1, 0], share_land.at[subs - 2 + k], base + k - 1, {"group": (g + k) % groups})
        for k in range(1, groups)
    ]
    for copy in first:
        copy.start()

    def right(c):
        return pltpu.make_async_remote_copy(
            to_right.at[c % 4], from_left.at[c], send_right.at[c % 4], recv_right.at[c],
            device_id={"group": (g + 1) % groups}, device_id_type=MESH,
        )

    def left(c):
        return pltpu.make_async_remote_copy(
            to_left.at[c % 4], from_right.at[c], send_left.at[c % 4], recv_left.at[c],
            device_id={"group": (g + groups - 1) % groups}, device_id_type=MESH,
        )

    def outputs(c, act):
        row = c * chunk
        slot = c % 4
        block = result.at[slot]

        def region(begin, end, copies):
            @pl.when(jnp.logical_and(row >= begin, row < end))
            def _():
                for i, (source, target) in enumerate(copies(pl.multiple_of(row - begin, chunk))):
                    act(pltpu.make_async_copy(source, target, store.at[2 * slot + i]))

        def whole(output):
            return lambda at: [(block, output.at[pl.ds(at, chunk)])]

        region(0, piece, whole(o_down))
        region(piece, start_qkv, whole(o_up))
        region(
            start_qkv, start_kv,
            lambda at: [
                (block.at[:, pl.ds(0, width)], o_qkv.at[pl.ds(at, chunk)]),
                (block.at[:, pl.ds(width, cq_width)], o_cq.at[pl.ds(at, chunk)]),
            ],
        )
        region(
            start_kv, start_out,
            lambda at: [
                (block.at[:, pl.ds(0, kv_width)], o_kv.at[pl.ds(at, chunk)]),
                (
                    block.at[:, pl.ds(kv_width, kv_width)],
                    o_kv.at[pl.ds(pl.multiple_of(kv_rows + at, chunk), chunk)],
                ),
            ],
        )
        region(start_out, start_co, whole(o_out))
        region(start_co, start_co + out_rows, whole(o_co))

    lag = 2
    far = jnp.maximum(g, groups - 1 - g)

    def step(k, carry):
        c = k - lag * g

        @pl.when(jnp.logical_and(c >= 0, c < count))
        def _():
            @pl.when(g > 0)
            def _():
                right(c).wait_recv()

            @pl.when(g < groups - 1)
            def _():
                @pl.when(c >= 4)
                def _():
                    right(c - 4).wait_send()

                mine = own[rows_at(c, chunk)]

                @pl.when(g > 0)
                def _():
                    to_right[c % 4] = (mine.astype(F32) + from_left[c].astype(F32)).astype(BF)

                @pl.when(g == 0)
                def _():
                    to_right[c % 4] = mine

                right(c).start()

        e = k - lag * (groups - 1 - g)

        @pl.when(jnp.logical_and(e >= 0, e < count))
        def _():
            @pl.when(g < groups - 1)
            def _():
                left(e).wait_recv()

            @pl.when(g > 0)
            def _():
                @pl.when(e >= 4)
                def _():
                    left(e - 4).wait_send()

                mine = own[rows_at(e, chunk)]

                @pl.when(g < groups - 1)
                def _():
                    to_left[e % 4] = (mine.astype(F32) + from_right[e].astype(F32)).astype(BF)

                @pl.when(g == groups - 1)
                def _():
                    to_left[e % 4] = mine

                left(e).start()

        f = k - lag * far

        @pl.when(jnp.logical_and(f >= 0, f < count))
        def _():
            @pl.when(f >= 4)
            def _():
                outputs(f - 4, lambda copy: copy.wait())

            mine = own[rows_at(f, chunk)].astype(F32)

            @pl.when(jnp.logical_and(g > 0, g < groups - 1))
            def _():
                result[f % 4] = mine + from_left[f].astype(F32) + from_right[f].astype(F32)

            @pl.when(g == 0)
            def _():
                result[f % 4] = mine + from_right[f].astype(F32)

            @pl.when(g == groups - 1)
            def _():
                result[f % 4] = mine + from_left[f].astype(F32)

            outputs(f, lambda copy: copy.start())

        return carry

    steps = count + lag * (groups - 1)
    lax.fori_loop(0, 3, step, 0)
    for copy in first:
        copy.wait_recv()
    for j in range(subs):
        share[0, j] = vectors[j] + vectors_land[0, j] + vectors_land[1, j] + vectors_land[2, j]
    text_full[rows_at(t, strip)] = text[rows_at(t, strip)] + text_land[0] + text_land[1] + text_land[2]
    for copy in first:
        copy.wait_send()
    for copy in second:
        copy.start()
    lax.fori_loop(3, 6, step, 0)
    for copy in second:
        copy.wait_recv()
    total = share[0, s]
    for k in range(1, subs):
        total = total + share_land[k - 1]
    share[1, 0] = total
    text_store = pltpu.make_async_copy(text_full, o_text, store.at[8])
    text_store.start()
    for copy in third:
        copy.start()
    lax.fori_loop(6, steps, step, 0)
    for copy in third:
        copy.wait_recv()
    total = share[1, 0]
    for k in range(1, groups):
        total = total + share_land[subs - 2 + k]
    share[2, 0] = total
    vector_store = pltpu.make_async_copy(share.at[2, 0], o_vectors, store.at[9])
    vector_store.start()
    for copy in second + third:
        copy.wait_send()

    @pl.when(g < groups - 1)
    def _():
        for i in range(4):
            right(count - 4 + i).wait_send()

    @pl.when(g > 0)
    def _():
        for i in range(4):
            left(count - 4 + i).wait_send()

    for i in range(4):
        outputs(count - 4 + i, lambda copy: copy.wait())
    text_store.wait()
    vector_store.wait()


def total(pieces, qkv, cq, kv, out, co, sums_a, sums_b, text, subs, groups):
    _, piece, m = pieces.shape
    rows = 2 * piece + qkv.shape[0] + kv.shape[0] // 2 + out.shape[0] + co.shape[0]
    chunk = 96 if out.shape[0] % 96 == 0 else 48
    count = rows // chunk
    v = pltpu.VMEM
    sems = 8 + subs + groups
    return pl.pallas_call(
        total_kernel,
        name="total",
        out_shape=[shape(*dims, kind=F32) for dims in (
            (piece, m), (piece, m), qkv.shape, cq.shape, kv.shape, out.shape, co.shape, text.shape, (8, m // subs),
        )],
        in_specs=[ANY] * 9,
        out_specs=[ANY] * 9,
        scratch_shapes=[
            v((rows, m), BF), v((count, chunk, m), BF), v((count, chunk, m), BF), v((4, chunk, m), BF), v((4, chunk, m), BF),
            v((4, chunk, m), F32), v(sums_a.shape, F32), v(sums_b.shape, F32), v(text.shape, F32),
            v((3, text.shape[0] // 4, m), F32), v(text.shape, F32), v((subs, 8, m // subs), F32), v((3, subs, 8, m // subs), F32),
            v((3, subs, 8, m // subs), F32), v((subs - 1 + groups - 1, 8, m // subs), F32),
            dma(11), dma(10), dma(4), dma(count), dma(4), dma(count), dma(sems), dma(sems),
        ],
        compiler_params=params(7),
    )(pieces, qkv, cq, kv, out, co, sums_a, sums_b, text)


def local(
    frames, text_states, selfgain, selfbias, selfqkv, selfout, crossgain, crossbias, crossquery, crosskv, crossout,
    feedgain, feedbias, feedup, feeddown, cotangent,
):
    subs, groups = lax.axis_size("sub"), lax.axis_size("group")
    m = frames.shape[2]
    width = selfout.shape[0]
    qkv = selfqkv.reshape(m, 3 * width)
    kv = crosskv.reshape(m, 2 * width)
    self_gains = jnp.stack([selfgain, selfbias])
    gains = jnp.stack([crossgain, crossbias, feedgain, feedbias])
    rows, triple, memory = enter(frames[0], self_gains[0:1], self_gains[1:2], qkv, text_states[0], kv)
    flat, sums, after_self, wq, wo = attend(triple, selfout, frames[0], crossquery, crossout, subs)
    wo = wo.reshape(4 * width, m)
    query, cross_flat, after_cross, feed_rows, grads = cross(after_self, gains, wq, wo, memory, cotangent[0])
    layer_output, norm_grad, pieces = feed(feed_rows, grads, feedup, feeddown, after_cross, subs)
    grad_out, branch, sums_a, memory_grad, piece_q, piece_o = cross_back(
        cotangent[0], norm_grad, after_cross, after_self, gains, query, cross_flat, memory, wq, wo, subs
    )
    frame_grad, sums_b, text_part, grad_qkv, grad_out_weight, grad_kv, grad_cq, grad_co = attend_back(
        branch, triple, flat, sums, selfout, qkv, rows, frames[0], self_gains, grad_out, memory_grad, text_states[0], kv,
        piece_q, piece_o, subs,
    )
    up, down, full_qkv, full_cq, full_kv, full_out, full_co, text_grad, vectors = total(
        pieces, grad_qkv, grad_cq, grad_kv, grad_out_weight, grad_co, sums_a, sums_b, text_part, subs, groups
    )
    return (
        layer_output[None],
        frame_grad[None],
        text_grad[None],
        vectors[4],
        vectors[5],
        full_qkv.reshape(-1, 3, width),
        full_out,
        vectors[2],
        vectors[3],
        full_cq,
        full_kv.reshape(-1, 2, width),
        full_co,
        vectors[0],
        vectors[1],
        up,
        down,
    )


def solution(mesh):
    clips = P(("sub", "group"), "tensor", None)
    whole = P(("sub", "group"), None, None)
    narrow, wide = P("tensor", None), P(None, "tensor")
    third = P(None, None, "tensor")
    vector = P("sub")
    return jax.shard_map(
        local,
        mesh=mesh,
        in_specs=(
            clips, whole, P(), P(), third, narrow, P(), P(), wide, third, narrow, P(), P(), wide, narrow, clips,
        ),
        out_specs=(
            clips, clips, whole, vector, vector, P("sub", None, "tensor"), P(("tensor", "sub"), None), vector, vector,
            P("sub", "tensor"), P("sub", None, "tensor"), P(("tensor", "sub"), None), vector, vector,
            P("sub", "tensor"), P(("tensor", "sub"), None),
        ),
        check_vma=False,
    )
```

```python
from functools import partial

import jax
import jax.numpy as jnp
from jax import lax
from jax.experimental import pallas as pl
from jax.experimental.pallas import tpu as pltpu
from jax.sharding import PartitionSpec as P

HEAD = 64
EPSILON = 1e-05
NEG_BIG = -1e30
LOG2E = 1.4426950408889634
MESH = pl.DeviceIdType.MESH
F32 = jnp.float32
BF = jnp.bfloat16
ANY = pl.BlockSpec(memory_space=pl.ANY)
VMEM_LIMIT = 63 << 20


def neighbours():
    t = lax.axis_index("tensor")
    return t, t + 1 - 2 * (t % 2), (t + 2) % 4, 3 - t


def greet(targets):
    barrier = pltpu.get_barrier_semaphore()
    for target in targets:
        pl.semaphore_signal(barrier, inc=1, device_id=target, device_id_type=MESH)
    pl.semaphore_wait(barrier, len(targets))


def dot(a, b):
    return lax.dot_general(a, b, (((1,), (0,)), ((), ())), preferred_element_type=F32)


def dot_t(a, b):
    return lax.dot_general(a, b, (((1,), (1,)), ((), ())), preferred_element_type=F32)


def dot_c(a, b):
    return lax.dot_general(a, b, (((0,), (0,)), ((), ())), preferred_element_type=F32)


def cols(j, width):
    return pl.ds(pl.multiple_of(j * width, width), width)


def rows_at(j, height):
    return pl.ds(pl.multiple_of(j * height, height), height)


def split(count):
    first = (count // 2 + 15) // 16 * 16
    return pl.ds(0, first), pl.ds(first, count - first)


class Gather:
    def __init__(self, own, dst, send, recv, base, halves=None):
        self.own, self.dst, self.send, self.recv, self.base = own, dst, send, recv, base
        self.halves = halves or split(own.shape[0])

    def copy(self, k):
        t, x, y, _ = neighbours()
        first, second = self.halves
        half = (first, second, second, first, first, second)[k]
        place = (t, t, t, t, x, y)[k]
        target = (x, y, x, y, y, x)[k]
        source = self.own.at[half] if k < 4 else self.dst.at[place, half]
        return pltpu.make_async_remote_copy(
            source,
            self.dst.at[place, half],
            self.send.at[self.base + k],
            self.recv.at[self.base + k],
            device_id={"tensor": target},
            device_id_type=MESH,
        )

    def start(self):
        for k in range(4):
            self.copy(k).start()

    def relay_x(self):
        self.copy(0).wait_recv()
        self.copy(4).start()

    def relay_y(self):
        self.copy(1).wait_recv()
        self.copy(5).start()

    def have_x(self):
        self.copy(2).wait_recv()

    def have_y(self):
        self.copy(3).wait_recv()

    def have_d(self):
        self.copy(4).wait_recv()
        self.copy(5).wait_recv()

    def drain(self):
        for k in range(6):
            self.copy(k).wait_send()


class Scatter:
    def __init__(self, part, land, stage, send, recv, base):
        self.part, self.land, self.stage = part, land, stage
        self.send, self.recv, self.base = send, recv, base
        self.half = part.shape[1] // 2

    def copy(self, k):
        t, x, y, d = neighbours()
        low, high = pl.ds(0, self.half), pl.ds(self.half, self.half)
        source = (
            self.part.at[d, low],
            self.part.at[d, high],
            self.part.at[x, low],
            self.stage.at[1],
            self.part.at[y, high],
            self.stage.at[0],
        )[k]
        target = (x, y, x, x, y, y)[k]
        return pltpu.make_async_remote_copy(
            source,
            self.land.at[k],
            self.send.at[self.base + k],
            self.recv.at[self.base + k],
            device_id={"tensor": target},
            device_id_type=MESH,
        )

    def diagonal(self):
        self.copy(0).start()
        self.copy(1).start()

    def along_x(self):
        self.copy(2).start()

    def along_y(self):
        self.copy(4).start()

    def relay(self):
        t, x, y, d = neighbours()
        low, high = pl.ds(0, self.half), pl.ds(self.half, self.half)
        self.copy(0).wait_recv()
        self.stage[0] = (self.part[y, low].astype(F32) + self.land[0].astype(F32)).astype(BF)
        self.copy(5).start()
        self.copy(1).wait_recv()
        self.stage[1] = (self.part[x, high].astype(F32) + self.land[1].astype(F32)).astype(BF)
        self.copy(3).start()

    def finish(self, take, step):
        t, x, y, d = neighbours()
        for k in (2, 4, 5, 3):
            self.copy(k).wait_recv()
        for base, a, b in ((0, 2, 5), (self.half, 4, 3)):

            def block(i, carry, base=base, a=a, b=b):
                here = rows_at(i, step)
                rows = pl.ds(pl.multiple_of(base + i * step, step), step)
                take(
                    rows,
                    self.part[t, rows].astype(F32)
                    + self.land[a, here].astype(F32)
                    + self.land[b, here].astype(F32),
                )
                return carry

            lax.fori_loop(0, self.half // step, block, 0)

    def drain(self):
        for k in range(6):
            self.copy(k).wait_send()


def normed_rows(values):
    centre = values - jnp.mean(values, -1, keepdims=True)
    inverse = lax.rsqrt(jnp.mean(centre * centre, -1, keepdims=True) + EPSILON)
    return centre * inverse, inverse


def params(cid, **more):
    return pltpu.CompilerParams(
        collective_id=cid, has_side_effects=True, vmem_limit_bytes=VMEM_LIMIT, **more
    )


def dma(count):
    return pltpu.SemaphoreType.DMA((count,))


def shape(*dims, kind=BF):
    return jax.ShapeDtypeStruct(dims, kind)


LAG = 2
RING = 4


def either(condition, other):
    return jnp.logical_and(condition, other)


class Pump:
    def __init__(self, own, land, ring, result, send, recv, store, first, last, count, outputs):
        self.own, self.land, self.ring, self.result = own, land, ring, result
        self.send, self.recv, self.store = send, recv, store
        self.first, self.last, self.count, self.outputs = first, last, count, outputs
        self.window = land.shape[1]
        self.g, self.n = lax.axis_index("group"), lax.axis_size("group")

    def copy(self, way, c):
        target = (self.g + 1) % self.n if way == 0 else (self.g + self.n - 1) % self.n
        return pltpu.make_async_remote_copy(
            self.ring.at[way, c % RING],
            self.land.at[way, c % self.window],
            self.send.at[way, c % RING],
            self.recv.at[way, c % self.window],
            device_id={"group": target},
            device_id_type=MESH,
        )

    def flow(self, way, k):
        place = self.g if way == 0 else self.n - 1 - self.g
        c = k - LAG * place

        @pl.when(either(c >= 0, c < self.count))
        def _():
            @pl.when(either(place > 0, k - LAG >= self.first))
            def _():
                self.copy(way, c).wait_recv()

            @pl.when(place < self.n - 1)
            def _():
                @pl.when(either(c >= RING, k - RING >= self.first))
                def _():
                    self.copy(way, c - RING).wait_send()

                @pl.when(place > 0)
                def _():
                    before = self.land[way, c % self.window].astype(F32)
                    self.ring[way, c % RING] = (self.own[c].astype(F32) + before).astype(BF)

                @pl.when(place == 0)
                def _():
                    self.ring[way, c % RING] = self.own[c]

                self.copy(way, c).start()

    def finished(self, k):
        far = jnp.maximum(self.g, self.n - 1 - self.g)
        return k - LAG * far

    def step(self, k):
        self.flow(0, k)
        self.flow(1, k)
        f = self.finished(k)

        @pl.when(either(f >= 0, f < self.count))
        def _():
            @pl.when(either(f >= RING, k - RING >= self.first))
            def _():
                self.outputs(f - RING, self.result.at[f % RING], self.store, lambda copy: copy.wait())

            mine = self.own[f].astype(F32)
            slot, held = f % RING, f % self.window

            @pl.when(either(self.g > 0, self.g < self.n - 1))
            def _():
                both = self.land[0, held].astype(F32) + self.land[1, held].astype(F32)
                self.result[slot] = (mine + both).astype(BF)

            @pl.when(self.g == 0)
            def _():
                self.result[slot] = (mine + self.land[1, held].astype(F32)).astype(BF)

            @pl.when(self.g == self.n - 1)
            def _():
                self.result[slot] = (mine + self.land[0, held].astype(F32)).astype(BF)

            self.outputs(f, self.result.at[slot], self.store, lambda copy: copy.start())

    def drain(self):
        for way in range(2):
            place = self.g if way == 0 else self.n - 1 - self.g
            top = jnp.minimum(self.last - LAG * place, self.count)
            for j in range(1, RING + 1):
                c = top - j

                @pl.when(either(place < self.n - 1, either(c >= 0, c + LAG * place >= self.first)))
                def _(way=way, c=c):
                    self.copy(way, c).wait_send()

            for k in range(max(self.first, self.last - LAG), self.last):
                c = k - LAG * (place - 1)

                @pl.when(either(place > 0, either(c >= 0, c < self.count)))
                def _(way=way, c=c):
                    self.copy(way, c).wait_recv()

        far = jnp.maximum(self.g, self.n - 1 - self.g)
        top = jnp.minimum(self.last - LAG * far, self.count)
        for j in range(1, RING + 1):
            f = top - j

            @pl.when(either(f >= 0, f + LAG * far >= self.first))
            def _(f=f):
                self.outputs(f, self.result.at[f % RING], self.store, lambda copy: copy.wait())


class Layout:
    def __init__(self, m, local, subs, groups):
        piece = m // subs
        self.m, self.piece, self.local = m, piece, local
        self.out_rows = local // subs
        self.chunk = 48
        self.feed = 2 * piece
        self.qkv = self.feed
        self.kv = self.qkv + 3 * piece // 4
        self.out = self.kv + piece // 2
        self.cq = self.out + self.out_rows
        self.co = self.cq + piece // 4
        self.rows = self.co + self.out_rows
        self.count = self.rows // self.chunk
        self.feed_count = self.feed // self.chunk
        self.window = LAG * (groups + 1)
        self.middle = min(10, self.feed_count // 3)
        self.later = min(32, self.feed_count)
        self.end = self.count + LAG * (groups - 1)


def feed_outputs(layout, o_feed):
    def outputs(c, block, store, act):
        act(pltpu.make_async_copy(block, o_feed.at[c], store.at[c % RING, 0]))

    return outputs


def pump_scratch(layout, count):
    chunk, m = layout.chunk, layout.m
    return [
        pltpu.VMEM((count, chunk, m), BF),
        pltpu.VMEM((2, layout.window, chunk, m), BF),
        pltpu.VMEM((2, RING, chunk, m), BF),
        pltpu.VMEM((RING, chunk, m), BF),
        pltpu.SemaphoreType.DMA((2, RING)),
        pltpu.SemaphoreType.DMA((2, layout.window)),
        pltpu.SemaphoreType.DMA((RING, 4)),
    ]


def group_ring():
    g, n = lax.axis_index("group"), lax.axis_size("group")
    return [{"group": (g + 1) % n}, {"group": (g + n - 1) % n}]


def enter_kernel(
    frames, gain, bias, qkv, text, kv, o_rows, o_triple, o_memory,
    v_frames, v_gain, v_bias, v_qkv, v_text, v_kv, rows, triple, memory, load, store, send, recv,
):
    t, x, y, d = neighbours()
    loads = [
        pltpu.make_async_copy(a, b, load.at[i])
        for i, (a, b) in enumerate(
            ((frames, v_frames), (gain, v_gain), (bias, v_bias), (qkv, v_qkv), (text, v_text), (kv, v_kv))
        )
    ]
    for copy in loads:
        copy.start()
    greet([{"tensor": x}, {"tensor": y}])
    for copy in loads[:3]:
        copy.wait()
    count, width = v_qkv.shape
    block = 384

    def norm_block(i, carry):
        here = rows_at(i, 64)
        hat, _ = normed_rows(v_frames[here].astype(F32))
        rows[t, here] = (hat * v_gain[...] + v_bias[...]).astype(BF)
        return carry

    lax.fori_loop(0, v_frames.shape[0] // 64, norm_block, 0)
    gather = Gather(rows.at[t], rows, send, recv, 0)
    gather.start()
    texts = Gather(memory.at[t], memory, send, recv, 6)

    def project(place):
        def step(j, carry):
            triple[place, :, cols(j, block)] = dot(rows[place], v_qkv[:, cols(j, block)]).astype(BF)
            return carry

        lax.fori_loop(0, width // block, step, 0)

    def put(k, place):
        a = pltpu.make_async_copy(rows.at[place], o_rows.at[place], store.at[2 * k])
        b = pltpu.make_async_copy(triple.at[place], o_triple.at[place], store.at[2 * k + 1])
        a.start()
        b.start()
        return [a, b]

    loads[4].wait()
    loads[5].wait()

    def texts_step(j, carry):
        memory[t, :, cols(j, block)] = dot(v_text[...], v_kv[:, cols(j, block)]).astype(BF)
        return carry

    lax.fori_loop(0, v_kv.shape[1] // block, texts_step, 0)
    texts.start()
    loads[3].wait()
    project(t)
    stores = put(0, t)
    gather.relay_x()
    gather.relay_y()
    gather.have_x()
    project(x)
    stores += put(1, x)
    gather.have_y()
    project(y)
    stores += put(2, y)
    texts.relay_x()
    texts.relay_y()
    texts.have_x()
    texts.have_y()
    gather.have_d()
    project(d)
    stores += put(3, d)
    texts.have_d()
    last = pltpu.make_async_copy(memory, o_memory, store.at[8])
    last.start()
    gather.drain()
    texts.drain()
    for copy in stores:
        copy.wait()
    last.wait()


def enter(frames, gain, bias, qkv, text, kv):
    n, m = frames.shape
    width, texts, kvw = qkv.shape[1], text.shape[0], kv.shape[1]
    return pl.pallas_call(
        enter_kernel,
        name="enter",
        out_shape=[shape(4, n, m), shape(4, n, width), shape(4, texts, kvw)],
        in_specs=[ANY] * 6,
        out_specs=[ANY] * 3,
        scratch_shapes=[
            pltpu.VMEM((n, m), frames.dtype), pltpu.VMEM((1, m), F32), pltpu.VMEM((1, m), F32),
            pltpu.VMEM(qkv.shape, BF), pltpu.VMEM(text.shape, BF), pltpu.VMEM(kv.shape, BF),
            pltpu.VMEM((4, n, m), BF), pltpu.VMEM((4, n, width), BF), pltpu.VMEM((4, texts, kvw), BF),
            dma(6), dma(9), dma(12), dma(12),
        ],
        compiler_params=params(1),
    )(frames, gain, bias, qkv, text, kv)


def head_lanes(rows):
    return lax.broadcasted_iota(jnp.int32, (rows, 128), 1)


def attend_rows(triple, place, blocks, heads, flat, sums):
    n = triple.shape[1]
    width = heads * HEAD
    scale = HEAD ** (-0.5) * LOG2E
    lanes = head_lanes(n)

    def pair(p, stats):
        here = pl.ds(pl.multiple_of(p * 128, 128), 128)
        key_cols = pl.ds(pl.multiple_of(width + p * 128, 128), 128)
        value_cols = pl.ds(pl.multiple_of(2 * width + p * 128, 128), 128)
        query = triple[place, :, here]
        keys = triple[0:blocks, :, key_cols].reshape(blocks * n, 128)
        values = triple[0:blocks, :, value_cols].reshape(blocks * n, 128)
        outs = []
        for h in range(2):
            mine = (lanes < HEAD) if h == 0 else (lanes >= HEAD)
            scores = dot_t(jnp.where(mine, query, jnp.zeros_like(query)), keys)
            row = lax.broadcasted_iota(jnp.int32, scores.shape, 0)
            col = lax.broadcasted_iota(jnp.int32, scores.shape, 1)
            scores = jnp.where(col <= row + (blocks - 1) * n, scores, NEG_BIG)
            peak = jnp.max(scores, -1, keepdims=True) * scale
            exponent = jnp.exp2(scores * scale - peak)
            total = jnp.sum(exponent, -1, keepdims=True)
            outs.append(dot(exponent.astype(BF), values) / total)
            stats = jnp.where(lanes == 2 * p + h, peak + jnp.log2(total), stats)
        flat[place, :, here] = jnp.where(lanes < HEAD, outs[0], outs[1]).astype(BF)
        return stats

    sums[place] = lax.fori_loop(0, heads // 2, pair, jnp.zeros((n, 128), F32))


def attend_kernel(
    triple_in, out_in, frames_in, wq, wo, o_flat, o_sums, o_after, o_wq, o_wo,
    triple, v_out, v_frames, flat, sums, after, part, land, stage, v_wq, v_wo, load, store, send, recv, side,
):
    t, x, y, d = neighbours()
    s = lax.axis_index("sub")
    subs = lax.axis_size("sub")
    n = triple.shape[1]
    m = v_out.shape[1]
    heads = v_out.shape[0] // HEAD
    loads = [
        pltpu.make_async_copy(a, b, load.at[i])
        for i, (a, b) in enumerate(
            ((triple_in, triple), (out_in, v_out), (frames_in, v_frames), (wq, v_wq), (wo, v_wo))
        )
    ]
    for copy in loads:
        copy.start()
    greet(
        [{"tensor": x}, {"tensor": y}]
        + [{"sub": (s + k) % subs} for k in range(1, subs)]
    )
    scatter = Scatter(part, land, stage, send, recv, 0)
    gathers = []
    for i, (weight, full) in enumerate(((wq, o_wq), (wo, o_wo))):
        piece = weight.shape[0] // subs
        first, second = split(piece)
        offset = pl.multiple_of(s * piece, piece)
        halves = (
            pl.ds(offset, first.size),
            pl.ds(pl.multiple_of(offset + first.size, 16), second.size),
        )
        gathers.append((Gather(weight, full, send, recv, 6 + 6 * i, halves), full, pl.ds(offset, piece)))

    def shared(i, j, k):
        _, full, piece = gathers[i]
        place = (x, y, d)[j]
        slot = (i * 3 + j) * (subs - 1) + k - 1
        return pltpu.make_async_remote_copy(
            full.at[place, piece], full.at[place, piece],
            send.at[18 + slot], recv.at[18 + slot],
            device_id={"sub": (s + k) % subs}, device_id_type=MESH,
        )

    for gather, _, _ in gathers:
        gather.start()
    for copy in loads[:2]:
        copy.wait()

    def one(i, carry):
        far_y = 1 - i // 2
        far_x = 1 - i % 2
        place = (t // 2 + far_y - 2 * (t // 2) * far_y) * 2 + (t % 2 + far_x - 2 * (t % 2) * far_x)
        for blocks in range(1, 5):

            @pl.when(place == blocks - 1)
            def _(blocks=blocks):
                attend_rows(triple, blocks - 1, blocks, heads, flat, sums)

        def out_step(j, carry):
            part[place, :, cols(j, 512)] = dot(flat[place], v_out[:, cols(j, 512)]).astype(BF)
            return carry

        lax.fori_loop(0, m // 512, out_step, 0)

        @pl.when(i == 0)
        def _():
            scatter.diagonal()

        @pl.when(i == 1)
        def _():
            scatter.along_y()

        @pl.when(i == 2)
        def _():
            scatter.along_x()

        return carry

    lax.fori_loop(0, 4, one, 0)
    for gather, _, _ in gathers:
        gather.relay_x()
        gather.relay_y()
    stores = [
        pltpu.make_async_copy(flat, o_flat, store.at[0]),
        pltpu.make_async_copy(sums, o_sums, store.at[1]),
    ]
    loads[3].wait()
    loads[4].wait()
    stores += [
        pltpu.make_async_copy(v_wq, o_wq.at[t], store.at[2]),
        pltpu.make_async_copy(v_wo, o_wo.at[t], store.at[3]),
    ]
    for copy in stores:
        copy.start()
    scatter.relay()
    for i, (gather, _, _) in enumerate(gathers):
        gather.have_x()
        gather.have_y()
        gather.have_d()
        for j in range(3):
            for k in range(1, subs):
                shared(i, j, k).start()
    loads[2].wait()

    def take(rows, total):
        after[rows] = v_frames[rows].astype(F32) + total

    scatter.finish(take, 64)
    last = pltpu.make_async_copy(after, o_after, store.at[4])
    last.start()
    scatter.drain()
    for i, (gather, _, _) in enumerate(gathers):
        gather.drain()
        for j in range(3):
            for k in range(1, subs):
                shared(i, j, k).wait()
    for copy in stores:
        copy.wait()
    last.wait()


def attend(triple, out, frames, wq, wo, subs):
    _, n, width = triple.shape
    local, m = out.shape
    extra = 18 + 6 * (subs - 1)
    return pl.pallas_call(
        attend_kernel,
        name="attend",
        out_shape=[
            shape(4, n, local), shape(4, n, 128, kind=F32), shape(n, m, kind=F32),
            shape(4, *wq.shape), shape(4, *wo.shape),
        ],
        in_specs=[ANY] * 5,
        out_specs=[ANY] * 5,
        scratch_shapes=[
            pltpu.VMEM((4, n, width), BF), pltpu.VMEM((local, m), BF), pltpu.VMEM((n, m), frames.dtype),
            pltpu.VMEM((4, n, local), BF), pltpu.VMEM((4, n, 128), F32), pltpu.VMEM((n, m), F32),
            pltpu.VMEM((4, n, m), BF), pltpu.VMEM((6, n // 2, m), BF), pltpu.VMEM((2, n // 2, m), BF),
            pltpu.VMEM(wq.shape, BF), pltpu.VMEM(wo.shape, BF),
            dma(5), dma(5), dma(extra), dma(extra), dma(1),
        ],
        compiler_params=params(2),
    )(triple, out, frames, wq, wo)


def stack_pair(block, rows):
    lanes = head_lanes(rows)
    zero = jnp.zeros_like(block)
    return jnp.concatenate([jnp.where(lanes < HEAD, block, zero), jnp.where(lanes >= HEAD, block, zero)], 0)


def pair_softmax(query, keys):
    scale = HEAD ** (-0.5) * LOG2E
    scores = dot_t(query, keys)
    left = head_lanes(scores.shape[0]) < HEAD
    low = jnp.max(jnp.where(left, scores, -jnp.inf), -1, keepdims=True)
    high = jnp.max(jnp.where(left, -jnp.inf, scores), -1, keepdims=True)
    exponent = jnp.exp2((scores - jnp.where(left, low, high)) * scale)
    total = pair_sum(exponent, left)
    return exponent / total, left


def pair_sum(values, left):
    low = jnp.sum(jnp.where(left, values, 0.0), -1, keepdims=True)
    high = jnp.sum(jnp.where(left, 0.0, values), -1, keepdims=True)
    return jnp.where(left, low, high)


def cross_kernel(
    after_in, gains_in, wq_in, wo_in, memory_in, cot_in,
    o_query, o_flat, o_after, o_rows, o_grads,
    after, gains, wq, wo, memory, cot, rows, query, flat, result, feed, grads, load, store, send, recv,
):
    t, x, y, d = neighbours()
    loads = [
        pltpu.make_async_copy(a, b, load.at[i])
        for i, (a, b) in enumerate(
            ((cot_in, cot), (after_in, after), (gains_in, gains), (wq_in, wq), (memory_in, memory), (wo_in, wo))
        )
    ]
    for copy in loads:
        copy.start()
    greet([{"tensor": x}, {"tensor": y}])
    n, m = after.shape
    width = wq.shape[2]
    texts = memory.shape[1]
    loads[0].wait()

    def round_block(i, carry):
        here = rows_at(i, 64)
        grads[t, here] = cot[here].astype(BF)
        return carry

    lax.fori_loop(0, n // 64, round_block, 0)
    gather = Gather(grads.at[t], grads, send, recv, 0)
    gather.start()
    loads[1].wait()
    loads[2].wait()

    def norm_block(i, carry):
        here = rows_at(i, 64)
        hat, _ = normed_rows(after[here])
        rows[here] = (hat * gains[0:1] + gains[1:2]).astype(BF)
        return carry

    lax.fori_loop(0, n // 64, norm_block, 0)
    loads[3].wait()
    loads[4].wait()

    def quarter(q, carry):
        query[:, cols(q, width)] = dot(rows[...], wq[q]).astype(BF)

        def pair(p, carry):
            keys = stack_pair(memory[q, :, cols(p, 128)], texts)
            values = stack_pair(memory[q, :, pl.ds(pl.multiple_of(width + p * 128, 128), 128)], texts)
            here = pl.ds(pl.multiple_of(q * width + p * 128, 128), 128)
            probs, _ = pair_softmax(query[:, here], keys)
            flat[:, here] = dot(probs.astype(BF), values).astype(BF)
            return carry

        lax.fori_loop(0, width // 128, pair, 0)
        return carry

    lax.fori_loop(0, 4, quarter, 0)
    gather.relay_x()
    gather.relay_y()
    stores = [pltpu.make_async_copy(query, o_query, store.at[0]), pltpu.make_async_copy(flat, o_flat, store.at[1])]
    loads[5].wait()

    def out_step(j, carry):
        result[:, cols(j, 512)] = after[:, cols(j, 512)] + dot(flat[...], wo[:, cols(j, 512)])
        return carry

    lax.fori_loop(0, m // 512, out_step, 0)

    def feed_block(i, carry):
        here = rows_at(i, 64)
        hat, _ = normed_rows(result[here])
        feed[here] = (hat * gains[2:3] + gains[3:4]).astype(BF)
        return carry

    lax.fori_loop(0, n // 64, feed_block, 0)
    stores += [pltpu.make_async_copy(result, o_after, store.at[2]), pltpu.make_async_copy(feed, o_rows, store.at[3])]
    for copy in stores:
        copy.start()
    gather.have_x()
    gather.have_y()
    gather.have_d()
    last = pltpu.make_async_copy(grads, o_grads, store.at[4])
    last.start()
    gather.drain()
    for copy in stores:
        copy.wait()
    last.wait()


def cross(after, gains, wq, wo, memory, cot):
    n, m = after.shape
    return pl.pallas_call(
        cross_kernel,
        name="cross",
        out_shape=[shape(n, m), shape(n, m), shape(n, m, kind=F32), shape(n, m), shape(4, n, m)],
        in_specs=[ANY] * 6,
        out_specs=[ANY] * 5,
        scratch_shapes=[
            pltpu.VMEM((n, m), F32), pltpu.VMEM(gains.shape, F32), pltpu.VMEM(wq.shape, BF), pltpu.VMEM(wo.shape, BF),
            pltpu.VMEM(memory.shape, BF), pltpu.VMEM((n, m), F32), pltpu.VMEM((n, m), BF), pltpu.VMEM((n, m), BF),
            pltpu.VMEM((n, m), BF), pltpu.VMEM((n, m), F32), pltpu.VMEM((n, m), BF), pltpu.VMEM((4, n, m), BF),
            dma(6), dma(5), dma(6), dma(6),
        ],
        compiler_params=params(3),
    )(after, gains, wq, wo, memory, cot)


def gelu_both(pre):
    size = jnp.abs(pre) * 0.7071067811865476
    rate = 1.0 / (1.0 + 0.3275911 * size)
    bell = jnp.exp2(pre * pre * (-0.5 * LOG2E))
    series = rate * (
        0.254829592
        + rate * (-0.284496736 + rate * (1.421413741 + rate * (-1.453152027 + rate * 1.061405429)))
    )
    tail = 0.5 * series * bell
    gate = jnp.where(pre >= 0, 1.0 - tail, tail)
    return pre * gate, gate + pre * (0.3989422804014327 * bell)


class Halves:
    def __init__(self, whole, land, send, recv, base):
        self.whole, self.land, self.send, self.recv, self.base = whole, land, send, recv, base
        self.subs = lax.axis_size("sub")
        self.piece = whole.shape[1] // self.subs

    def copies(self, w):
        s = lax.axis_index("sub")
        made = []
        for k in range(1, self.subs):
            target = (s + k) % self.subs
            slot = w * (self.subs - 1) + k - 1
            made.append(
                pltpu.make_async_remote_copy(
                    self.whole.at[w, rows_at(target, self.piece)],
                    self.land.at[w, k - 1],
                    self.send.at[self.base + slot],
                    self.recv.at[self.base + slot],
                    device_id={"sub": target},
                    device_id_type=MESH,
                )
            )
        return made

    def start(self, w):
        for copy in self.copies(w):
            copy.start()

    def total(self, w, take, step):
        s = lax.axis_index("sub")
        for copy in self.copies(w):
            copy.wait_recv()

        def block(i, carry):
            here = rows_at(i, step)
            value = self.whole[w, pl.ds(pl.multiple_of(s * self.piece + i * step, step), step)].astype(F32)
            for k in range(1, self.subs):
                value = value + self.land[w, k - 1, here].astype(F32)
            take(here, value)
            return carry

        lax.fori_loop(0, self.piece // step, block, 0)

    def drain(self, w):
        for copy in self.copies(w):
            copy.wait_send()


def weight_grad(left, right, whole, w, halves, block):
    s = lax.axis_index("sub")
    subs = lax.axis_size("sub")
    total_rows = left.shape[0] * left.shape[1]
    count = whole.shape[1] // block
    begin = ((s + 1) % subs) * halves.piece // block

    def one(j, carry):
        b = (begin + j) % count
        turned = left[:, :, cols(b, block)].reshape(total_rows, block)

        def inner(i, carry):
            other = right[:, :, cols(i, 512)].reshape(total_rows, 512)
            whole[w, rows_at(b, block), cols(i, 512)] = dot_c(turned, other).astype(BF)
            return carry

        lax.fori_loop(0, whole.shape[2] // 512, inner, 0)
        return carry

    if subs == 2:
        lax.fori_loop(0, count // 2, one, 0)
        halves.start(w)
        lax.fori_loop(count // 2, count, one, 0)
    else:
        lax.fori_loop(0, count, one, 0)
        halves.start(w)


def feed_kernel(
    rows_in, grads_in, up_in, down_in, o_part, o_norm, o_pieces,
    rows, grads, up, down, act, pre_grad, part_out, part_norm, land_norm, stage_norm,
    whole, land_whole, load, store, send, recv,
):
    t, x, y, d = neighbours()
    s = lax.axis_index("sub")
    subs = lax.axis_size("sub")
    loads = [
        pltpu.make_async_copy(a, b, load.at[i])
        for i, (a, b) in enumerate(
            ((rows_in, rows.at[t]), (up_in, up), (grads_in, grads), (down_in, down))
        )
    ]
    for copy in loads:
        copy.start()
    greet([{"tensor": x}, {"tensor": y}] + [{"sub": (s + k) % subs} for k in range(1, subs)])
    _, n, m = rows.shape
    hidden = up.shape[1]
    loads[0].wait()
    gather = Gather(rows.at[t], rows, send, recv, 0)
    gather.start()
    back = Scatter(part_norm, land_norm, stage_norm, send, recv, 6)
    halves = Halves(whole, land_whole, send, recv, 12)
    for copy in loads[1:4]:
        copy.wait()

    def work(place):
        def step(j, carry):
            here = cols(j, 256)
            value, slope = gelu_both(dot(rows[place], up[:, here]))
            act[place, :, here] = value.astype(BF)
            pre_grad[place, :, here] = (dot_t(grads[place], down[here]) * slope).astype(BF)
            return carry

        lax.fori_loop(0, hidden // 256, step, 0)

        def out_step(j, carry):
            part_norm[place, :, cols(j, 512)] = dot_t(pre_grad[place], up[rows_at(j, 512)]).astype(BF)
            part_out[place, :, cols(j, 512)] = dot(act[place], down[:, cols(j, 512)]).astype(BF)
            return carry

        lax.fori_loop(0, m // 512, out_step, 0)

    def turn(i, carry):
        far_y = i // 2
        far_x = i % 2
        place = (t // 2 + far_y - 2 * (t // 2) * far_y) * 2 + (t % 2 + far_x - 2 * (t % 2) * far_x)

        @pl.when(i == 1)
        def _():
            gather.relay_x()
            gather.relay_y()
            gather.have_x()

        @pl.when(i == 2)
        def _():
            gather.have_y()

        @pl.when(i == 3)
        def _():
            gather.have_d()

        work(place)

        @pl.when(i == 1)
        def _():
            back.along_x()

        @pl.when(i == 2)
        def _():
            back.along_y()

        @pl.when(i == 3)
        def _():
            back.diagonal()

        return carry

    lax.fori_loop(0, 4, turn, 0)
    stores = [pltpu.make_async_copy(part_out, o_part, store.at[1])]
    stores[0].start()
    weight_grad(act, grads, whole, 0, halves, 256)
    back.relay()
    weight_grad(rows, pre_grad, whole, 1, halves, 256)
    pieces = land_whole
    for w in range(2):

        def take(here, value, w=w):
            pieces[w, 0, here] = value.astype(BF)

        halves.total(w, take, 64)
    stores.append(pltpu.make_async_copy(pieces.at[:, 0], o_pieces, store.at[0]))
    stores[1].start()
    norm_total = part_norm


    def take_norm(here, total):
        norm_total[t, here] = total.astype(BF)

    back.finish(take_norm, 64)
    stores.append(pltpu.make_async_copy(norm_total.at[t], o_norm, store.at[2]))
    stores[2].start()
    gather.drain()
    back.drain()
    for w in range(2):
        halves.drain(w)
    for copy in stores:
        copy.wait()


def feed(rows, grads, up, down, subs):
    n, m = rows.shape
    hidden = up.shape[1]
    count = 12 + 2 * (subs - 1)
    return pl.pallas_call(
        feed_kernel,
        name="feed",
        out_shape=[shape(4, n, m), shape(n, m), shape(2, m // subs, hidden)],
        in_specs=[ANY] * 4,
        out_specs=[ANY] * 3,
        scratch_shapes=[
            pltpu.VMEM((4, n, m), BF), pltpu.VMEM((4, n, m), BF), pltpu.VMEM((m, hidden), BF), pltpu.VMEM((hidden, m), BF),
            pltpu.VMEM((4, n, hidden), BF), pltpu.VMEM((4, n, hidden), BF),
            pltpu.VMEM((4, n, m), BF), pltpu.VMEM((4, n, m), BF),
            pltpu.VMEM((6, n // 2, m), BF), pltpu.VMEM((2, n // 2, m), BF),
            pltpu.VMEM((2, m, hidden), BF), pltpu.VMEM((2, subs - 1, m // subs, hidden), BF),
            dma(4), dma(3), dma(count), dma(count),
        ],
        compiler_params=params(4),
    )(rows, grads, up, down)


def norm_back_block(grad, source, gain):
    hat, inverse = normed_rows(source)
    scaled = grad * gain
    inner = scaled - jnp.mean(scaled, -1, keepdims=True) - hat * jnp.mean(scaled * hat, -1, keepdims=True)
    return inverse * inner, grad * hat


def fold(block):
    total = block[0:8]
    for i in range(1, block.shape[0] // 8):
        total = total + block[8 * i : 8 * i + 8]
    return total


def unstack(block):
    lanes = head_lanes(block.shape[0] // 2)
    return jnp.where(lanes < HEAD, block[: block.shape[0] // 2], block[block.shape[0] // 2 :])


def cross_back_kernel(
    layout,
    cot_in, norm_in, cross_in, self_in, gains_in, query_in, flat_in, memory_in, wq_in, wo_in, part_in, own_in,
    o_out, o_branch, o_sums, o_memory, o_wq, o_wo, o_layer, o_feed, o_land,
    cot, norm, after_cross, after_self, gains, query, flat, memory, wq, wo,
    branch, rows, query_grad, memory_grad, sums, whole_q, whole_o, land_q, land_o, piece_q, piece_o,
    norm_self, part, land_part, stage_part, own, land, ring, result, ring_send, ring_recv, ring_store,
    load, store, send, recv,
):
    t, x, y, d = neighbours()
    s = lax.axis_index("sub")
    subs = lax.axis_size("sub")
    loads = [
        pltpu.make_async_copy(a, b, load.at[i])
        for i, (a, b) in enumerate(
            (
                (cot_in, cot), (norm_in, norm), (cross_in, after_cross), (gains_in, gains), (wo_in, wo),
                (query_in, query), (flat_in, flat), (memory_in, memory), (self_in, after_self), (wq_in, wq),
                (part_in, part), (own_in, own),
            )
        )
    ]
    for copy in loads:
        copy.start()
    greet([{"tensor": x}, {"tensor": y}] + [{"sub": (s + k) % subs} for k in range(1, subs)] + group_ring())
    scatter = Scatter(part, land_part, stage_part, send, recv, 8 * (subs - 1))
    pump = Pump(
        own, land, ring, result, ring_send, ring_recv, ring_store, 0, layout.middle, layout.count,
        feed_outputs(layout, o_feed),
    )
    n, m = cot.shape
    width = wq.shape[2]
    texts = memory.shape[1]
    for copy in (*loads[:4], *loads[10:]):
        copy.wait()
    scatter.diagonal()
    scatter.along_x()
    scatter.along_y()
    pump.step(jnp.int32(0))
    scale = HEAD ** (-0.5)

    def feed_block(i, carry):
        here = rows_at(i, 64)
        grad = norm[here].astype(F32)
        inner, terms = norm_back_block(grad, after_cross[here], gains[2:3])
        total = cot[here] + inner
        cot[here] = total
        branch[here] = total.astype(BF)
        return carry[0] + fold(terms), carry[1] + fold(grad)

    zero = jnp.zeros((8, m), F32)
    gain_sum, bias_sum = lax.fori_loop(0, n // 64, feed_block, (zero, zero))
    sums[0:8] = gain_sum
    sums[8:16] = bias_sum
    loads[8].wait()

    def norm_block(i, carry):
        here = rows_at(i, 64)
        hat, _ = normed_rows(after_self[here])
        rows[here] = (hat * gains[0:1] + gains[1:2]).astype(BF)
        return carry

    lax.fori_loop(0, n // 64, norm_block, 0)
    for copy in loads[4:8]:
        copy.wait()
    middle = layout.middle

    def tick(k):
        @pl.when(k < middle)
        def _():
            pump.step(k)

    tick(jnp.int32(1))

    def quarter(q, carry):
        tick(q + 2)
        grad_heads = dot_t(branch[...], wo[rows_at(q, width)]).astype(BF)
        whole_q_cols = cols(q, width)
        query_grad_block = []
        for p in range(width // 128):
            lane = slice(p * 128, p * 128 + 128)
            keys = stack_pair(memory[q, :, lane], texts)
            values = stack_pair(memory[q, :, width + p * 128 : width + p * 128 + 128], texts)
            here = pl.ds(pl.multiple_of(q * width + p * 128, 128), 128)
            grad = grad_heads[:, lane]
            ask = query[:, here]
            probs, left = pair_softmax(ask, keys)
            grad_probs = dot_t(grad, values)
            centred = pair_sum(grad_probs * probs, left)
            grad_scores = (probs * (grad_probs - centred)).astype(BF)
            query_grad[:, here] = (dot(grad_scores, keys) * scale).astype(BF)
            memory_grad[q, :, lane] = unstack(dot_c(grad_scores, ask) * scale).astype(BF)
            memory_grad[q, :, width + p * 128 : width + p * 128 + 128] = unstack(
                dot_c(probs.astype(BF), grad)
            ).astype(BF)
        return carry

    lax.fori_loop(0, 4, quarter, 0)
    stores = [pltpu.make_async_copy(memory_grad, o_memory, store.at[0])]
    stores[0].start()
    halves_q = Halves(whole_q, land_q, send, recv, 0)
    halves_o = Halves(whole_o, land_o, send, recv, 4 * (subs - 1))

    scatter.relay()

    def weights(q, carry):
        tick(q + 6)

        def grad_o(j, carry):
            whole_o[q, :, cols(j, 512)] = dot_c(flat[:, cols(q, width)], branch[:, cols(j, 512)]).astype(BF)
            return carry

        lax.fori_loop(0, m // 512, grad_o, 0)

        def grad_q(j, carry):
            whole_q[q, rows_at(j, 256)] = dot_c(rows[:, cols(j, 256)], query_grad[:, cols(q, width)]).astype(BF)
            return carry

        lax.fori_loop(0, m // 256, grad_q, 0)
        return carry

    lax.fori_loop(0, 4, weights, 0)
    for q in range(4):
        halves_q.start(q)
        halves_o.start(q)
    loads[9].wait()

    def norm_grad(j, carry):
        here = rows_at(j, 256)
        total = jnp.zeros((n, 256), F32)
        for q in range(4):
            total = total + dot_t(query_grad[:, q * width : (q + 1) * width], wq[q, here])
        norm_self[:, cols(j, 256)] = total
        return carry

    lax.fori_loop(0, m // 256, norm_grad, 0)

    def self_block(i, carry):
        here = rows_at(i, 64)
        grad = norm_self[here]
        inner, terms = norm_back_block(grad, after_self[here], gains[0:1])
        total = cot[here] + inner
        cot[here] = total
        branch[here] = total.astype(BF)
        return carry[0] + fold(terms), carry[1] + fold(grad)

    gain_sum, bias_sum = lax.fori_loop(0, n // 64, self_block, (zero, zero))
    sums[16:24] = gain_sum
    sums[24:32] = bias_sum
    stores += [
        pltpu.make_async_copy(cot, o_out, store.at[1]),
        pltpu.make_async_copy(branch, o_branch, store.at[2]),
        pltpu.make_async_copy(sums, o_sums, store.at[3]),
    ]
    for copy in stores[1:]:
        copy.start()

    def take_layer(here, total):
        after_cross[here] = after_cross[here] + total

    scatter.finish(take_layer, 64)
    stores.append(pltpu.make_async_copy(after_cross, o_layer, store.at[6]))
    stores[-1].start()
    for halves, piece in ((halves_q, piece_q), (halves_o, piece_o)):
        for q in range(4):

            def take(here, value, q=q, piece=piece):
                piece[q, here] = value.astype(BF)

            halves.total(q, take, 16)
    stores += [pltpu.make_async_copy(piece_q, o_wq, store.at[4]), pltpu.make_async_copy(piece_o, o_wo, store.at[5])]
    for copy in stores[5:]:
        copy.start()
    pump.drain()
    stores.append(pltpu.make_async_copy(land, o_land, store.at[7]))
    stores[-1].start()
    scatter.drain()
    for q in range(4):
        halves_q.drain(q)
        halves_o.drain(q)
    for copy in stores:
        copy.wait()


def cross_back(layout, cot, norm, after_cross, after_self, gains, query, flat, memory, wq, wo, part, own, subs):
    n, m = cot.shape
    width = wq.shape[2]
    count = 8 * (subs - 1) + 6
    chunks = layout.feed_count
    held = (2, layout.window, layout.chunk, m)
    part_q, part_o = (4, m // subs, width), (4, width // subs, m)
    return pl.pallas_call(
        partial(cross_back_kernel, layout),
        name="cross_back",
        out_shape=[
            shape(n, m, kind=F32), shape(n, m), shape(32, m, kind=F32), shape(*memory.shape), shape(*part_q), shape(*part_o),
            shape(n, m, kind=F32), shape(layout.feed_count, layout.chunk, m), shape(*held),
        ],
        in_specs=[ANY] * 12,
        out_specs=[ANY] * 9,
        scratch_shapes=[
            pltpu.VMEM((n, m), F32), pltpu.VMEM((n, m), BF), pltpu.VMEM((n, m), F32), pltpu.VMEM((n, m), F32),
            pltpu.VMEM(gains.shape, F32), pltpu.VMEM((n, m), BF), pltpu.VMEM((n, m), BF), pltpu.VMEM(memory.shape, BF),
            pltpu.VMEM(wq.shape, BF), pltpu.VMEM(wo.shape, BF),
            pltpu.VMEM((n, m), BF), pltpu.VMEM((n, m), BF), pltpu.VMEM((n, m), BF), pltpu.VMEM(memory.shape, BF),
            pltpu.VMEM((32, m), F32), pltpu.VMEM((4, m, width), BF), pltpu.VMEM((4, width, m), BF),
            pltpu.VMEM((4, subs - 1, m // subs, width), BF), pltpu.VMEM((4, subs - 1, width // subs, m), BF),
            pltpu.VMEM(part_q, BF), pltpu.VMEM(part_o, BF),
            pltpu.VMEM((n, m), F32), pltpu.VMEM((4, n, m), BF), pltpu.VMEM((6, n // 2, m), BF), pltpu.VMEM((2, n // 2, m), BF),
            *pump_scratch(layout, chunks),
            dma(12), dma(8), dma(count), dma(count),
        ],
        compiler_params=params(5),
    )(cot, norm, after_cross, after_self, gains, query, flat, memory, wq, wo, part, own)


def attend_pair_back(p, triple, place, blocks, heads, grad_heads, deltas, sums, grads, grad_keys, grad_values):
    n = triple.shape[1]
    width = heads * HEAD
    scale = HEAD ** (-0.5)
    lanes = head_lanes(n)
    key_lanes = head_lanes(blocks * n)

    here = pl.ds(pl.multiple_of(p * 128, 128), 128)
    key_cols = pl.ds(pl.multiple_of(width + p * 128, 128), 128)
    value_cols = pl.ds(pl.multiple_of(2 * width + p * 128, 128), 128)
    query = triple[place, :, here]
    grad = grad_heads[place, :, here]
    keys = triple[0:blocks, :, key_cols].reshape(blocks * n, 128)
    values = triple[0:blocks, :, value_cols].reshape(blocks * n, 128)
    stats = sums[place]
    means = deltas[place]
    found = []
    for h in range(2):
        mine = (lanes < HEAD) if h == 0 else (lanes >= HEAD)
        log_sum = jnp.sum(jnp.where(lanes == 2 * p + h, stats, 0.0), -1, keepdims=True)
        delta = jnp.sum(jnp.where(lanes == 2 * p + h, means, 0.0), -1, keepdims=True)
        scores = dot_t(jnp.where(mine, query, jnp.zeros_like(query)), keys)
        row = lax.broadcasted_iota(jnp.int32, scores.shape, 0)
        col = lax.broadcasted_iota(jnp.int32, scores.shape, 1)
        probs = jnp.where(
            col <= row + (blocks - 1) * n, jnp.exp2(scores * (scale * LOG2E) - log_sum), 0.0
        )
        grad_probs = dot_t(jnp.where(mine, grad, jnp.zeros_like(grad)), values)
        grad_scores = (probs * (grad_probs - delta)).astype(BF)
        found.append((dot(grad_scores, keys), dot_c(grad_scores, query), dot_c(probs.astype(BF), grad)))
    grads[place, :, here] = (jnp.where(lanes < HEAD, found[0][0], found[1][0]) * scale).astype(BF)
    grad_keys[0 : blocks * n, here] += jnp.where(key_lanes < HEAD, found[0][1], found[1][1]) * scale
    grad_values[0 : blocks * n, here] += jnp.where(key_lanes < HEAD, found[0][2], found[1][2])


def attend_back_kernel(
    layout,
    branch_in, triple_in, flat_in, sums_in, out_in, qkv_in, rows_in, frames_in, gains_in, grad_in, memory_in, text_in, kv_in,
    own_in, land_in, feed_in,
    o_frames, o_sums, o_text, o_qkv, o_out, o_kv, o_feed, o_land,
    branch, triple, flat, sums, out, qkv, rows, frames, gains, grad_out, memory, text, kv,
    land_m, stage_m,
    grad_heads, deltas, grads, grad_keys, grad_values, part, land, stage, whole_qkv, land_qkv, whole_out, land_out,
    whole_kv, land_kv, text_grad, sums_out, sum_m, own, held, ring, result, ring_send, ring_recv, ring_store,
    load, store, send, recv,
):
    t, x, y, d = neighbours()
    s = lax.axis_index("sub")
    subs = lax.axis_size("sub")
    names = (
        (branch_in, branch.at[t]), (out_in, out), (flat_in, flat), (triple_in, triple), (sums_in, sums),
        (memory_in, memory), (own_in, own), (land_in, held), (qkv_in, qkv), (rows_in, rows),
        (text_in, text), (kv_in, kv), (frames_in, frames), (gains_in, gains), (grad_in, grad_out),
    )
    loads = [pltpu.make_async_copy(a, b, load.at[i]) for i, (a, b) in enumerate(names)]
    loads[7].start()
    for copy in loads[:7] + loads[8:]:
        copy.start()
    loads[7].wait()
    greet([{"tensor": x}, {"tensor": y}] + [{"sub": (s + k) % subs} for k in range(1, subs)] + group_ring())
    first, last = layout.middle, layout.later
    pump = Pump(
        own, held, ring, result, ring_send, ring_recv, ring_store, first, last, layout.count,
        feed_outputs(layout, o_feed),
    )

    def tick(k):
        @pl.when(k + first < last)
        def _():
            pump.step(k + first)

    n, m = grad_out.shape
    width = triple.shape[2]
    local = out.shape[0]
    heads = local // HEAD
    gather = Gather(branch.at[t], branch, send, recv, 0)
    scatter = Scatter(part, land, stage, send, recv, 6)
    scatter_m = Scatter(memory, land_m, stage_m, send, recv, 12)
    halves_qkv = Halves(whole_qkv, land_qkv, send, recv, 18)
    halves_out = Halves(whole_out, land_out, send, recv, 18 + subs - 1)
    halves_kv = Halves(whole_kv, land_kv, send, recv, 18 + 2 * (subs - 1))
    loads[0].wait()
    gather.start()
    for copy in loads[5:7]:
        copy.wait()
    scatter_m.diagonal()
    scatter_m.along_x()
    scatter_m.along_y()
    for copy in loads[1:5]:
        copy.wait()
    grad_keys[...] = jnp.zeros_like(grad_keys)
    grad_values[...] = jnp.zeros_like(grad_values)
    lanes = head_lanes(n)

    def turn(i, carry):
        far_y = i // 2
        far_x = i % 2
        place = (t // 2 + far_y - 2 * (t // 2) * far_y) * 2 + (t % 2 + far_x - 2 * (t % 2) * far_x)

        @pl.when(i == 1)
        def _():
            gather.relay_x()
            gather.relay_y()
            gather.have_x()

        @pl.when(i == 2)
        def _():
            gather.have_y()

        @pl.when(i == 3)
        def _():
            gather.have_d()

        grad_heads[place] = dot_t(branch[place], out[...]).astype(BF)

        def delta(p, stats):
            here = pl.ds(pl.multiple_of(p * 128, 128), 128)
            product = grad_heads[place, :, here].astype(F32) * flat[place, :, here].astype(F32)
            low = jnp.sum(jnp.where(lanes < HEAD, product, 0.0), -1, keepdims=True)
            high = jnp.sum(jnp.where(lanes < HEAD, 0.0, product), -1, keepdims=True)
            return jnp.where(lanes == 2 * p, low, jnp.where(lanes == 2 * p + 1, high, stats))

        deltas[place] = lax.fori_loop(0, heads // 2, delta, jnp.zeros((n, 128), F32))

        def pair(p, carry):
            tick(i * (heads // 2) + p)
            for blocks in range(1, 5):

                @pl.when(place == blocks - 1)
                def _(blocks=blocks):
                    attend_pair_back(
                        p, triple, blocks - 1, blocks, heads, grad_heads, deltas, sums, grads, grad_keys, grad_values
                    )

            return carry

        lax.fori_loop(0, heads // 2, pair, 0)
        return carry

    lax.fori_loop(0, 4, turn, 0)
    for copy in loads[8:12]:
        copy.wait()

    def finish_grads(i, carry):
        grads[i, :, local : 2 * local] = grad_keys[rows_at(i, n)].astype(BF)
        grads[i, :, 2 * local :] = grad_values[rows_at(i, n)].astype(BF)
        return carry

    lax.fori_loop(0, 4, finish_grads, 0)

    def back(i, carry):
        far_y = 1 - i // 2
        far_x = 1 - i % 2
        place = (t // 2 + far_y - 2 * (t // 2) * far_y) * 2 + (t % 2 + far_x - 2 * (t % 2) * far_x)

        def step(j, carry):
            part[place, :, cols(j, 512)] = dot_t(grads[place], qkv[rows_at(j, 512)]).astype(BF)
            return carry

        lax.fori_loop(0, m // 512, step, 0)
        tick(12 + i)

        @pl.when(i == 0)
        def _():
            scatter.diagonal()

        @pl.when(i == 1)
        def _():
            scatter.along_y()

        @pl.when(i == 2)
        def _():
            scatter.along_x()

        return carry

    lax.fori_loop(0, 4, back, 0)
    scatter_m.relay()

    def take_m(here, total):
        sum_m[here] = total.astype(BF)

    scatter_m.finish(take_m, 16)
    text_grad[...] = dot_t(sum_m[...], kv[...])
    stores = [pltpu.make_async_copy(text_grad, o_text, store.at[0])]
    stores[0].start()

    def grad_kv(j, carry):
        whole_kv[0, rows_at(j, 384)] = dot_c(text[:, cols(j, 384)], sum_m[...]).astype(BF)
        return carry

    lax.fori_loop(0, m // 384, grad_kv, 0)
    halves_kv.start(0)

    def grad_wout(j, carry):
        whole_out[0, :, cols(j, 512)] = dot_c(
            flat[...].reshape(4 * n, local), branch[:, :, cols(j, 512)].reshape(4 * n, 512)
        ).astype(BF)
        return carry

    lax.fori_loop(0, m // 512, grad_wout, 0)
    halves_out.start(0)
    scatter.relay()

    def grad_wqkv(j, carry):
        tick(16 + j)
        turned = rows[:, :, cols(j, 256)].reshape(4 * n, 256)

        def inner(i, carry):
            whole_qkv[0, rows_at(j, 256), cols(i, 384)] = dot_c(
                turned, grads[:, :, cols(i, 384)].reshape(4 * n, 384)
            ).astype(BF)
            return carry

        lax.fori_loop(0, width // 384, inner, 0)
        return carry

    lax.fori_loop(0, m // 256, grad_wqkv, 0)
    halves_qkv.start(0)
    for each, output, slot in ((halves_kv, o_kv, 1), (halves_out, o_out, 2), (halves_qkv, o_qkv, 3)):

        def take(here, total, each=each):
            each.land[0, 0, here] = total.astype(BF)

        each.total(0, take, 16)
        stores.append(pltpu.make_async_copy(each.land.at[0, 0], output, store.at[slot]))
        stores[-1].start()
    for copy in loads[12:]:
        copy.wait()

    def take_norm(here, total):
        part[t, here] = total.astype(BF)

    scatter.finish(take_norm, 64)

    def frame_block(i, carry):
        here = rows_at(i, 64)
        grad = part[t, here].astype(F32)
        inner, terms = norm_back_block(grad, frames[here].astype(F32), gains[0:1])
        grad_out[here] = grad_out[here] + inner
        return carry[0] + fold(terms), carry[1] + fold(grad)

    zero = jnp.zeros((8, m), F32)
    gain_sum, bias_sum = lax.fori_loop(0, n // 64, frame_block, (zero, zero))
    sums_out[0:8] = gain_sum
    sums_out[8:16] = bias_sum
    stores += [pltpu.make_async_copy(grad_out, o_frames, store.at[4]), pltpu.make_async_copy(sums_out, o_sums, store.at[5])]
    for copy in stores[-2:]:
        copy.start()
    pump.drain()
    stores.append(pltpu.make_async_copy(held, o_land, store.at[6]))
    stores[-1].start()
    gather.drain()
    for each in (scatter, scatter_m):
        each.drain()
    for each in (halves_qkv, halves_out, halves_kv):
        each.drain(0)
    for copy in stores:
        copy.wait()


def attend_back(
    layout, branch, triple, flat, sums, out, qkv, rows, frames, gains, grad, memory, text, kv, own, land, feed_sums, subs
):
    n, m = grad.shape
    width = triple.shape[2]
    local = out.shape[0]
    texts, kvw = text.shape[0], kv.shape[1]
    count = 18 + 3 * (subs - 1)
    v = pltpu.VMEM
    return pl.pallas_call(
        partial(attend_back_kernel, layout),
        name="attend_back",
        out_shape=[
            shape(n, m, kind=F32), shape(16, m, kind=F32), shape(texts, m, kind=F32), shape(m // subs, width),
            shape(local // subs, m), shape(m // subs, kvw), shape(*feed_sums.shape), shape(*land.shape),
        ],
        in_specs=[ANY] * 16,
        out_specs=[ANY] * 8,
        input_output_aliases={15: 6},
        scratch_shapes=[
            v((4, n, m), BF), v(triple.shape, BF), v(flat.shape, BF), v(sums.shape, F32), v(out.shape, BF), v(qkv.shape, BF),
            v(rows.shape, BF), v(frames.shape, frames.dtype), v(gains.shape, F32), v((n, m), F32), v(memory.shape, BF),
            v(text.shape, BF), v(kv.shape, BF),
            v((6, texts // 2, kvw), BF), v((2, texts // 2, kvw), BF),
            v((4, n, local), BF), v((4, n, 128), F32), v((4, n, width), BF), v((4 * n, local), F32), v((4 * n, local), F32),
            v((4, n, m), BF), v((6, n // 2, m), BF), v((2, n // 2, m), BF),
            v((1, m, width), BF), v((1, subs - 1, m // subs, width), BF),
            v((1, local, m), BF), v((1, subs - 1, local // subs, m), BF),
            v((1, m, kvw), BF), v((1, subs - 1, m // subs, kvw), BF),
            v((texts, m), F32), v((16, m), F32), v((texts, kvw), BF),
            *pump_scratch(layout, layout.feed_count),
            dma(15), dma(7), dma(count), dma(count),
        ],
        compiler_params=params(6),
    )(branch, triple, flat, sums, out, qkv, rows, frames, gains, grad, memory, text, kv, own, land, feed_sums)


def total_kernel(
    layout,
    feed_in, qkv_in, kv_in, out_in, cross_q_in, cross_o_in, sums_a_in, sums_b_in, text_in, land_in, summed_in,
    o_qkv, o_cq, o_kv, o_out, o_co, o_text, o_vectors, o_feed,
    own, held, ring, result, ring_send, ring_recv, ring_store,
    cross_q, cross_o, land_q, land_o, stage_q, stage_o,
    sums_a, sums_b, text, text_land, text_full, vectors, vectors_land, share, share_land, load, store, send, recv,
):
    t, x, y, d = neighbours()
    s, subs = lax.axis_index("sub"), lax.axis_size("sub")
    g, groups = lax.axis_index("group"), lax.axis_size("group")
    chunk, m, local = layout.chunk, layout.m, layout.local
    width, quarter = 3 * local, layout.piece // 4 // chunk
    at_qkv, at_kv, at_out, at_cq, at_co = (
        r // chunk for r in (layout.qkv, layout.kv, layout.out, layout.cq, layout.co)
    )
    outs = layout.out_rows // chunk
    pairs = [
        (land_in, held),
        (feed_in, own.at[pl.ds(0, at_qkv)]),
        (qkv_in.at[pl.ds(0, 3 * quarter)], own.at[pl.ds(at_qkv, 3 * quarter), :, pl.ds(0, width)]),
    ]
    for i in range(3):
        pairs.append(
            (
                qkv_in.at[pl.ds(3 * quarter, quarter), :, pl.ds(i * local, local)],
                own.at[pl.ds(at_qkv + i * quarter, quarter), :, pl.ds(width, local)],
            )
        )
    for i in range(2):
        pairs.append(
            (
                kv_in.at[pl.ds(2 * i * quarter, 2 * quarter)],
                own.at[pl.ds(at_kv, 2 * quarter), :, pl.ds(2 * i * local, 2 * local)],
            )
        )
    pairs += [
        (out_in, own.at[pl.ds(at_out, outs)]),
        (sums_a_in, sums_a), (sums_b_in, sums_b), (text_in, text), (cross_q_in, cross_q), (cross_o_in, cross_o),
    ]
    loads = [pltpu.make_async_copy(a, b, load.at[i]) for i, (a, b) in enumerate(pairs)]
    for copy in loads:
        copy.start()
    loads[0].wait()
    greet(
        [{"tensor": x}, {"tensor": y}, {"tensor": d}]
        + [{"sub": (s + k) % subs} for k in range(1, subs)]
        + [{"group": (g + k) % groups} for k in range(1, groups)]
    )
    for copy in loads[1:]:
        copy.wait()
    share_width = m // subs
    for i in range(6):
        source, at = (sums_a, i) if i < 4 else (sums_b, i - 4)
        row = jnp.sum(source[8 * at : 8 * at + 8], 0, keepdims=True)
        for j in range(subs):
            vectors[j, i : i + 1] = row[:, j * share_width : (j + 1) * share_width]
    strip = text.shape[0] // 4

    def remote(source, target, k, device):
        return pltpu.make_async_remote_copy(
            source, target, send.at[k], recv.at[k], device_id=device, device_id_type=MESH
        )

    square = (x, y, d)
    first = [remote(vectors, vectors_land.at[k], k, {"tensor": square[k]}) for k in range(3)]
    first += [
        remote(text.at[rows_at(square[k], strip)], text_land.at[k], 3 + k, {"tensor": square[k]}) for k in range(3)
    ]
    second = [
        remote(share.at[0, (s + k) % subs], share_land.at[k - 1], 5 + k, {"sub": (s + k) % subs}) for k in range(1, subs)
    ]
    base = 5 + subs
    second += [
        remote(text_full.at[rows_at(t, strip)], text_full.at[rows_at(t, strip)], base + k, {"tensor": square[k]}) for k in range(3)
    ]
    base += 3
    third = [
        remote(share.at[1, 0], share_land.at[subs - 2 + k], base + k - 1, {"group": (g + k) % groups})
        for k in range(1, groups)
    ]
    base += groups - 1
    scatter_q = Scatter(cross_q, land_q, stage_q, send, recv, base)
    scatter_o = Scatter(cross_o, land_o, stage_o, send, recv, base + 6)
    for copy in first:
        copy.start()
    for each in (scatter_q, scatter_o):
        each.diagonal()
    for each in (scatter_q, scatter_o):
        each.along_x()
        each.along_y()

    def outputs(c, block, slots, act):
        slot = c % RING

        def region(begin, end, copies):
            @pl.when(jnp.logical_and(c >= begin, c < end))
            def _():
                for i, (source, target) in enumerate(copies(c - begin)):
                    act(pltpu.make_async_copy(source, target, slots.at[slot, i]))

        def whole(output):
            return lambda r: [(block, output.at[r])]

        region(layout.later - LAG * (groups - 1), at_qkv, lambda r: [(block, o_feed.at[c])])
        region(
            at_qkv, at_kv,
            lambda r: [
                (block.at[:, pl.ds(0, width)], o_qkv.at[r]),
                (
                    block.at[:, pl.ds(width, local)],
                    o_qkv.at[3 * quarter + r % quarter, :, pl.ds(pl.multiple_of(r // quarter * local, local), local)],
                ),
            ],
        )
        region(
            at_kv, at_out,
            lambda r: [
                (block.at[:, pl.ds(2 * i * local, 2 * local)], o_kv.at[2 * i * quarter + r]) for i in range(2)
            ],
        )
        region(at_out, at_cq, whole(o_out))
        region(
            at_cq, at_co,
            lambda r: [(block.at[:, pl.ds(i * local, local)], o_cq.at[i * quarter + r]) for i in range(4)],
        )
        region(at_co, at_co + outs, whole(o_co))

    begin, end = layout.later, layout.end
    pump = Pump(own, held, ring, result, ring_send, ring_recv, ring_store, begin, end, layout.count, outputs)

    def run(a, b):
        def step(k, carry):
            pump.step(k)
            return carry

        lax.fori_loop(a, b, step, 0)

    run(begin, begin + 3)
    for copy in first:
        copy.wait_recv()
    for j in range(subs):
        share[0, j] = vectors[j] + vectors_land[0, j] + vectors_land[1, j] + vectors_land[2, j]
    text_full[rows_at(t, strip)] = text[rows_at(t, strip)] + text_land[0] + text_land[1] + text_land[2]
    for copy in first:
        copy.wait_send()
    for copy in second:
        copy.start()
    run(begin + 3, begin + 6)
    for copy in second:
        copy.wait_recv()
    total = share[0, s]
    for k in range(1, subs):
        total = total + share_land[k - 1]
    share[1, 0] = total
    text_store = pltpu.make_async_copy(text_full, o_text, store.at[0])
    text_store.start()
    for copy in third:
        copy.start()
    relay = max(begin + 6, begin + (at_cq - begin) // 2)
    run(begin + 6, relay)
    for each in (scatter_q, scatter_o):
        each.relay()
    finish = min(at_cq, relay + 8)
    run(relay, finish)

    def take_q(rows, value):
        row = rows.start
        part = row // (quarter * chunk)
        c = row // chunk - part * quarter
        own[at_cq + c, :, pl.ds(pl.multiple_of(part * local, local), local)] = value.astype(BF)

    scatter_q.finish(take_q, chunk)
    step = min(chunk, scatter_o.half)

    def take_o(rows, value):
        own[at_co + rows.start // chunk, rows_at(rows.start % chunk // step, step)] = value.astype(BF)

    scatter_o.finish(take_o, step)
    run(finish, end)
    for copy in third:
        copy.wait_recv()
    total = share[1, 0]
    for k in range(1, groups):
        total = total + share_land[subs - 2 + k]
    share[2, 0] = total
    vector_store = pltpu.make_async_copy(share.at[2, 0], o_vectors, store.at[1])
    vector_store.start()
    for copy in second + third:
        copy.wait_send()
    for each in (scatter_q, scatter_o):
        each.drain()
    pump.drain()
    text_store.wait()
    vector_store.wait()


def total(layout, pieces, qkv, kv, out, cross_q, cross_o, sums_a, sums_b, text, land, summed, subs, groups):
    m, chunk = layout.m, layout.chunk
    v = pltpu.VMEM
    sems = 7 + subs + groups + 12
    tall = lambda a: a.reshape(-1, chunk, a.shape[1])
    qkv, kv, out = tall(qkv), tall(kv), tall(out)
    piece_q, piece_o = cross_q.shape[1:], cross_o.shape[1:]
    return pl.pallas_call(
        partial(total_kernel, layout),
        name="total",
        out_shape=[
            shape(*qkv.shape), shape(layout.piece // chunk, chunk, layout.local), shape(*kv.shape), shape(*out.shape),
            shape(*out.shape), shape(*text.shape, kind=F32), shape(8, m // subs, kind=F32), shape(*summed.shape),
        ],
        in_specs=[ANY] * 11,
        out_specs=[ANY] * 8,
        input_output_aliases={10: 7},
        scratch_shapes=[
            *pump_scratch(layout, layout.count),
            v(cross_q.shape, BF), v(cross_o.shape, BF),
            v((6, piece_q[0] // 2, piece_q[1]), BF), v((6, piece_o[0] // 2, piece_o[1]), BF),
            v((2, piece_q[0] // 2, piece_q[1]), BF), v((2, piece_o[0] // 2, piece_o[1]), BF),
            v(sums_a.shape, F32), v(sums_b.shape, F32), v(text.shape, F32),
            v((3, text.shape[0] // 4, m), F32), v(text.shape, F32), v((subs, 8, m // subs), F32), v((3, subs, 8, m // subs), F32),
            v((3, subs, 8, m // subs), F32), v((subs - 1 + groups - 1, 8, m // subs), F32),
            dma(14), dma(2), dma(sems), dma(sems),
        ],
        compiler_params=params(7),
    )(pieces, qkv, kv, out, cross_q, cross_o, sums_a, sums_b, text, land, summed)


def local(
    frames, text_states, selfgain, selfbias, selfqkv, selfout, crossgain, crossbias, crossquery, crosskv, crossout,
    feedgain, feedbias, feedup, feeddown, cotangent,
):
    subs, groups = lax.axis_size("sub"), lax.axis_size("group")
    m = frames.shape[2]
    width = selfout.shape[0]
    qkv = selfqkv.reshape(m, 3 * width)
    kv = crosskv.reshape(m, 2 * width)
    self_gains = jnp.stack([selfgain, selfbias])
    gains = jnp.stack([crossgain, crossbias, feedgain, feedbias])
    rows, triple, memory = enter(frames[0], self_gains[0:1], self_gains[1:2], qkv, text_states[0], kv)
    flat, sums, after_self, wq, wo = attend(triple, selfout, frames[0], crossquery, crossout, subs)
    wo = wo.reshape(4 * width, m)
    query, cross_flat, after_cross, feed_rows, grads = cross(after_self, gains, wq, wo, memory, cotangent[0])
    layout = Layout(m, width, subs, groups)
    part, norm_grad, pieces = feed(feed_rows, grads, feedup, feeddown, subs)
    pieces = pieces.reshape(-1, layout.chunk, m)
    grad_out, branch, sums_a, memory_grad, piece_q, piece_o, layer_output, summed, land = cross_back(
        layout, cotangent[0], norm_grad, after_cross, after_self, gains, query, cross_flat, memory, wq, wo, part, pieces, subs
    )
    frame_grad, sums_b, text_part, grad_qkv, grad_out_weight, grad_kv, summed, land = attend_back(
        layout, branch, triple, flat, sums, selfout, qkv, rows, frames[0], self_gains, grad_out, memory_grad,
        text_states[0], kv, pieces, land, summed, subs,
    )
    full_qkv, full_cq, full_kv, full_out, full_co, text_grad, vectors, summed = total(
        layout, pieces, grad_qkv, grad_kv, grad_out_weight, piece_q, piece_o, sums_a, sums_b, text_part, land, summed,
        subs, groups,
    )
    down, up = summed.reshape(2, -1, m)
    return (
        layer_output[None],
        frame_grad[None],
        text_grad[None],
        vectors[4],
        vectors[5],
        full_qkv.astype(F32).reshape(-1, 3, width),
        full_out.astype(F32).reshape(-1, m),
        vectors[2],
        vectors[3],
        full_cq.astype(F32).reshape(-1, width),
        full_kv.astype(F32).reshape(-1, 2, width),
        full_co.astype(F32).reshape(-1, m),
        vectors[0],
        vectors[1],
        up.astype(F32),
        down.astype(F32),
    )


def solution(mesh):
    clips = P(("sub", "group"), "tensor", None)
    whole = P(("sub", "group"), None, None)
    narrow, wide = P("tensor", None), P(None, "tensor")
    third = P(None, None, "tensor")
    vector = P("sub")
    return jax.shard_map(
        local,
        mesh=mesh,
        in_specs=(
            clips, whole, P(), P(), third, narrow, P(), P(), wide, third, narrow, P(), P(), wide, narrow, clips,
        ),
        out_specs=(
            clips, clips, whole, vector, vector, P("sub", None, "tensor"), P(("tensor", "sub"), None), vector, vector,
            P("sub", "tensor"), P("sub", None, "tensor"), P(("tensor", "sub"), None), vector, vector,
            P("sub", "tensor"), P(("tensor", "sub"), None),
        ),
        check_vma=False,
    )
```

```python
from functools import partial

import jax
import jax.numpy as jnp
from jax import lax
from jax.experimental import pallas as pl
from jax.experimental.pallas import tpu as pltpu
from jax.sharding import PartitionSpec as P

HEAD = 64
EPSILON = 1e-05
NEG_BIG = -1e30
LOG2E = 1.4426950408889634
MESH = pl.DeviceIdType.MESH
F32 = jnp.float32
BF = jnp.bfloat16
ANY = pl.BlockSpec(memory_space=pl.ANY)
VMEM_LIMIT = 63 << 20


def neighbours():
    t = lax.axis_index("tensor")
    return t, t + 1 - 2 * (t % 2), (t + 2) % 4, 3 - t


def greet(targets):
    barrier = pltpu.get_barrier_semaphore()
    for target in targets:
        pl.semaphore_signal(barrier, inc=1, device_id=target, device_id_type=MESH)
    pl.semaphore_wait(barrier, len(targets))


def dot(a, b):
    return lax.dot_general(a, b, (((1,), (0,)), ((), ())), preferred_element_type=F32)


def dot_t(a, b):
    return lax.dot_general(a, b, (((1,), (1,)), ((), ())), preferred_element_type=F32)


def dot_c(a, b):
    return lax.dot_general(a, b, (((0,), (0,)), ((), ())), preferred_element_type=F32)


def cols(j, width):
    return pl.ds(pl.multiple_of(j * width, width), width)


def rows_at(j, height):
    return pl.ds(pl.multiple_of(j * height, height), height)


def split(count):
    first = (count // 2 + 15) // 16 * 16
    return pl.ds(0, first), pl.ds(first, count - first)


class Gather:
    def __init__(self, own, dst, send, recv, base, halves=None):
        self.own, self.dst, self.send, self.recv, self.base = own, dst, send, recv, base
        self.halves = halves or split(own.shape[0])

    def copy(self, k):
        t, x, y, _ = neighbours()
        first, second = self.halves
        half = (first, second, second, first, first, second)[k]
        place = (t, t, t, t, x, y)[k]
        target = (x, y, x, y, y, x)[k]
        source = self.own.at[half] if k < 4 else self.dst.at[place, half]
        return pltpu.make_async_remote_copy(
            source,
            self.dst.at[place, half],
            self.send.at[self.base + k],
            self.recv.at[self.base + k],
            device_id={"tensor": target},
            device_id_type=MESH,
        )

    def start(self):
        for k in range(4):
            self.copy(k).start()

    def relay_x(self):
        self.copy(0).wait_recv()
        self.copy(4).start()

    def relay_y(self):
        self.copy(1).wait_recv()
        self.copy(5).start()

    def have_x(self):
        self.copy(2).wait_recv()

    def have_y(self):
        self.copy(3).wait_recv()

    def have_d(self):
        self.copy(4).wait_recv()
        self.copy(5).wait_recv()

    def drain(self):
        for k in range(6):
            self.copy(k).wait_send()


class Scatter:
    def __init__(self, part, land, stage, send, recv, base):
        self.part, self.land, self.stage = part, land, stage
        self.send, self.recv, self.base = send, recv, base
        self.half = part.shape[1] // 2

    def copy(self, k):
        t, x, y, d = neighbours()
        low, high = pl.ds(0, self.half), pl.ds(self.half, self.half)
        source = (
            self.part.at[d, low],
            self.part.at[d, high],
            self.part.at[x, low],
            self.stage.at[1],
            self.part.at[y, high],
            self.stage.at[0],
        )[k]
        target = (x, y, x, x, y, y)[k]
        return pltpu.make_async_remote_copy(
            source,
            self.land.at[k],
            self.send.at[self.base + k],
            self.recv.at[self.base + k],
            device_id={"tensor": target},
            device_id_type=MESH,
        )

    def diagonal(self):
        self.copy(0).start()
        self.copy(1).start()

    def along_x(self):
        self.copy(2).start()

    def along_y(self):
        self.copy(4).start()

    def relay(self):
        t, x, y, d = neighbours()
        low, high = pl.ds(0, self.half), pl.ds(self.half, self.half)
        self.copy(0).wait_recv()
        self.stage[0] = (self.part[y, low].astype(F32) + self.land[0].astype(F32)).astype(BF)
        self.copy(5).start()
        self.copy(1).wait_recv()
        self.stage[1] = (self.part[x, high].astype(F32) + self.land[1].astype(F32)).astype(BF)
        self.copy(3).start()

    def finish(self, take, step):
        t, x, y, d = neighbours()
        for k in (2, 4, 5, 3):
            self.copy(k).wait_recv()
        for base, a, b in ((0, 2, 5), (self.half, 4, 3)):

            def block(i, carry, base=base, a=a, b=b):
                here = rows_at(i, step)
                rows = pl.ds(pl.multiple_of(base + i * step, step), step)
                take(
                    rows,
                    self.part[t, rows].astype(F32)
                    + self.land[a, here].astype(F32)
                    + self.land[b, here].astype(F32),
                )
                return carry

            lax.fori_loop(0, self.half // step, block, 0)

    def drain(self):
        for k in range(6):
            self.copy(k).wait_send()


def normed_rows(values):
    centre = values - jnp.mean(values, -1, keepdims=True)
    inverse = lax.rsqrt(jnp.mean(centre * centre, -1, keepdims=True) + EPSILON)
    return centre * inverse, inverse


def params(cid, **more):
    return pltpu.CompilerParams(
        collective_id=cid, has_side_effects=True, vmem_limit_bytes=VMEM_LIMIT, **more
    )


def dma(count):
    return pltpu.SemaphoreType.DMA((count,))


def shape(*dims, kind=BF):
    return jax.ShapeDtypeStruct(dims, kind)


LAG = 2
RING = 4


def either(condition, other):
    return jnp.logical_and(condition, other)


class Pump:
    def __init__(self, own, land, ring, result, send, recv, store, first, last, count, outputs):
        self.own, self.land, self.ring, self.result = own, land, ring, result
        self.send, self.recv, self.store = send, recv, store
        self.first, self.last, self.count, self.outputs = first, last, count, outputs
        self.window = land.shape[1]
        self.g, self.n = lax.axis_index("group"), lax.axis_size("group")

    def copy(self, way, c):
        target = (self.g + 1) % self.n if way == 0 else (self.g + self.n - 1) % self.n
        return pltpu.make_async_remote_copy(
            self.ring.at[way, c % RING],
            self.land.at[way, c % self.window],
            self.send.at[way, c % RING],
            self.recv.at[way, c % self.window],
            device_id={"group": target},
            device_id_type=MESH,
        )

    def flow(self, way, k):
        place = self.g if way == 0 else self.n - 1 - self.g
        c = k - LAG * place

        @pl.when(either(c >= 0, c < self.count))
        def _():
            @pl.when(either(place > 0, k - LAG >= self.first))
            def _():
                self.copy(way, c).wait_recv()

            @pl.when(place < self.n - 1)
            def _():
                @pl.when(either(c >= RING, k - RING >= self.first))
                def _():
                    self.copy(way, c - RING).wait_send()

                @pl.when(place > 0)
                def _():
                    before = self.land[way, c % self.window].astype(F32)
                    self.ring[way, c % RING] = (self.own[c].astype(F32) + before).astype(BF)

                @pl.when(place == 0)
                def _():
                    self.ring[way, c % RING] = self.own[c]

                self.copy(way, c).start()

    def finished(self, k):
        far = jnp.maximum(self.g, self.n - 1 - self.g)
        return k - LAG * far

    def step(self, k):
        self.flow(0, k)
        self.flow(1, k)
        f = self.finished(k)

        @pl.when(either(f >= 0, f < self.count))
        def _():
            @pl.when(either(f >= RING, k - RING >= self.first))
            def _():
                self.outputs(f - RING, self.result.at[f % RING], self.store, lambda copy: copy.wait())

            mine = self.own[f].astype(F32)
            slot, held = f % RING, f % self.window

            @pl.when(either(self.g > 0, self.g < self.n - 1))
            def _():
                both = self.land[0, held].astype(F32) + self.land[1, held].astype(F32)
                self.result[slot] = (mine + both).astype(BF)

            @pl.when(self.g == 0)
            def _():
                self.result[slot] = (mine + self.land[1, held].astype(F32)).astype(BF)

            @pl.when(self.g == self.n - 1)
            def _():
                self.result[slot] = (mine + self.land[0, held].astype(F32)).astype(BF)

            self.outputs(f, self.result.at[slot], self.store, lambda copy: copy.start())

    def drain(self):
        for way in range(2):
            place = self.g if way == 0 else self.n - 1 - self.g
            top = jnp.minimum(self.last - LAG * place, self.count)
            for j in range(1, RING + 1):
                c = top - j

                @pl.when(either(place < self.n - 1, either(c >= 0, c + LAG * place >= self.first)))
                def _(way=way, c=c):
                    self.copy(way, c).wait_send()

            for k in range(max(self.first, self.last - LAG), self.last):
                c = k - LAG * (place - 1)

                @pl.when(either(place > 0, either(c >= 0, c < self.count)))
                def _(way=way, c=c):
                    self.copy(way, c).wait_recv()

        far = jnp.maximum(self.g, self.n - 1 - self.g)
        top = jnp.minimum(self.last - LAG * far, self.count)
        for j in range(1, RING + 1):
            f = top - j

            @pl.when(either(f >= 0, f + LAG * far >= self.first))
            def _(f=f):
                self.outputs(f, self.result.at[f % RING], self.store, lambda copy: copy.wait())


class Layout:
    def __init__(self, m, local, subs, groups):
        piece = m // subs
        self.m, self.piece, self.local = m, piece, local
        self.out_rows = local // subs
        self.chunk = 48
        self.feed = 2 * piece
        self.qkv = self.feed
        self.kv = self.qkv + 3 * piece // 4
        self.out = self.kv + piece // 2
        self.cq = self.out + self.out_rows
        self.co = self.cq + piece // 4
        self.rows = self.co + self.out_rows
        self.count = self.rows // self.chunk
        self.feed_count = self.feed // self.chunk
        self.window = LAG * (groups + 1)
        self.middle = min(10, self.feed_count // 3)
        self.later = min(32, self.feed_count)
        self.end = self.count + LAG * (groups - 1)


def feed_outputs(layout, *halves):
    def outputs(c, block, store, act):
        count = layout.feed_count // 2
        for i, half in enumerate(halves):

            @pl.when(either(c >= i * count, c < (i + 1) * count))
            def _(i=i, half=half):
                act(pltpu.make_async_copy(block, half.at[c - i * count], store.at[c % RING, 0]))

    return outputs


def pump_scratch(layout, count):
    chunk, m = layout.chunk, layout.m
    return [
        pltpu.VMEM((count, chunk, m), BF),
        pltpu.VMEM((2, layout.window, chunk, m), BF),
        pltpu.VMEM((2, RING, chunk, m), BF),
        pltpu.VMEM((RING, chunk, m), BF),
        pltpu.SemaphoreType.DMA((2, RING)),
        pltpu.SemaphoreType.DMA((2, layout.window)),
        pltpu.SemaphoreType.DMA((RING, 4)),
    ]


def group_ring():
    g, n = lax.axis_index("group"), lax.axis_size("group")
    return [{"group": (g + 1) % n}, {"group": (g + n - 1) % n}]


def enter_kernel(
    frames, gains, qkv, text, kv, o_rows, o_triple, o_memory,
    v_frames, v_gains, v_qkv, v_text, v_kv, rows, triple, memory, load, store, send, recv,
):
    t, x, y, d = neighbours()
    loads = [
        pltpu.make_async_copy(a, b, load.at[i])
        for i, (a, b) in enumerate(
            (
                (frames, v_frames), (gains, v_gains), (text, v_text), (kv, v_kv),
                *((qkv.at[i], v_qkv.at[:, pl.ds(i * qkv.shape[2], qkv.shape[2])]) for i in range(3)),
            )
        )
    ]
    for copy in loads:
        copy.start()
    greet([{"tensor": x}, {"tensor": y}])
    for copy in loads[:2]:
        copy.wait()
    count, width = v_qkv.shape
    block = 384

    def norm_block(i, carry):
        here = rows_at(i, 64)
        hat, _ = normed_rows(v_frames[here].astype(F32))
        rows[t, here] = (hat * v_gains[4:5] + v_gains[5:6]).astype(BF)
        return carry

    lax.fori_loop(0, v_frames.shape[0] // 64, norm_block, 0)
    gather = Gather(rows.at[t], rows, send, recv, 0)
    gather.start()
    texts = Gather(memory.at[t], memory, send, recv, 6)

    def project(place):
        def step(j, carry):
            triple[place, :, cols(j, block)] = dot(rows[place], v_qkv[:, cols(j, block)]).astype(BF)
            return carry

        lax.fori_loop(0, width // block, step, 0)

    def put(k, place):
        a = pltpu.make_async_copy(rows.at[place], o_rows.at[place], store.at[2 * k])
        b = pltpu.make_async_copy(triple.at[place], o_triple.at[place], store.at[2 * k + 1])
        a.start()
        b.start()
        return [a, b]

    loads[2].wait()
    loads[3].wait()

    def texts_step(j, carry):
        memory[t, :, cols(j, block)] = dot(v_text[...], v_kv[:, cols(j, block)]).astype(BF)
        return carry

    lax.fori_loop(0, v_kv.shape[1] // block, texts_step, 0)
    texts.start()
    for copy in loads[4:]:
        copy.wait()
    project(t)
    stores = put(0, t)
    gather.relay_x()
    gather.relay_y()
    gather.have_x()
    project(x)
    stores += put(1, x)
    gather.have_y()
    project(y)
    stores += put(2, y)
    texts.relay_x()
    texts.relay_y()
    texts.have_x()
    texts.have_y()
    gather.have_d()
    project(d)
    stores += put(3, d)
    texts.have_d()
    last = pltpu.make_async_copy(memory, o_memory, store.at[8])
    last.start()
    gather.drain()
    texts.drain()
    for copy in stores:
        copy.wait()
    last.wait()


def enter(frames, gains, qkv, text, kv):
    n, m = frames.shape
    width, texts, kvw = 3 * qkv.shape[2], text.shape[0], kv.shape[1]
    return pl.pallas_call(
        enter_kernel,
        name="enter",
        out_shape=[shape(4, n, m), shape(4, n, width), shape(4, texts, kvw)],
        in_specs=[ANY] * 5,
        out_specs=[ANY] * 3,
        scratch_shapes=[
            pltpu.VMEM((n, m), frames.dtype), pltpu.VMEM(gains.shape, F32),
            pltpu.VMEM((m, width), BF), pltpu.VMEM(text.shape, BF), pltpu.VMEM(kv.shape, BF),
            pltpu.VMEM((4, n, m), BF), pltpu.VMEM((4, n, width), BF), pltpu.VMEM((4, texts, kvw), BF),
            dma(7), dma(9), dma(12), dma(12),
        ],
        compiler_params=params(1),
    )(frames, gains, qkv, text, kv)


def head_lanes(rows):
    return lax.broadcasted_iota(jnp.int32, (rows, 128), 1)


def attend_rows(triple, place, blocks, heads, flat, sums):
    n = triple.shape[1]
    width = heads * HEAD
    scale = HEAD ** (-0.5) * LOG2E
    lanes = head_lanes(n)

    def pair(p, stats):
        here = pl.ds(pl.multiple_of(p * 128, 128), 128)
        key_cols = pl.ds(pl.multiple_of(width + p * 128, 128), 128)
        value_cols = pl.ds(pl.multiple_of(2 * width + p * 128, 128), 128)
        query = triple[place, :, here]
        keys = triple[0:blocks, :, key_cols].reshape(blocks * n, 128)
        values = triple[0:blocks, :, value_cols].reshape(blocks * n, 128)
        outs = []
        for h in range(2):
            mine = (lanes < HEAD) if h == 0 else (lanes >= HEAD)
            scores = dot_t(jnp.where(mine, query, jnp.zeros_like(query)), keys)
            row = lax.broadcasted_iota(jnp.int32, scores.shape, 0)
            col = lax.broadcasted_iota(jnp.int32, scores.shape, 1)
            scores = jnp.where(col <= row + (blocks - 1) * n, scores, NEG_BIG)
            peak = jnp.max(scores, -1, keepdims=True) * scale
            exponent = jnp.exp2(scores * scale - peak)
            total = jnp.sum(exponent, -1, keepdims=True)
            outs.append(dot(exponent.astype(BF), values) / total)
            stats = jnp.where(lanes == 2 * p + h, peak + jnp.log2(total), stats)
        flat[place, :, here] = jnp.where(lanes < HEAD, outs[0], outs[1]).astype(BF)
        return stats

    sums[place] = lax.fori_loop(0, heads // 2, pair, jnp.zeros((n, 128), F32))


def attend_kernel(
    triple_in, out_in, frames_in, wq, wo, o_flat, o_sums, o_after, o_wq, o_wo,
    triple, v_out, v_frames, flat, sums, after, part, land, stage, v_wq, v_wo, load, store, send, recv, side,
):
    t, x, y, d = neighbours()
    s = lax.axis_index("sub")
    subs = lax.axis_size("sub")
    n = triple.shape[1]
    m = v_out.shape[1]
    heads = v_out.shape[0] // HEAD
    loads = [
        pltpu.make_async_copy(a, b, load.at[i])
        for i, (a, b) in enumerate(
            ((triple_in, triple), (out_in, v_out), (frames_in, v_frames), (wq, v_wq), (wo, v_wo))
        )
    ]
    for copy in loads:
        copy.start()
    greet(
        [{"tensor": x}, {"tensor": y}]
        + [{"sub": (s + k) % subs} for k in range(1, subs)]
    )
    scatter = Scatter(part, land, stage, send, recv, 0)
    gathers = []
    for i, (weight, full) in enumerate(((wq, o_wq), (wo, o_wo))):
        piece = weight.shape[0] // subs
        first, second = split(piece)
        offset = pl.multiple_of(s * piece, piece)
        halves = (
            pl.ds(offset, first.size),
            pl.ds(pl.multiple_of(offset + first.size, 16), second.size),
        )
        gathers.append((Gather(weight, full, send, recv, 6 + 6 * i, halves), full, pl.ds(offset, piece)))

    def shared(i, j, k):
        _, full, piece = gathers[i]
        place = (x, y, d)[j]
        slot = (i * 3 + j) * (subs - 1) + k - 1
        return pltpu.make_async_remote_copy(
            full.at[place, piece], full.at[place, piece],
            send.at[18 + slot], recv.at[18 + slot],
            device_id={"sub": (s + k) % subs}, device_id_type=MESH,
        )

    for gather, _, _ in gathers:
        gather.start()
    for copy in loads[:2]:
        copy.wait()

    def one(i, carry):
        far_y = 1 - i // 2
        far_x = 1 - i % 2
        place = (t // 2 + far_y - 2 * (t // 2) * far_y) * 2 + (t % 2 + far_x - 2 * (t % 2) * far_x)
        for blocks in range(1, 5):

            @pl.when(place == blocks - 1)
            def _(blocks=blocks):
                attend_rows(triple, blocks - 1, blocks, heads, flat, sums)

        def out_step(j, carry):
            part[place, :, cols(j, 512)] = dot(flat[place], v_out[:, cols(j, 512)]).astype(BF)
            return carry

        lax.fori_loop(0, m // 512, out_step, 0)

        @pl.when(i == 0)
        def _():
            scatter.diagonal()

        @pl.when(i == 1)
        def _():
            scatter.along_y()

        @pl.when(i == 2)
        def _():
            scatter.along_x()

        return carry

    lax.fori_loop(0, 4, one, 0)
    for gather, _, _ in gathers:
        gather.relay_x()
        gather.relay_y()
    stores = [
        pltpu.make_async_copy(flat, o_flat, store.at[0]),
        pltpu.make_async_copy(sums, o_sums, store.at[1]),
    ]
    loads[3].wait()
    loads[4].wait()
    stores += [
        pltpu.make_async_copy(v_wq, o_wq.at[t], store.at[2]),
        pltpu.make_async_copy(v_wo, o_wo.at[t], store.at[3]),
    ]
    for copy in stores:
        copy.start()
    scatter.relay()
    for i, (gather, _, _) in enumerate(gathers):
        gather.have_x()
        gather.have_y()
        gather.have_d()
        for j in range(3):
            for k in range(1, subs):
                shared(i, j, k).start()
    loads[2].wait()

    def take(rows, total):
        after[rows] = v_frames[rows].astype(F32) + total

    scatter.finish(take, 64)
    last = pltpu.make_async_copy(after, o_after, store.at[4])
    last.start()
    scatter.drain()
    for i, (gather, _, _) in enumerate(gathers):
        gather.drain()
        for j in range(3):
            for k in range(1, subs):
                shared(i, j, k).wait()
    for copy in stores:
        copy.wait()
    last.wait()


def attend(triple, out, frames, wq, wo, subs):
    _, n, width = triple.shape
    local, m = out.shape
    extra = 18 + 6 * (subs - 1)
    return pl.pallas_call(
        attend_kernel,
        name="attend",
        out_shape=[
            shape(4, n, local), shape(4, n, 128, kind=F32), shape(n, m, kind=F32),
            shape(4, *wq.shape), shape(4, *wo.shape),
        ],
        in_specs=[ANY] * 5,
        out_specs=[ANY] * 5,
        scratch_shapes=[
            pltpu.VMEM((4, n, width), BF), pltpu.VMEM((local, m), BF), pltpu.VMEM((n, m), frames.dtype),
            pltpu.VMEM((4, n, local), BF), pltpu.VMEM((4, n, 128), F32), pltpu.VMEM((n, m), F32),
            pltpu.VMEM((4, n, m), BF), pltpu.VMEM((6, n // 2, m), BF), pltpu.VMEM((2, n // 2, m), BF),
            pltpu.VMEM(wq.shape, BF), pltpu.VMEM(wo.shape, BF),
            dma(5), dma(5), dma(extra), dma(extra), dma(1),
        ],
        compiler_params=params(2),
    )(triple, out, frames, wq, wo)


def stack_pair(block, rows):
    lanes = head_lanes(rows)
    zero = jnp.zeros_like(block)
    return jnp.concatenate([jnp.where(lanes < HEAD, block, zero), jnp.where(lanes >= HEAD, block, zero)], 0)


def pair_softmax(query, keys):
    scale = HEAD ** (-0.5) * LOG2E
    scores = dot_t(query, keys)
    left = head_lanes(scores.shape[0]) < HEAD
    low = jnp.max(jnp.where(left, scores, -jnp.inf), -1, keepdims=True)
    high = jnp.max(jnp.where(left, -jnp.inf, scores), -1, keepdims=True)
    exponent = jnp.exp2((scores - jnp.where(left, low, high)) * scale)
    total = pair_sum(exponent, left)
    return exponent / total, left


def pair_sum(values, left):
    low = jnp.sum(jnp.where(left, values, 0.0), -1, keepdims=True)
    high = jnp.sum(jnp.where(left, 0.0, values), -1, keepdims=True)
    return jnp.where(left, low, high)


def cross_kernel(
    after_in, gains_in, wq_in, wo_in, memory_in, cot_in,
    o_query, o_flat, o_after, o_rows, o_grads,
    after, gains, wq, wo, memory, cot, rows, query, flat, result, feed, grads, load, store, send, recv,
):
    t, x, y, d = neighbours()
    loads = [
        pltpu.make_async_copy(a, b, load.at[i])
        for i, (a, b) in enumerate(
            ((cot_in, cot), (after_in, after), (gains_in, gains), (wq_in, wq), (memory_in, memory), (wo_in, wo))
        )
    ]
    for copy in loads:
        copy.start()
    greet([{"tensor": x}, {"tensor": y}])
    n, m = after.shape
    width = wq.shape[2]
    texts = memory.shape[1]
    loads[0].wait()

    def round_block(i, carry):
        here = rows_at(i, 64)
        grads[t, here] = cot[here].astype(BF)
        return carry

    lax.fori_loop(0, n // 64, round_block, 0)
    gather = Gather(grads.at[t], grads, send, recv, 0)
    gather.start()
    loads[1].wait()
    loads[2].wait()

    def norm_block(i, carry):
        here = rows_at(i, 64)
        hat, _ = normed_rows(after[here])
        rows[here] = (hat * gains[0:1] + gains[1:2]).astype(BF)
        return carry

    lax.fori_loop(0, n // 64, norm_block, 0)
    loads[3].wait()
    loads[4].wait()

    def quarter(q, carry):
        query[:, cols(q, width)] = dot(rows[...], wq[q]).astype(BF)

        def pair(p, carry):
            keys = stack_pair(memory[q, :, cols(p, 128)], texts)
            values = stack_pair(memory[q, :, pl.ds(pl.multiple_of(width + p * 128, 128), 128)], texts)
            here = pl.ds(pl.multiple_of(q * width + p * 128, 128), 128)
            probs, _ = pair_softmax(query[:, here], keys)
            flat[:, here] = dot(probs.astype(BF), values).astype(BF)
            return carry

        lax.fori_loop(0, width // 128, pair, 0)
        return carry

    lax.fori_loop(0, 4, quarter, 0)
    gather.relay_x()
    gather.relay_y()
    stores = [pltpu.make_async_copy(query, o_query, store.at[0]), pltpu.make_async_copy(flat, o_flat, store.at[1])]
    loads[5].wait()

    def out_step(j, carry):
        result[:, cols(j, 512)] = after[:, cols(j, 512)] + dot(flat[...], wo[:, cols(j, 512)])
        return carry

    lax.fori_loop(0, m // 512, out_step, 0)

    def feed_block(i, carry):
        here = rows_at(i, 64)
        hat, _ = normed_rows(result[here])
        feed[here] = (hat * gains[2:3] + gains[3:4]).astype(BF)
        return carry

    lax.fori_loop(0, n // 64, feed_block, 0)
    stores += [pltpu.make_async_copy(result, o_after, store.at[2]), pltpu.make_async_copy(feed, o_rows, store.at[3])]
    for copy in stores:
        copy.start()
    gather.have_x()
    gather.have_y()
    gather.have_d()
    last = pltpu.make_async_copy(grads, o_grads, store.at[4])
    last.start()
    gather.drain()
    for copy in stores:
        copy.wait()
    last.wait()


def cross(after, gains, wq, wo, memory, cot):
    n, m = after.shape
    return pl.pallas_call(
        cross_kernel,
        name="cross",
        out_shape=[shape(n, m), shape(n, m), shape(n, m, kind=F32), shape(n, m), shape(4, n, m)],
        in_specs=[ANY] * 6,
        out_specs=[ANY] * 5,
        scratch_shapes=[
            pltpu.VMEM((n, m), F32), pltpu.VMEM(gains.shape, F32), pltpu.VMEM(wq.shape, BF), pltpu.VMEM(wo.shape, BF),
            pltpu.VMEM(memory.shape, BF), pltpu.VMEM((n, m), F32), pltpu.VMEM((n, m), BF), pltpu.VMEM((n, m), BF),
            pltpu.VMEM((n, m), BF), pltpu.VMEM((n, m), F32), pltpu.VMEM((n, m), BF), pltpu.VMEM((4, n, m), BF),
            dma(6), dma(5), dma(6), dma(6),
        ],
        compiler_params=params(3),
    )(after, gains, wq, wo, memory, cot)


def gelu_both(pre):
    size = jnp.abs(pre) * 0.7071067811865476
    rate = 1.0 / (1.0 + 0.3275911 * size)
    bell = jnp.exp2(pre * pre * (-0.5 * LOG2E))
    series = rate * (
        0.254829592
        + rate * (-0.284496736 + rate * (1.421413741 + rate * (-1.453152027 + rate * 1.061405429)))
    )
    tail = 0.5 * series * bell
    gate = jnp.where(pre >= 0, 1.0 - tail, tail)
    return pre * gate, gate + pre * (0.3989422804014327 * bell)


class Halves:
    def __init__(self, whole, land, send, recv, base):
        self.whole, self.land, self.send, self.recv, self.base = whole, land, send, recv, base
        self.subs = lax.axis_size("sub")
        self.piece = whole.shape[1] // self.subs

    def copies(self, w):
        s = lax.axis_index("sub")
        made = []
        for k in range(1, self.subs):
            target = (s + k) % self.subs
            slot = w * (self.subs - 1) + k - 1
            made.append(
                pltpu.make_async_remote_copy(
                    self.whole.at[w, rows_at(target, self.piece)],
                    self.land.at[w, k - 1],
                    self.send.at[self.base + slot],
                    self.recv.at[self.base + slot],
                    device_id={"sub": target},
                    device_id_type=MESH,
                )
            )
        return made

    def start(self, w):
        for copy in self.copies(w):
            copy.start()

    def total(self, w, take, step):
        s = lax.axis_index("sub")
        for copy in self.copies(w):
            copy.wait_recv()

        def block(i, carry):
            here = rows_at(i, step)
            value = self.whole[w, pl.ds(pl.multiple_of(s * self.piece + i * step, step), step)].astype(F32)
            for k in range(1, self.subs):
                value = value + self.land[w, k - 1, here].astype(F32)
            take(here, value)
            return carry

        lax.fori_loop(0, self.piece // step, block, 0)

    def drain(self, w):
        for copy in self.copies(w):
            copy.wait_send()


def weight_grad(left, right, whole, w, halves, block):
    s = lax.axis_index("sub")
    subs = lax.axis_size("sub")
    total_rows = left.shape[0] * left.shape[1]
    count = whole.shape[1] // block
    begin = ((s + 1) % subs) * halves.piece // block

    def one(j, carry):
        b = (begin + j) % count
        turned = left[:, :, cols(b, block)].reshape(total_rows, block)

        def inner(i, carry):
            other = right[:, :, cols(i, 512)].reshape(total_rows, 512)
            whole[w, rows_at(b, block), cols(i, 512)] = dot_c(turned, other).astype(BF)
            return carry

        lax.fori_loop(0, whole.shape[2] // 512, inner, 0)
        return carry

    if subs == 2:
        lax.fori_loop(0, count // 2, one, 0)
        halves.start(w)
        lax.fori_loop(count // 2, count, one, 0)
    else:
        lax.fori_loop(0, count, one, 0)
        halves.start(w)


def feed_kernel(
    rows_in, grads_in, up_in, down_in, o_part, o_norm, o_pieces,
    rows, grads, up, down, act, pre_grad, part_out, part_norm, land_norm, stage_norm,
    whole, land_whole, load, store, send, recv,
):
    t, x, y, d = neighbours()
    s = lax.axis_index("sub")
    subs = lax.axis_size("sub")
    loads = [
        pltpu.make_async_copy(a, b, load.at[i])
        for i, (a, b) in enumerate(
            ((rows_in, rows.at[t]), (up_in, up), (grads_in, grads), (down_in, down))
        )
    ]
    for copy in loads:
        copy.start()
    greet([{"tensor": x}, {"tensor": y}] + [{"sub": (s + k) % subs} for k in range(1, subs)])
    _, n, m = rows.shape
    hidden = up.shape[1]
    loads[0].wait()
    gather = Gather(rows.at[t], rows, send, recv, 0)
    gather.start()
    back = Scatter(part_norm, land_norm, stage_norm, send, recv, 6)
    halves = Halves(whole, land_whole, send, recv, 12)
    for copy in loads[1:4]:
        copy.wait()

    def work(place):
        def step(j, carry):
            here = cols(j, 256)
            value, slope = gelu_both(dot(rows[place], up[:, here]))
            act[place, :, here] = value.astype(BF)
            pre_grad[place, :, here] = (dot_t(grads[place], down[here]) * slope).astype(BF)
            return carry

        lax.fori_loop(0, hidden // 256, step, 0)

        def out_step(j, carry):
            part_norm[place, :, cols(j, 512)] = dot_t(pre_grad[place], up[rows_at(j, 512)]).astype(BF)
            part_out[place, :, cols(j, 512)] = dot(act[place], down[:, cols(j, 512)]).astype(BF)
            return carry

        lax.fori_loop(0, m // 512, out_step, 0)

    def turn(i, carry):
        far_y = i // 2
        far_x = i % 2
        place = (t // 2 + far_y - 2 * (t // 2) * far_y) * 2 + (t % 2 + far_x - 2 * (t % 2) * far_x)

        @pl.when(i == 1)
        def _():
            gather.relay_x()
            gather.relay_y()
            gather.have_x()

        @pl.when(i == 2)
        def _():
            gather.have_y()

        @pl.when(i == 3)
        def _():
            gather.have_d()

        work(place)

        @pl.when(i == 1)
        def _():
            back.along_x()

        @pl.when(i == 2)
        def _():
            back.along_y()

        @pl.when(i == 3)
        def _():
            back.diagonal()

        return carry

    lax.fori_loop(0, 4, turn, 0)
    stores = [pltpu.make_async_copy(part_out, o_part, store.at[1])]
    stores[0].start()
    weight_grad(act, grads, whole, 0, halves, 256)
    back.relay()
    weight_grad(rows, pre_grad, whole, 1, halves, 256)
    pieces = land_whole
    for w in range(2):

        def take(here, value, w=w):
            pieces[w, 0, here] = value.astype(BF)

        halves.total(w, take, 64)
    stores.append(pltpu.make_async_copy(pieces.at[:, 0], o_pieces, store.at[0]))
    stores[1].start()
    norm_total = part_norm


    def take_norm(here, total):
        norm_total[t, here] = total.astype(BF)

    back.finish(take_norm, 64)
    stores.append(pltpu.make_async_copy(norm_total.at[t], o_norm, store.at[2]))
    stores[2].start()
    gather.drain()
    back.drain()
    for w in range(2):
        halves.drain(w)
    for copy in stores:
        copy.wait()


def feed(rows, grads, up, down, subs):
    n, m = rows.shape
    hidden = up.shape[1]
    count = 12 + 2 * (subs - 1)
    return pl.pallas_call(
        feed_kernel,
        name="feed",
        out_shape=[shape(4, n, m), shape(n, m), shape(2, m // subs, hidden)],
        in_specs=[ANY] * 4,
        out_specs=[ANY] * 3,
        scratch_shapes=[
            pltpu.VMEM((4, n, m), BF), pltpu.VMEM((4, n, m), BF), pltpu.VMEM((m, hidden), BF), pltpu.VMEM((hidden, m), BF),
            pltpu.VMEM((4, n, hidden), BF), pltpu.VMEM((4, n, hidden), BF),
            pltpu.VMEM((4, n, m), BF), pltpu.VMEM((4, n, m), BF),
            pltpu.VMEM((6, n // 2, m), BF), pltpu.VMEM((2, n // 2, m), BF),
            pltpu.VMEM((2, m, hidden), BF), pltpu.VMEM((2, subs - 1, m // subs, hidden), BF),
            dma(4), dma(3), dma(count), dma(count),
        ],
        compiler_params=params(4),
    )(rows, grads, up, down)


def norm_back_block(grad, source, gain):
    hat, inverse = normed_rows(source)
    scaled = grad * gain
    inner = scaled - jnp.mean(scaled, -1, keepdims=True) - hat * jnp.mean(scaled * hat, -1, keepdims=True)
    return inverse * inner, grad * hat


def fold(block):
    total = block[0:8]
    for i in range(1, block.shape[0] // 8):
        total = total + block[8 * i : 8 * i + 8]
    return total


def unstack(block):
    lanes = head_lanes(block.shape[0] // 2)
    return jnp.where(lanes < HEAD, block[: block.shape[0] // 2], block[block.shape[0] // 2 :])


def cross_back_kernel(
    layout,
    cot_in, norm_in, cross_in, self_in, gains_in, query_in, flat_in, memory_in, wq_in, wo_in, part_in, own_in,
    o_out, o_branch, o_sums, o_memory, o_wq, o_wo, o_layer, o_down, o_land,
    cot, norm, after_cross, after_self, gains, query, flat, memory, wq, wo,
    branch, rows, query_grad, memory_grad, sums, whole_q, whole_o, land_q, land_o, piece_q, piece_o,
    norm_self, part, land_part, stage_part, own, land, ring, result, ring_send, ring_recv, ring_store,
    load, store, send, recv,
):
    t, x, y, d = neighbours()
    s = lax.axis_index("sub")
    subs = lax.axis_size("sub")
    loads = [
        pltpu.make_async_copy(a, b, load.at[i])
        for i, (a, b) in enumerate(
            (
                (cot_in, cot), (norm_in, norm), (cross_in, after_cross), (gains_in, gains), (wo_in, wo),
                (query_in, query), (flat_in, flat), (memory_in, memory), (self_in, after_self), (wq_in, wq),
                (part_in, part), (own_in, own),
            )
        )
    ]
    for copy in loads:
        copy.start()
    greet([{"tensor": x}, {"tensor": y}] + [{"sub": (s + k) % subs} for k in range(1, subs)] + group_ring())
    scatter = Scatter(part, land_part, stage_part, send, recv, 8 * (subs - 1))
    pump = Pump(
        own, land, ring, result, ring_send, ring_recv, ring_store, 0, layout.middle, layout.count,
        feed_outputs(layout, o_down),
    )
    n, m = cot.shape
    width = wq.shape[2]
    texts = memory.shape[1]
    for copy in (*loads[:4], *loads[10:]):
        copy.wait()
    scatter.diagonal()
    scatter.along_x()
    scatter.along_y()
    pump.step(jnp.int32(0))
    scale = HEAD ** (-0.5)

    def feed_block(i, carry):
        here = rows_at(i, 64)
        grad = norm[here].astype(F32)
        inner, terms = norm_back_block(grad, after_cross[here], gains[2:3])
        total = cot[here] + inner
        cot[here] = total
        branch[here] = total.astype(BF)
        return carry[0] + fold(terms), carry[1] + fold(grad)

    zero = jnp.zeros((8, m), F32)
    gain_sum, bias_sum = lax.fori_loop(0, n // 64, feed_block, (zero, zero))
    sums[0:8] = gain_sum
    sums[8:16] = bias_sum
    loads[8].wait()

    def norm_block(i, carry):
        here = rows_at(i, 64)
        hat, _ = normed_rows(after_self[here])
        rows[here] = (hat * gains[0:1] + gains[1:2]).astype(BF)
        return carry

    lax.fori_loop(0, n // 64, norm_block, 0)
    for copy in loads[4:8]:
        copy.wait()
    middle = layout.middle

    def tick(k):
        @pl.when(k < middle)
        def _():
            pump.step(k)

    tick(jnp.int32(1))

    def quarter(q, carry):
        tick(q + 2)
        grad_heads = dot_t(branch[...], wo[rows_at(q, width)]).astype(BF)
        whole_q_cols = cols(q, width)
        query_grad_block = []
        for p in range(width // 128):
            lane = slice(p * 128, p * 128 + 128)
            keys = stack_pair(memory[q, :, lane], texts)
            values = stack_pair(memory[q, :, width + p * 128 : width + p * 128 + 128], texts)
            here = pl.ds(pl.multiple_of(q * width + p * 128, 128), 128)
            grad = grad_heads[:, lane]
            ask = query[:, here]
            probs, left = pair_softmax(ask, keys)
            grad_probs = dot_t(grad, values)
            centred = pair_sum(grad_probs * probs, left)
            grad_scores = (probs * (grad_probs - centred)).astype(BF)
            query_grad[:, here] = (dot(grad_scores, keys) * scale).astype(BF)
            memory_grad[q, :, lane] = unstack(dot_c(grad_scores, ask) * scale).astype(BF)
            memory_grad[q, :, width + p * 128 : width + p * 128 + 128] = unstack(
                dot_c(probs.astype(BF), grad)
            ).astype(BF)
        return carry

    lax.fori_loop(0, 4, quarter, 0)
    stores = [pltpu.make_async_copy(memory_grad, o_memory, store.at[0])]
    stores[0].start()
    halves_q = Halves(whole_q, land_q, send, recv, 0)
    halves_o = Halves(whole_o, land_o, send, recv, 4 * (subs - 1))

    scatter.relay()

    def weights(q, carry):
        tick(q + 6)

        def grad_o(j, carry):
            whole_o[q, :, cols(j, 512)] = dot_c(flat[:, cols(q, width)], branch[:, cols(j, 512)]).astype(BF)
            return carry

        lax.fori_loop(0, m // 512, grad_o, 0)

        def grad_q(j, carry):
            whole_q[q, rows_at(j, 256)] = dot_c(rows[:, cols(j, 256)], query_grad[:, cols(q, width)]).astype(BF)
            return carry

        lax.fori_loop(0, m // 256, grad_q, 0)
        return carry

    lax.fori_loop(0, 4, weights, 0)
    for q in range(4):
        halves_q.start(q)
        halves_o.start(q)
    loads[9].wait()

    def norm_grad(j, carry):
        here = rows_at(j, 256)
        total = jnp.zeros((n, 256), F32)
        for q in range(4):
            total = total + dot_t(query_grad[:, q * width : (q + 1) * width], wq[q, here])
        norm_self[:, cols(j, 256)] = total
        return carry

    lax.fori_loop(0, m // 256, norm_grad, 0)

    def self_block(i, carry):
        here = rows_at(i, 64)
        grad = norm_self[here]
        inner, terms = norm_back_block(grad, after_self[here], gains[0:1])
        total = cot[here] + inner
        cot[here] = total
        branch[here] = total.astype(BF)
        return carry[0] + fold(terms), carry[1] + fold(grad)

    gain_sum, bias_sum = lax.fori_loop(0, n // 64, self_block, (zero, zero))
    sums[16:24] = gain_sum
    sums[24:32] = bias_sum
    stores += [
        pltpu.make_async_copy(cot, o_out, store.at[1]),
        pltpu.make_async_copy(branch, o_branch, store.at[2]),
        pltpu.make_async_copy(sums, o_sums, store.at[3]),
    ]
    for copy in stores[1:]:
        copy.start()

    def take_layer(here, total):
        after_cross[here] = after_cross[here] + total

    scatter.finish(take_layer, 64)
    stores.append(pltpu.make_async_copy(after_cross, o_layer, store.at[6]))
    stores[-1].start()
    for halves, piece in ((halves_q, piece_q), (halves_o, piece_o)):
        for q in range(4):

            def take(here, value, q=q, piece=piece):
                piece[q, here] = value.astype(BF)

            halves.total(q, take, 16)
    stores += [pltpu.make_async_copy(piece_q, o_wq, store.at[4]), pltpu.make_async_copy(piece_o, o_wo, store.at[5])]
    for copy in stores[5:]:
        copy.start()
    pump.drain()
    stores.append(pltpu.make_async_copy(land, o_land, store.at[7]))
    stores[-1].start()
    scatter.drain()
    for q in range(4):
        halves_q.drain(q)
        halves_o.drain(q)
    for copy in stores:
        copy.wait()


def cross_back(layout, cot, norm, after_cross, after_self, gains, query, flat, memory, wq, wo, part, own, subs):
    n, m = cot.shape
    width = wq.shape[2]
    count = 8 * (subs - 1) + 6
    chunks = layout.feed_count
    held = (2, layout.window, layout.chunk, m)
    part_q, part_o = (4, m // subs, width), (4, width // subs, m)
    return pl.pallas_call(
        partial(cross_back_kernel, layout),
        name="cross_back",
        out_shape=[
            shape(n, m, kind=F32), shape(n, m), shape(32, m, kind=F32), shape(*memory.shape), shape(*part_q), shape(*part_o),
            shape(n, m, kind=F32), shape(layout.feed_count // 2, layout.chunk, m), shape(*held),
        ],
        in_specs=[ANY] * 12,
        out_specs=[ANY] * 9,
        scratch_shapes=[
            pltpu.VMEM((n, m), F32), pltpu.VMEM((n, m), BF), pltpu.VMEM((n, m), F32), pltpu.VMEM((n, m), F32),
            pltpu.VMEM(gains.shape, F32), pltpu.VMEM((n, m), BF), pltpu.VMEM((n, m), BF), pltpu.VMEM(memory.shape, BF),
            pltpu.VMEM(wq.shape, BF), pltpu.VMEM(wo.shape, BF),
            pltpu.VMEM((n, m), BF), pltpu.VMEM((n, m), BF), pltpu.VMEM((n, m), BF), pltpu.VMEM(memory.shape, BF),
            pltpu.VMEM((32, m), F32), pltpu.VMEM((4, m, width), BF), pltpu.VMEM((4, width, m), BF),
            pltpu.VMEM((4, subs - 1, m // subs, width), BF), pltpu.VMEM((4, subs - 1, width // subs, m), BF),
            pltpu.VMEM(part_q, BF), pltpu.VMEM(part_o, BF),
            pltpu.VMEM((n, m), F32), pltpu.VMEM((4, n, m), BF), pltpu.VMEM((6, n // 2, m), BF), pltpu.VMEM((2, n // 2, m), BF),
            *pump_scratch(layout, chunks),
            dma(12), dma(8), dma(count), dma(count),
        ],
        compiler_params=params(5),
    )(cot, norm, after_cross, after_self, gains, query, flat, memory, wq, wo, part, own)


def attend_pair_back(p, triple, place, blocks, heads, grad_heads, deltas, sums, grads, grad_keys, grad_values):
    n = triple.shape[1]
    width = heads * HEAD
    scale = HEAD ** (-0.5)
    lanes = head_lanes(n)
    key_lanes = head_lanes(blocks * n)

    here = pl.ds(pl.multiple_of(p * 128, 128), 128)
    key_cols = pl.ds(pl.multiple_of(width + p * 128, 128), 128)
    value_cols = pl.ds(pl.multiple_of(2 * width + p * 128, 128), 128)
    query = triple[place, :, here]
    grad = grad_heads[place, :, here]
    keys = triple[0:blocks, :, key_cols].reshape(blocks * n, 128)
    values = triple[0:blocks, :, value_cols].reshape(blocks * n, 128)
    stats = sums[place]
    means = deltas[place]
    found = []
    for h in range(2):
        mine = (lanes < HEAD) if h == 0 else (lanes >= HEAD)
        log_sum = jnp.sum(jnp.where(lanes == 2 * p + h, stats, 0.0), -1, keepdims=True)
        delta = jnp.sum(jnp.where(lanes == 2 * p + h, means, 0.0), -1, keepdims=True)
        scores = dot_t(jnp.where(mine, query, jnp.zeros_like(query)), keys)
        row = lax.broadcasted_iota(jnp.int32, scores.shape, 0)
        col = lax.broadcasted_iota(jnp.int32, scores.shape, 1)
        probs = jnp.where(
            col <= row + (blocks - 1) * n, jnp.exp2(scores * (scale * LOG2E) - log_sum), 0.0
        )
        grad_probs = dot_t(jnp.where(mine, grad, jnp.zeros_like(grad)), values)
        grad_scores = (probs * (grad_probs - delta)).astype(BF)
        found.append((dot(grad_scores, keys), dot_c(grad_scores, query), dot_c(probs.astype(BF), grad)))
    grads[place, :, here] = (jnp.where(lanes < HEAD, found[0][0], found[1][0]) * scale).astype(BF)
    grad_keys[0 : blocks * n, here] += jnp.where(key_lanes < HEAD, found[0][1], found[1][1]) * scale
    grad_values[0 : blocks * n, here] += jnp.where(key_lanes < HEAD, found[0][2], found[1][2])


def attend_back_kernel(
    layout,
    branch_in, triple_in, flat_in, sums_in, out_in, qkv_in, rows_in, frames_in, gains_in, grad_in, memory_in, text_in, kv_in,
    own_in, land_in, down_in,
    o_frames, o_sums, o_text, o_qkv, o_out, o_kv, o_down, o_up, o_land,
    branch, triple, flat, sums, out, qkv, rows, frames, gains, grad_out, memory, text, kv,
    land_m, stage_m,
    grad_heads, deltas, grads, grad_keys, grad_values, part, land, stage, whole_qkv, land_qkv, whole_out, land_out,
    whole_kv, land_kv, text_grad, sums_out, sum_m, own, held, ring, result, ring_send, ring_recv, ring_store,
    load, store, send, recv,
):
    t, x, y, d = neighbours()
    s = lax.axis_index("sub")
    subs = lax.axis_size("sub")
    names = (
        (branch_in, branch.at[t]), (out_in, out), (flat_in, flat), (triple_in, triple), (sums_in, sums),
        (memory_in, memory), (own_in, own), (land_in, held),
        *((qkv_in.at[i], qkv.at[:, pl.ds(i * qkv_in.shape[2], qkv_in.shape[2])]) for i in range(3)), (rows_in, rows),
        (text_in, text), (kv_in, kv), (frames_in, frames), (gains_in, gains), (grad_in, grad_out),
    )
    loads = [pltpu.make_async_copy(a, b, load.at[i]) for i, (a, b) in enumerate(names)]
    loads[7].start()
    for copy in loads[:7] + loads[8:]:
        copy.start()
    loads[7].wait()
    greet([{"tensor": x}, {"tensor": y}] + [{"sub": (s + k) % subs} for k in range(1, subs)] + group_ring())
    first, last = layout.middle, layout.later
    pump = Pump(
        own, held, ring, result, ring_send, ring_recv, ring_store, first, last, layout.count,
        feed_outputs(layout, o_down, o_up),
    )

    def tick(k):
        @pl.when(k + first < last)
        def _():
            pump.step(k + first)

    n, m = grad_out.shape
    width = triple.shape[2]
    local = out.shape[0]
    heads = local // HEAD
    gather = Gather(branch.at[t], branch, send, recv, 0)
    scatter = Scatter(part, land, stage, send, recv, 6)
    scatter_m = Scatter(memory, land_m, stage_m, send, recv, 12)
    halves_qkv = Halves(whole_qkv, land_qkv, send, recv, 18)
    halves_out = Halves(whole_out, land_out, send, recv, 18 + subs - 1)
    halves_kv = Halves(whole_kv, land_kv, send, recv, 18 + 2 * (subs - 1))
    loads[0].wait()
    gather.start()
    for copy in loads[5:7]:
        copy.wait()
    scatter_m.diagonal()
    scatter_m.along_x()
    scatter_m.along_y()
    for copy in loads[1:5]:
        copy.wait()
    grad_keys[...] = jnp.zeros_like(grad_keys)
    grad_values[...] = jnp.zeros_like(grad_values)
    lanes = head_lanes(n)

    def turn(i, carry):
        far_y = i // 2
        far_x = i % 2
        place = (t // 2 + far_y - 2 * (t // 2) * far_y) * 2 + (t % 2 + far_x - 2 * (t % 2) * far_x)

        @pl.when(i == 1)
        def _():
            gather.relay_x()
            gather.relay_y()
            gather.have_x()

        @pl.when(i == 2)
        def _():
            gather.have_y()

        @pl.when(i == 3)
        def _():
            gather.have_d()

        grad_heads[place] = dot_t(branch[place], out[...]).astype(BF)

        def delta(p, stats):
            here = pl.ds(pl.multiple_of(p * 128, 128), 128)
            product = grad_heads[place, :, here].astype(F32) * flat[place, :, here].astype(F32)
            low = jnp.sum(jnp.where(lanes < HEAD, product, 0.0), -1, keepdims=True)
            high = jnp.sum(jnp.where(lanes < HEAD, 0.0, product), -1, keepdims=True)
            return jnp.where(lanes == 2 * p, low, jnp.where(lanes == 2 * p + 1, high, stats))

        deltas[place] = lax.fori_loop(0, heads // 2, delta, jnp.zeros((n, 128), F32))

        def pair(p, carry):
            tick(i * (heads // 2) + p)
            for blocks in range(1, 5):

                @pl.when(place == blocks - 1)
                def _(blocks=blocks):
                    attend_pair_back(
                        p, triple, blocks - 1, blocks, heads, grad_heads, deltas, sums, grads, grad_keys, grad_values
                    )

            return carry

        lax.fori_loop(0, heads // 2, pair, 0)
        return carry

    lax.fori_loop(0, 4, turn, 0)
    for copy in loads[8:14]:
        copy.wait()

    def finish_grads(i, carry):
        grads[i, :, local : 2 * local] = grad_keys[rows_at(i, n)].astype(BF)
        grads[i, :, 2 * local :] = grad_values[rows_at(i, n)].astype(BF)
        return carry

    lax.fori_loop(0, 4, finish_grads, 0)

    def back(i, carry):
        far_y = 1 - i // 2
        far_x = 1 - i % 2
        place = (t // 2 + far_y - 2 * (t // 2) * far_y) * 2 + (t % 2 + far_x - 2 * (t % 2) * far_x)

        def step(j, carry):
            part[place, :, cols(j, 512)] = dot_t(grads[place], qkv[rows_at(j, 512)]).astype(BF)
            return carry

        lax.fori_loop(0, m // 512, step, 0)
        tick(12 + i)

        @pl.when(i == 0)
        def _():
            scatter.diagonal()

        @pl.when(i == 1)
        def _():
            scatter.along_y()

        @pl.when(i == 2)
        def _():
            scatter.along_x()

        return carry

    lax.fori_loop(0, 4, back, 0)
    scatter_m.relay()

    def take_m(here, total):
        sum_m[here] = total.astype(BF)

    scatter_m.finish(take_m, 16)
    text_grad[...] = dot_t(sum_m[...], kv[...])
    stores = [pltpu.make_async_copy(text_grad, o_text, store.at[0])]
    stores[0].start()

    def grad_kv(j, carry):
        whole_kv[0, rows_at(j, 384)] = dot_c(text[:, cols(j, 384)], sum_m[...]).astype(BF)
        return carry

    lax.fori_loop(0, m // 384, grad_kv, 0)
    halves_kv.start(0)

    def grad_wout(j, carry):
        whole_out[0, :, cols(j, 512)] = dot_c(
            flat[...].reshape(4 * n, local), branch[:, :, cols(j, 512)].reshape(4 * n, 512)
        ).astype(BF)
        return carry

    lax.fori_loop(0, m // 512, grad_wout, 0)
    halves_out.start(0)
    scatter.relay()

    def grad_wqkv(j, carry):
        tick(16 + j)
        turned = rows[:, :, cols(j, 256)].reshape(4 * n, 256)

        def inner(i, carry):
            whole_qkv[0, rows_at(j, 256), cols(i, 384)] = dot_c(
                turned, grads[:, :, cols(i, 384)].reshape(4 * n, 384)
            ).astype(BF)
            return carry

        lax.fori_loop(0, width // 384, inner, 0)
        return carry

    lax.fori_loop(0, m // 256, grad_wqkv, 0)
    halves_qkv.start(0)
    for each, output, slot in ((halves_kv, o_kv, 1), (halves_out, o_out, 2), (halves_qkv, o_qkv, 3)):

        def take(here, total, each=each):
            each.land[0, 0, here] = total.astype(BF)

        each.total(0, take, 16)
        stores.append(pltpu.make_async_copy(each.land.at[0, 0], output, store.at[slot]))
        stores[-1].start()
    for copy in loads[14:]:
        copy.wait()

    def take_norm(here, total):
        part[t, here] = total.astype(BF)

    scatter.finish(take_norm, 64)

    def frame_block(i, carry):
        here = rows_at(i, 64)
        grad = part[t, here].astype(F32)
        inner, terms = norm_back_block(grad, frames[here].astype(F32), gains[4:5])
        grad_out[here] = grad_out[here] + inner
        return carry[0] + fold(terms), carry[1] + fold(grad)

    zero = jnp.zeros((8, m), F32)
    gain_sum, bias_sum = lax.fori_loop(0, n // 64, frame_block, (zero, zero))
    sums_out[0:8] = gain_sum
    sums_out[8:16] = bias_sum
    stores += [pltpu.make_async_copy(grad_out, o_frames, store.at[4]), pltpu.make_async_copy(sums_out, o_sums, store.at[5])]
    for copy in stores[-2:]:
        copy.start()
    pump.drain()
    stores.append(pltpu.make_async_copy(held, o_land, store.at[6]))
    stores[-1].start()
    gather.drain()
    for each in (scatter, scatter_m):
        each.drain()
    for each in (halves_qkv, halves_out, halves_kv):
        each.drain(0)
    for copy in stores:
        copy.wait()


def attend_back(
    layout, branch, triple, flat, sums, out, qkv, rows, frames, gains, grad, memory, text, kv, own, land, down, subs
):
    n, m = grad.shape
    width = triple.shape[2]
    local = out.shape[0]
    texts, kvw = text.shape[0], kv.shape[1]
    count = 18 + 3 * (subs - 1)
    v = pltpu.VMEM
    return pl.pallas_call(
        partial(attend_back_kernel, layout),
        name="attend_back",
        out_shape=[
            shape(n, m, kind=F32), shape(16, m, kind=F32), shape(texts, m, kind=F32), shape(m // subs, width),
            shape(local // subs, m), shape(m // subs, kvw), shape(*down.shape), shape(*down.shape), shape(*land.shape),
        ],
        in_specs=[ANY] * 16,
        out_specs=[ANY] * 9,
        input_output_aliases={15: 6},
        scratch_shapes=[
            v((4, n, m), BF), v(triple.shape, BF), v(flat.shape, BF), v(sums.shape, F32), v(out.shape, BF), v((m, width), BF),
            v(rows.shape, BF), v(frames.shape, frames.dtype), v(gains.shape, F32), v((n, m), F32), v(memory.shape, BF),
            v(text.shape, BF), v(kv.shape, BF),
            v((6, texts // 2, kvw), BF), v((2, texts // 2, kvw), BF),
            v((4, n, local), BF), v((4, n, 128), F32), v((4, n, width), BF), v((4 * n, local), F32), v((4 * n, local), F32),
            v((4, n, m), BF), v((6, n // 2, m), BF), v((2, n // 2, m), BF),
            v((1, m, width), BF), v((1, subs - 1, m // subs, width), BF),
            v((1, local, m), BF), v((1, subs - 1, local // subs, m), BF),
            v((1, m, kvw), BF), v((1, subs - 1, m // subs, kvw), BF),
            v((texts, m), F32), v((16, m), F32), v((texts, kvw), BF),
            *pump_scratch(layout, layout.feed_count),
            dma(17), dma(7), dma(count), dma(count),
        ],
        compiler_params=params(6),
    )(branch, triple, flat, sums, out, qkv, rows, frames, gains, grad, memory, text, kv, own, land, down)


def total_kernel(
    layout,
    feed_in, qkv_in, kv_in, out_in, cross_q_in, cross_o_in, sums_a_in, sums_b_in, text_in, land_in, down_in, up_in,
    o_qkv, o_cq, o_kv, o_out, o_co, o_text, o_vectors, o_down, o_up,
    own, held, ring, result, ring_send, ring_recv, ring_store,
    cross_q, cross_o, land_q, land_o, stage_q, stage_o,
    sums_a, sums_b, text, text_land, text_full, vectors, vectors_land, share, share_land, load, store, send, recv,
):
    t, x, y, d = neighbours()
    s, subs = lax.axis_index("sub"), lax.axis_size("sub")
    g, groups = lax.axis_index("group"), lax.axis_size("group")
    chunk, m, local = layout.chunk, layout.m, layout.local
    width, quarter = 3 * local, layout.piece // 4 // chunk
    at_qkv, at_kv, at_out, at_cq, at_co = (
        r // chunk for r in (layout.qkv, layout.kv, layout.out, layout.cq, layout.co)
    )
    outs = layout.out_rows // chunk
    def outputs(c, block, slots, act):
        slot = c % RING

        def region(begin, end, copies):
            @pl.when(jnp.logical_and(c >= begin, c < end))
            def _():
                for i, (source, target) in enumerate(copies(c - begin)):
                    act(pltpu.make_async_copy(source, target, slots.at[slot, i]))

        def whole(output):
            return lambda r: [(block, output.at[r])]

        region(0, at_qkv // 2, whole(o_down))
        region(at_qkv // 2, at_qkv, whole(o_up))
        region(
            at_qkv, at_kv,
            lambda r: [
                *((block.at[:, pl.ds(i * local, local)], o_qkv.at[i, r]) for i in range(3)),
                (block.at[:, pl.ds(width, local)], o_qkv.at[r // quarter, 3 * quarter + r % quarter]),
            ],
        )
        region(
            at_kv, at_out,
            lambda r: [
                (block.at[:, pl.ds(2 * i * local, 2 * local)], o_kv.at[2 * i * quarter + r]) for i in range(2)
            ],
        )
        region(at_out, at_cq, whole(o_out))
        region(
            at_cq, at_co,
            lambda r: [(block.at[:, pl.ds(i * local, local)], o_cq.at[i * quarter + r]) for i in range(4)],
        )
        region(at_co, at_co + outs, whole(o_co))

    fresh = max(0, layout.later - LAG * (groups - 1))
    pairs = [
        (land_in, held),
        (feed_in.at[pl.ds(fresh, at_qkv - fresh)], own.at[pl.ds(fresh, at_qkv - fresh)]),
        (qkv_in.at[pl.ds(0, 3 * quarter)], own.at[pl.ds(at_qkv, 3 * quarter), :, pl.ds(0, width)]),
    ]
    for i in range(3):
        pairs.append(
            (
                qkv_in.at[pl.ds(3 * quarter, quarter), :, pl.ds(i * local, local)],
                own.at[pl.ds(at_qkv + i * quarter, quarter), :, pl.ds(width, local)],
            )
        )
    pairs += [(sums_a_in, sums_a), (sums_b_in, sums_b), (text_in, text), (cross_q_in, cross_q), (cross_o_in, cross_o)]
    for i in range(2):
        pairs.append(
            (
                kv_in.at[pl.ds(2 * i * quarter, 2 * quarter)],
                own.at[pl.ds(at_kv, 2 * quarter), :, pl.ds(2 * i * local, 2 * local)],
            )
        )
    pairs.append((out_in, own.at[pl.ds(at_out, outs)]))
    loads = [pltpu.make_async_copy(a, b, load.at[i]) for i, (a, b) in enumerate(pairs)]
    for copy in loads:
        copy.start()
    loads[0].wait()
    greet(
        [{"tensor": x}, {"tensor": y}, {"tensor": d}]
        + [{"sub": (s + k) % subs} for k in range(1, subs)]
        + [{"group": (g + k) % groups} for k in range(1, groups)]
    )
    begin, end = layout.later, layout.end
    loads[1].wait()
    pump = Pump(own, held, ring, result, ring_send, ring_recv, ring_store, begin, end, layout.count, outputs)

    def run(a, b):
        def step(k, carry):
            pump.step(k)
            return carry

        lax.fori_loop(a, b, step, 0)

    for copy in loads[2:6]:
        copy.wait()
    run(begin, begin + 1)
    for copy in loads[6:]:
        copy.wait()
    share_width = m // subs
    for i in range(6):
        source, at = (sums_a, i) if i < 4 else (sums_b, i - 4)
        row = jnp.sum(source[8 * at : 8 * at + 8], 0, keepdims=True)
        for j in range(subs):
            vectors[j, i : i + 1] = row[:, j * share_width : (j + 1) * share_width]
    strip = text.shape[0] // 4

    def remote(source, target, k, device):
        return pltpu.make_async_remote_copy(
            source, target, send.at[k], recv.at[k], device_id=device, device_id_type=MESH
        )

    square = (x, y, d)
    first = [remote(vectors, vectors_land.at[k], k, {"tensor": square[k]}) for k in range(3)]
    first += [
        remote(text.at[rows_at(square[k], strip)], text_land.at[k], 3 + k, {"tensor": square[k]}) for k in range(3)
    ]
    second = [
        remote(share.at[0, (s + k) % subs], share_land.at[k - 1], 5 + k, {"sub": (s + k) % subs}) for k in range(1, subs)
    ]
    base = 5 + subs
    second += [
        remote(text_full.at[rows_at(t, strip)], text_full.at[rows_at(t, strip)], base + k, {"tensor": square[k]}) for k in range(3)
    ]
    base += 3
    third = [
        remote(share.at[1, 0], share_land.at[subs - 2 + k], base + k - 1, {"group": (g + k) % groups})
        for k in range(1, groups)
    ]
    base += groups - 1
    scatter_q = Scatter(cross_q, land_q, stage_q, send, recv, base)
    scatter_o = Scatter(cross_o, land_o, stage_o, send, recv, base + 6)
    for copy in first:
        copy.start()
    for each in (scatter_q, scatter_o):
        each.diagonal()
    for each in (scatter_q, scatter_o):
        each.along_x()
        each.along_y()

    run(begin + 1, begin + 3)
    for copy in first:
        copy.wait_recv()
    for j in range(subs):
        share[0, j] = vectors[j] + vectors_land[0, j] + vectors_land[1, j] + vectors_land[2, j]
    text_full[rows_at(t, strip)] = text[rows_at(t, strip)] + text_land[0] + text_land[1] + text_land[2]
    for copy in first:
        copy.wait_send()
    for copy in second:
        copy.start()
    run(begin + 3, begin + 6)
    for copy in second:
        copy.wait_recv()
    total = share[0, s]
    for k in range(1, subs):
        total = total + share_land[k - 1]
    share[1, 0] = total
    text_store = pltpu.make_async_copy(text_full, o_text, store.at[0])
    text_store.start()
    for copy in third:
        copy.start()
    relay = max(begin + 6, begin + (at_cq - begin) // 2)
    run(begin + 6, relay)
    for each in (scatter_q, scatter_o):
        each.relay()
    finish = min(at_cq, relay + 8)
    run(relay, finish)

    def take_q(rows, value):
        row = rows.start
        part = row // (quarter * chunk)
        c = row // chunk - part * quarter
        own[at_cq + c, :, pl.ds(pl.multiple_of(part * local, local), local)] = value.astype(BF)

    scatter_q.finish(take_q, chunk)
    step = min(chunk, scatter_o.half)

    def take_o(rows, value):
        own[at_co + rows.start // chunk, rows_at(rows.start % chunk // step, step)] = value.astype(BF)

    scatter_o.finish(take_o, step)
    run(finish, end)
    for copy in third:
        copy.wait_recv()
    total = share[1, 0]
    for k in range(1, groups):
        total = total + share_land[subs - 2 + k]
    share[2, 0] = total
    vector_store = pltpu.make_async_copy(share.at[2, 0], o_vectors, store.at[1])
    vector_store.start()
    for copy in second + third:
        copy.wait_send()
    for each in (scatter_q, scatter_o):
        each.drain()
    pump.drain()
    text_store.wait()
    vector_store.wait()


def total(layout, pieces, qkv, kv, out, cross_q, cross_o, sums_a, sums_b, text, land, down, up, subs, groups):
    m, chunk = layout.m, layout.chunk
    v = pltpu.VMEM
    sems = 7 + subs + groups + 12
    tall = lambda a: a.reshape(-1, chunk, a.shape[1])
    qkv, kv, out = tall(qkv), tall(kv), tall(out)
    piece_q, piece_o = cross_q.shape[1:], cross_o.shape[1:]
    return pl.pallas_call(
        partial(total_kernel, layout),
        name="total",
        out_shape=[
            shape(3, *qkv.shape[:2], layout.local), shape(layout.piece // chunk, chunk, layout.local), shape(*kv.shape), shape(*out.shape),
            shape(*out.shape), shape(*text.shape, kind=F32), shape(8, m // subs, kind=F32), shape(*down.shape), shape(*up.shape),
        ],
        in_specs=[ANY] * 12,
        out_specs=[ANY] * 9,
        input_output_aliases={10: 7, 11: 8},
        scratch_shapes=[
            *pump_scratch(layout, layout.count),
            v(cross_q.shape, BF), v(cross_o.shape, BF),
            v((6, piece_q[0] // 2, piece_q[1]), BF), v((6, piece_o[0] // 2, piece_o[1]), BF),
            v((2, piece_q[0] // 2, piece_q[1]), BF), v((2, piece_o[0] // 2, piece_o[1]), BF),
            v(sums_a.shape, F32), v(sums_b.shape, F32), v(text.shape, F32),
            v((3, text.shape[0] // 4, m), F32), v(text.shape, F32), v((subs, 8, m // subs), F32), v((3, subs, 8, m // subs), F32),
            v((3, subs, 8, m // subs), F32), v((subs - 1 + groups - 1, 8, m // subs), F32),
            dma(14), dma(2), dma(sems), dma(sems),
        ],
        compiler_params=params(7),
    )(pieces, qkv, kv, out, cross_q, cross_o, sums_a, sums_b, text, land, down, up)


def local(
    frames, text_states, selfgain, selfbias, selfqkv, selfout, crossgain, crossbias, crossquery, crosskv, crossout,
    feedgain, feedbias, feedup, feeddown, cotangent,
):
    subs, groups = lax.axis_size("sub"), lax.axis_size("group")
    m = frames.shape[2]
    width = selfout.shape[0]
    qkv = selfqkv.transpose(1, 0, 2)
    kv = crosskv.reshape(m, 2 * width)
    gains = jnp.concatenate([crossgain, crossbias, feedgain, feedbias, selfgain, selfbias]).reshape(6, m)
    rows, triple, memory = enter(frames[0], gains, qkv, text_states[0], kv)
    flat, sums, after_self, wq, wo = attend(triple, selfout, frames[0], crossquery, crossout, subs)
    wo = wo.reshape(4 * width, m)
    query, cross_flat, after_cross, feed_rows, grads = cross(after_self, gains, wq, wo, memory, cotangent[0])
    layout = Layout(m, width, subs, groups)
    part, norm_grad, pieces = feed(feed_rows, grads, feedup, feeddown, subs)
    pieces = pieces.reshape(-1, layout.chunk, m)
    grad_out, branch, sums_a, memory_grad, piece_q, piece_o, layer_output, down, land = cross_back(
        layout, cotangent[0], norm_grad, after_cross, after_self, gains, query, cross_flat, memory, wq, wo, part, pieces, subs
    )
    frame_grad, sums_b, text_part, grad_qkv, grad_out_weight, grad_kv, down, up, land = attend_back(
        layout, branch, triple, flat, sums, selfout, qkv, rows, frames[0], gains, grad_out, memory_grad,
        text_states[0], kv, pieces, land, down, subs,
    )
    full_qkv, full_cq, full_kv, full_out, full_co, text_grad, vectors, down, up = total(
        layout, pieces, grad_qkv, grad_kv, grad_out_weight, piece_q, piece_o, sums_a, sums_b, text_part, land, down, up,
        subs, groups,
    )
    return (
        layer_output[None],
        frame_grad[None],
        text_grad[None],
        vectors[4],
        vectors[5],
        full_qkv.astype(F32).reshape(3, -1, width).transpose(1, 0, 2),
        full_out.astype(F32).reshape(-1, m),
        vectors[2],
        vectors[3],
        full_cq.astype(F32).reshape(-1, width),
        full_kv.astype(F32).reshape(-1, 2, width),
        full_co.astype(F32).reshape(-1, m),
        vectors[0],
        vectors[1],
        up.astype(F32).reshape(-1, m),
        down.astype(F32).reshape(-1, m),
    )


def solution(mesh):
    clips = P(("sub", "group"), "tensor", None)
    whole = P(("sub", "group"), None, None)
    narrow, wide = P("tensor", None), P(None, "tensor")
    third = P(None, None, "tensor")
    vector = P("sub")
    return jax.shard_map(
        local,
        mesh=mesh,
        in_specs=(
            clips, whole, P(), P(), third, narrow, P(), P(), wide, third, narrow, P(), P(), wide, narrow, clips,
        ),
        out_specs=(
            clips, clips, whole, vector, vector, P("sub", None, "tensor"), P(("tensor", "sub"), None), vector, vector,
            P("sub", "tensor"), P("sub", None, "tensor"), P(("tensor", "sub"), None), vector, vector,
            P("sub", "tensor"), P(("tensor", "sub"), None),
        ),
        check_vma=False,
    )
```

```python
from functools import partial

import jax
import jax.numpy as jnp
from jax import lax
from jax.experimental import pallas as pl
from jax.experimental.pallas import tpu as pltpu
from jax.sharding import PartitionSpec as P

HEAD = 64
EPSILON = 1e-05
NEG_BIG = -1e30
LOG2E = 1.4426950408889634
MESH = pl.DeviceIdType.MESH
F32 = jnp.float32
BF = jnp.bfloat16
ANY = pl.BlockSpec(memory_space=pl.ANY)
VMEM_LIMIT = 63 << 20


def neighbours():
    t = lax.axis_index("tensor")
    return t, t + 1 - 2 * (t % 2), (t + 2) % 4, 3 - t


def greet(targets):
    barrier = pltpu.get_barrier_semaphore()
    for target in targets:
        pl.semaphore_signal(barrier, inc=1, device_id=target, device_id_type=MESH)
    pl.semaphore_wait(barrier, len(targets))


def dot(a, b):
    return lax.dot_general(a, b, (((1,), (0,)), ((), ())), preferred_element_type=F32)


def dot_t(a, b):
    return lax.dot_general(a, b, (((1,), (1,)), ((), ())), preferred_element_type=F32)


def dot_c(a, b):
    return lax.dot_general(a, b, (((0,), (0,)), ((), ())), preferred_element_type=F32)


def cols(j, width):
    return pl.ds(pl.multiple_of(j * width, width), width)


def rows_at(j, height):
    return pl.ds(pl.multiple_of(j * height, height), height)


def split(count):
    first = (count // 2 + 15) // 16 * 16
    return pl.ds(0, first), pl.ds(first, count - first)


class Gather:
    def __init__(self, own, dst, send, recv, base, halves=None):
        self.own, self.dst, self.send, self.recv, self.base = own, dst, send, recv, base
        self.halves = halves or split(own.shape[0])

    def copy(self, k):
        t, x, y, _ = neighbours()
        first, second = self.halves
        half = (first, second, second, first, first, second)[k]
        place = (t, t, t, t, x, y)[k]
        target = (x, y, x, y, y, x)[k]
        source = self.own.at[half] if k < 4 else self.dst.at[place, half]
        return pltpu.make_async_remote_copy(
            source,
            self.dst.at[place, half],
            self.send.at[self.base + k],
            self.recv.at[self.base + k],
            device_id={"tensor": target},
            device_id_type=MESH,
        )

    def start(self):
        for k in range(4):
            self.copy(k).start()

    def relay_x(self):
        self.copy(0).wait_recv()
        self.copy(4).start()

    def relay_y(self):
        self.copy(1).wait_recv()
        self.copy(5).start()

    def have_x(self):
        self.copy(2).wait_recv()

    def have_y(self):
        self.copy(3).wait_recv()

    def have_d(self):
        self.copy(4).wait_recv()
        self.copy(5).wait_recv()

    def drain(self):
        for k in range(6):
            self.copy(k).wait_send()


class Scatter:
    def __init__(self, part, land, stage, send, recv, base):
        self.part, self.land, self.stage = part, land, stage
        self.send, self.recv, self.base = send, recv, base
        self.half = part.shape[1] // 2

    def copy(self, k):
        t, x, y, d = neighbours()
        low, high = pl.ds(0, self.half), pl.ds(self.half, self.half)
        source = (
            self.part.at[d, low],
            self.part.at[d, high],
            self.part.at[x, low],
            self.stage.at[1],
            self.part.at[y, high],
            self.stage.at[0],
        )[k]
        target = (x, y, x, x, y, y)[k]
        return pltpu.make_async_remote_copy(
            source,
            self.land.at[k],
            self.send.at[self.base + k],
            self.recv.at[self.base + k],
            device_id={"tensor": target},
            device_id_type=MESH,
        )

    def diagonal(self):
        self.copy(0).start()
        self.copy(1).start()

    def along_x(self):
        self.copy(2).start()

    def along_y(self):
        self.copy(4).start()

    def relay(self):
        t, x, y, d = neighbours()
        low, high = pl.ds(0, self.half), pl.ds(self.half, self.half)
        self.copy(0).wait_recv()
        self.stage[0] = (self.part[y, low].astype(F32) + self.land[0].astype(F32)).astype(BF)
        self.copy(5).start()
        self.copy(1).wait_recv()
        self.stage[1] = (self.part[x, high].astype(F32) + self.land[1].astype(F32)).astype(BF)
        self.copy(3).start()

    def finish(self, take, step):
        t, x, y, d = neighbours()
        for k in (2, 4, 5, 3):
            self.copy(k).wait_recv()
        for base, a, b in ((0, 2, 5), (self.half, 4, 3)):

            def block(i, carry, base=base, a=a, b=b):
                here = rows_at(i, step)
                rows = pl.ds(pl.multiple_of(base + i * step, step), step)
                take(
                    rows,
                    self.part[t, rows].astype(F32)
                    + self.land[a, here].astype(F32)
                    + self.land[b, here].astype(F32),
                )
                return carry

            lax.fori_loop(0, self.half // step, block, 0)

    def drain(self):
        for k in range(6):
            self.copy(k).wait_send()


def normed_rows(values):
    centre = values - jnp.mean(values, -1, keepdims=True)
    inverse = lax.rsqrt(jnp.mean(centre * centre, -1, keepdims=True) + EPSILON)
    return centre * inverse, inverse


def params(cid, **more):
    return pltpu.CompilerParams(
        collective_id=cid, has_side_effects=True, vmem_limit_bytes=VMEM_LIMIT, **more
    )


def dma(count):
    return pltpu.SemaphoreType.DMA((count,))


def shape(*dims, kind=BF):
    return jax.ShapeDtypeStruct(dims, kind)


LAG = 3
RING = 4


def either(condition, other):
    return jnp.logical_and(condition, other)


class Pump:
    def __init__(self, own, land, ring, result, send, recv, store, first, last, count, outputs):
        self.own, self.land, self.ring, self.result = own, land, ring, result
        self.send, self.recv, self.store = send, recv, store
        self.first, self.last, self.count, self.outputs = first, last, count, outputs
        self.window = land.shape[1]
        self.g, self.n = lax.axis_index("group"), lax.axis_size("group")

    def copy(self, way, c):
        target = (self.g + 1) % self.n if way == 0 else (self.g + self.n - 1) % self.n
        return pltpu.make_async_remote_copy(
            self.ring.at[way, c % RING],
            self.land.at[way, c % self.window],
            self.send.at[way, c % RING],
            self.recv.at[way, c % self.window],
            device_id={"group": target},
            device_id_type=MESH,
        )

    def flow(self, way, k):
        place = self.g if way == 0 else self.n - 1 - self.g
        c = k - LAG * place

        @pl.when(either(c >= 0, c < self.count))
        def _():
            @pl.when(either(place > 0, k - LAG >= self.first))
            def _():
                self.copy(way, c).wait_recv()

            @pl.when(place < self.n - 1)
            def _():
                @pl.when(either(c >= RING, k - RING >= self.first))
                def _():
                    self.copy(way, c - RING).wait_send()

                @pl.when(place > 0)
                def _():
                    before = self.land[way, c % self.window].astype(F32)
                    self.ring[way, c % RING] = (self.own[c].astype(F32) + before).astype(BF)

                @pl.when(place == 0)
                def _():
                    self.ring[way, c % RING] = self.own[c]

                self.copy(way, c).start()

    def finished(self, k):
        far = jnp.maximum(self.g, self.n - 1 - self.g)
        return k - LAG * far

    def step(self, k):
        self.flow(0, k)
        self.flow(1, k)
        f = self.finished(k)

        @pl.when(either(f >= 0, f < self.count))
        def _():
            @pl.when(either(f >= RING, k - RING >= self.first))
            def _():
                self.outputs(f - RING, self.result.at[f % RING], self.store, lambda copy: copy.wait())

            mine = self.own[f].astype(F32)
            slot, held = f % RING, f % self.window

            @pl.when(either(self.g > 0, self.g < self.n - 1))
            def _():
                both = self.land[0, held].astype(F32) + self.land[1, held].astype(F32)
                self.result[slot] = (mine + both).astype(BF)

            @pl.when(self.g == 0)
            def _():
                self.result[slot] = (mine + self.land[1, held].astype(F32)).astype(BF)

            @pl.when(self.g == self.n - 1)
            def _():
                self.result[slot] = (mine + self.land[0, held].astype(F32)).astype(BF)

            self.outputs(f, self.result.at[slot], self.store, lambda copy: copy.start())

    def drain(self):
        for way in range(2):
            place = self.g if way == 0 else self.n - 1 - self.g
            top = jnp.minimum(self.last - LAG * place, self.count)
            for j in range(1, RING + 1):
                c = top - j

                @pl.when(either(place < self.n - 1, either(c >= 0, c + LAG * place >= self.first)))
                def _(way=way, c=c):
                    self.copy(way, c).wait_send()

            for k in range(max(self.first, self.last - LAG), self.last):
                c = k - LAG * (place - 1)

                @pl.when(either(place > 0, either(c >= 0, c < self.count)))
                def _(way=way, c=c):
                    self.copy(way, c).wait_recv()

        far = jnp.maximum(self.g, self.n - 1 - self.g)
        top = jnp.minimum(self.last - LAG * far, self.count)
        for j in range(1, RING + 1):
            f = top - j

            @pl.when(either(f >= 0, f + LAG * far >= self.first))
            def _(f=f):
                self.outputs(f, self.result.at[f % RING], self.store, lambda copy: copy.wait())


KV_TICKS, OUT_TICKS = 20, 28


class Layout:
    def __init__(self, m, local, subs, groups):
        piece = m // subs
        self.m, self.piece, self.local = m, piece, local
        self.out_rows = local // subs
        self.chunk = 48
        quarter = piece // 4 // self.chunk
        self.quarter = quarter
        self.feed_count = 2 * piece // self.chunk
        self.kv = self.feed_count
        self.out = self.kv + 2 * quarter
        self.qkv = self.out + self.out_rows // self.chunk
        self.cq = self.qkv + 3 * quarter
        self.co = self.cq + quarter
        self.count = self.co + self.out_rows // self.chunk
        self.window = LAG * (groups + 1)
        self.end = self.count + LAG * (groups - 1)
        self.middle = min(12, self.feed_count // 3)
        self.later = self.feed_count
        if self.middle + KV_TICKS <= self.kv and self.middle + OUT_TICKS <= self.out:
            self.later = self.middle + OUT_TICKS + 2


def sum_outputs(layout, halves, text=None):
    def outputs(c, block, store, act):
        count = layout.feed_count // 2
        for i, half in enumerate(halves):

            @pl.when(either(c >= i * count, c < (i + 1) * count))
            def _(i=i, half=half):
                act(pltpu.make_async_copy(block, half.at[c - i * count], store.at[c % RING, 0]))

        if text is not None:

            @pl.when(either(c >= layout.kv, c < layout.out))
            def _():
                for i in range(2):
                    lanes = pl.ds(2 * i * layout.local, 2 * layout.local)
                    target = text.at[2 * i * layout.quarter + c - layout.kv]
                    act(pltpu.make_async_copy(block.at[:, lanes], target, store.at[c % RING, i]))

    return outputs


def pump_scratch(layout, count):
    chunk, m = layout.chunk, layout.m
    return [
        pltpu.VMEM((count, chunk, m), BF),
        pltpu.VMEM((2, layout.window, chunk, m), BF),
        pltpu.VMEM((2, RING, chunk, m), BF),
        pltpu.VMEM((RING, chunk, m), BF),
        pltpu.SemaphoreType.DMA((2, RING)),
        pltpu.SemaphoreType.DMA((2, layout.window)),
        pltpu.SemaphoreType.DMA((RING, 4)),
    ]


def group_ring():
    g, n = lax.axis_index("group"), lax.axis_size("group")
    return [{"group": (g + 1) % n}, {"group": (g + n - 1) % n}]


def enter_kernel(
    frames, gains, qkv, text, kv, o_rows, o_triple, o_memory,
    v_frames, v_gains, v_qkv, v_text, v_kv, rows, triple, memory, load, store, send, recv,
):
    t, x, y, d = neighbours()
    loads = [
        pltpu.make_async_copy(a, b, load.at[i])
        for i, (a, b) in enumerate(
            (
                (frames, v_frames), (gains, v_gains), (text, v_text), (kv, v_kv),
                *((qkv.at[i], v_qkv.at[:, pl.ds(i * qkv.shape[2], qkv.shape[2])]) for i in range(3)),
            )
        )
    ]
    for copy in loads:
        copy.start()
    greet([{"tensor": x}, {"tensor": y}])
    for copy in loads[:2]:
        copy.wait()
    count, width = v_qkv.shape
    block = 384

    def norm_block(i, carry):
        here = rows_at(i, 64)
        hat, _ = normed_rows(v_frames[here].astype(F32))
        rows[t, here] = (hat * v_gains[4:5] + v_gains[5:6]).astype(BF)
        return carry

    lax.fori_loop(0, v_frames.shape[0] // 64, norm_block, 0)
    gather = Gather(rows.at[t], rows, send, recv, 0)
    gather.start()
    texts = Gather(memory.at[t], memory, send, recv, 6)

    def project(place):
        def step(j, carry):
            triple[place, :, cols(j, block)] = dot(rows[place], v_qkv[:, cols(j, block)]).astype(BF)
            return carry

        lax.fori_loop(0, width // block, step, 0)

    def put(k, place):
        a = pltpu.make_async_copy(rows.at[place], o_rows.at[place], store.at[2 * k])
        b = pltpu.make_async_copy(triple.at[place], o_triple.at[place], store.at[2 * k + 1])
        a.start()
        b.start()
        return [a, b]

    loads[2].wait()
    loads[3].wait()

    def texts_step(j, carry):
        memory[t, :, cols(j, block)] = dot(v_text[...], v_kv[:, cols(j, block)]).astype(BF)
        return carry

    lax.fori_loop(0, v_kv.shape[1] // block, texts_step, 0)
    texts.start()
    for copy in loads[4:]:
        copy.wait()
    project(t)
    stores = put(0, t)
    gather.relay_x()
    gather.relay_y()
    gather.have_x()
    project(x)
    stores += put(1, x)
    gather.have_y()
    project(y)
    stores += put(2, y)
    texts.relay_x()
    texts.relay_y()
    texts.have_x()
    texts.have_y()
    gather.have_d()
    project(d)
    stores += put(3, d)
    texts.have_d()
    last = pltpu.make_async_copy(memory, o_memory, store.at[8])
    last.start()
    gather.drain()
    texts.drain()
    for copy in stores:
        copy.wait()
    last.wait()


def enter(frames, gains, qkv, text, kv):
    n, m = frames.shape
    width, texts, kvw = 3 * qkv.shape[2], text.shape[0], kv.shape[1]
    return pl.pallas_call(
        enter_kernel,
        name="enter",
        out_shape=[shape(4, n, m), shape(4, n, width), shape(4, texts, kvw)],
        in_specs=[ANY] * 5,
        out_specs=[ANY] * 3,
        scratch_shapes=[
            pltpu.VMEM((n, m), frames.dtype), pltpu.VMEM(gains.shape, F32),
            pltpu.VMEM((m, width), BF), pltpu.VMEM(text.shape, BF), pltpu.VMEM(kv.shape, BF),
            pltpu.VMEM((4, n, m), BF), pltpu.VMEM((4, n, width), BF), pltpu.VMEM((4, texts, kvw), BF),
            dma(7), dma(9), dma(12), dma(12),
        ],
        compiler_params=params(1),
    )(frames, gains, qkv, text, kv)


def head_lanes(rows):
    return lax.broadcasted_iota(jnp.int32, (rows, 128), 1)


def attend_rows(triple, place, blocks, heads, flat, sums):
    n = triple.shape[1]
    width = heads * HEAD
    scale = HEAD ** (-0.5) * LOG2E
    lanes = head_lanes(n)

    def pair(p, stats):
        here = pl.ds(pl.multiple_of(p * 128, 128), 128)
        key_cols = pl.ds(pl.multiple_of(width + p * 128, 128), 128)
        value_cols = pl.ds(pl.multiple_of(2 * width + p * 128, 128), 128)
        query = triple[place, :, here]
        keys = triple[0:blocks, :, key_cols].reshape(blocks * n, 128)
        values = triple[0:blocks, :, value_cols].reshape(blocks * n, 128)
        outs = []
        for h in range(2):
            mine = (lanes < HEAD) if h == 0 else (lanes >= HEAD)
            scores = dot_t(jnp.where(mine, query, jnp.zeros_like(query)), keys)
            row = lax.broadcasted_iota(jnp.int32, scores.shape, 0)
            col = lax.broadcasted_iota(jnp.int32, scores.shape, 1)
            scores = jnp.where(col <= row + (blocks - 1) * n, scores, NEG_BIG)
            peak = jnp.max(scores, -1, keepdims=True) * scale
            exponent = jnp.exp2(scores * scale - peak)
            total = jnp.sum(exponent, -1, keepdims=True)
            outs.append(dot(exponent.astype(BF), values) / total)
            stats = jnp.where(lanes == 2 * p + h, peak + jnp.log2(total), stats)
        flat[place, :, here] = jnp.where(lanes < HEAD, outs[0], outs[1]).astype(BF)
        return stats

    sums[place] = lax.fori_loop(0, heads // 2, pair, jnp.zeros((n, 128), F32))


def attend_kernel(
    triple_in, out_in, frames_in, wq, wo, o_flat, o_sums, o_after, o_wq, o_wo,
    triple, v_out, v_frames, flat, sums, after, part, land, stage, v_wq, v_wo, load, store, send, recv, side,
):
    t, x, y, d = neighbours()
    s = lax.axis_index("sub")
    subs = lax.axis_size("sub")
    n = triple.shape[1]
    m = v_out.shape[1]
    heads = v_out.shape[0] // HEAD
    loads = [
        pltpu.make_async_copy(a, b, load.at[i])
        for i, (a, b) in enumerate(
            ((triple_in, triple), (out_in, v_out), (frames_in, v_frames), (wq, v_wq), (wo, v_wo))
        )
    ]
    for copy in loads:
        copy.start()
    greet(
        [{"tensor": x}, {"tensor": y}]
        + [{"sub": (s + k) % subs} for k in range(1, subs)]
    )
    scatter = Scatter(part, land, stage, send, recv, 0)
    gathers = []
    for i, (weight, full) in enumerate(((wq, o_wq), (wo, o_wo))):
        piece = weight.shape[0] // subs
        first, second = split(piece)
        offset = pl.multiple_of(s * piece, piece)
        halves = (
            pl.ds(offset, first.size),
            pl.ds(pl.multiple_of(offset + first.size, 16), second.size),
        )
        gathers.append((Gather(weight, full, send, recv, 6 + 6 * i, halves), full, pl.ds(offset, piece)))

    def shared(i, j, k):
        _, full, piece = gathers[i]
        place = (x, y, d)[j]
        slot = (i * 3 + j) * (subs - 1) + k - 1
        return pltpu.make_async_remote_copy(
            full.at[place, piece], full.at[place, piece],
            send.at[18 + slot], recv.at[18 + slot],
            device_id={"sub": (s + k) % subs}, device_id_type=MESH,
        )

    for gather, _, _ in gathers:
        gather.start()
    for copy in loads[:2]:
        copy.wait()

    def one(i, carry):
        far_y = 1 - i // 2
        far_x = 1 - i % 2
        place = (t // 2 + far_y - 2 * (t // 2) * far_y) * 2 + (t % 2 + far_x - 2 * (t % 2) * far_x)
        for blocks in range(1, 5):

            @pl.when(place == blocks - 1)
            def _(blocks=blocks):
                attend_rows(triple, blocks - 1, blocks, heads, flat, sums)

        def out_step(j, carry):
            part[place, :, cols(j, 512)] = dot(flat[place], v_out[:, cols(j, 512)]).astype(BF)
            return carry

        lax.fori_loop(0, m // 512, out_step, 0)

        @pl.when(i == 0)
        def _():
            scatter.diagonal()

        @pl.when(i == 1)
        def _():
            scatter.along_y()

        @pl.when(i == 2)
        def _():
            scatter.along_x()

        return carry

    lax.fori_loop(0, 4, one, 0)
    for gather, _, _ in gathers:
        gather.relay_x()
        gather.relay_y()
    stores = [
        pltpu.make_async_copy(flat, o_flat, store.at[0]),
        pltpu.make_async_copy(sums, o_sums, store.at[1]),
    ]
    loads[3].wait()
    loads[4].wait()
    stores += [
        pltpu.make_async_copy(v_wq, o_wq.at[t], store.at[2]),
        pltpu.make_async_copy(v_wo, o_wo.at[t], store.at[3]),
    ]
    for copy in stores:
        copy.start()
    scatter.relay()
    for i, (gather, _, _) in enumerate(gathers):
        gather.have_x()
        gather.have_y()
        gather.have_d()
        for j in range(3):
            for k in range(1, subs):
                shared(i, j, k).start()
    loads[2].wait()

    def take(rows, total):
        after[rows] = v_frames[rows].astype(F32) + total

    scatter.finish(take, 64)
    last = pltpu.make_async_copy(after, o_after, store.at[4])
    last.start()
    scatter.drain()
    for i, (gather, _, _) in enumerate(gathers):
        gather.drain()
        for j in range(3):
            for k in range(1, subs):
                shared(i, j, k).wait()
    for copy in stores:
        copy.wait()
    last.wait()


def attend(triple, out, frames, wq, wo, subs):
    _, n, width = triple.shape
    local, m = out.shape
    extra = 18 + 6 * (subs - 1)
    return pl.pallas_call(
        attend_kernel,
        name="attend",
        out_shape=[
            shape(4, n, local), shape(4, n, 128, kind=F32), shape(n, m, kind=F32),
            shape(4, *wq.shape), shape(4, *wo.shape),
        ],
        in_specs=[ANY] * 5,
        out_specs=[ANY] * 5,
        scratch_shapes=[
            pltpu.VMEM((4, n, width), BF), pltpu.VMEM((local, m), BF), pltpu.VMEM((n, m), frames.dtype),
            pltpu.VMEM((4, n, local), BF), pltpu.VMEM((4, n, 128), F32), pltpu.VMEM((n, m), F32),
            pltpu.VMEM((4, n, m), BF), pltpu.VMEM((6, n // 2, m), BF), pltpu.VMEM((2, n // 2, m), BF),
            pltpu.VMEM(wq.shape, BF), pltpu.VMEM(wo.shape, BF),
            dma(5), dma(5), dma(extra), dma(extra), dma(1),
        ],
        compiler_params=params(2),
    )(triple, out, frames, wq, wo)


def stack_pair(block, rows):
    lanes = head_lanes(rows)
    zero = jnp.zeros_like(block)
    return jnp.concatenate([jnp.where(lanes < HEAD, block, zero), jnp.where(lanes >= HEAD, block, zero)], 0)


def pair_softmax(query, keys):
    scale = HEAD ** (-0.5) * LOG2E
    scores = dot_t(query, keys)
    left = head_lanes(scores.shape[0]) < HEAD
    low = jnp.max(jnp.where(left, scores, -jnp.inf), -1, keepdims=True)
    high = jnp.max(jnp.where(left, -jnp.inf, scores), -1, keepdims=True)
    exponent = jnp.exp2((scores - jnp.where(left, low, high)) * scale)
    total = pair_sum(exponent, left)
    return exponent / total, left


def pair_sum(values, left):
    low = jnp.sum(jnp.where(left, values, 0.0), -1, keepdims=True)
    high = jnp.sum(jnp.where(left, 0.0, values), -1, keepdims=True)
    return jnp.where(left, low, high)


def cross_kernel(
    after_in, gains_in, wq_in, wo_in, memory_in, cot_in,
    o_query, o_flat, o_after, o_rows, o_grads,
    after, gains, wq, wo, memory, cot, rows, query, flat, result, feed, grads, load, store, send, recv,
):
    t, x, y, d = neighbours()
    loads = [
        pltpu.make_async_copy(a, b, load.at[i])
        for i, (a, b) in enumerate(
            ((cot_in, cot), (after_in, after), (gains_in, gains), (wq_in, wq), (memory_in, memory), (wo_in, wo))
        )
    ]
    for copy in loads:
        copy.start()
    greet([{"tensor": x}, {"tensor": y}])
    n, m = after.shape
    width = wq.shape[2]
    texts = memory.shape[1]
    loads[0].wait()

    def round_block(i, carry):
        here = rows_at(i, 64)
        grads[t, here] = cot[here].astype(BF)
        return carry

    lax.fori_loop(0, n // 64, round_block, 0)
    gather = Gather(grads.at[t], grads, send, recv, 0)
    gather.start()
    loads[1].wait()
    loads[2].wait()

    def norm_block(i, carry):
        here = rows_at(i, 64)
        hat, _ = normed_rows(after[here])
        rows[here] = (hat * gains[0:1] + gains[1:2]).astype(BF)
        return carry

    lax.fori_loop(0, n // 64, norm_block, 0)
    loads[3].wait()
    loads[4].wait()

    def quarter(q, carry):
        query[:, cols(q, width)] = dot(rows[...], wq[q]).astype(BF)

        def pair(p, carry):
            keys = stack_pair(memory[q, :, cols(p, 128)], texts)
            values = stack_pair(memory[q, :, pl.ds(pl.multiple_of(width + p * 128, 128), 128)], texts)
            here = pl.ds(pl.multiple_of(q * width + p * 128, 128), 128)
            probs, _ = pair_softmax(query[:, here], keys)
            flat[:, here] = dot(probs.astype(BF), values).astype(BF)
            return carry

        lax.fori_loop(0, width // 128, pair, 0)
        return carry

    lax.fori_loop(0, 4, quarter, 0)
    gather.relay_x()
    gather.relay_y()
    stores = [pltpu.make_async_copy(query, o_query, store.at[0]), pltpu.make_async_copy(flat, o_flat, store.at[1])]
    loads[5].wait()

    def out_step(j, carry):
        result[:, cols(j, 512)] = after[:, cols(j, 512)] + dot(flat[...], wo[:, cols(j, 512)])
        return carry

    lax.fori_loop(0, m // 512, out_step, 0)

    def feed_block(i, carry):
        here = rows_at(i, 64)
        hat, _ = normed_rows(result[here])
        feed[here] = (hat * gains[2:3] + gains[3:4]).astype(BF)
        return carry

    lax.fori_loop(0, n // 64, feed_block, 0)
    stores += [pltpu.make_async_copy(result, o_after, store.at[2]), pltpu.make_async_copy(feed, o_rows, store.at[3])]
    for copy in stores:
        copy.start()
    gather.have_x()
    gather.have_y()
    gather.have_d()
    last = pltpu.make_async_copy(grads, o_grads, store.at[4])
    last.start()
    gather.drain()
    for copy in stores:
        copy.wait()
    last.wait()


def cross(after, gains, wq, wo, memory, cot):
    n, m = after.shape
    return pl.pallas_call(
        cross_kernel,
        name="cross",
        out_shape=[shape(n, m), shape(n, m), shape(n, m, kind=F32), shape(n, m), shape(4, n, m)],
        in_specs=[ANY] * 6,
        out_specs=[ANY] * 5,
        scratch_shapes=[
            pltpu.VMEM((n, m), F32), pltpu.VMEM(gains.shape, F32), pltpu.VMEM(wq.shape, BF), pltpu.VMEM(wo.shape, BF),
            pltpu.VMEM(memory.shape, BF), pltpu.VMEM((n, m), F32), pltpu.VMEM((n, m), BF), pltpu.VMEM((n, m), BF),
            pltpu.VMEM((n, m), BF), pltpu.VMEM((n, m), F32), pltpu.VMEM((n, m), BF), pltpu.VMEM((4, n, m), BF),
            dma(6), dma(5), dma(6), dma(6),
        ],
        compiler_params=params(3),
    )(after, gains, wq, wo, memory, cot)


def gelu_both(pre):
    size = jnp.abs(pre) * 0.7071067811865476
    rate = 1.0 / (1.0 + 0.3275911 * size)
    bell = jnp.exp2(pre * pre * (-0.5 * LOG2E))
    series = rate * (
        0.254829592
        + rate * (-0.284496736 + rate * (1.421413741 + rate * (-1.453152027 + rate * 1.061405429)))
    )
    tail = 0.5 * series * bell
    gate = jnp.where(pre >= 0, 1.0 - tail, tail)
    return pre * gate, gate + pre * (0.3989422804014327 * bell)


class Halves:
    def __init__(self, whole, land, send, recv, base):
        self.whole, self.land, self.send, self.recv, self.base = whole, land, send, recv, base
        self.subs = lax.axis_size("sub")
        self.piece = whole.shape[1] // self.subs

    def copies(self, w):
        s = lax.axis_index("sub")
        made = []
        for k in range(1, self.subs):
            target = (s + k) % self.subs
            slot = w * (self.subs - 1) + k - 1
            made.append(
                pltpu.make_async_remote_copy(
                    self.whole.at[w, rows_at(target, self.piece)],
                    self.land.at[w, k - 1],
                    self.send.at[self.base + slot],
                    self.recv.at[self.base + slot],
                    device_id={"sub": target},
                    device_id_type=MESH,
                )
            )
        return made

    def start(self, w):
        for copy in self.copies(w):
            copy.start()

    def total(self, w, take, step):
        s = lax.axis_index("sub")
        for copy in self.copies(w):
            copy.wait_recv()

        def block(i, carry):
            here = rows_at(i, step)
            value = self.whole[w, pl.ds(pl.multiple_of(s * self.piece + i * step, step), step)].astype(F32)
            for k in range(1, self.subs):
                value = value + self.land[w, k - 1, here].astype(F32)
            take(here, value)
            return carry

        lax.fori_loop(0, self.piece // step, block, 0)

    def drain(self, w):
        for copy in self.copies(w):
            copy.wait_send()


def weight_grad(left, right, whole, w, halves, block):
    s = lax.axis_index("sub")
    subs = lax.axis_size("sub")
    total_rows = left.shape[0] * left.shape[1]
    count = whole.shape[1] // block
    begin = ((s + 1) % subs) * halves.piece // block

    def one(j, carry):
        b = (begin + j) % count
        turned = left[:, :, cols(b, block)].reshape(total_rows, block)

        def inner(i, carry):
            other = right[:, :, cols(i, 512)].reshape(total_rows, 512)
            whole[w, rows_at(b, block), cols(i, 512)] = dot_c(turned, other).astype(BF)
            return carry

        lax.fori_loop(0, whole.shape[2] // 512, inner, 0)
        return carry

    if subs == 2:
        lax.fori_loop(0, count // 2, one, 0)
        halves.start(w)
        lax.fori_loop(count // 2, count, one, 0)
    else:
        lax.fori_loop(0, count, one, 0)
        halves.start(w)


def feed_kernel(
    rows_in, grads_in, up_in, down_in, o_part, o_norm, o_pieces,
    rows, grads, up, down, act, pre_grad, part_out, part_norm, land_norm, stage_norm,
    whole, land_whole, load, store, send, recv,
):
    t, x, y, d = neighbours()
    s = lax.axis_index("sub")
    subs = lax.axis_size("sub")
    loads = [
        pltpu.make_async_copy(a, b, load.at[i])
        for i, (a, b) in enumerate(
            ((rows_in, rows.at[t]), (up_in, up), (grads_in, grads), (down_in, down))
        )
    ]
    for copy in loads:
        copy.start()
    greet([{"tensor": x}, {"tensor": y}] + [{"sub": (s + k) % subs} for k in range(1, subs)])
    _, n, m = rows.shape
    hidden = up.shape[1]
    loads[0].wait()
    gather = Gather(rows.at[t], rows, send, recv, 0)
    gather.start()
    back = Scatter(part_norm, land_norm, stage_norm, send, recv, 6)
    halves = Halves(whole, land_whole, send, recv, 12)
    for copy in loads[1:4]:
        copy.wait()

    def work(place):
        def step(j, carry):
            here = cols(j, 256)
            value, slope = gelu_both(dot(rows[place], up[:, here]))
            act[place, :, here] = value.astype(BF)
            pre_grad[place, :, here] = (dot_t(grads[place], down[here]) * slope).astype(BF)
            return carry

        lax.fori_loop(0, hidden // 256, step, 0)

        def out_step(j, carry):
            part_norm[place, :, cols(j, 512)] = dot_t(pre_grad[place], up[rows_at(j, 512)]).astype(BF)
            part_out[place, :, cols(j, 512)] = dot(act[place], down[:, cols(j, 512)]).astype(BF)
            return carry

        lax.fori_loop(0, m // 512, out_step, 0)

    def turn(i, carry):
        far_y = i // 2
        far_x = i % 2
        place = (t // 2 + far_y - 2 * (t // 2) * far_y) * 2 + (t % 2 + far_x - 2 * (t % 2) * far_x)

        @pl.when(i == 1)
        def _():
            gather.relay_x()
            gather.relay_y()
            gather.have_x()

        @pl.when(i == 2)
        def _():
            gather.have_y()

        @pl.when(i == 3)
        def _():
            gather.have_d()

        work(place)

        @pl.when(i == 1)
        def _():
            back.along_x()

        @pl.when(i == 2)
        def _():
            back.along_y()

        @pl.when(i == 3)
        def _():
            back.diagonal()

        return carry

    lax.fori_loop(0, 4, turn, 0)
    stores = [pltpu.make_async_copy(part_out, o_part, store.at[1])]
    stores[0].start()
    weight_grad(act, grads, whole, 0, halves, 256)
    back.relay()
    weight_grad(rows, pre_grad, whole, 1, halves, 256)
    pieces = land_whole
    for w in range(2):

        def take(here, value, w=w):
            pieces[w, 0, here] = value.astype(BF)

        halves.total(w, take, 64)
    stores.append(pltpu.make_async_copy(pieces.at[:, 0], o_pieces, store.at[0]))
    stores[1].start()
    norm_total = part_norm


    def take_norm(here, total):
        norm_total[t, here] = total.astype(BF)

    back.finish(take_norm, 64)
    stores.append(pltpu.make_async_copy(norm_total.at[t], o_norm, store.at[2]))
    stores[2].start()
    gather.drain()
    back.drain()
    for w in range(2):
        halves.drain(w)
    for copy in stores:
        copy.wait()


def feed(rows, grads, up, down, subs):
    n, m = rows.shape
    hidden = up.shape[1]
    count = 12 + 2 * (subs - 1)
    return pl.pallas_call(
        feed_kernel,
        name="feed",
        out_shape=[shape(4, n, m), shape(n, m), shape(2, m // subs, hidden)],
        in_specs=[ANY] * 4,
        out_specs=[ANY] * 3,
        scratch_shapes=[
            pltpu.VMEM((4, n, m), BF), pltpu.VMEM((4, n, m), BF), pltpu.VMEM((m, hidden), BF), pltpu.VMEM((hidden, m), BF),
            pltpu.VMEM((4, n, hidden), BF), pltpu.VMEM((4, n, hidden), BF),
            pltpu.VMEM((4, n, m), BF), pltpu.VMEM((4, n, m), BF),
            pltpu.VMEM((6, n // 2, m), BF), pltpu.VMEM((2, n // 2, m), BF),
            pltpu.VMEM((2, m, hidden), BF), pltpu.VMEM((2, subs - 1, m // subs, hidden), BF),
            dma(4), dma(3), dma(count), dma(count),
        ],
        compiler_params=params(4),
    )(rows, grads, up, down)


def norm_back_block(grad, source, gain):
    hat, inverse = normed_rows(source)
    scaled = grad * gain
    inner = scaled - jnp.mean(scaled, -1, keepdims=True) - hat * jnp.mean(scaled * hat, -1, keepdims=True)
    return inverse * inner, grad * hat


def fold(block):
    total = block[0:8]
    for i in range(1, block.shape[0] // 8):
        total = total + block[8 * i : 8 * i + 8]
    return total


def unstack(block):
    lanes = head_lanes(block.shape[0] // 2)
    return jnp.where(lanes < HEAD, block[: block.shape[0] // 2], block[block.shape[0] // 2 :])


def cross_back_kernel(
    layout,
    cot_in, norm_in, cross_in, self_in, gains_in, query_in, flat_in, memory_in, wq_in, wo_in, own_in,
    o_out, o_branch, o_sums, o_memory, o_wq, o_wo, o_down, o_land,
    cot, norm, after_cross, after_self, gains, query, flat, memory, wq, wo,
    branch, rows, query_grad, memory_grad, sums, whole_q, whole_o, land_q, land_o, piece_q, piece_o,
    norm_self, own, land, ring, result, ring_send, ring_recv, ring_store,
    load, store, send, recv,
):
    s = lax.axis_index("sub")
    subs = lax.axis_size("sub")
    loads = [
        pltpu.make_async_copy(a, b, load.at[i])
        for i, (a, b) in enumerate(
            (
                (cot_in, cot), (norm_in, norm), (cross_in, after_cross), (gains_in, gains), (wo_in, wo),
                (query_in, query), (flat_in, flat), (memory_in, memory), (self_in, after_self), (wq_in, wq),
                (own_in.at[pl.ds(0, layout.middle)], own),
            )
        )
    ]
    for copy in loads[10:] + loads[:10]:
        copy.start()
    greet([{"sub": (s + k) % subs} for k in range(1, subs)] + group_ring())
    pump = Pump(
        own, land, ring, result, ring_send, ring_recv, ring_store, 0, layout.middle, layout.count,
        sum_outputs(layout, (o_down,)),
    )
    n, m = cot.shape
    width = wq.shape[2]
    texts = memory.shape[1]
    loads[10].wait()
    pump.step(jnp.int32(0))
    for copy in loads[:4]:
        copy.wait()
    scale = HEAD ** (-0.5)

    def feed_block(i, carry):
        here = rows_at(i, 64)
        grad = norm[here].astype(F32)
        inner, terms = norm_back_block(grad, after_cross[here], gains[2:3])
        total = cot[here] + inner
        cot[here] = total
        branch[here] = total.astype(BF)
        return carry[0] + fold(terms), carry[1] + fold(grad)

    zero = jnp.zeros((8, m), F32)
    gain_sum, bias_sum = lax.fori_loop(0, n // 64, feed_block, (zero, zero))
    sums[0:8] = gain_sum
    sums[8:16] = bias_sum
    loads[8].wait()

    def norm_block(i, carry):
        here = rows_at(i, 64)
        hat, _ = normed_rows(after_self[here])
        rows[here] = (hat * gains[0:1] + gains[1:2]).astype(BF)
        return carry

    lax.fori_loop(0, n // 64, norm_block, 0)
    for copy in loads[4:8]:
        copy.wait()
    middle = layout.middle

    def tick(k):
        @pl.when(k < middle)
        def _():
            pump.step(k)

    tick(jnp.int32(1))

    def quarter(q, carry):
        tick(q + 2)
        grad_heads = dot_t(branch[...], wo[rows_at(q, width)]).astype(BF)
        whole_q_cols = cols(q, width)
        query_grad_block = []
        for p in range(width // 128):
            lane = slice(p * 128, p * 128 + 128)
            keys = stack_pair(memory[q, :, lane], texts)
            values = stack_pair(memory[q, :, width + p * 128 : width + p * 128 + 128], texts)
            here = pl.ds(pl.multiple_of(q * width + p * 128, 128), 128)
            grad = grad_heads[:, lane]
            ask = query[:, here]
            probs, left = pair_softmax(ask, keys)
            grad_probs = dot_t(grad, values)
            centred = pair_sum(grad_probs * probs, left)
            grad_scores = (probs * (grad_probs - centred)).astype(BF)
            query_grad[:, here] = (dot(grad_scores, keys) * scale).astype(BF)
            memory_grad[q, :, lane] = unstack(dot_c(grad_scores, ask) * scale).astype(BF)
            memory_grad[q, :, width + p * 128 : width + p * 128 + 128] = unstack(
                dot_c(probs.astype(BF), grad)
            ).astype(BF)
        return carry

    lax.fori_loop(0, 4, quarter, 0)
    stores = [pltpu.make_async_copy(memory_grad, o_memory, store.at[0])]
    stores[0].start()
    halves_q = Halves(whole_q, land_q, send, recv, 0)
    halves_o = Halves(whole_o, land_o, send, recv, 4 * (subs - 1))

    def weights(q, carry):
        @pl.when(q % 2 == 0)
        def _():
            tick(6 + q // 2)


        def grad_o(j, carry):
            whole_o[q, :, cols(j, 512)] = dot_c(flat[:, cols(q, width)], branch[:, cols(j, 512)]).astype(BF)
            return carry

        lax.fori_loop(0, m // 512, grad_o, 0)

        def grad_q(j, carry):
            whole_q[q, rows_at(j, 256)] = dot_c(rows[:, cols(j, 256)], query_grad[:, cols(q, width)]).astype(BF)
            return carry

        lax.fori_loop(0, m // 256, grad_q, 0)
        return carry

    lax.fori_loop(0, 4, weights, 0)
    for q in range(4):
        halves_q.start(q)
        halves_o.start(q)
    loads[9].wait()

    def norm_grad(j, carry):
        @pl.when(j % 3 == 0)
        def _():
            tick(8 + j // 3)

        here = rows_at(j, 256)
        total = jnp.zeros((n, 256), F32)
        for q in range(4):
            total = total + dot_t(query_grad[:, q * width : (q + 1) * width], wq[q, here])
        norm_self[:, cols(j, 256)] = total
        return carry

    lax.fori_loop(0, m // 256, norm_grad, 0)

    def self_block(i, carry):
        here = rows_at(i, 64)
        grad = norm_self[here]
        inner, terms = norm_back_block(grad, after_self[here], gains[0:1])
        total = cot[here] + inner
        cot[here] = total
        branch[here] = total.astype(BF)
        return carry[0] + fold(terms), carry[1] + fold(grad)

    gain_sum, bias_sum = lax.fori_loop(0, n // 64, self_block, (zero, zero))
    sums[16:24] = gain_sum
    sums[24:32] = bias_sum
    stores += [
        pltpu.make_async_copy(cot, o_out, store.at[1]),
        pltpu.make_async_copy(branch, o_branch, store.at[2]),
        pltpu.make_async_copy(sums, o_sums, store.at[3]),
    ]
    for copy in stores[1:]:
        copy.start()

    tick(jnp.int32(10))
    for halves, piece in ((halves_q, piece_q), (halves_o, piece_o)):
        for q in range(4):

            def take(here, value, q=q, piece=piece):
                piece[q, here] = value.astype(BF)

            halves.total(q, take, 16)
    stores += [pltpu.make_async_copy(piece_q, o_wq, store.at[4]), pltpu.make_async_copy(piece_o, o_wo, store.at[5])]
    for copy in stores[4:]:
        copy.start()
    tick(jnp.int32(11))
    pump.drain()
    stores.append(pltpu.make_async_copy(land, o_land, store.at[6]))
    stores[-1].start()
    for q in range(4):
        halves_q.drain(q)
        halves_o.drain(q)
    for copy in stores:
        copy.wait()


def cross_back(layout, cot, norm, after_cross, after_self, gains, query, flat, memory, wq, wo, own, subs):
    n, m = cot.shape
    width = wq.shape[2]
    count = 8 * (subs - 1)
    held = (2, layout.window, layout.chunk, m)
    part_q, part_o = (4, m // subs, width), (4, width // subs, m)
    return pl.pallas_call(
        partial(cross_back_kernel, layout),
        name="cross_back",
        out_shape=[
            shape(n, m, kind=F32), shape(n, m), shape(32, m, kind=F32), shape(*memory.shape), shape(*part_q), shape(*part_o),
            shape(layout.feed_count // 2, layout.chunk, m), shape(*held),
        ],
        in_specs=[ANY] * 11,
        out_specs=[ANY] * 8,
        scratch_shapes=[
            pltpu.VMEM((n, m), F32), pltpu.VMEM((n, m), BF), pltpu.VMEM((n, m), F32), pltpu.VMEM((n, m), F32),
            pltpu.VMEM(gains.shape, F32), pltpu.VMEM((n, m), BF), pltpu.VMEM((n, m), BF), pltpu.VMEM(memory.shape, BF),
            pltpu.VMEM(wq.shape, BF), pltpu.VMEM(wo.shape, BF),
            pltpu.VMEM((n, m), BF), pltpu.VMEM((n, m), BF), pltpu.VMEM((n, m), BF), pltpu.VMEM(memory.shape, BF),
            pltpu.VMEM((32, m), F32), pltpu.VMEM((4, m, width), BF), pltpu.VMEM((4, width, m), BF),
            pltpu.VMEM((4, subs - 1, m // subs, width), BF), pltpu.VMEM((4, subs - 1, width // subs, m), BF),
            pltpu.VMEM(part_q, BF), pltpu.VMEM(part_o, BF),
            pltpu.VMEM((n, m), F32),
            *pump_scratch(layout, layout.middle),
            dma(11), dma(7), dma(count), dma(count),
        ],
        compiler_params=params(5),
    )(cot, norm, after_cross, after_self, gains, query, flat, memory, wq, wo, own)


def attend_pair_back(p, triple, place, blocks, heads, grad_heads, deltas, sums, grads, grad_keys, grad_values):
    n = triple.shape[1]
    width = heads * HEAD
    scale = HEAD ** (-0.5)
    lanes = head_lanes(n)
    key_lanes = head_lanes(blocks * n)

    here = pl.ds(pl.multiple_of(p * 128, 128), 128)
    key_cols = pl.ds(pl.multiple_of(width + p * 128, 128), 128)
    value_cols = pl.ds(pl.multiple_of(2 * width + p * 128, 128), 128)
    query = triple[place, :, here]
    grad = grad_heads[place, :, here]
    keys = triple[0:blocks, :, key_cols].reshape(blocks * n, 128)
    values = triple[0:blocks, :, value_cols].reshape(blocks * n, 128)
    stats = sums[place]
    means = deltas[place]
    found = []
    for h in range(2):
        mine = (lanes < HEAD) if h == 0 else (lanes >= HEAD)
        log_sum = jnp.sum(jnp.where(lanes == 2 * p + h, stats, 0.0), -1, keepdims=True)
        delta = jnp.sum(jnp.where(lanes == 2 * p + h, means, 0.0), -1, keepdims=True)
        scores = dot_t(jnp.where(mine, query, jnp.zeros_like(query)), keys)
        row = lax.broadcasted_iota(jnp.int32, scores.shape, 0)
        col = lax.broadcasted_iota(jnp.int32, scores.shape, 1)
        probs = jnp.where(
            col <= row + (blocks - 1) * n, jnp.exp2(scores * (scale * LOG2E) - log_sum), 0.0
        )
        grad_probs = dot_t(jnp.where(mine, grad, jnp.zeros_like(grad)), values)
        grad_scores = (probs * (grad_probs - delta)).astype(BF)
        found.append((dot(grad_scores, keys), dot_c(grad_scores, query), dot_c(probs.astype(BF), grad)))
    grads[place, :, here] = (jnp.where(lanes < HEAD, found[0][0], found[1][0]) * scale).astype(BF)
    grad_keys[0 : blocks * n, here] += jnp.where(key_lanes < HEAD, found[0][1], found[1][1]) * scale
    grad_values[0 : blocks * n, here] += jnp.where(key_lanes < HEAD, found[0][2], found[1][2])


def attend_back_kernel(
    layout,
    branch_in, triple_in, flat_in, sums_in, out_in, qkv_in, rows_in, frames_in, gains_in, grad_in, memory_in, text_in, kv_in,
    own_in, land_in, down_in,
    o_frames, o_sums, o_text, o_qkv, o_more, o_down, o_up, o_kv, o_land,
    branch, triple, flat, sums, out, qkv, rows, frames, gains, grad_out, memory, text, kv,
    land_m, stage_m,
    grad_heads, deltas, grads, grad_keys, grad_values, part, land, stage, whole_qkv, land_qkv, whole_out, land_out,
    whole_kv, land_kv, text_grad, sums_out, sum_m, own, held, ring, result, ring_send, ring_recv, ring_store,
    load, store, send, recv,
):
    t, x, y, d = neighbours()
    s = lax.axis_index("sub")
    subs = lax.axis_size("sub")
    names = (
        (branch_in, branch.at[t]), (out_in, out), (flat_in, flat), (triple_in, triple), (sums_in, sums),
        (memory_in, memory), (own_in, own.at[pl.ds(0, layout.feed_count)]), (land_in, held),
        *((qkv_in.at[i], qkv.at[:, pl.ds(i * qkv_in.shape[2], qkv_in.shape[2])]) for i in range(3)), (rows_in, rows),
        (text_in, text), (kv_in, kv), (frames_in, frames), (gains_in, gains), (grad_in, grad_out),
    )
    loads = [pltpu.make_async_copy(a, b, load.at[i]) for i, (a, b) in enumerate(names)]
    loads[7].start()
    for copy in loads[:7] + loads[8:]:
        copy.start()
    loads[7].wait()
    greet([{"tensor": x}, {"tensor": y}] + [{"sub": (s + k) % subs} for k in range(1, subs)] + group_ring())
    first, last = layout.middle, layout.later
    pump = Pump(
        own, held, ring, result, ring_send, ring_recv, ring_store, first, last, layout.count,
        sum_outputs(layout, (o_down, o_up), o_kv),
    )

    def tick(k):
        @pl.when(k + first < last)
        def _():
            pump.step(k + first)

    n, m = grad_out.shape
    width = triple.shape[2]
    local = out.shape[0]
    heads = local // HEAD
    gather = Gather(branch.at[t], branch, send, recv, 0)
    scatter = Scatter(part, land, stage, send, recv, 6)
    scatter_m = Scatter(memory, land_m, stage_m, send, recv, 12)
    halves_qkv = Halves(whole_qkv, land_qkv, send, recv, 18)
    halves_out = Halves(whole_out, land_out, send, recv, 18 + subs - 1)
    halves_kv = Halves(whole_kv, land_kv, send, recv, 18 + 2 * (subs - 1))
    loads[0].wait()
    gather.start()
    for copy in loads[5:7]:
        copy.wait()
    scatter_m.diagonal()
    scatter_m.along_x()
    scatter_m.along_y()
    for copy in loads[1:5]:
        copy.wait()
    grad_keys[...] = jnp.zeros_like(grad_keys)
    grad_values[...] = jnp.zeros_like(grad_values)
    lanes = head_lanes(n)

    def turn(i, carry):
        far_y = i // 2
        far_x = i % 2
        place = (t // 2 + far_y - 2 * (t // 2) * far_y) * 2 + (t % 2 + far_x - 2 * (t % 2) * far_x)

        @pl.when(i == 1)
        def _():
            gather.relay_x()
            gather.relay_y()
            gather.have_x()

        @pl.when(i == 2)
        def _():
            gather.have_y()

        @pl.when(i == 3)
        def _():
            gather.have_d()

        grad_heads[place] = dot_t(branch[place], out[...]).astype(BF)

        def delta(p, stats):
            here = pl.ds(pl.multiple_of(p * 128, 128), 128)
            product = grad_heads[place, :, here].astype(F32) * flat[place, :, here].astype(F32)
            low = jnp.sum(jnp.where(lanes < HEAD, product, 0.0), -1, keepdims=True)
            high = jnp.sum(jnp.where(lanes < HEAD, 0.0, product), -1, keepdims=True)
            return jnp.where(lanes == 2 * p, low, jnp.where(lanes == 2 * p + 1, high, stats))

        deltas[place] = lax.fori_loop(0, heads // 2, delta, jnp.zeros((n, 128), F32))

        def pair(p, carry):
            tick(i * (heads // 2) + p)
            for blocks in range(1, 5):

                @pl.when(place == blocks - 1)
                def _(blocks=blocks):
                    attend_pair_back(
                        p, triple, blocks - 1, blocks, heads, grad_heads, deltas, sums, grads, grad_keys, grad_values
                    )

            return carry

        lax.fori_loop(0, heads // 2, pair, 0)
        return carry

    lax.fori_loop(0, 4, turn, 0)
    for copy in loads[8:14]:
        copy.wait()

    def finish_grads(i, carry):
        grads[i, :, local : 2 * local] = grad_keys[rows_at(i, n)].astype(BF)
        grads[i, :, 2 * local :] = grad_values[rows_at(i, n)].astype(BF)
        return carry

    lax.fori_loop(0, 4, finish_grads, 0)

    def back(i, carry):
        far_y = 1 - i // 2
        far_x = 1 - i % 2
        place = (t // 2 + far_y - 2 * (t // 2) * far_y) * 2 + (t % 2 + far_x - 2 * (t % 2) * far_x)

        def step(j, carry):
            part[place, :, cols(j, 512)] = dot_t(grads[place], qkv[rows_at(j, 512)]).astype(BF)
            return carry

        lax.fori_loop(0, m // 512, step, 0)
        tick(12 + i)

        @pl.when(i == 0)
        def _():
            scatter.diagonal()

        @pl.when(i == 1)
        def _():
            scatter.along_y()

        @pl.when(i == 2)
        def _():
            scatter.along_x()

        return carry

    lax.fori_loop(0, 4, back, 0)
    tick(16)
    scatter_m.relay()

    def take_m(here, total):
        sum_m[here] = total.astype(BF)

    scatter_m.finish(take_m, 16)
    text_grad[...] = dot_t(sum_m[...], kv[...])
    stores = [pltpu.make_async_copy(text_grad, o_text, store.at[0])]
    stores[0].start()

    def grad_kv(j, carry):
        whole_kv[0, rows_at(j, 384)] = dot_c(text[:, cols(j, 384)], sum_m[...]).astype(BF)
        return carry

    lax.fori_loop(0, m // 384, grad_kv, 0)
    halves_kv.start(0)
    tick(17)

    def grad_wout(j, carry):
        whole_out[0, :, cols(j, 512)] = dot_c(
            flat[...].reshape(4 * n, local), branch[:, :, cols(j, 512)].reshape(4 * n, 512)
        ).astype(BF)
        return carry

    lax.fori_loop(0, m // 512, grad_wout, 0)
    halves_out.start(0)
    tick(18)
    chunk, half = layout.chunk, 2 * layout.quarter

    def take_kv(here, total):
        c = here.start // chunk
        own[layout.kv + c % half, :, cols(c // half, 2 * local)] = total.astype(BF)

    halves_kv.total(0, take_kv, chunk)
    tick(19)

    def grad_wqkv(j, carry):
        tick(20 + j)
        turned = rows[:, :, cols(j, 256)].reshape(4 * n, 256)

        def inner(i, carry):
            whole_qkv[0, rows_at(j, 256), cols(i, 384)] = dot_c(
                turned, grads[:, :, cols(i, 384)].reshape(4 * n, 384)
            ).astype(BF)
            return carry

        lax.fori_loop(0, width // 384, inner, 0)
        return carry

    lax.fori_loop(0, m // 256, grad_wqkv, 0)
    halves_qkv.start(0)
    tick(26)

    def take_out(here, total):
        own[layout.out + here.start // chunk] = total.astype(BF)

    halves_out.total(0, take_out, chunk)
    scatter.relay()
    tick(27)

    def take(here, total):
        land_qkv[0, 0, here] = total.astype(BF)

    halves_qkv.total(0, take, 16)
    stores.append(pltpu.make_async_copy(land_qkv.at[0, 0], o_qkv, store.at[1]))
    stores.append(pltpu.make_async_copy(own.at[pl.ds(layout.kv, layout.qkv - layout.kv)], o_more, store.at[2]))
    for copy in stores[-2:]:
        copy.start()
    tick(28)
    for copy in loads[14:]:
        copy.wait()

    def take_norm(here, total):
        part[t, here] = total.astype(BF)

    scatter.finish(take_norm, 64)

    def frame_block(i, carry):
        here = rows_at(i, 64)
        grad = part[t, here].astype(F32)
        inner, terms = norm_back_block(grad, frames[here].astype(F32), gains[4:5])
        grad_out[here] = grad_out[here] + inner
        return carry[0] + fold(terms), carry[1] + fold(grad)

    zero = jnp.zeros((8, m), F32)
    gain_sum, bias_sum = lax.fori_loop(0, n // 64, frame_block, (zero, zero))
    tick(29)
    sums_out[0:8] = gain_sum
    sums_out[8:16] = bias_sum
    stores += [pltpu.make_async_copy(grad_out, o_frames, store.at[3]), pltpu.make_async_copy(sums_out, o_sums, store.at[4])]
    for copy in stores[-2:]:
        copy.start()
    pump.drain()
    stores.append(pltpu.make_async_copy(held, o_land, store.at[5]))
    stores[-1].start()
    gather.drain()
    for each in (scatter, scatter_m):
        each.drain()
    for each in (halves_qkv, halves_out, halves_kv):
        each.drain(0)
    for copy in stores:
        copy.wait()


def attend_back(
    layout, branch, triple, flat, sums, out, qkv, rows, frames, gains, grad, memory, text, kv, own, land, down, subs
):
    n, m = grad.shape
    width = triple.shape[2]
    local = out.shape[0]
    texts, kvw = text.shape[0], kv.shape[1]
    count = 18 + 3 * (subs - 1)
    v = pltpu.VMEM
    return pl.pallas_call(
        partial(attend_back_kernel, layout),
        name="attend_back",
        out_shape=[
            shape(n, m, kind=F32), shape(16, m, kind=F32), shape(texts, m, kind=F32), shape(m // subs, width),
            shape(layout.qkv - layout.kv, layout.chunk, m), shape(*down.shape), shape(*down.shape),
            shape(4 * layout.quarter, layout.chunk, kvw), shape(*land.shape),
        ],
        in_specs=[ANY] * 16,
        out_specs=[ANY] * 9,
        input_output_aliases={15: 5},
        scratch_shapes=[
            v((4, n, m), BF), v(triple.shape, BF), v(flat.shape, BF), v(sums.shape, F32), v(out.shape, BF), v((m, width), BF),
            v(rows.shape, BF), v(frames.shape, frames.dtype), v(gains.shape, F32), v((n, m), F32), v(memory.shape, BF),
            v(text.shape, BF), v(kv.shape, BF),
            v((6, texts // 2, kvw), BF), v((2, texts // 2, kvw), BF),
            v((4, n, local), BF), v((4, n, 128), F32), v((4, n, width), BF), v((4 * n, local), F32), v((4 * n, local), F32),
            v((4, n, m), BF), v((6, n // 2, m), BF), v((2, n // 2, m), BF),
            v((1, m, width), BF), v((1, subs - 1, m // subs, width), BF),
            v((1, local, m), BF), v((1, subs - 1, local // subs, m), BF),
            v((1, m, kvw), BF), v((1, subs - 1, m // subs, kvw), BF),
            v((texts, m), F32), v((16, m), F32), v((texts, kvw), BF),
            *pump_scratch(layout, layout.qkv),
            dma(17), dma(6), dma(count), dma(count),
        ],
        compiler_params=params(6),
    )(branch, triple, flat, sums, out, qkv, rows, frames, gains, grad, memory, text, kv, own, land, down)


def total_kernel(
    layout,
    feed_in, qkv_in, more_in, cross_q_in, cross_o_in, sums_a_in, sums_b_in, text_in, land_in, part_in, after_in,
    down_in, up_in, kv_in,
    o_qkv, o_cq, o_out, o_co, o_text, o_vectors, o_layer, o_down, o_up, o_kv,
    own, held, ring, result, ring_send, ring_recv, ring_store,
    cross_q, cross_o, land_q, land_o, stage_q, stage_o, part, land_p, stage_p, after,
    sums_a, sums_b, text, text_land, text_full, vectors, vectors_land, share, share_land, load, store, send, recv,
):
    t, x, y, d = neighbours()
    s, subs = lax.axis_index("sub"), lax.axis_size("sub")
    g, groups = lax.axis_index("group"), lax.axis_size("group")
    chunk, m, local = layout.chunk, layout.m, layout.local
    width, quarter = 3 * local, layout.quarter
    at_kv, at_out, at_qkv, at_cq, at_co = layout.kv, layout.out, layout.qkv, layout.cq, layout.co
    def outputs(c, block, slots, act):
        slot = c % RING

        def region(begin, end, copies):
            @pl.when(jnp.logical_and(c >= begin, c < end))
            def _():
                for i, (source, target) in enumerate(copies(c - begin)):
                    act(pltpu.make_async_copy(source, target, slots.at[slot, i]))

        def whole(output):
            return lambda r: [(block, output.at[r])]

        region(0, at_kv // 2, whole(o_down))
        region(at_kv // 2, at_kv, whole(o_up))
        region(
            at_qkv, at_cq,
            lambda r: [
                *((block.at[:, pl.ds(i * local, local)], o_qkv.at[i, r]) for i in range(3)),
                (block.at[:, pl.ds(width, local)], o_qkv.at[r // quarter, 3 * quarter + r % quarter]),
            ],
        )
        region(
            at_kv, at_out,
            lambda r: [
                (block.at[:, pl.ds(2 * i * local, 2 * local)], o_kv.at[2 * i * quarter + r]) for i in range(2)
            ],
        )
        region(at_out, at_qkv, whole(o_out))
        region(
            at_cq, at_co,
            lambda r: [(block.at[:, pl.ds(i * local, local)], o_cq.at[i * quarter + r]) for i in range(4)],
        )
        region(at_co, layout.count, whole(o_co))

    fresh = max(0, layout.later - LAG * (groups - 1))
    newer = max(fresh, at_kv)
    pairs = [
        (land_in, held),
        (more_in.at[pl.ds(newer - at_kv, at_qkv - newer)], own.at[pl.ds(newer, at_qkv - newer)]),
        (qkv_in.at[pl.ds(0, 3 * quarter)], own.at[pl.ds(at_qkv, 3 * quarter), :, pl.ds(0, width)]),
    ]
    for i in range(3):
        pairs.append(
            (
                qkv_in.at[pl.ds(3 * quarter, quarter), :, pl.ds(i * local, local)],
                own.at[pl.ds(at_qkv + i * quarter, quarter), :, pl.ds(width, local)],
            )
        )
    if fresh < at_kv:
        pairs.append((feed_in.at[pl.ds(fresh, at_kv - fresh)], own.at[pl.ds(fresh, at_kv - fresh)]))
    early = len(pairs)
    pairs += [
        (sums_a_in, sums_a), (sums_b_in, sums_b), (text_in, text), (cross_q_in, cross_q), (cross_o_in, cross_o),
        (part_in, part), (after_in, after),
    ]
    loads = [pltpu.make_async_copy(a, b, load.at[i]) for i, (a, b) in enumerate(pairs)]
    for copy in loads:
        copy.start()
    loads[0].wait()
    greet(
        [{"tensor": x}, {"tensor": y}, {"tensor": d}]
        + [{"sub": (s + k) % subs} for k in range(1, subs)]
        + [{"group": (g + k) % groups} for k in range(1, groups)]
    )
    begin, end = layout.later, layout.end
    pump = Pump(own, held, ring, result, ring_send, ring_recv, ring_store, begin, end, layout.count, outputs)

    def run(a, b):
        def step(k, carry):
            pump.step(k)
            return carry

        lax.fori_loop(a, b, step, 0)

    for copy in loads[1:early]:
        copy.wait()
    run(begin, begin + 1)
    for copy in loads[early:]:
        copy.wait()
    share_width = m // subs
    for i in range(6):
        source, at = (sums_a, i) if i < 4 else (sums_b, i - 4)
        row = jnp.sum(source[8 * at : 8 * at + 8], 0, keepdims=True)
        for j in range(subs):
            vectors[j, i : i + 1] = row[:, j * share_width : (j + 1) * share_width]
    strip = text.shape[0] // 4

    def remote(source, target, k, device):
        return pltpu.make_async_remote_copy(
            source, target, send.at[k], recv.at[k], device_id=device, device_id_type=MESH
        )

    square = (x, y, d)
    first = [remote(vectors, vectors_land.at[k], k, {"tensor": square[k]}) for k in range(3)]
    first += [
        remote(text.at[rows_at(square[k], strip)], text_land.at[k], 3 + k, {"tensor": square[k]}) for k in range(3)
    ]
    second = [
        remote(share.at[0, (s + k) % subs], share_land.at[k - 1], 5 + k, {"sub": (s + k) % subs}) for k in range(1, subs)
    ]
    base = 5 + subs
    second += [
        remote(text_full.at[rows_at(t, strip)], text_full.at[rows_at(t, strip)], base + k, {"tensor": square[k]}) for k in range(3)
    ]
    base += 3
    third = [
        remote(share.at[1, 0], share_land.at[subs - 2 + k], base + k - 1, {"group": (g + k) % groups})
        for k in range(1, groups)
    ]
    base += groups - 1
    scatter_q = Scatter(cross_q, land_q, stage_q, send, recv, base)
    scatter_o = Scatter(cross_o, land_o, stage_o, send, recv, base + 6)
    for copy in first:
        copy.start()
    scatter_p = Scatter(part, land_p, stage_p, send, recv, base + 12)
    for each in (scatter_q, scatter_o):
        each.diagonal()
    for each in (scatter_q, scatter_o):
        each.along_x()
        each.along_y()

    run(begin + 1, begin + 3)
    for copy in first:
        copy.wait_recv()
    for j in range(subs):
        share[0, j] = vectors[j] + vectors_land[0, j] + vectors_land[1, j] + vectors_land[2, j]
    text_full[rows_at(t, strip)] = text[rows_at(t, strip)] + text_land[0] + text_land[1] + text_land[2]
    for copy in first:
        copy.wait_send()
    for copy in second:
        copy.start()
    run(begin + 3, begin + 6)
    for copy in second:
        copy.wait_recv()
    total = share[0, s]
    for k in range(1, subs):
        total = total + share_land[k - 1]
    share[1, 0] = total
    text_store = pltpu.make_async_copy(text_full, o_text, store.at[0])
    text_store.start()
    for copy in third:
        copy.start()
    relay = max(begin + 6, begin + (at_cq - begin) // 2)
    run(begin + 6, relay)
    scatter_p.diagonal()
    scatter_p.along_x()
    scatter_p.along_y()
    for each in (scatter_q, scatter_o):
        each.relay()
    finish = at_cq
    run(relay, finish)

    def take_q(rows, value):
        row = rows.start
        part = row // (quarter * chunk)
        c = row // chunk - part * quarter
        own[at_cq + c, :, pl.ds(pl.multiple_of(part * local, local), local)] = value.astype(BF)

    scatter_q.finish(take_q, chunk)
    step = min(chunk, scatter_o.half)

    def take_o(rows, value):
        own[at_co + rows.start // chunk, rows_at(rows.start % chunk // step, step)] = value.astype(BF)

    scatter_o.finish(take_o, step)
    late = min(finish + 8, end)
    run(finish, late)
    scatter_p.relay()
    run(late, end)

    def take_layer(rows, value):
        after[rows] = after[rows] + value

    scatter_p.finish(take_layer, 64)
    layer_store = pltpu.make_async_copy(after, o_layer, store.at[2])
    layer_store.start()
    for copy in third:
        copy.wait_recv()
    total = share[1, 0]
    for k in range(1, groups):
        total = total + share_land[subs - 2 + k]
    share[2, 0] = total
    vector_store = pltpu.make_async_copy(share.at[2, 0], o_vectors, store.at[1])
    vector_store.start()
    for copy in second + third:
        copy.wait_send()
    for each in (scatter_q, scatter_o, scatter_p):
        each.drain()
    pump.drain()
    layer_store.wait()
    text_store.wait()
    vector_store.wait()


def total(layout, pieces, qkv, more, cross_q, cross_o, sums_a, sums_b, text, land, part, after, down, up, kv, subs, groups):
    m, chunk = layout.m, layout.chunk
    n = after.shape[0]
    v = pltpu.VMEM
    sems = 7 + subs + groups + 18
    qkv = qkv.reshape(-1, chunk, qkv.shape[1])
    piece_q, piece_o = cross_q.shape[1:], cross_o.shape[1:]
    out_shape = shape(layout.qkv - layout.out, chunk, m)
    return pl.pallas_call(
        partial(total_kernel, layout),
        name="total",
        out_shape=[
            shape(3, *qkv.shape[:2], layout.local), shape(layout.piece // chunk, chunk, layout.local), out_shape, out_shape,
            shape(*text.shape, kind=F32), shape(8, m // subs, kind=F32), shape(n, m, kind=F32),
            shape(*down.shape), shape(*up.shape), shape(*kv.shape),
        ],
        in_specs=[ANY] * 14,
        out_specs=[ANY] * 10,
        input_output_aliases={11: 7, 12: 8, 13: 9},
        scratch_shapes=[
            *pump_scratch(layout, layout.count),
            v(cross_q.shape, BF), v(cross_o.shape, BF),
            v((6, piece_q[0] // 2, piece_q[1]), BF), v((6, piece_o[0] // 2, piece_o[1]), BF),
            v((2, piece_q[0] // 2, piece_q[1]), BF), v((2, piece_o[0] // 2, piece_o[1]), BF),
            v((4, n, m), BF), v((6, n // 2, m), BF), v((2, n // 2, m), BF), v((n, m), F32),
            v(sums_a.shape, F32), v(sums_b.shape, F32), v(text.shape, F32),
            v((3, text.shape[0] // 4, m), F32), v(text.shape, F32), v((subs, 8, m // subs), F32), v((3, subs, 8, m // subs), F32),
            v((3, subs, 8, m // subs), F32), v((subs - 1 + groups - 1, 8, m // subs), F32),
            dma(14), dma(3), dma(sems), dma(sems),
        ],
        compiler_params=params(7),
    )(pieces, qkv, more, cross_q, cross_o, sums_a, sums_b, text, land, part, after, down, up, kv)


def local(
    frames, text_states, selfgain, selfbias, selfqkv, selfout, crossgain, crossbias, crossquery, crosskv, crossout,
    feedgain, feedbias, feedup, feeddown, cotangent,
):
    subs, groups = lax.axis_size("sub"), lax.axis_size("group")
    m = frames.shape[2]
    width = selfout.shape[0]
    qkv = selfqkv.transpose(1, 0, 2)
    kv = crosskv.reshape(m, 2 * width)
    gains = jnp.concatenate([crossgain, crossbias, feedgain, feedbias, selfgain, selfbias]).reshape(6, m)
    rows, triple, memory = enter(frames[0], gains, qkv, text_states[0], kv)
    flat, sums, after_self, wq, wo = attend(triple, selfout, frames[0], crossquery, crossout, subs)
    wo = wo.reshape(4 * width, m)
    query, cross_flat, after_cross, feed_rows, grads = cross(after_self, gains, wq, wo, memory, cotangent[0])
    layout = Layout(m, width, subs, groups)
    part, norm_grad, pieces = feed(feed_rows, grads, feedup, feeddown, subs)
    pieces = pieces.reshape(-1, layout.chunk, m)
    grad_out, branch, sums_a, memory_grad, piece_q, piece_o, down, land = cross_back(
        layout, cotangent[0], norm_grad, after_cross, after_self, gains, query, cross_flat, memory, wq, wo, pieces, subs
    )
    frame_grad, sums_b, text_part, grad_qkv, more, down, up, full_kv, land = attend_back(
        layout, branch, triple, flat, sums, selfout, qkv, rows, frames[0], gains, grad_out, memory_grad,
        text_states[0], kv, pieces, land, down, subs,
    )
    full_qkv, full_cq, full_out, full_co, text_grad, vectors, layer_output, down, up, full_kv = total(
        layout, pieces, grad_qkv, more, piece_q, piece_o, sums_a, sums_b, text_part, land, part, after_cross,
        down, up, full_kv, subs, groups,
    )
    return (
        layer_output[None],
        frame_grad[None],
        text_grad[None],
        vectors[4],
        vectors[5],
        full_qkv.astype(F32).reshape(3, -1, width).transpose(1, 0, 2),
        full_out.astype(F32).reshape(-1, m),
        vectors[2],
        vectors[3],
        full_cq.astype(F32).reshape(-1, width),
        full_kv.astype(F32).reshape(-1, 2, width),
        full_co.astype(F32).reshape(-1, m),
        vectors[0],
        vectors[1],
        up.astype(F32).reshape(-1, m),
        down.astype(F32).reshape(-1, m),
    )


def solution(mesh):
    clips = P(("sub", "group"), "tensor", None)
    whole = P(("sub", "group"), None, None)
    narrow, wide = P("tensor", None), P(None, "tensor")
    third = P(None, None, "tensor")
    vector = P("sub")
    return jax.shard_map(
        local,
        mesh=mesh,
        in_specs=(
            clips, whole, P(), P(), third, narrow, P(), P(), wide, third, narrow, P(), P(), wide, narrow, clips,
        ),
        out_specs=(
            clips, clips, whole, vector, vector, P("sub", None, "tensor"), P(("tensor", "sub"), None), vector, vector,
            P("sub", "tensor"), P("sub", None, "tensor"), P(("tensor", "sub"), None), vector, vector,
            P("sub", "tensor"), P(("tensor", "sub"), None),
        ),
        check_vma=False,
    )
```

```python
from functools import partial

import jax
import jax.numpy as jnp
from jax import lax
from jax.experimental import pallas as pl
from jax.experimental.pallas import tpu as pltpu
from jax.sharding import PartitionSpec as P

HEAD = 64
EPSILON = 1e-05
NEG_BIG = -1e30
LOG2E = 1.4426950408889634
MESH = pl.DeviceIdType.MESH
F32 = jnp.float32
BF = jnp.bfloat16
ANY = pl.BlockSpec(memory_space=pl.ANY)
VMEM_LIMIT = 63 << 20


def neighbours():
    t = lax.axis_index("tensor")
    return t, t + 1 - 2 * (t % 2), (t + 2) % 4, 3 - t


def greet(targets):
    barrier = pltpu.get_barrier_semaphore()
    for target in targets:
        pl.semaphore_signal(barrier, inc=1, device_id=target, device_id_type=MESH)
    pl.semaphore_wait(barrier, len(targets))


def dot(a, b):
    return lax.dot_general(a, b, (((1,), (0,)), ((), ())), preferred_element_type=F32)


def dot_t(a, b):
    return lax.dot_general(a, b, (((1,), (1,)), ((), ())), preferred_element_type=F32)


def dot_c(a, b):
    return lax.dot_general(a, b, (((0,), (0,)), ((), ())), preferred_element_type=F32)


def cols(j, width):
    return pl.ds(pl.multiple_of(j * width, width), width)


def rows_at(j, height):
    return pl.ds(pl.multiple_of(j * height, height), height)


def split(count):
    first = (count // 2 + 15) // 16 * 16
    return pl.ds(0, first), pl.ds(first, count - first)


class Gather:
    def __init__(self, own, dst, send, recv, base, halves=None):
        self.own, self.dst, self.send, self.recv, self.base = own, dst, send, recv, base
        self.halves = halves or split(own.shape[0])

    def copy(self, k):
        t, x, y, _ = neighbours()
        first, second = self.halves
        half = (first, second, second, first, first, second)[k]
        place = (t, t, t, t, x, y)[k]
        target = (x, y, x, y, y, x)[k]
        source = self.own.at[half] if k < 4 else self.dst.at[place, half]
        return pltpu.make_async_remote_copy(
            source,
            self.dst.at[place, half],
            self.send.at[self.base + k],
            self.recv.at[self.base + k],
            device_id={"tensor": target},
            device_id_type=MESH,
        )

    def start(self):
        for k in range(4):
            self.copy(k).start()

    def relay_x(self):
        self.copy(0).wait_recv()
        self.copy(4).start()

    def relay_y(self):
        self.copy(1).wait_recv()
        self.copy(5).start()

    def have_x(self):
        self.copy(2).wait_recv()

    def have_y(self):
        self.copy(3).wait_recv()

    def have_d(self):
        self.copy(4).wait_recv()
        self.copy(5).wait_recv()

    def drain(self):
        for k in range(6):
            self.copy(k).wait_send()


class Scatter:
    def __init__(self, part, land, stage, send, recv, base):
        self.part, self.land, self.stage = part, land, stage
        self.send, self.recv, self.base = send, recv, base
        self.half = part.shape[1] // 2

    def copy(self, k):
        t, x, y, d = neighbours()
        low, high = pl.ds(0, self.half), pl.ds(self.half, self.half)
        source = (
            self.part.at[d, low],
            self.part.at[d, high],
            self.part.at[x, low],
            self.stage.at[1],
            self.part.at[y, high],
            self.stage.at[0],
        )[k]
        target = (x, y, x, x, y, y)[k]
        return pltpu.make_async_remote_copy(
            source,
            self.land.at[k],
            self.send.at[self.base + k],
            self.recv.at[self.base + k],
            device_id={"tensor": target},
            device_id_type=MESH,
        )

    def diagonal(self):
        self.copy(0).start()
        self.copy(1).start()

    def along_x(self):
        self.copy(2).start()

    def along_y(self):
        self.copy(4).start()

    def relay(self):
        t, x, y, d = neighbours()
        low, high = pl.ds(0, self.half), pl.ds(self.half, self.half)
        self.copy(0).wait_recv()
        self.stage[0] = (self.part[y, low].astype(F32) + self.land[0].astype(F32)).astype(BF)
        self.copy(5).start()
        self.copy(1).wait_recv()
        self.stage[1] = (self.part[x, high].astype(F32) + self.land[1].astype(F32)).astype(BF)
        self.copy(3).start()

    def finish(self, take, step):
        t, x, y, d = neighbours()
        for k in (2, 4, 5, 3):
            self.copy(k).wait_recv()
        for base, a, b in ((0, 2, 5), (self.half, 4, 3)):

            def block(i, carry, base=base, a=a, b=b):
                here = rows_at(i, step)
                rows = pl.ds(pl.multiple_of(base + i * step, step), step)
                take(
                    rows,
                    self.part[t, rows].astype(F32)
                    + self.land[a, here].astype(F32)
                    + self.land[b, here].astype(F32),
                )
                return carry

            lax.fori_loop(0, self.half // step, block, 0)

    def drain(self):
        for k in range(6):
            self.copy(k).wait_send()


def normed_rows(values):
    centre = values - jnp.mean(values, -1, keepdims=True)
    inverse = lax.rsqrt(jnp.mean(centre * centre, -1, keepdims=True) + EPSILON)
    return centre * inverse, inverse


def params(cid, **more):
    return pltpu.CompilerParams(
        collective_id=cid, has_side_effects=True, vmem_limit_bytes=VMEM_LIMIT, **more
    )


def dma(count):
    return pltpu.SemaphoreType.DMA((count,))


def shape(*dims, kind=BF):
    return jax.ShapeDtypeStruct(dims, kind)


LAG = 3
RING = 4


def either(condition, other):
    return jnp.logical_and(condition, other)


class Pump:
    def __init__(self, own, land, ring, result, send, recv, store, first, last, count, outputs):
        self.own, self.land, self.ring, self.result = own, land, ring, result
        self.send, self.recv, self.store = send, recv, store
        self.first, self.last, self.count, self.outputs = first, last, count, outputs
        self.window = land.shape[1]
        self.g, self.n = lax.axis_index("group"), lax.axis_size("group")

    def copy(self, way, c):
        target = (self.g + 1) % self.n if way == 0 else (self.g + self.n - 1) % self.n
        return pltpu.make_async_remote_copy(
            self.ring.at[way, c % RING],
            self.land.at[way, c % self.window],
            self.send.at[way, c % RING],
            self.recv.at[way, c % self.window],
            device_id={"group": target},
            device_id_type=MESH,
        )

    def flow(self, way, k):
        place = self.g if way == 0 else self.n - 1 - self.g
        c = k - LAG * place

        @pl.when(either(c >= 0, c < self.count))
        def _():
            @pl.when(either(place > 0, k - LAG >= self.first))
            def _():
                self.copy(way, c).wait_recv()

            @pl.when(place < self.n - 1)
            def _():
                @pl.when(either(c >= RING, k - RING >= self.first))
                def _():
                    self.copy(way, c - RING).wait_send()

                @pl.when(place > 0)
                def _():
                    before = self.land[way, c % self.window].astype(F32)
                    self.ring[way, c % RING] = (self.own[c].astype(F32) + before).astype(BF)

                @pl.when(place == 0)
                def _():
                    self.ring[way, c % RING] = self.own[c]

                self.copy(way, c).start()

    def finished(self, k):
        far = jnp.maximum(self.g, self.n - 1 - self.g)
        return k - LAG * far

    def step(self, k):
        self.flow(0, k)
        self.flow(1, k)
        f = self.finished(k)

        @pl.when(either(f >= 0, f < self.count))
        def _():
            @pl.when(either(f >= RING, k - RING >= self.first))
            def _():
                self.outputs(f - RING, self.result.at[f % RING], self.store, lambda copy: copy.wait())

            mine = self.own[f].astype(F32)
            slot, held = f % RING, f % self.window

            @pl.when(either(self.g > 0, self.g < self.n - 1))
            def _():
                both = self.land[0, held].astype(F32) + self.land[1, held].astype(F32)
                self.result[slot] = (mine + both).astype(BF)

            @pl.when(self.g == 0)
            def _():
                self.result[slot] = (mine + self.land[1, held].astype(F32)).astype(BF)

            @pl.when(self.g == self.n - 1)
            def _():
                self.result[slot] = (mine + self.land[0, held].astype(F32)).astype(BF)

            self.outputs(f, self.result.at[slot], self.store, lambda copy: copy.start())

    def drain(self):
        for way in range(2):
            place = self.g if way == 0 else self.n - 1 - self.g
            top = jnp.minimum(self.last - LAG * place, self.count)
            for j in range(1, RING + 1):
                c = top - j

                @pl.when(either(place < self.n - 1, either(c >= 0, c + LAG * place >= self.first)))
                def _(way=way, c=c):
                    self.copy(way, c).wait_send()

            for k in range(max(self.first, self.last - LAG), self.last):
                c = k - LAG * (place - 1)

                @pl.when(either(place > 0, either(c >= 0, c < self.count)))
                def _(way=way, c=c):
                    self.copy(way, c).wait_recv()

        far = jnp.maximum(self.g, self.n - 1 - self.g)
        top = jnp.minimum(self.last - LAG * far, self.count)
        for j in range(1, RING + 1):
            f = top - j

            @pl.when(either(f >= 0, f + LAG * far >= self.first))
            def _(f=f):
                self.outputs(f, self.result.at[f % RING], self.store, lambda copy: copy.wait())


KV_TICKS, OUT_TICKS = 20, 28


class Layout:
    def __init__(self, m, local, subs, groups):
        piece = m // subs
        self.m, self.piece, self.local = m, piece, local
        self.out_rows = local // subs
        self.chunk = 48
        quarter = piece // 4 // self.chunk
        self.quarter = quarter
        self.feed_count = 2 * piece // self.chunk
        self.kv = self.feed_count
        self.out = self.kv + 2 * quarter
        self.qkv = self.out + self.out_rows // self.chunk
        self.cq = self.qkv + 3 * quarter
        self.co = self.cq + quarter
        self.count = self.co + self.out_rows // self.chunk
        self.window = LAG * (groups + 1)
        self.end = self.count + LAG * (groups - 1)
        self.middle = min(12, self.feed_count // 3)
        self.later = self.feed_count
        if self.middle + KV_TICKS <= self.kv and self.middle + OUT_TICKS <= self.out:
            self.later = self.middle + OUT_TICKS + 2


def sum_outputs(layout, halves, text=None):
    def outputs(c, block, store, act):
        count = layout.feed_count // 2
        for i, half in enumerate(halves):

            @pl.when(either(c >= i * count, c < (i + 1) * count))
            def _(i=i, half=half):
                act(pltpu.make_async_copy(block, half.at[c - i * count], store.at[c % RING, 0]))

        if text is not None:

            @pl.when(either(c >= layout.kv, c < layout.out))
            def _():
                for i in range(2):
                    lanes = pl.ds(2 * i * layout.local, 2 * layout.local)
                    target = text.at[2 * i * layout.quarter + c - layout.kv]
                    act(pltpu.make_async_copy(block.at[:, lanes], target, store.at[c % RING, i]))

    return outputs


def pump_scratch(layout, count):
    chunk, m = layout.chunk, layout.m
    return [
        pltpu.VMEM((count, chunk, m), BF),
        pltpu.VMEM((2, layout.window, chunk, m), BF),
        pltpu.VMEM((2, RING, chunk, m), BF),
        pltpu.VMEM((RING, chunk, m), BF),
        pltpu.SemaphoreType.DMA((2, RING)),
        pltpu.SemaphoreType.DMA((2, layout.window)),
        pltpu.SemaphoreType.DMA((RING, 4)),
    ]


def group_ring():
    g, n = lax.axis_index("group"), lax.axis_size("group")
    return [{"group": (g + 1) % n}, {"group": (g + n - 1) % n}]


def enter_kernel(
    frames, gains, qkv, text, kv, o_rows, o_triple, o_memory,
    v_frames, v_gains, v_qkv, v_text, v_kv, rows, triple, memory, load, store, send, recv,
):
    t, x, y, d = neighbours()
    loads = [
        pltpu.make_async_copy(a, b, load.at[i])
        for i, (a, b) in enumerate(
            (
                (frames, v_frames), (gains, v_gains), (text, v_text), (kv, v_kv),
                *((qkv.at[i], v_qkv.at[:, pl.ds(i * qkv.shape[2], qkv.shape[2])]) for i in range(3)),
            )
        )
    ]
    for copy in loads:
        copy.start()
    greet([{"tensor": x}, {"tensor": y}])
    for copy in loads[:2]:
        copy.wait()
    count, width = v_qkv.shape
    block = 384

    def norm_block(i, carry):
        here = rows_at(i, 64)
        hat, _ = normed_rows(v_frames[here].astype(F32))
        rows[t, here] = (hat * v_gains[4:5] + v_gains[5:6]).astype(BF)
        return carry

    lax.fori_loop(0, v_frames.shape[0] // 64, norm_block, 0)
    gather = Gather(rows.at[t], rows, send, recv, 0)
    gather.start()
    texts = Gather(memory.at[t], memory, send, recv, 6)

    def project(place):
        def step(j, carry):
            triple[place, :, cols(j, block)] = dot(rows[place], v_qkv[:, cols(j, block)]).astype(BF)
            return carry

        lax.fori_loop(0, width // block, step, 0)

    def put(k, place):
        a = pltpu.make_async_copy(rows.at[place], o_rows.at[place], store.at[2 * k])
        b = pltpu.make_async_copy(triple.at[place], o_triple.at[place], store.at[2 * k + 1])
        a.start()
        b.start()
        return [a, b]

    loads[2].wait()
    loads[3].wait()

    def texts_step(j, carry):
        memory[t, :, cols(j, block)] = dot(v_text[...], v_kv[:, cols(j, block)]).astype(BF)
        return carry

    lax.fori_loop(0, v_kv.shape[1] // block, texts_step, 0)
    texts.start()
    for copy in loads[4:]:
        copy.wait()
    project(t)
    stores = put(0, t)
    gather.relay_x()
    gather.relay_y()
    gather.have_x()
    project(x)
    stores += put(1, x)
    gather.have_y()
    project(y)
    stores += put(2, y)
    texts.relay_x()
    texts.relay_y()
    texts.have_x()
    texts.have_y()
    gather.have_d()
    project(d)
    stores += put(3, d)
    texts.have_d()
    last = pltpu.make_async_copy(memory, o_memory, store.at[8])
    last.start()
    gather.drain()
    texts.drain()
    for copy in stores:
        copy.wait()
    last.wait()


def enter(frames, gains, qkv, text, kv):
    n, m = frames.shape
    width, texts, kvw = 3 * qkv.shape[2], text.shape[0], kv.shape[1]
    return pl.pallas_call(
        enter_kernel,
        name="enter",
        out_shape=[shape(4, n, m), shape(4, n, width), shape(4, texts, kvw)],
        in_specs=[ANY] * 5,
        out_specs=[ANY] * 3,
        scratch_shapes=[
            pltpu.VMEM((n, m), frames.dtype), pltpu.VMEM(gains.shape, F32),
            pltpu.VMEM((m, width), BF), pltpu.VMEM(text.shape, BF), pltpu.VMEM(kv.shape, BF),
            pltpu.VMEM((4, n, m), BF), pltpu.VMEM((4, n, width), BF), pltpu.VMEM((4, texts, kvw), BF),
            dma(7), dma(9), dma(12), dma(12),
        ],
        compiler_params=params(1),
    )(frames, gains, qkv, text, kv)


def head_lanes(rows):
    return lax.broadcasted_iota(jnp.int32, (rows, 128), 1)


def attend_rows(triple, place, blocks, heads, flat, sums):
    n = triple.shape[1]
    width = heads * HEAD
    scale = HEAD ** (-0.5) * LOG2E
    lanes = head_lanes(n)

    def pair(p, stats):
        here = pl.ds(pl.multiple_of(p * 128, 128), 128)
        key_cols = pl.ds(pl.multiple_of(width + p * 128, 128), 128)
        value_cols = pl.ds(pl.multiple_of(2 * width + p * 128, 128), 128)
        query = triple[place, :, here]
        keys = triple[0:blocks, :, key_cols].reshape(blocks * n, 128)
        values = triple[0:blocks, :, value_cols].reshape(blocks * n, 128)
        outs = []
        for h in range(2):
            mine = (lanes < HEAD) if h == 0 else (lanes >= HEAD)
            scores = dot_t(jnp.where(mine, query, jnp.zeros_like(query)), keys)
            row = lax.broadcasted_iota(jnp.int32, scores.shape, 0)
            col = lax.broadcasted_iota(jnp.int32, scores.shape, 1)
            scores = jnp.where(col <= row + (blocks - 1) * n, scores, NEG_BIG)
            peak = jnp.max(scores, -1, keepdims=True) * scale
            exponent = jnp.exp2(scores * scale - peak)
            total = jnp.sum(exponent, -1, keepdims=True)
            outs.append(dot(exponent.astype(BF), values) / total)
            stats = jnp.where(lanes == 2 * p + h, peak + jnp.log2(total), stats)
        flat[place, :, here] = jnp.where(lanes < HEAD, outs[0], outs[1]).astype(BF)
        return stats

    sums[place] = lax.fori_loop(0, heads // 2, pair, jnp.zeros((n, 128), F32))


def attend_kernel(
    triple_in, out_in, frames_in, wq, wo, o_flat, o_sums, o_after, o_wq, o_wo,
    triple, v_out, v_frames, flat, sums, after, part, land, stage, v_wq, v_wo, load, store, send, recv, side,
):
    t, x, y, d = neighbours()
    s = lax.axis_index("sub")
    subs = lax.axis_size("sub")
    n = triple.shape[1]
    m = v_out.shape[1]
    heads = v_out.shape[0] // HEAD
    loads = [
        pltpu.make_async_copy(a, b, load.at[i])
        for i, (a, b) in enumerate(
            ((triple_in, triple), (out_in, v_out), (frames_in, v_frames), (wq, v_wq), (wo, v_wo))
        )
    ]
    for copy in loads:
        copy.start()
    greet(
        [{"tensor": x}, {"tensor": y}]
        + [{"sub": (s + k) % subs} for k in range(1, subs)]
    )
    scatter = Scatter(part, land, stage, send, recv, 0)
    gathers = []
    for i, (weight, full) in enumerate(((wq, o_wq), (wo, o_wo))):
        piece = weight.shape[0] // subs
        first, second = split(piece)
        offset = pl.multiple_of(s * piece, piece)
        halves = (
            pl.ds(offset, first.size),
            pl.ds(pl.multiple_of(offset + first.size, 16), second.size),
        )
        gathers.append((Gather(weight, full, send, recv, 6 + 6 * i, halves), full, pl.ds(offset, piece)))

    def shared(i, j, k):
        _, full, piece = gathers[i]
        place = (x, y, d)[j]
        slot = (i * 3 + j) * (subs - 1) + k - 1
        return pltpu.make_async_remote_copy(
            full.at[place, piece], full.at[place, piece],
            send.at[18 + slot], recv.at[18 + slot],
            device_id={"sub": (s + k) % subs}, device_id_type=MESH,
        )

    for gather, _, _ in gathers:
        gather.start()
    for copy in loads[:2]:
        copy.wait()

    def one(i, carry):
        far_y = 1 - i // 2
        far_x = 1 - i % 2
        place = (t // 2 + far_y - 2 * (t // 2) * far_y) * 2 + (t % 2 + far_x - 2 * (t % 2) * far_x)
        for blocks in range(1, 5):

            @pl.when(place == blocks - 1)
            def _(blocks=blocks):
                attend_rows(triple, blocks - 1, blocks, heads, flat, sums)

        def out_step(j, carry):
            part[place, :, cols(j, 512)] = dot(flat[place], v_out[:, cols(j, 512)]).astype(BF)
            return carry

        lax.fori_loop(0, m // 512, out_step, 0)

        @pl.when(i == 0)
        def _():
            scatter.diagonal()

        @pl.when(i == 1)
        def _():
            scatter.along_y()

        @pl.when(i == 2)
        def _():
            scatter.along_x()

        return carry

    lax.fori_loop(0, 4, one, 0)
    for gather, _, _ in gathers:
        gather.relay_x()
        gather.relay_y()
    stores = [
        pltpu.make_async_copy(flat, o_flat, store.at[0]),
        pltpu.make_async_copy(sums, o_sums, store.at[1]),
    ]
    loads[3].wait()
    loads[4].wait()
    stores += [
        pltpu.make_async_copy(v_wq, o_wq.at[t], store.at[2]),
        pltpu.make_async_copy(v_wo, o_wo.at[t], store.at[3]),
    ]
    for copy in stores:
        copy.start()
    scatter.relay()
    for i, (gather, _, _) in enumerate(gathers):
        gather.have_x()
        gather.have_y()
        gather.have_d()
        for j in range(3):
            for k in range(1, subs):
                shared(i, j, k).start()
    loads[2].wait()

    def take(rows, total):
        after[rows] = v_frames[rows].astype(F32) + total

    scatter.finish(take, 64)
    last = pltpu.make_async_copy(after, o_after, store.at[4])
    last.start()
    scatter.drain()
    for i, (gather, _, _) in enumerate(gathers):
        gather.drain()
        for j in range(3):
            for k in range(1, subs):
                shared(i, j, k).wait()
    for copy in stores:
        copy.wait()
    last.wait()


def attend(triple, out, frames, wq, wo, subs):
    _, n, width = triple.shape
    local, m = out.shape
    extra = 18 + 6 * (subs - 1)
    return pl.pallas_call(
        attend_kernel,
        name="attend",
        out_shape=[
            shape(4, n, local), shape(4, n, 128, kind=F32), shape(n, m, kind=F32),
            shape(4, *wq.shape), shape(4, *wo.shape),
        ],
        in_specs=[ANY] * 5,
        out_specs=[ANY] * 5,
        scratch_shapes=[
            pltpu.VMEM((4, n, width), BF), pltpu.VMEM((local, m), BF), pltpu.VMEM((n, m), frames.dtype),
            pltpu.VMEM((4, n, local), BF), pltpu.VMEM((4, n, 128), F32), pltpu.VMEM((n, m), F32),
            pltpu.VMEM((4, n, m), BF), pltpu.VMEM((6, n // 2, m), BF), pltpu.VMEM((2, n // 2, m), BF),
            pltpu.VMEM(wq.shape, BF), pltpu.VMEM(wo.shape, BF),
            dma(5), dma(5), dma(extra), dma(extra), dma(1),
        ],
        compiler_params=params(2),
    )(triple, out, frames, wq, wo)


def stack_pair(block, rows):
    lanes = head_lanes(rows)
    zero = jnp.zeros_like(block)
    return jnp.concatenate([jnp.where(lanes < HEAD, block, zero), jnp.where(lanes >= HEAD, block, zero)], 0)


def pair_softmax(query, keys):
    scale = HEAD ** (-0.5) * LOG2E
    scores = dot_t(query, keys)
    left = head_lanes(scores.shape[0]) < HEAD
    low = jnp.max(jnp.where(left, scores, -jnp.inf), -1, keepdims=True)
    high = jnp.max(jnp.where(left, -jnp.inf, scores), -1, keepdims=True)
    exponent = jnp.exp2((scores - jnp.where(left, low, high)) * scale)
    total = pair_sum(exponent, left)
    return exponent / total, left


def pair_sum(values, left):
    low = jnp.sum(jnp.where(left, values, 0.0), -1, keepdims=True)
    high = jnp.sum(jnp.where(left, 0.0, values), -1, keepdims=True)
    return jnp.where(left, low, high)


def cross_kernel(
    after_in, gains_in, wq_in, wo_in, memory_in, cot_in,
    o_query, o_flat, o_after, o_rows, o_grads,
    after, gains, wq, wo, memory, cot, rows, query, flat, result, feed, grads, load, store, send, recv,
):
    t, x, y, d = neighbours()
    loads = [
        pltpu.make_async_copy(a, b, load.at[i])
        for i, (a, b) in enumerate(
            ((cot_in, cot), (after_in, after), (gains_in, gains), (wq_in, wq), (memory_in, memory), (wo_in, wo))
        )
    ]
    for copy in loads:
        copy.start()
    greet([{"tensor": x}, {"tensor": y}])
    n, m = after.shape
    width = wq.shape[2]
    texts = memory.shape[1]
    loads[0].wait()

    def round_block(i, carry):
        here = rows_at(i, 64)
        grads[t, here] = cot[here].astype(BF)
        return carry

    lax.fori_loop(0, n // 64, round_block, 0)
    gather = Gather(grads.at[t], grads, send, recv, 0)
    gather.start()
    loads[1].wait()
    loads[2].wait()

    def norm_block(i, carry):
        here = rows_at(i, 64)
        hat, _ = normed_rows(after[here])
        rows[here] = (hat * gains[0:1] + gains[1:2]).astype(BF)
        return carry

    lax.fori_loop(0, n // 64, norm_block, 0)
    loads[3].wait()
    loads[4].wait()

    def quarter(q, carry):
        query[:, cols(q, width)] = dot(rows[...], wq[q]).astype(BF)

        def pair(p, carry):
            keys = stack_pair(memory[q, :, cols(p, 128)], texts)
            values = stack_pair(memory[q, :, pl.ds(pl.multiple_of(width + p * 128, 128), 128)], texts)
            here = pl.ds(pl.multiple_of(q * width + p * 128, 128), 128)
            probs, _ = pair_softmax(query[:, here], keys)
            flat[:, here] = dot(probs.astype(BF), values).astype(BF)
            return carry

        lax.fori_loop(0, width // 128, pair, 0)
        return carry

    lax.fori_loop(0, 4, quarter, 0)
    gather.relay_x()
    gather.relay_y()
    stores = [pltpu.make_async_copy(query, o_query, store.at[0]), pltpu.make_async_copy(flat, o_flat, store.at[1])]
    loads[5].wait()

    def out_step(j, carry):
        result[:, cols(j, 512)] = after[:, cols(j, 512)] + dot(flat[...], wo[:, cols(j, 512)])
        return carry

    lax.fori_loop(0, m // 512, out_step, 0)

    def feed_block(i, carry):
        here = rows_at(i, 64)
        hat, _ = normed_rows(result[here])
        feed[here] = (hat * gains[2:3] + gains[3:4]).astype(BF)
        return carry

    lax.fori_loop(0, n // 64, feed_block, 0)
    stores += [pltpu.make_async_copy(result, o_after, store.at[2]), pltpu.make_async_copy(feed, o_rows, store.at[3])]
    for copy in stores:
        copy.start()
    gather.have_x()
    gather.have_y()
    gather.have_d()
    last = pltpu.make_async_copy(grads, o_grads, store.at[4])
    last.start()
    gather.drain()
    for copy in stores:
        copy.wait()
    last.wait()


def cross(after, gains, wq, wo, memory, cot):
    n, m = after.shape
    return pl.pallas_call(
        cross_kernel,
        name="cross",
        out_shape=[shape(n, m), shape(n, m), shape(n, m, kind=F32), shape(n, m), shape(4, n, m)],
        in_specs=[ANY] * 6,
        out_specs=[ANY] * 5,
        scratch_shapes=[
            pltpu.VMEM((n, m), F32), pltpu.VMEM(gains.shape, F32), pltpu.VMEM(wq.shape, BF), pltpu.VMEM(wo.shape, BF),
            pltpu.VMEM(memory.shape, BF), pltpu.VMEM((n, m), F32), pltpu.VMEM((n, m), BF), pltpu.VMEM((n, m), BF),
            pltpu.VMEM((n, m), BF), pltpu.VMEM((n, m), F32), pltpu.VMEM((n, m), BF), pltpu.VMEM((4, n, m), BF),
            dma(6), dma(5), dma(6), dma(6),
        ],
        compiler_params=params(3),
    )(after, gains, wq, wo, memory, cot)


def gelu_both(pre):
    size = jnp.abs(pre) * 0.7071067811865476
    rate = 1.0 / (1.0 + 0.3275911 * size)
    bell = jnp.exp2(pre * pre * (-0.5 * LOG2E))
    series = rate * (
        0.254829592
        + rate * (-0.284496736 + rate * (1.421413741 + rate * (-1.453152027 + rate * 1.061405429)))
    )
    tail = 0.5 * series * bell
    gate = jnp.where(pre >= 0, 1.0 - tail, tail)
    return pre * gate, gate + pre * (0.3989422804014327 * bell)


class Halves:
    def __init__(self, whole, land, send, recv, base):
        self.whole, self.land, self.send, self.recv, self.base = whole, land, send, recv, base
        self.subs = lax.axis_size("sub")
        self.piece = whole.shape[1] // self.subs

    def copies(self, w):
        s = lax.axis_index("sub")
        made = []
        for k in range(1, self.subs):
            target = (s + k) % self.subs
            slot = w * (self.subs - 1) + k - 1
            made.append(
                pltpu.make_async_remote_copy(
                    self.whole.at[w, rows_at(target, self.piece)],
                    self.land.at[w, k - 1],
                    self.send.at[self.base + slot],
                    self.recv.at[self.base + slot],
                    device_id={"sub": target},
                    device_id_type=MESH,
                )
            )
        return made

    def start(self, w):
        for copy in self.copies(w):
            copy.start()

    def total(self, w, take, step):
        s = lax.axis_index("sub")
        for copy in self.copies(w):
            copy.wait_recv()

        def block(i, carry):
            here = rows_at(i, step)
            value = self.whole[w, pl.ds(pl.multiple_of(s * self.piece + i * step, step), step)].astype(F32)
            for k in range(1, self.subs):
                value = value + self.land[w, k - 1, here].astype(F32)
            take(here, value)
            return carry

        lax.fori_loop(0, self.piece // step, block, 0)

    def drain(self, w):
        for copy in self.copies(w):
            copy.wait_send()


def weight_grad(left, right, whole, w, halves, block):
    s = lax.axis_index("sub")
    subs = lax.axis_size("sub")
    total_rows = left.shape[0] * left.shape[1]
    count = whole.shape[1] // block
    begin = ((s + 1) % subs) * halves.piece // block

    def one(j, carry):
        b = (begin + j) % count
        turned = left[:, :, cols(b, block)].reshape(total_rows, block)

        def inner(i, carry):
            other = right[:, :, cols(i, 512)].reshape(total_rows, 512)
            whole[w, rows_at(b, block), cols(i, 512)] = dot_c(turned, other).astype(BF)
            return carry

        lax.fori_loop(0, whole.shape[2] // 512, inner, 0)
        return carry

    if subs == 2:
        lax.fori_loop(0, count // 2, one, 0)
        halves.start(w)
        lax.fori_loop(count // 2, count, one, 0)
    else:
        lax.fori_loop(0, count, one, 0)
        halves.start(w)


def feed_kernel(
    rows_in, grads_in, up_in, down_in, o_part, o_norm, o_pieces,
    rows, grads, up, down, act, pre_grad, part_out, part_norm, land_norm, stage_norm,
    whole, land_whole, load, store, send, recv,
):
    t, x, y, d = neighbours()
    s = lax.axis_index("sub")
    subs = lax.axis_size("sub")
    loads = [
        pltpu.make_async_copy(a, b, load.at[i])
        for i, (a, b) in enumerate(
            ((rows_in, rows.at[t]), (up_in, up), (grads_in, grads), (down_in, down))
        )
    ]
    for copy in loads:
        copy.start()
    greet([{"tensor": x}, {"tensor": y}] + [{"sub": (s + k) % subs} for k in range(1, subs)])
    _, n, m = rows.shape
    hidden = up.shape[1]
    loads[0].wait()
    gather = Gather(rows.at[t], rows, send, recv, 0)
    gather.start()
    back = Scatter(part_norm, land_norm, stage_norm, send, recv, 6)
    halves = Halves(whole, land_whole, send, recv, 12)
    for copy in loads[1:4]:
        copy.wait()

    def work(place):
        def step(j, carry):
            here = cols(j, 256)
            value, slope = gelu_both(dot(rows[place], up[:, here]))
            act[place, :, here] = value.astype(BF)
            pre_grad[place, :, here] = (dot_t(grads[place], down[here]) * slope).astype(BF)
            return carry

        lax.fori_loop(0, hidden // 256, step, 0)

        def out_step(j, carry):
            part_norm[place, :, cols(j, 512)] = dot_t(pre_grad[place], up[rows_at(j, 512)]).astype(BF)
            part_out[place, :, cols(j, 512)] = dot(act[place], down[:, cols(j, 512)]).astype(BF)
            return carry

        lax.fori_loop(0, m // 512, out_step, 0)

    def turn(i, carry):
        far_y = i // 2
        far_x = i % 2
        place = (t // 2 + far_y - 2 * (t // 2) * far_y) * 2 + (t % 2 + far_x - 2 * (t % 2) * far_x)

        @pl.when(i == 1)
        def _():
            gather.relay_x()
            gather.relay_y()
            gather.have_x()

        @pl.when(i == 2)
        def _():
            gather.have_y()

        @pl.when(i == 3)
        def _():
            gather.have_d()

        work(place)

        @pl.when(i == 1)
        def _():
            back.along_x()

        @pl.when(i == 2)
        def _():
            back.along_y()

        @pl.when(i == 3)
        def _():
            back.diagonal()

        return carry

    lax.fori_loop(0, 4, turn, 0)
    stores = [pltpu.make_async_copy(part_out, o_part, store.at[1])]
    stores[0].start()
    weight_grad(act, grads, whole, 0, halves, 256)
    back.relay()
    weight_grad(rows, pre_grad, whole, 1, halves, 256)
    pieces = land_whole
    for w in range(2):

        def take(here, value, w=w):
            pieces[w, 0, here] = value.astype(BF)

        halves.total(w, take, 64)
    stores.append(pltpu.make_async_copy(pieces.at[:, 0], o_pieces, store.at[0]))
    stores[1].start()
    norm_total = part_norm


    def take_norm(here, total):
        norm_total[t, here] = total.astype(BF)

    back.finish(take_norm, 64)
    stores.append(pltpu.make_async_copy(norm_total.at[t], o_norm, store.at[2]))
    stores[2].start()
    gather.drain()
    back.drain()
    for w in range(2):
        halves.drain(w)
    for copy in stores:
        copy.wait()


def feed(rows, grads, up, down, subs):
    n, m = rows.shape
    hidden = up.shape[1]
    count = 12 + 2 * (subs - 1)
    return pl.pallas_call(
        feed_kernel,
        name="feed",
        out_shape=[shape(4, n, m), shape(n, m), shape(2, m // subs, hidden)],
        in_specs=[ANY] * 4,
        out_specs=[ANY] * 3,
        scratch_shapes=[
            pltpu.VMEM((4, n, m), BF), pltpu.VMEM((4, n, m), BF), pltpu.VMEM((m, hidden), BF), pltpu.VMEM((hidden, m), BF),
            pltpu.VMEM((4, n, hidden), BF), pltpu.VMEM((4, n, hidden), BF),
            pltpu.VMEM((4, n, m), BF), pltpu.VMEM((4, n, m), BF),
            pltpu.VMEM((6, n // 2, m), BF), pltpu.VMEM((2, n // 2, m), BF),
            pltpu.VMEM((2, m, hidden), BF), pltpu.VMEM((2, subs - 1, m // subs, hidden), BF),
            dma(4), dma(3), dma(count), dma(count),
        ],
        compiler_params=params(4),
    )(rows, grads, up, down)


def norm_back_block(grad, source, gain):
    hat, inverse = normed_rows(source)
    scaled = grad * gain
    inner = scaled - jnp.mean(scaled, -1, keepdims=True) - hat * jnp.mean(scaled * hat, -1, keepdims=True)
    return inverse * inner, grad * hat


def fold(block):
    total = block[0:8]
    for i in range(1, block.shape[0] // 8):
        total = total + block[8 * i : 8 * i + 8]
    return total


def unstack(block):
    lanes = head_lanes(block.shape[0] // 2)
    return jnp.where(lanes < HEAD, block[: block.shape[0] // 2], block[block.shape[0] // 2 :])


def cross_back_kernel(
    layout,
    cot_in, norm_in, cross_in, self_in, gains_in, query_in, flat_in, memory_in, wq_in, wo_in, own_in,
    o_out, o_branch, o_sums, o_memory, o_wq, o_wo, o_down, o_land,
    cot, norm, after_cross, after_self, gains, query, flat, memory, wq, wo,
    branch, rows, query_grad, memory_grad, sums, whole_q, whole_o, land_q, land_o, piece_q, piece_o,
    norm_self, own, land, ring, result, ring_send, ring_recv, ring_store,
    load, store, send, recv,
):
    s = lax.axis_index("sub")
    subs = lax.axis_size("sub")
    loads = [
        pltpu.make_async_copy(a, b, load.at[i])
        for i, (a, b) in enumerate(
            (
                (cot_in, cot), (norm_in, norm), (cross_in, after_cross), (gains_in, gains), (wo_in, wo),
                (query_in, query), (flat_in, flat), (memory_in, memory), (self_in, after_self), (wq_in, wq),
                (own_in.at[pl.ds(0, layout.middle)], own),
            )
        )
    ]
    for copy in loads[10:] + loads[:10]:
        copy.start()
    greet([{"sub": (s + k) % subs} for k in range(1, subs)] + group_ring())
    pump = Pump(
        own, land, ring, result, ring_send, ring_recv, ring_store, 0, layout.middle, layout.count,
        sum_outputs(layout, (o_down,)),
    )
    n, m = cot.shape
    width = wq.shape[2]
    texts = memory.shape[1]
    loads[10].wait()
    pump.step(jnp.int32(0))
    for copy in loads[:4]:
        copy.wait()
    scale = HEAD ** (-0.5)

    def feed_block(i, carry):
        here = rows_at(i, 64)
        grad = norm[here].astype(F32)
        inner, terms = norm_back_block(grad, after_cross[here], gains[2:3])
        total = cot[here] + inner
        cot[here] = total
        branch[here] = total.astype(BF)
        return carry[0] + fold(terms), carry[1] + fold(grad)

    zero = jnp.zeros((8, m), F32)
    gain_sum, bias_sum = lax.fori_loop(0, n // 64, feed_block, (zero, zero))
    sums[0:8] = gain_sum
    sums[8:16] = bias_sum
    loads[8].wait()

    def norm_block(i, carry):
        here = rows_at(i, 64)
        hat, _ = normed_rows(after_self[here])
        rows[here] = (hat * gains[0:1] + gains[1:2]).astype(BF)
        return carry

    lax.fori_loop(0, n // 64, norm_block, 0)
    for copy in loads[4:8]:
        copy.wait()
    middle = layout.middle

    def tick(k):
        @pl.when(k < middle)
        def _():
            pump.step(k)

    tick(jnp.int32(1))

    def quarter(q, carry):
        tick(q + 2)
        grad_heads = dot_t(branch[...], wo[rows_at(q, width)]).astype(BF)
        whole_q_cols = cols(q, width)
        query_grad_block = []
        for p in range(width // 128):
            lane = slice(p * 128, p * 128 + 128)
            keys = stack_pair(memory[q, :, lane], texts)
            values = stack_pair(memory[q, :, width + p * 128 : width + p * 128 + 128], texts)
            here = pl.ds(pl.multiple_of(q * width + p * 128, 128), 128)
            grad = grad_heads[:, lane]
            ask = query[:, here]
            probs, left = pair_softmax(ask, keys)
            grad_probs = dot_t(grad, values)
            centred = pair_sum(grad_probs * probs, left)
            grad_scores = (probs * (grad_probs - centred)).astype(BF)
            query_grad[:, here] = (dot(grad_scores, keys) * scale).astype(BF)
            memory_grad[q, :, lane] = unstack(dot_c(grad_scores, ask) * scale).astype(BF)
            memory_grad[q, :, width + p * 128 : width + p * 128 + 128] = unstack(
                dot_c(probs.astype(BF), grad)
            ).astype(BF)
        return carry

    lax.fori_loop(0, 4, quarter, 0)
    stores = [pltpu.make_async_copy(memory_grad, o_memory, store.at[0])]
    stores[0].start()
    halves_q = Halves(whole_q, land_q, send, recv, 0)
    halves_o = Halves(whole_o, land_o, send, recv, 4 * (subs - 1))

    def weights(q, carry):
        @pl.when(q % 2 == 0)
        def _():
            tick(6 + q // 2)


        def grad_o(j, carry):
            whole_o[q, :, cols(j, 512)] = dot_c(flat[:, cols(q, width)], branch[:, cols(j, 512)]).astype(BF)
            return carry

        lax.fori_loop(0, m // 512, grad_o, 0)

        def grad_q(j, carry):
            whole_q[q, rows_at(j, 256)] = dot_c(rows[:, cols(j, 256)], query_grad[:, cols(q, width)]).astype(BF)
            return carry

        lax.fori_loop(0, m // 256, grad_q, 0)
        return carry

    lax.fori_loop(0, 4, weights, 0)
    for q in range(4):
        halves_q.start(q)
        halves_o.start(q)
    loads[9].wait()

    def norm_grad(j, carry):
        @pl.when(j % 3 == 0)
        def _():
            tick(8 + j // 3)

        here = rows_at(j, 256)
        total = jnp.zeros((n, 256), F32)
        for q in range(4):
            total = total + dot_t(query_grad[:, q * width : (q + 1) * width], wq[q, here])
        norm_self[:, cols(j, 256)] = total
        return carry

    lax.fori_loop(0, m // 256, norm_grad, 0)

    def self_block(i, carry):
        here = rows_at(i, 64)
        grad = norm_self[here]
        inner, terms = norm_back_block(grad, after_self[here], gains[0:1])
        total = cot[here] + inner
        cot[here] = total
        branch[here] = total.astype(BF)
        return carry[0] + fold(terms), carry[1] + fold(grad)

    gain_sum, bias_sum = lax.fori_loop(0, n // 64, self_block, (zero, zero))
    sums[16:24] = gain_sum
    sums[24:32] = bias_sum
    stores += [
        pltpu.make_async_copy(cot, o_out, store.at[1]),
        pltpu.make_async_copy(branch, o_branch, store.at[2]),
        pltpu.make_async_copy(sums, o_sums, store.at[3]),
    ]
    for copy in stores[1:]:
        copy.start()

    tick(jnp.int32(10))
    for halves, piece in ((halves_q, piece_q), (halves_o, piece_o)):
        for q in range(4):

            def take(here, value, q=q, piece=piece):
                piece[q, here] = value.astype(BF)

            halves.total(q, take, 16)
    stores += [pltpu.make_async_copy(piece_q, o_wq, store.at[4]), pltpu.make_async_copy(piece_o, o_wo, store.at[5])]
    for copy in stores[4:]:
        copy.start()
    tick(jnp.int32(11))
    pump.drain()
    stores.append(pltpu.make_async_copy(land, o_land, store.at[6]))
    stores[-1].start()
    for q in range(4):
        halves_q.drain(q)
        halves_o.drain(q)
    for copy in stores:
        copy.wait()


def cross_back(layout, cot, norm, after_cross, after_self, gains, query, flat, memory, wq, wo, own, subs):
    n, m = cot.shape
    width = wq.shape[2]
    count = 8 * (subs - 1)
    held = (2, layout.window, layout.chunk, m)
    part_q, part_o = (4, m // subs, width), (4, width // subs, m)
    return pl.pallas_call(
        partial(cross_back_kernel, layout),
        name="cross_back",
        out_shape=[
            shape(n, m, kind=F32), shape(n, m), shape(32, m, kind=F32), shape(*memory.shape), shape(*part_q), shape(*part_o),
            shape(layout.feed_count // 2, layout.chunk, m), shape(*held),
        ],
        in_specs=[ANY] * 11,
        out_specs=[ANY] * 8,
        scratch_shapes=[
            pltpu.VMEM((n, m), F32), pltpu.VMEM((n, m), BF), pltpu.VMEM((n, m), F32), pltpu.VMEM((n, m), F32),
            pltpu.VMEM(gains.shape, F32), pltpu.VMEM((n, m), BF), pltpu.VMEM((n, m), BF), pltpu.VMEM(memory.shape, BF),
            pltpu.VMEM(wq.shape, BF), pltpu.VMEM(wo.shape, BF),
            pltpu.VMEM((n, m), BF), pltpu.VMEM((n, m), BF), pltpu.VMEM((n, m), BF), pltpu.VMEM(memory.shape, BF),
            pltpu.VMEM((32, m), F32), pltpu.VMEM((4, m, width), BF), pltpu.VMEM((4, width, m), BF),
            pltpu.VMEM((4, subs - 1, m // subs, width), BF), pltpu.VMEM((4, subs - 1, width // subs, m), BF),
            pltpu.VMEM(part_q, BF), pltpu.VMEM(part_o, BF),
            pltpu.VMEM((n, m), F32),
            *pump_scratch(layout, layout.middle),
            dma(11), dma(7), dma(count), dma(count),
        ],
        compiler_params=params(5),
    )(cot, norm, after_cross, after_self, gains, query, flat, memory, wq, wo, own)


def attend_pair_back(p, triple, place, blocks, heads, grad_heads, deltas, sums, grads, grad_keys, grad_values):
    n = triple.shape[1]
    width = heads * HEAD
    scale = HEAD ** (-0.5)
    lanes = head_lanes(n)
    key_lanes = head_lanes(blocks * n)

    here = pl.ds(pl.multiple_of(p * 128, 128), 128)
    key_cols = pl.ds(pl.multiple_of(width + p * 128, 128), 128)
    value_cols = pl.ds(pl.multiple_of(2 * width + p * 128, 128), 128)
    query = triple[place, :, here]
    grad = grad_heads[place, :, here]
    keys = triple[0:blocks, :, key_cols].reshape(blocks * n, 128)
    values = triple[0:blocks, :, value_cols].reshape(blocks * n, 128)
    stats = sums[place]
    means = deltas[place]
    found = []
    for h in range(2):
        mine = (lanes < HEAD) if h == 0 else (lanes >= HEAD)
        log_sum = jnp.sum(jnp.where(lanes == 2 * p + h, stats, 0.0), -1, keepdims=True)
        delta = jnp.sum(jnp.where(lanes == 2 * p + h, means, 0.0), -1, keepdims=True)
        scores = dot_t(jnp.where(mine, query, jnp.zeros_like(query)), keys)
        row = lax.broadcasted_iota(jnp.int32, scores.shape, 0)
        col = lax.broadcasted_iota(jnp.int32, scores.shape, 1)
        probs = jnp.where(
            col <= row + (blocks - 1) * n, jnp.exp2(scores * (scale * LOG2E) - log_sum), 0.0
        )
        grad_probs = dot_t(jnp.where(mine, grad, jnp.zeros_like(grad)), values)
        grad_scores = (probs * (grad_probs - delta)).astype(BF)
        found.append((dot(grad_scores, keys), dot_c(grad_scores, query), dot_c(probs.astype(BF), grad)))
    grads[place, :, here] = (jnp.where(lanes < HEAD, found[0][0], found[1][0]) * scale).astype(BF)
    grad_keys[0 : blocks * n, here] += jnp.where(key_lanes < HEAD, found[0][1], found[1][1]) * scale
    grad_values[0 : blocks * n, here] += jnp.where(key_lanes < HEAD, found[0][2], found[1][2])


def attend_back_kernel(
    layout,
    branch_in, triple_in, flat_in, sums_in, out_in, qkv_in, rows_in, frames_in, gains_in, grad_in, memory_in, text_in, kv_in,
    own_in, land_in, down_in,
    o_frames, o_sums, o_text, o_qkv, o_more, o_down, o_up, o_kv, o_land,
    branch, triple, flat, sums, out, qkv, rows, frames, gains, grad_out, memory, text, kv,
    land_m, stage_m,
    grad_heads, deltas, grads, grad_keys, grad_values, part, land, stage, whole_qkv, land_qkv, whole_out, land_out,
    whole_kv, land_kv, text_grad, sums_out, sum_m, own, held, ring, result, ring_send, ring_recv, ring_store,
    load, store, send, recv,
):
    t, x, y, d = neighbours()
    s = lax.axis_index("sub")
    subs = lax.axis_size("sub")
    names = (
        (branch_in, branch.at[t]), (out_in, out), (flat_in, flat), (triple_in, triple), (sums_in, sums),
        (memory_in, memory), (own_in, own.at[pl.ds(0, layout.feed_count)]), (land_in, held),
        *((qkv_in.at[i], qkv.at[:, pl.ds(i * qkv_in.shape[2], qkv_in.shape[2])]) for i in range(3)), (rows_in, rows),
        (text_in, text), (kv_in, kv), (frames_in, frames), (gains_in, gains), (grad_in, grad_out),
    )
    loads = [pltpu.make_async_copy(a, b, load.at[i]) for i, (a, b) in enumerate(names)]
    loads[7].start()
    for copy in loads[:7] + loads[8:]:
        copy.start()
    loads[7].wait()
    greet([{"tensor": x}, {"tensor": y}] + [{"sub": (s + k) % subs} for k in range(1, subs)] + group_ring())
    first, last = layout.middle, layout.later
    pump = Pump(
        own, held, ring, result, ring_send, ring_recv, ring_store, first, last, layout.count,
        sum_outputs(layout, (o_down, o_up), o_kv),
    )

    def tick(k):
        @pl.when(k + first < last)
        def _():
            pump.step(k + first)

    n, m = grad_out.shape
    width = triple.shape[2]
    local = out.shape[0]
    heads = local // HEAD
    gather = Gather(branch.at[t], branch, send, recv, 0)
    scatter = Scatter(part, land, stage, send, recv, 6)
    scatter_m = Scatter(memory, land_m, stage_m, send, recv, 12)
    halves_qkv = Halves(whole_qkv, land_qkv, send, recv, 18)
    halves_out = Halves(whole_out, land_out, send, recv, 18 + subs - 1)
    halves_kv = Halves(whole_kv, land_kv, send, recv, 18 + 2 * (subs - 1))
    loads[0].wait()
    gather.start()
    for copy in loads[5:7]:
        copy.wait()
    scatter_m.diagonal()
    scatter_m.along_x()
    scatter_m.along_y()
    for copy in loads[1:5]:
        copy.wait()
    grad_keys[...] = jnp.zeros_like(grad_keys)
    grad_values[...] = jnp.zeros_like(grad_values)
    lanes = head_lanes(n)

    def turn(i, carry):
        far_y = i // 2
        far_x = i % 2
        place = (t // 2 + far_y - 2 * (t // 2) * far_y) * 2 + (t % 2 + far_x - 2 * (t % 2) * far_x)

        @pl.when(i == 1)
        def _():
            gather.relay_x()
            gather.relay_y()
            gather.have_x()

        @pl.when(i == 2)
        def _():
            gather.have_y()

        @pl.when(i == 3)
        def _():
            gather.have_d()

        grad_heads[place] = dot_t(branch[place], out[...]).astype(BF)

        def delta(p, stats):
            here = pl.ds(pl.multiple_of(p * 128, 128), 128)
            product = grad_heads[place, :, here].astype(F32) * flat[place, :, here].astype(F32)
            low = jnp.sum(jnp.where(lanes < HEAD, product, 0.0), -1, keepdims=True)
            high = jnp.sum(jnp.where(lanes < HEAD, 0.0, product), -1, keepdims=True)
            return jnp.where(lanes == 2 * p, low, jnp.where(lanes == 2 * p + 1, high, stats))

        deltas[place] = lax.fori_loop(0, heads // 2, delta, jnp.zeros((n, 128), F32))

        def pair(p, carry):
            tick(i * (heads // 2) + p)
            for blocks in range(1, 5):

                @pl.when(place == blocks - 1)
                def _(blocks=blocks):
                    attend_pair_back(
                        p, triple, blocks - 1, blocks, heads, grad_heads, deltas, sums, grads, grad_keys, grad_values
                    )

            return carry

        lax.fori_loop(0, heads // 2, pair, 0)
        return carry

    lax.fori_loop(0, 4, turn, 0)
    for copy in loads[8:14]:
        copy.wait()

    def finish_grads(i, carry):
        grads[i, :, local : 2 * local] = grad_keys[rows_at(i, n)].astype(BF)
        grads[i, :, 2 * local :] = grad_values[rows_at(i, n)].astype(BF)
        return carry

    lax.fori_loop(0, 4, finish_grads, 0)

    def back(i, carry):
        far_y = 1 - i // 2
        far_x = 1 - i % 2
        place = (t // 2 + far_y - 2 * (t // 2) * far_y) * 2 + (t % 2 + far_x - 2 * (t % 2) * far_x)

        def step(j, carry):
            part[place, :, cols(j, 512)] = dot_t(grads[place], qkv[rows_at(j, 512)]).astype(BF)
            return carry

        lax.fori_loop(0, m // 512, step, 0)
        tick(12 + i)

        @pl.when(i == 0)
        def _():
            scatter.diagonal()

        @pl.when(i == 1)
        def _():
            scatter.along_y()

        @pl.when(i == 2)
        def _():
            scatter.along_x()

        return carry

    lax.fori_loop(0, 4, back, 0)
    tick(16)
    scatter_m.relay()

    def take_m(here, total):
        sum_m[here] = total.astype(BF)

    scatter_m.finish(take_m, 16)
    text_grad[...] = dot_t(sum_m[...], kv[...])
    stores = [pltpu.make_async_copy(text_grad, o_text, store.at[0])]
    stores[0].start()

    def grad_kv(j, carry):
        whole_kv[0, rows_at(j, 384)] = dot_c(text[:, cols(j, 384)], sum_m[...]).astype(BF)
        return carry

    lax.fori_loop(0, m // 384, grad_kv, 0)
    halves_kv.start(0)
    tick(17)

    def grad_wout(j, carry):
        whole_out[0, :, cols(j, 512)] = dot_c(
            flat[...].reshape(4 * n, local), branch[:, :, cols(j, 512)].reshape(4 * n, 512)
        ).astype(BF)
        return carry

    lax.fori_loop(0, m // 512, grad_wout, 0)
    halves_out.start(0)
    tick(18)
    chunk, half = layout.chunk, 2 * layout.quarter

    def take_kv(here, total):
        c = here.start // chunk
        own[layout.kv + c % half, :, cols(c // half, 2 * local)] = total.astype(BF)

    halves_kv.total(0, take_kv, chunk)
    scatter.relay()
    tick(19)

    def grad_wqkv(j, carry):
        tick(20 + j)
        turned = rows[:, :, cols(j, 256)].reshape(4 * n, 256)

        def inner(i, carry):
            whole_qkv[0, rows_at(j, 256), cols(i, 384)] = dot_c(
                turned, grads[:, :, cols(i, 384)].reshape(4 * n, 384)
            ).astype(BF)
            return carry

        lax.fori_loop(0, width // 384, inner, 0)
        return carry

    lax.fori_loop(0, m // 256, grad_wqkv, 0)
    halves_qkv.start(0)
    tick(26)

    def take_out(here, total):
        own[layout.out + here.start // chunk] = total.astype(BF)

    halves_out.total(0, take_out, chunk)
    tick(27)

    def take(here, total):
        land_qkv[0, 0, here] = total.astype(BF)

    halves_qkv.total(0, take, 16)
    stores.append(pltpu.make_async_copy(land_qkv.at[0, 0], o_qkv, store.at[1]))
    stores.append(pltpu.make_async_copy(own.at[pl.ds(layout.kv, layout.qkv - layout.kv)], o_more, store.at[2]))
    for copy in stores[-2:]:
        copy.start()
    tick(28)
    for copy in loads[14:]:
        copy.wait()

    def take_norm(here, total):
        part[t, here] = total.astype(BF)

    scatter.finish(take_norm, 64)

    def frame_block(i, carry):
        here = rows_at(i, 64)
        grad = part[t, here].astype(F32)
        inner, terms = norm_back_block(grad, frames[here].astype(F32), gains[4:5])
        grad_out[here] = grad_out[here] + inner
        return carry[0] + fold(terms), carry[1] + fold(grad)

    zero = jnp.zeros((8, m), F32)
    gain_sum, bias_sum = lax.fori_loop(0, n // 64, frame_block, (zero, zero))
    tick(29)
    sums_out[0:8] = gain_sum
    sums_out[8:16] = bias_sum
    stores += [pltpu.make_async_copy(grad_out, o_frames, store.at[3]), pltpu.make_async_copy(sums_out, o_sums, store.at[4])]
    for copy in stores[-2:]:
        copy.start()
    pump.drain()
    stores.append(pltpu.make_async_copy(held, o_land, store.at[5]))
    stores[-1].start()
    gather.drain()
    for each in (scatter, scatter_m):
        each.drain()
    for each in (halves_qkv, halves_out, halves_kv):
        each.drain(0)
    for copy in stores:
        copy.wait()


def attend_back(
    layout, branch, triple, flat, sums, out, qkv, rows, frames, gains, grad, memory, text, kv, own, land, down, subs
):
    n, m = grad.shape
    width = triple.shape[2]
    local = out.shape[0]
    texts, kvw = text.shape[0], kv.shape[1]
    count = 18 + 3 * (subs - 1)
    v = pltpu.VMEM
    return pl.pallas_call(
        partial(attend_back_kernel, layout),
        name="attend_back",
        out_shape=[
            shape(n, m, kind=F32), shape(16, m, kind=F32), shape(texts, m, kind=F32), shape(m // subs, width),
            shape(layout.qkv - layout.kv, layout.chunk, m), shape(*down.shape), shape(*down.shape),
            shape(4 * layout.quarter, layout.chunk, kvw), shape(*land.shape),
        ],
        in_specs=[ANY] * 16,
        out_specs=[ANY] * 9,
        input_output_aliases={15: 5},
        scratch_shapes=[
            v((4, n, m), BF), v(triple.shape, BF), v(flat.shape, BF), v(sums.shape, F32), v(out.shape, BF), v((m, width), BF),
            v(rows.shape, BF), v(frames.shape, frames.dtype), v(gains.shape, F32), v((n, m), F32), v(memory.shape, BF),
            v(text.shape, BF), v(kv.shape, BF),
            v((6, texts // 2, kvw), BF), v((2, texts // 2, kvw), BF),
            v((4, n, local), BF), v((4, n, 128), F32), v((4, n, width), BF), v((4 * n, local), F32), v((4 * n, local), F32),
            v((4, n, m), BF), v((6, n // 2, m), BF), v((2, n // 2, m), BF),
            v((1, m, width), BF), v((1, subs - 1, m // subs, width), BF),
            v((1, local, m), BF), v((1, subs - 1, local // subs, m), BF),
            v((1, m, kvw), BF), v((1, subs - 1, m // subs, kvw), BF),
            v((texts, m), F32), v((16, m), F32), v((texts, kvw), BF),
            *pump_scratch(layout, layout.qkv),
            dma(17), dma(6), dma(count), dma(count),
        ],
        compiler_params=params(6),
    )(branch, triple, flat, sums, out, qkv, rows, frames, gains, grad, memory, text, kv, own, land, down)


def total_kernel(
    layout,
    feed_in, qkv_in, more_in, cross_q_in, cross_o_in, sums_a_in, sums_b_in, text_in, land_in, part_in, after_in,
    down_in, up_in, kv_in,
    o_qkv, o_cq, o_out, o_co, o_text, o_vectors, o_layer, o_down, o_up, o_kv,
    own, held, ring, result, ring_send, ring_recv, ring_store,
    cross_q, cross_o, land_q, land_o, stage_q, stage_o, part, land_p, stage_p, after,
    sums_a, sums_b, text, text_land, text_full, vectors, vectors_land, share, share_land, load, store, send, recv,
):
    t, x, y, d = neighbours()
    s, subs = lax.axis_index("sub"), lax.axis_size("sub")
    g, groups = lax.axis_index("group"), lax.axis_size("group")
    chunk, m, local = layout.chunk, layout.m, layout.local
    width, quarter = 3 * local, layout.quarter
    at_kv, at_out, at_qkv, at_cq, at_co = layout.kv, layout.out, layout.qkv, layout.cq, layout.co
    def outputs(c, block, slots, act):
        slot = c % RING

        def region(begin, end, copies):
            @pl.when(jnp.logical_and(c >= begin, c < end))
            def _():
                for i, (source, target) in enumerate(copies(c - begin)):
                    act(pltpu.make_async_copy(source, target, slots.at[slot, i]))

        def whole(output):
            return lambda r: [(block, output.at[r])]

        region(0, at_kv // 2, whole(o_down))
        region(at_kv // 2, at_kv, whole(o_up))
        region(
            at_qkv, at_cq,
            lambda r: [
                *((block.at[:, pl.ds(i * local, local)], o_qkv.at[i, r]) for i in range(3)),
                (block.at[:, pl.ds(width, local)], o_qkv.at[r // quarter, 3 * quarter + r % quarter]),
            ],
        )
        region(
            at_kv, at_out,
            lambda r: [
                (block.at[:, pl.ds(2 * i * local, 2 * local)], o_kv.at[2 * i * quarter + r]) for i in range(2)
            ],
        )
        region(at_out, at_qkv, whole(o_out))
        region(
            at_cq, at_co,
            lambda r: [(block.at[:, pl.ds(i * local, local)], o_cq.at[i * quarter + r]) for i in range(4)],
        )
        region(at_co, layout.count, whole(o_co))

    fresh = max(0, layout.later - LAG * (groups - 1))
    newer = max(fresh, at_kv)
    pairs = [
        (land_in, held),
        (more_in.at[pl.ds(newer - at_kv, at_qkv - newer)], own.at[pl.ds(newer, at_qkv - newer)]),
        (qkv_in.at[pl.ds(0, 3 * quarter)], own.at[pl.ds(at_qkv, 3 * quarter), :, pl.ds(0, width)]),
    ]
    for i in range(3):
        pairs.append(
            (
                qkv_in.at[pl.ds(3 * quarter, quarter), :, pl.ds(i * local, local)],
                own.at[pl.ds(at_qkv + i * quarter, quarter), :, pl.ds(width, local)],
            )
        )
    if fresh < at_kv:
        pairs.append((feed_in.at[pl.ds(fresh, at_kv - fresh)], own.at[pl.ds(fresh, at_kv - fresh)]))
    early = len(pairs)
    pairs += [
        (cross_q_in, cross_q), (cross_o_in, cross_o), (sums_a_in, sums_a), (sums_b_in, sums_b), (text_in, text),
        (part_in, part), (after_in, after),
    ]
    loads = [pltpu.make_async_copy(a, b, load.at[i]) for i, (a, b) in enumerate(pairs)]
    for copy in loads:
        copy.start()
    loads[0].wait()
    greet(
        [{"tensor": x}, {"tensor": y}, {"tensor": d}]
        + [{"sub": (s + k) % subs} for k in range(1, subs)]
        + [{"group": (g + k) % groups} for k in range(1, groups)]
    )
    begin, end = layout.later, layout.end
    pump = Pump(own, held, ring, result, ring_send, ring_recv, ring_store, begin, end, layout.count, outputs)

    def run(a, b):
        def step(k, carry):
            pump.step(k)
            return carry

        lax.fori_loop(a, b, step, 0)

    for copy in loads[1:early]:
        copy.wait()
    run(begin, begin + 1)
    for copy in loads[early:-2]:
        copy.wait()
    share_width = m // subs
    for i in range(6):
        source, at = (sums_a, i) if i < 4 else (sums_b, i - 4)
        row = jnp.sum(source[8 * at : 8 * at + 8], 0, keepdims=True)
        for j in range(subs):
            vectors[j, i : i + 1] = row[:, j * share_width : (j + 1) * share_width]
    strip = text.shape[0] // 4

    def remote(source, target, k, device):
        return pltpu.make_async_remote_copy(
            source, target, send.at[k], recv.at[k], device_id=device, device_id_type=MESH
        )

    square = (x, y, d)
    first = [remote(vectors, vectors_land.at[k], k, {"tensor": square[k]}) for k in range(3)]
    first += [
        remote(text.at[rows_at(square[k], strip)], text_land.at[k], 3 + k, {"tensor": square[k]}) for k in range(3)
    ]
    second = [
        remote(share.at[0, (s + k) % subs], share_land.at[k - 1], 5 + k, {"sub": (s + k) % subs}) for k in range(1, subs)
    ]
    base = 5 + subs
    second += [
        remote(text_full.at[rows_at(t, strip)], text_full.at[rows_at(t, strip)], base + k, {"tensor": square[k]}) for k in range(3)
    ]
    base += 3
    third = [
        remote(share.at[1, 0], share_land.at[subs - 2 + k], base + k - 1, {"group": (g + k) % groups})
        for k in range(1, groups)
    ]
    base += groups - 1
    scatter_q = Scatter(cross_q, land_q, stage_q, send, recv, base)
    scatter_o = Scatter(cross_o, land_o, stage_o, send, recv, base + 6)
    for copy in first:
        copy.start()
    scatter_p = Scatter(part, land_p, stage_p, send, recv, base + 12)
    for each in (scatter_q, scatter_o):
        each.diagonal()
        each.along_x()
        each.along_y()

    run(begin + 1, begin + 3)
    for copy in first:
        copy.wait_recv()
    for j in range(subs):
        share[0, j] = vectors[j] + vectors_land[0, j] + vectors_land[1, j] + vectors_land[2, j]
    text_full[rows_at(t, strip)] = text[rows_at(t, strip)] + text_land[0] + text_land[1] + text_land[2]
    for copy in first:
        copy.wait_send()
    for copy in second:
        copy.start()
    run(begin + 3, begin + 6)
    for copy in second:
        copy.wait_recv()
    total = share[0, s]
    for k in range(1, subs):
        total = total + share_land[k - 1]
    share[1, 0] = total
    text_store = pltpu.make_async_copy(text_full, o_text, store.at[0])
    text_store.start()
    for copy in third:
        copy.start()
    scatter_q.relay()
    scatter_o.relay()
    loads[-2].wait()
    loads[-1].wait()
    scatter_p.diagonal()
    scatter_p.along_x()
    scatter_p.along_y()
    run(begin + 6, at_cq)

    def take_q(rows, value):
        row = rows.start
        c = row // chunk
        own[at_cq + c % quarter, :, cols(c // quarter, local)] = value.astype(BF)

    scatter_q.finish(take_q, chunk)
    run(at_cq, at_co)
    step = min(chunk, scatter_o.half)

    def take_o(rows, value):
        own[at_co + rows.start // chunk, rows_at(rows.start % chunk // step, step)] = value.astype(BF)

    scatter_o.finish(take_o, step)
    run(at_co, layout.count)
    scatter_p.relay()
    run(layout.count, end)

    def take_layer(rows, value):
        after[rows] = after[rows] + value

    scatter_p.finish(take_layer, 64)
    layer_store = pltpu.make_async_copy(after, o_layer, store.at[2])
    layer_store.start()
    for copy in third:
        copy.wait_recv()
    total = share[1, 0]
    for k in range(1, groups):
        total = total + share_land[subs - 2 + k]
    share[2, 0] = total
    vector_store = pltpu.make_async_copy(share.at[2, 0], o_vectors, store.at[1])
    vector_store.start()
    for copy in second + third:
        copy.wait_send()
    for each in (scatter_q, scatter_o, scatter_p):
        each.drain()
    pump.drain()
    layer_store.wait()
    text_store.wait()
    vector_store.wait()


def total(layout, pieces, qkv, more, cross_q, cross_o, sums_a, sums_b, text, land, part, after, down, up, kv, subs, groups):
    m, chunk = layout.m, layout.chunk
    n = after.shape[0]
    v = pltpu.VMEM
    sems = 7 + subs + groups + 18
    qkv = qkv.reshape(-1, chunk, qkv.shape[1])
    piece_q, piece_o = cross_q.shape[1:], cross_o.shape[1:]
    out_shape = shape(layout.qkv - layout.out, chunk, m)
    return pl.pallas_call(
        partial(total_kernel, layout),
        name="total",
        out_shape=[
            shape(3, *qkv.shape[:2], layout.local), shape(layout.piece // chunk, chunk, layout.local), out_shape, out_shape,
            shape(*text.shape, kind=F32), shape(8, m // subs, kind=F32), shape(n, m, kind=F32),
            shape(*down.shape), shape(*up.shape), shape(*kv.shape),
        ],
        in_specs=[ANY] * 14,
        out_specs=[ANY] * 10,
        input_output_aliases={11: 7, 12: 8, 13: 9},
        scratch_shapes=[
            *pump_scratch(layout, layout.count),
            v(cross_q.shape, BF), v(cross_o.shape, BF),
            v((6, piece_q[0] // 2, piece_q[1]), BF), v((6, piece_o[0] // 2, piece_o[1]), BF),
            v((2, piece_q[0] // 2, piece_q[1]), BF), v((2, piece_o[0] // 2, piece_o[1]), BF),
            v((4, n, m), BF), v((6, n // 2, m), BF), v((2, n // 2, m), BF), v((n, m), F32),
            v(sums_a.shape, F32), v(sums_b.shape, F32), v(text.shape, F32),
            v((3, text.shape[0] // 4, m), F32), v(text.shape, F32), v((subs, 8, m // subs), F32), v((3, subs, 8, m // subs), F32),
            v((3, subs, 8, m // subs), F32), v((subs - 1 + groups - 1, 8, m // subs), F32),
            dma(14), dma(3), dma(sems), dma(sems),
        ],
        compiler_params=params(7),
    )(pieces, qkv, more, cross_q, cross_o, sums_a, sums_b, text, land, part, after, down, up, kv)


def local(
    frames, text_states, selfgain, selfbias, selfqkv, selfout, crossgain, crossbias, crossquery, crosskv, crossout,
    feedgain, feedbias, feedup, feeddown, cotangent,
):
    subs, groups = lax.axis_size("sub"), lax.axis_size("group")
    m = frames.shape[2]
    width = selfout.shape[0]
    qkv = selfqkv.transpose(1, 0, 2)
    kv = crosskv.reshape(m, 2 * width)
    gains = jnp.concatenate([crossgain, crossbias, feedgain, feedbias, selfgain, selfbias]).reshape(6, m)
    rows, triple, memory = enter(frames[0], gains, qkv, text_states[0], kv)
    flat, sums, after_self, wq, wo = attend(triple, selfout, frames[0], crossquery, crossout, subs)
    wo = wo.reshape(4 * width, m)
    query, cross_flat, after_cross, feed_rows, grads = cross(after_self, gains, wq, wo, memory, cotangent[0])
    layout = Layout(m, width, subs, groups)
    part, norm_grad, pieces = feed(feed_rows, grads, feedup, feeddown, subs)
    pieces = pieces.reshape(-1, layout.chunk, m)
    grad_out, branch, sums_a, memory_grad, piece_q, piece_o, down, land = cross_back(
        layout, cotangent[0], norm_grad, after_cross, after_self, gains, query, cross_flat, memory, wq, wo, pieces, subs
    )
    frame_grad, sums_b, text_part, grad_qkv, more, down, up, full_kv, land = attend_back(
        layout, branch, triple, flat, sums, selfout, qkv, rows, frames[0], gains, grad_out, memory_grad,
        text_states[0], kv, pieces, land, down, subs,
    )
    full_qkv, full_cq, full_out, full_co, text_grad, vectors, layer_output, down, up, full_kv = total(
        layout, pieces, grad_qkv, more, piece_q, piece_o, sums_a, sums_b, text_part, land, part, after_cross,
        down, up, full_kv, subs, groups,
    )
    return (
        layer_output[None],
        frame_grad[None],
        text_grad[None],
        vectors[4],
        vectors[5],
        full_qkv.astype(F32).reshape(3, -1, width).transpose(1, 0, 2),
        full_out.astype(F32).reshape(-1, m),
        vectors[2],
        vectors[3],
        full_cq.astype(F32).reshape(-1, width),
        full_kv.astype(F32).reshape(-1, 2, width),
        full_co.astype(F32).reshape(-1, m),
        vectors[0],
        vectors[1],
        up.astype(F32).reshape(-1, m),
        down.astype(F32).reshape(-1, m),
    )


def solution(mesh):
    clips = P(("sub", "group"), "tensor", None)
    whole = P(("sub", "group"), None, None)
    narrow, wide = P("tensor", None), P(None, "tensor")
    third = P(None, None, "tensor")
    vector = P("sub")
    return jax.shard_map(
        local,
        mesh=mesh,
        in_specs=(
            clips, whole, P(), P(), third, narrow, P(), P(), wide, third, narrow, P(), P(), wide, narrow, clips,
        ),
        out_specs=(
            clips, clips, whole, vector, vector, P("sub", None, "tensor"), P(("tensor", "sub"), None), vector, vector,
            P("sub", "tensor"), P("sub", None, "tensor"), P(("tensor", "sub"), None), vector, vector,
            P("sub", "tensor"), P(("tensor", "sub"), None),
        ),
        check_vma=False,
    )
```

```python
from functools import partial

import jax
import jax.numpy as jnp
from jax import lax
from jax.experimental import pallas as pl
from jax.experimental.pallas import tpu as pltpu
from jax.sharding import PartitionSpec as P

HEAD = 64
EPSILON = 1e-05
NEG_BIG = -1e30
LOG2E = 1.4426950408889634
MESH = pl.DeviceIdType.MESH
F32 = jnp.float32
BF = jnp.bfloat16
ANY = pl.BlockSpec(memory_space=pl.ANY)
VMEM_LIMIT = 63 << 20


def neighbours():
    t = lax.axis_index("tensor")
    return t, t + 1 - 2 * (t % 2), (t + 2) % 4, 3 - t


def greet(targets):
    barrier = pltpu.get_barrier_semaphore()
    for target in targets:
        pl.semaphore_signal(barrier, inc=1, device_id=target, device_id_type=MESH)
    pl.semaphore_wait(barrier, len(targets))


def dot(a, b):
    return lax.dot_general(a, b, (((1,), (0,)), ((), ())), preferred_element_type=F32)


def dot_t(a, b):
    return lax.dot_general(a, b, (((1,), (1,)), ((), ())), preferred_element_type=F32)


def dot_c(a, b):
    return lax.dot_general(a, b, (((0,), (0,)), ((), ())), preferred_element_type=F32)


def cols(j, width):
    return pl.ds(pl.multiple_of(j * width, width), width)


def rows_at(j, height):
    return pl.ds(pl.multiple_of(j * height, height), height)


def split(count):
    first = (count // 2 + 15) // 16 * 16
    return pl.ds(0, first), pl.ds(first, count - first)


class Gather:
    def __init__(self, own, dst, send, recv, base, halves=None):
        self.own, self.dst, self.send, self.recv, self.base = own, dst, send, recv, base
        self.halves = halves or split(own.shape[0])

    def copy(self, k):
        t, x, y, _ = neighbours()
        first, second = self.halves
        half = (first, second, second, first, first, second)[k]
        place = (t, t, t, t, x, y)[k]
        target = (x, y, x, y, y, x)[k]
        source = self.own.at[half] if k < 4 else self.dst.at[place, half]
        return pltpu.make_async_remote_copy(
            source,
            self.dst.at[place, half],
            self.send.at[self.base + k],
            self.recv.at[self.base + k],
            device_id={"tensor": target},
            device_id_type=MESH,
        )

    def start(self):
        for k in range(4):
            self.copy(k).start()

    def relay_x(self):
        self.copy(0).wait_recv()
        self.copy(4).start()

    def relay_y(self):
        self.copy(1).wait_recv()
        self.copy(5).start()

    def have_x(self):
        self.copy(2).wait_recv()

    def have_y(self):
        self.copy(3).wait_recv()

    def have_d(self):
        self.copy(4).wait_recv()
        self.copy(5).wait_recv()

    def drain(self):
        for k in range(6):
            self.copy(k).wait_send()


class Scatter:
    def __init__(self, part, land, stage, send, recv, base):
        self.part, self.land, self.stage = part, land, stage
        self.send, self.recv, self.base = send, recv, base
        self.half = part.shape[1] // 2

    def copy(self, k):
        t, x, y, d = neighbours()
        low, high = pl.ds(0, self.half), pl.ds(self.half, self.half)
        source = (
            self.part.at[d, low],
            self.part.at[d, high],
            self.part.at[x, low],
            self.stage.at[1],
            self.part.at[y, high],
            self.stage.at[0],
        )[k]
        target = (x, y, x, x, y, y)[k]
        return pltpu.make_async_remote_copy(
            source,
            self.land.at[k],
            self.send.at[self.base + k],
            self.recv.at[self.base + k],
            device_id={"tensor": target},
            device_id_type=MESH,
        )

    def diagonal(self):
        self.copy(0).start()
        self.copy(1).start()

    def along_x(self):
        self.copy(2).start()

    def along_y(self):
        self.copy(4).start()

    def relay(self):
        t, x, y, d = neighbours()
        low, high = pl.ds(0, self.half), pl.ds(self.half, self.half)
        self.copy(0).wait_recv()
        self.stage[0] = (self.part[y, low].astype(F32) + self.land[0].astype(F32)).astype(BF)
        self.copy(5).start()
        self.copy(1).wait_recv()
        self.stage[1] = (self.part[x, high].astype(F32) + self.land[1].astype(F32)).astype(BF)
        self.copy(3).start()

    def finish(self, take, step):
        t, x, y, d = neighbours()
        for k in (2, 4, 5, 3):
            self.copy(k).wait_recv()
        for base, a, b in ((0, 2, 5), (self.half, 4, 3)):

            def block(i, carry, base=base, a=a, b=b):
                here = rows_at(i, step)
                rows = pl.ds(pl.multiple_of(base + i * step, step), step)
                take(
                    rows,
                    self.part[t, rows].astype(F32)
                    + self.land[a, here].astype(F32)
                    + self.land[b, here].astype(F32),
                )
                return carry

            lax.fori_loop(0, self.half // step, block, 0)

    def drain(self):
        for k in range(6):
            self.copy(k).wait_send()


def normed_rows(values):
    centre = values - jnp.mean(values, -1, keepdims=True)
    inverse = lax.rsqrt(jnp.mean(centre * centre, -1, keepdims=True) + EPSILON)
    return centre * inverse, inverse


def params(cid, **more):
    return pltpu.CompilerParams(
        collective_id=cid, has_side_effects=True, vmem_limit_bytes=VMEM_LIMIT, **more
    )


def dma(count):
    return pltpu.SemaphoreType.DMA((count,))


def shape(*dims, kind=BF):
    return jax.ShapeDtypeStruct(dims, kind)


LAG = 2
RING = 4


def either(condition, other):
    return jnp.logical_and(condition, other)


class Pump:
    def __init__(self, own, land, ring, result, send, recv, store, first, last, count, outputs):
        self.own, self.land, self.ring, self.result = own, land, ring, result
        self.send, self.recv, self.store = send, recv, store
        self.first, self.last, self.count, self.outputs = first, last, count, outputs
        self.window = land.shape[1]
        self.g, self.n = lax.axis_index("group"), lax.axis_size("group")

    def copy(self, way, c):
        target = (self.g + 1) % self.n if way == 0 else (self.g + self.n - 1) % self.n
        return pltpu.make_async_remote_copy(
            self.ring.at[way, c % RING],
            self.land.at[way, c % self.window],
            self.send.at[way, c % RING],
            self.recv.at[way, c % self.window],
            device_id={"group": target},
            device_id_type=MESH,
        )

    def flow(self, way, k):
        place = self.g if way == 0 else self.n - 1 - self.g
        c = k - LAG * place

        @pl.when(either(c >= 0, c < self.count))
        def _():
            @pl.when(either(place > 0, k - LAG >= self.first))
            def _():
                self.copy(way, c).wait_recv()

            @pl.when(place < self.n - 1)
            def _():
                @pl.when(either(c >= RING, k - RING >= self.first))
                def _():
                    self.copy(way, c - RING).wait_send()

                @pl.when(place > 0)
                def _():
                    self.fill(self.ring.at[way, c % RING], (self.own.at[c], self.land.at[way, c % self.window]))

                @pl.when(place == 0)
                def _():
                    self.fill(self.ring.at[way, c % RING], (self.own.at[c],))

                self.copy(way, c).start()

    def fill(self, target, terms):
        def block(i, carry):
            here = rows_at(i, 48)
            value = terms[0][here].astype(F32)
            for term in terms[1:]:
                value = value + term[here].astype(F32)
            target[here] = value.astype(BF)
            return carry

        lax.fori_loop(0, target.shape[0] // 48, block, 0)

    def finished(self, k):
        far = jnp.maximum(self.g, self.n - 1 - self.g)
        return k - LAG * far

    def step(self, k):
        self.flow(0, k)
        self.flow(1, k)
        f = self.finished(k)

        @pl.when(either(f >= 0, f < self.count))
        def _():
            @pl.when(either(f >= RING, k - RING >= self.first))
            def _():
                self.outputs(f - RING, self.result.at[f % RING], self.store, lambda copy: copy.wait())

            slot, held = f % RING, f % self.window
            mine, target = self.own.at[f], self.result.at[slot]

            @pl.when(either(self.g > 0, self.g < self.n - 1))
            def _():
                self.fill(target, (mine, self.land.at[0, held], self.land.at[1, held]))

            @pl.when(self.g == 0)
            def _():
                self.fill(target, (mine, self.land.at[1, held]))

            @pl.when(self.g == self.n - 1)
            def _():
                self.fill(target, (mine, self.land.at[0, held]))

            self.outputs(f, self.result.at[slot], self.store, lambda copy: copy.start())

    def drain(self):
        for way in range(2):
            place = self.g if way == 0 else self.n - 1 - self.g
            top = jnp.minimum(self.last - LAG * place, self.count)
            for j in range(1, RING + 1):
                c = top - j

                @pl.when(either(place < self.n - 1, either(c >= 0, c + LAG * place >= self.first)))
                def _(way=way, c=c):
                    self.copy(way, c).wait_send()

            for k in range(max(self.first, self.last - LAG), self.last):
                c = k - LAG * (place - 1)

                @pl.when(either(place > 0, either(c >= 0, c < self.count)))
                def _(way=way, c=c):
                    self.copy(way, c).wait_recv()

        far = jnp.maximum(self.g, self.n - 1 - self.g)
        top = jnp.minimum(self.last - LAG * far, self.count)
        for j in range(1, RING + 1):
            f = top - j

            @pl.when(either(f >= 0, f + LAG * far >= self.first))
            def _(f=f):
                self.outputs(f, self.result.at[f % RING], self.store, lambda copy: copy.wait())


KV_TICKS, OUT_TICKS = 10, 14


class Layout:
    def __init__(self, m, local, subs, groups):
        piece = m // subs
        self.m, self.piece, self.local = m, piece, local
        self.out_rows = local // subs
        self.chunk = 96 if piece % 384 == 0 and self.out_rows % 96 == 0 else 48
        quarter = piece // 4 // self.chunk
        self.quarter = quarter
        self.feed_count = 2 * piece // self.chunk
        self.kv = self.feed_count
        self.out = self.kv + 2 * quarter
        self.qkv = self.out + self.out_rows // self.chunk
        self.cq = self.qkv + 3 * quarter
        self.co = self.cq + quarter
        self.count = self.co + self.out_rows // self.chunk
        self.window = LAG * groups
        self.end = self.count + LAG * (groups - 1)
        self.middle = min(6, self.feed_count // 2 - 2)
        self.later = self.feed_count
        if self.middle + KV_TICKS <= self.kv and self.middle + OUT_TICKS <= self.out:
            self.later = self.middle + OUT_TICKS + 2


def sum_outputs(layout, halves, text=None):
    def outputs(c, block, store, act):
        count = layout.feed_count // 2
        for i, half in enumerate(halves):

            @pl.when(either(c >= i * count, c < (i + 1) * count))
            def _(i=i, half=half):
                act(pltpu.make_async_copy(block, half.at[c - i * count], store.at[c % RING, 0]))

        if text is not None:

            @pl.when(either(c >= layout.kv, c < layout.out))
            def _():
                for i in range(2):
                    lanes = pl.ds(2 * i * layout.local, 2 * layout.local)
                    target = text.at[2 * i * layout.quarter + c - layout.kv]
                    act(pltpu.make_async_copy(block.at[:, lanes], target, store.at[c % RING, i]))

    return outputs


def pump_scratch(layout, count):
    chunk, m = layout.chunk, layout.m
    return [
        pltpu.VMEM((count, chunk, m), BF),
        pltpu.VMEM((2, layout.window, chunk, m), BF),
        pltpu.VMEM((2, RING, chunk, m), BF),
        pltpu.VMEM((RING, chunk, m), BF),
        pltpu.SemaphoreType.DMA((2, RING)),
        pltpu.SemaphoreType.DMA((2, layout.window)),
        pltpu.SemaphoreType.DMA((RING, 4)),
    ]


def group_ring():
    g, n = lax.axis_index("group"), lax.axis_size("group")
    return [{"group": (g + 1) % n}, {"group": (g + n - 1) % n}]


def enter_kernel(
    frames, gains, qkv, text, kv, o_rows, o_triple, o_memory,
    v_frames, v_gains, v_qkv, v_text, v_kv, rows, triple, memory, load, store, send, recv,
):
    t, x, y, d = neighbours()
    loads = [
        pltpu.make_async_copy(a, b, load.at[i])
        for i, (a, b) in enumerate(
            (
                (frames, v_frames), (gains, v_gains), (text, v_text), (kv, v_kv),
                *((qkv.at[i], v_qkv.at[:, pl.ds(i * qkv.shape[2], qkv.shape[2])]) for i in range(3)),
            )
        )
    ]
    for copy in loads:
        copy.start()
    greet([{"tensor": x}, {"tensor": y}])
    for copy in loads[:2]:
        copy.wait()
    count, width = v_qkv.shape
    block = 384

    def norm_block(i, carry):
        here = rows_at(i, 64)
        hat, _ = normed_rows(v_frames[here].astype(F32))
        rows[t, here] = (hat * v_gains[4:5] + v_gains[5:6]).astype(BF)
        return carry

    lax.fori_loop(0, v_frames.shape[0] // 64, norm_block, 0)
    gather = Gather(rows.at[t], rows, send, recv, 0)
    gather.start()
    texts = Gather(memory.at[t], memory, send, recv, 6)

    def project(place):
        def step(j, carry):
            triple[place, :, cols(j, block)] = dot(rows[place], v_qkv[:, cols(j, block)]).astype(BF)
            return carry

        lax.fori_loop(0, width // block, step, 0)

    def put(k, place):
        a = pltpu.make_async_copy(rows.at[place], o_rows.at[place], store.at[2 * k])
        b = pltpu.make_async_copy(triple.at[place], o_triple.at[place], store.at[2 * k + 1])
        a.start()
        b.start()
        return [a, b]

    loads[2].wait()
    loads[3].wait()

    def texts_step(j, carry):
        memory[t, :, cols(j, block)] = dot(v_text[...], v_kv[:, cols(j, block)]).astype(BF)
        return carry

    lax.fori_loop(0, v_kv.shape[1] // block, texts_step, 0)
    texts.start()
    for copy in loads[4:]:
        copy.wait()
    project(t)
    stores = put(0, t)
    gather.relay_x()
    gather.relay_y()
    gather.have_x()
    project(x)
    stores += put(1, x)
    gather.have_y()
    project(y)
    stores += put(2, y)
    texts.relay_x()
    texts.relay_y()
    texts.have_x()
    texts.have_y()
    gather.have_d()
    project(d)
    stores += put(3, d)
    texts.have_d()
    last = pltpu.make_async_copy(memory, o_memory, store.at[8])
    last.start()
    gather.drain()
    texts.drain()
    for copy in stores:
        copy.wait()
    last.wait()


def enter(frames, gains, qkv, text, kv):
    n, m = frames.shape
    width, texts, kvw = 3 * qkv.shape[2], text.shape[0], kv.shape[1]
    return pl.pallas_call(
        enter_kernel,
        name="enter",
        out_shape=[shape(4, n, m), shape(4, n, width), shape(4, texts, kvw)],
        in_specs=[ANY] * 5,
        out_specs=[ANY] * 3,
        scratch_shapes=[
            pltpu.VMEM((n, m), frames.dtype), pltpu.VMEM(gains.shape, F32),
            pltpu.VMEM((m, width), BF), pltpu.VMEM(text.shape, BF), pltpu.VMEM(kv.shape, BF),
            pltpu.VMEM((4, n, m), BF), pltpu.VMEM((4, n, width), BF), pltpu.VMEM((4, texts, kvw), BF),
            dma(7), dma(9), dma(12), dma(12),
        ],
        compiler_params=params(1),
    )(frames, gains, qkv, text, kv)


def head_lanes(rows):
    return lax.broadcasted_iota(jnp.int32, (rows, 128), 1)


def attend_rows(triple, place, blocks, heads, flat, sums):
    n = triple.shape[1]
    width = heads * HEAD
    scale = HEAD ** (-0.5) * LOG2E
    lanes = head_lanes(n)

    def pair(p, stats):
        here = pl.ds(pl.multiple_of(p * 128, 128), 128)
        key_cols = pl.ds(pl.multiple_of(width + p * 128, 128), 128)
        value_cols = pl.ds(pl.multiple_of(2 * width + p * 128, 128), 128)
        query = triple[place, :, here]
        keys = triple[0:blocks, :, key_cols].reshape(blocks * n, 128)
        values = triple[0:blocks, :, value_cols].reshape(blocks * n, 128)
        outs = []
        for h in range(2):
            mine = (lanes < HEAD) if h == 0 else (lanes >= HEAD)
            scores = dot_t(jnp.where(mine, query, jnp.zeros_like(query)), keys)
            row = lax.broadcasted_iota(jnp.int32, scores.shape, 0)
            col = lax.broadcasted_iota(jnp.int32, scores.shape, 1)
            scores = jnp.where(col <= row + (blocks - 1) * n, scores, NEG_BIG)
            peak = jnp.max(scores, -1, keepdims=True) * scale
            exponent = jnp.exp2(scores * scale - peak)
            total = jnp.sum(exponent, -1, keepdims=True)
            outs.append(dot(exponent.astype(BF), values) / total)
            stats = jnp.where(lanes == 2 * p + h, peak + jnp.log2(total), stats)
        flat[place, :, here] = jnp.where(lanes < HEAD, outs[0], outs[1]).astype(BF)
        return stats

    sums[place] = lax.fori_loop(0, heads // 2, pair, jnp.zeros((n, 128), F32))


def attend_kernel(
    triple_in, out_in, frames_in, wq, wo, o_flat, o_sums, o_after, o_wq, o_wo,
    triple, v_out, v_frames, flat, sums, after, part, land, stage, v_wq, v_wo, load, store, send, recv, side,
):
    t, x, y, d = neighbours()
    s = lax.axis_index("sub")
    subs = lax.axis_size("sub")
    n = triple.shape[1]
    m = v_out.shape[1]
    heads = v_out.shape[0] // HEAD
    loads = [
        pltpu.make_async_copy(a, b, load.at[i])
        for i, (a, b) in enumerate(
            ((triple_in, triple), (out_in, v_out), (frames_in, v_frames), (wq, v_wq), (wo, v_wo))
        )
    ]
    for copy in loads:
        copy.start()
    greet(
        [{"tensor": x}, {"tensor": y}]
        + [{"sub": (s + k) % subs} for k in range(1, subs)]
    )
    scatter = Scatter(part, land, stage, send, recv, 0)
    gathers = []
    for i, (weight, full) in enumerate(((wq, o_wq), (wo, o_wo))):
        piece = weight.shape[0] // subs
        first, second = split(piece)
        offset = pl.multiple_of(s * piece, piece)
        halves = (
            pl.ds(offset, first.size),
            pl.ds(pl.multiple_of(offset + first.size, 16), second.size),
        )
        gathers.append((Gather(weight, full, send, recv, 6 + 6 * i, halves), full, pl.ds(offset, piece)))

    def shared(i, j, k):
        _, full, piece = gathers[i]
        place = (x, y, d)[j]
        slot = (i * 3 + j) * (subs - 1) + k - 1
        return pltpu.make_async_remote_copy(
            full.at[place, piece], full.at[place, piece],
            send.at[18 + slot], recv.at[18 + slot],
            device_id={"sub": (s + k) % subs}, device_id_type=MESH,
        )

    for gather, _, _ in gathers:
        gather.start()
    for copy in loads[:2]:
        copy.wait()

    def one(i, carry):
        far_y = 1 - i // 2
        far_x = 1 - i % 2
        place = (t // 2 + far_y - 2 * (t // 2) * far_y) * 2 + (t % 2 + far_x - 2 * (t % 2) * far_x)
        for blocks in range(1, 5):

            @pl.when(place == blocks - 1)
            def _(blocks=blocks):
                attend_rows(triple, blocks - 1, blocks, heads, flat, sums)

        def out_step(j, carry):
            part[place, :, cols(j, 512)] = dot(flat[place], v_out[:, cols(j, 512)]).astype(BF)
            return carry

        lax.fori_loop(0, m // 512, out_step, 0)

        @pl.when(i == 0)
        def _():
            scatter.diagonal()

        @pl.when(i == 1)
        def _():
            scatter.along_y()

        @pl.when(i == 2)
        def _():
            scatter.along_x()

        return carry

    lax.fori_loop(0, 4, one, 0)
    for gather, _, _ in gathers:
        gather.relay_x()
        gather.relay_y()
    stores = [
        pltpu.make_async_copy(flat, o_flat, store.at[0]),
        pltpu.make_async_copy(sums, o_sums, store.at[1]),
    ]
    loads[3].wait()
    loads[4].wait()
    stores += [
        pltpu.make_async_copy(v_wq, o_wq.at[t], store.at[2]),
        pltpu.make_async_copy(v_wo, o_wo.at[t], store.at[3]),
    ]
    for copy in stores:
        copy.start()
    scatter.relay()
    for i, (gather, _, _) in enumerate(gathers):
        gather.have_x()
        gather.have_y()
        gather.have_d()
        for j in range(3):
            for k in range(1, subs):
                shared(i, j, k).start()
    loads[2].wait()

    def take(rows, total):
        after[rows] = v_frames[rows].astype(F32) + total

    scatter.finish(take, 64)
    last = pltpu.make_async_copy(after, o_after, store.at[4])
    last.start()
    scatter.drain()
    for i, (gather, _, _) in enumerate(gathers):
        gather.drain()
        for j in range(3):
            for k in range(1, subs):
                shared(i, j, k).wait()
    for copy in stores:
        copy.wait()
    last.wait()


def attend(triple, out, frames, wq, wo, subs):
    _, n, width = triple.shape
    local, m = out.shape
    extra = 18 + 6 * (subs - 1)
    return pl.pallas_call(
        attend_kernel,
        name="attend",
        out_shape=[
            shape(4, n, local), shape(4, n, 128, kind=F32), shape(n, m, kind=F32),
            shape(4, *wq.shape), shape(4, *wo.shape),
        ],
        in_specs=[ANY] * 5,
        out_specs=[ANY] * 5,
        scratch_shapes=[
            pltpu.VMEM((4, n, width), BF), pltpu.VMEM((local, m), BF), pltpu.VMEM((n, m), frames.dtype),
            pltpu.VMEM((4, n, local), BF), pltpu.VMEM((4, n, 128), F32), pltpu.VMEM((n, m), F32),
            pltpu.VMEM((4, n, m), BF), pltpu.VMEM((6, n // 2, m), BF), pltpu.VMEM((2, n // 2, m), BF),
            pltpu.VMEM(wq.shape, BF), pltpu.VMEM(wo.shape, BF),
            dma(5), dma(5), dma(extra), dma(extra), dma(1),
        ],
        compiler_params=params(2),
    )(triple, out, frames, wq, wo)


def stack_pair(block, rows):
    lanes = head_lanes(rows)
    zero = jnp.zeros_like(block)
    return jnp.concatenate([jnp.where(lanes < HEAD, block, zero), jnp.where(lanes >= HEAD, block, zero)], 0)


def pair_softmax(query, keys):
    scale = HEAD ** (-0.5) * LOG2E
    scores = dot_t(query, keys)
    left = head_lanes(scores.shape[0]) < HEAD
    low = jnp.max(jnp.where(left, scores, -jnp.inf), -1, keepdims=True)
    high = jnp.max(jnp.where(left, -jnp.inf, scores), -1, keepdims=True)
    exponent = jnp.exp2((scores - jnp.where(left, low, high)) * scale)
    total = pair_sum(exponent, left)
    return exponent / total, left


def pair_sum(values, left):
    low = jnp.sum(jnp.where(left, values, 0.0), -1, keepdims=True)
    high = jnp.sum(jnp.where(left, 0.0, values), -1, keepdims=True)
    return jnp.where(left, low, high)


def cross_kernel(
    after_in, gains_in, wq_in, wo_in, memory_in, cot_in,
    o_query, o_flat, o_after, o_rows, o_grads,
    after, gains, wq, wo, memory, cot, rows, query, flat, result, feed, grads, load, store, send, recv,
):
    t, x, y, d = neighbours()
    loads = [
        pltpu.make_async_copy(a, b, load.at[i])
        for i, (a, b) in enumerate(
            ((cot_in, cot), (after_in, after), (gains_in, gains), (wq_in, wq), (memory_in, memory), (wo_in, wo))
        )
    ]
    for copy in loads:
        copy.start()
    greet([{"tensor": x}, {"tensor": y}])
    n, m = after.shape
    width = wq.shape[2]
    texts = memory.shape[1]
    loads[0].wait()

    def round_block(i, carry):
        here = rows_at(i, 64)
        grads[t, here] = cot[here].astype(BF)
        return carry

    lax.fori_loop(0, n // 64, round_block, 0)
    gather = Gather(grads.at[t], grads, send, recv, 0)
    gather.start()
    loads[1].wait()
    loads[2].wait()

    def norm_block(i, carry):
        here = rows_at(i, 64)
        hat, _ = normed_rows(after[here])
        rows[here] = (hat * gains[0:1] + gains[1:2]).astype(BF)
        return carry

    lax.fori_loop(0, n // 64, norm_block, 0)
    loads[3].wait()
    loads[4].wait()

    def quarter(q, carry):
        query[:, cols(q, width)] = dot(rows[...], wq[q]).astype(BF)

        def pair(p, carry):
            keys = stack_pair(memory[q, :, cols(p, 128)], texts)
            values = stack_pair(memory[q, :, pl.ds(pl.multiple_of(width + p * 128, 128), 128)], texts)
            here = pl.ds(pl.multiple_of(q * width + p * 128, 128), 128)
            probs, _ = pair_softmax(query[:, here], keys)
            flat[:, here] = dot(probs.astype(BF), values).astype(BF)
            return carry

        lax.fori_loop(0, width // 128, pair, 0)
        return carry

    lax.fori_loop(0, 4, quarter, 0)
    gather.relay_x()
    gather.relay_y()
    stores = [pltpu.make_async_copy(query, o_query, store.at[0]), pltpu.make_async_copy(flat, o_flat, store.at[1])]
    loads[5].wait()

    def out_step(j, carry):
        result[:, cols(j, 512)] = after[:, cols(j, 512)] + dot(flat[...], wo[:, cols(j, 512)])
        return carry

    lax.fori_loop(0, m // 512, out_step, 0)

    def feed_block(i, carry):
        here = rows_at(i, 64)
        hat, _ = normed_rows(result[here])
        feed[here] = (hat * gains[2:3] + gains[3:4]).astype(BF)
        return carry

    lax.fori_loop(0, n // 64, feed_block, 0)
    stores += [pltpu.make_async_copy(result, o_after, store.at[2]), pltpu.make_async_copy(feed, o_rows, store.at[3])]
    for copy in stores:
        copy.start()
    gather.have_x()
    gather.have_y()
    gather.have_d()
    last = pltpu.make_async_copy(grads, o_grads, store.at[4])
    last.start()
    gather.drain()
    for copy in stores:
        copy.wait()
    last.wait()


def cross(after, gains, wq, wo, memory, cot):
    n, m = after.shape
    return pl.pallas_call(
        cross_kernel,
        name="cross",
        out_shape=[shape(n, m), shape(n, m), shape(n, m, kind=F32), shape(n, m), shape(4, n, m)],
        in_specs=[ANY] * 6,
        out_specs=[ANY] * 5,
        scratch_shapes=[
            pltpu.VMEM((n, m), F32), pltpu.VMEM(gains.shape, F32), pltpu.VMEM(wq.shape, BF), pltpu.VMEM(wo.shape, BF),
            pltpu.VMEM(memory.shape, BF), pltpu.VMEM((n, m), F32), pltpu.VMEM((n, m), BF), pltpu.VMEM((n, m), BF),
            pltpu.VMEM((n, m), BF), pltpu.VMEM((n, m), F32), pltpu.VMEM((n, m), BF), pltpu.VMEM((4, n, m), BF),
            dma(6), dma(5), dma(6), dma(6),
        ],
        compiler_params=params(3),
    )(after, gains, wq, wo, memory, cot)


def gelu_both(pre):
    size = jnp.abs(pre) * 0.7071067811865476
    rate = 1.0 / (1.0 + 0.3275911 * size)
    bell = jnp.exp2(pre * pre * (-0.5 * LOG2E))
    series = rate * (
        0.254829592
        + rate * (-0.284496736 + rate * (1.421413741 + rate * (-1.453152027 + rate * 1.061405429)))
    )
    tail = 0.5 * series * bell
    gate = jnp.where(pre >= 0, 1.0 - tail, tail)
    return pre * gate, gate + pre * (0.3989422804014327 * bell)


class Halves:
    def __init__(self, whole, land, send, recv, base):
        self.whole, self.land, self.send, self.recv, self.base = whole, land, send, recv, base
        self.subs = lax.axis_size("sub")
        self.piece = whole.shape[1] // self.subs

    def copies(self, w):
        s = lax.axis_index("sub")
        made = []
        for k in range(1, self.subs):
            target = (s + k) % self.subs
            slot = w * (self.subs - 1) + k - 1
            made.append(
                pltpu.make_async_remote_copy(
                    self.whole.at[w, rows_at(target, self.piece)],
                    self.land.at[w, k - 1],
                    self.send.at[self.base + slot],
                    self.recv.at[self.base + slot],
                    device_id={"sub": target},
                    device_id_type=MESH,
                )
            )
        return made

    def start(self, w):
        for copy in self.copies(w):
            copy.start()

    def total(self, w, take, step):
        s = lax.axis_index("sub")
        for copy in self.copies(w):
            copy.wait_recv()

        def block(i, carry):
            here = rows_at(i, step)
            value = self.whole[w, pl.ds(pl.multiple_of(s * self.piece + i * step, step), step)].astype(F32)
            for k in range(1, self.subs):
                value = value + self.land[w, k - 1, here].astype(F32)
            take(here, value)
            return carry

        lax.fori_loop(0, self.piece // step, block, 0)

    def drain(self, w):
        for copy in self.copies(w):
            copy.wait_send()


def weight_grad(left, right, whole, w, halves, block):
    s = lax.axis_index("sub")
    subs = lax.axis_size("sub")
    total_rows = left.shape[0] * left.shape[1]
    count = whole.shape[1] // block
    begin = ((s + 1) % subs) * halves.piece // block

    def one(j, carry):
        b = (begin + j) % count
        turned = left[:, :, cols(b, block)].reshape(total_rows, block)

        def inner(i, carry):
            other = right[:, :, cols(i, 512)].reshape(total_rows, 512)
            whole[w, rows_at(b, block), cols(i, 512)] = dot_c(turned, other).astype(BF)
            return carry

        lax.fori_loop(0, whole.shape[2] // 512, inner, 0)
        return carry

    if subs == 2:
        lax.fori_loop(0, count // 2, one, 0)
        halves.start(w)
        lax.fori_loop(count // 2, count, one, 0)
    else:
        lax.fori_loop(0, count, one, 0)
        halves.start(w)


def feed_kernel(
    rows_in, grads_in, up_in, down_in, o_part, o_norm, o_pieces,
    rows, grads, up, down, act, pre_grad, part_out, part_norm, land_norm, stage_norm,
    whole, land_whole, load, store, send, recv,
):
    t, x, y, d = neighbours()
    s = lax.axis_index("sub")
    subs = lax.axis_size("sub")
    loads = [
        pltpu.make_async_copy(a, b, load.at[i])
        for i, (a, b) in enumerate(
            ((rows_in, rows.at[t]), (up_in, up), (grads_in, grads), (down_in, down))
        )
    ]
    for copy in loads:
        copy.start()
    greet([{"tensor": x}, {"tensor": y}] + [{"sub": (s + k) % subs} for k in range(1, subs)])
    _, n, m = rows.shape
    hidden = up.shape[1]
    loads[0].wait()
    gather = Gather(rows.at[t], rows, send, recv, 0)
    gather.start()
    back = Scatter(part_norm, land_norm, stage_norm, send, recv, 6)
    halves = Halves(whole, land_whole, send, recv, 12)
    for copy in loads[1:4]:
        copy.wait()

    def work(place):
        def step(j, carry):
            here = cols(j, 256)
            value, slope = gelu_both(dot(rows[place], up[:, here]))
            act[place, :, here] = value.astype(BF)
            pre_grad[place, :, here] = (dot_t(grads[place], down[here]) * slope).astype(BF)
            return carry

        lax.fori_loop(0, hidden // 256, step, 0)

        def out_step(j, carry):
            part_norm[place, :, cols(j, 512)] = dot_t(pre_grad[place], up[rows_at(j, 512)]).astype(BF)
            part_out[place, :, cols(j, 512)] = dot(act[place], down[:, cols(j, 512)]).astype(BF)
            return carry

        lax.fori_loop(0, m // 512, out_step, 0)

    def turn(i, carry):
        far_y = i // 2
        far_x = i % 2
        place = (t // 2 + far_y - 2 * (t // 2) * far_y) * 2 + (t % 2 + far_x - 2 * (t % 2) * far_x)

        @pl.when(i == 1)
        def _():
            gather.relay_x()
            gather.relay_y()
            gather.have_x()

        @pl.when(i == 2)
        def _():
            gather.have_y()

        @pl.when(i == 3)
        def _():
            gather.have_d()

        work(place)

        @pl.when(i == 1)
        def _():
            back.along_x()

        @pl.when(i == 2)
        def _():
            back.along_y()

        @pl.when(i == 3)
        def _():
            back.diagonal()

        return carry

    lax.fori_loop(0, 4, turn, 0)
    stores = [pltpu.make_async_copy(part_out, o_part, store.at[1])]
    stores[0].start()
    weight_grad(act, grads, whole, 0, halves, 256)
    back.relay()
    weight_grad(rows, pre_grad, whole, 1, halves, 256)
    pieces = land_whole
    for w in range(2):

        def take(here, value, w=w):
            pieces[w, 0, here] = value.astype(BF)

        halves.total(w, take, 64)
    stores.append(pltpu.make_async_copy(pieces.at[:, 0], o_pieces, store.at[0]))
    stores[1].start()
    norm_total = part_norm


    def take_norm(here, total):
        norm_total[t, here] = total.astype(BF)

    back.finish(take_norm, 64)
    stores.append(pltpu.make_async_copy(norm_total.at[t], o_norm, store.at[2]))
    stores[2].start()
    gather.drain()
    back.drain()
    for w in range(2):
        halves.drain(w)
    for copy in stores:
        copy.wait()


def feed(rows, grads, up, down, subs):
    n, m = rows.shape
    hidden = up.shape[1]
    count = 12 + 2 * (subs - 1)
    return pl.pallas_call(
        feed_kernel,
        name="feed",
        out_shape=[shape(4, n, m), shape(n, m), shape(2, m // subs, hidden)],
        in_specs=[ANY] * 4,
        out_specs=[ANY] * 3,
        scratch_shapes=[
            pltpu.VMEM((4, n, m), BF), pltpu.VMEM((4, n, m), BF), pltpu.VMEM((m, hidden), BF), pltpu.VMEM((hidden, m), BF),
            pltpu.VMEM((4, n, hidden), BF), pltpu.VMEM((4, n, hidden), BF),
            pltpu.VMEM((4, n, m), BF), pltpu.VMEM((4, n, m), BF),
            pltpu.VMEM((6, n // 2, m), BF), pltpu.VMEM((2, n // 2, m), BF),
            pltpu.VMEM((2, m, hidden), BF), pltpu.VMEM((2, subs - 1, m // subs, hidden), BF),
            dma(4), dma(3), dma(count), dma(count),
        ],
        compiler_params=params(4),
    )(rows, grads, up, down)


def norm_back_block(grad, source, gain):
    hat, inverse = normed_rows(source)
    scaled = grad * gain
    inner = scaled - jnp.mean(scaled, -1, keepdims=True) - hat * jnp.mean(scaled * hat, -1, keepdims=True)
    return inverse * inner, grad * hat


def fold(block):
    total = block[0:8]
    for i in range(1, block.shape[0] // 8):
        total = total + block[8 * i : 8 * i + 8]
    return total


def unstack(block):
    lanes = head_lanes(block.shape[0] // 2)
    return jnp.where(lanes < HEAD, block[: block.shape[0] // 2], block[block.shape[0] // 2 :])


def cross_back_kernel(
    layout,
    cot_in, norm_in, cross_in, self_in, gains_in, query_in, flat_in, memory_in, wq_in, wo_in, own_in,
    o_out, o_branch, o_sums, o_memory, o_wq, o_wo, o_down, o_land,
    cot, norm, after_cross, after_self, gains, query, flat, memory, wq, wo,
    branch, rows, query_grad, memory_grad, sums, whole_q, whole_o, land_q, land_o, piece_q, piece_o,
    norm_self, own, land, ring, result, ring_send, ring_recv, ring_store,
    load, store, send, recv,
):
    s = lax.axis_index("sub")
    subs = lax.axis_size("sub")
    loads = [
        pltpu.make_async_copy(a, b, load.at[i])
        for i, (a, b) in enumerate(
            (
                (cot_in, cot), (norm_in, norm), (cross_in, after_cross), (gains_in, gains), (wo_in, wo),
                (query_in, query), (flat_in, flat), (memory_in, memory), (self_in, after_self), (wq_in, wq),
                (own_in.at[pl.ds(0, layout.middle)], own),
            )
        )
    ]
    for copy in loads[10:] + loads[:10]:
        copy.start()
    greet([{"sub": (s + k) % subs} for k in range(1, subs)] + group_ring())
    pump = Pump(
        own, land, ring, result, ring_send, ring_recv, ring_store, 0, layout.middle, layout.count,
        sum_outputs(layout, (o_down,)),
    )
    n, m = cot.shape
    width = wq.shape[2]
    texts = memory.shape[1]
    loads[10].wait()
    pump.step(jnp.int32(0))
    for copy in loads[:4]:
        copy.wait()
    scale = HEAD ** (-0.5)

    def feed_block(i, carry):
        here = rows_at(i, 64)
        grad = norm[here].astype(F32)
        inner, terms = norm_back_block(grad, after_cross[here], gains[2:3])
        total = cot[here] + inner
        cot[here] = total
        branch[here] = total.astype(BF)
        return carry[0] + fold(terms), carry[1] + fold(grad)

    zero = jnp.zeros((8, m), F32)
    gain_sum, bias_sum = lax.fori_loop(0, n // 64, feed_block, (zero, zero))
    sums[0:8] = gain_sum
    sums[8:16] = bias_sum
    loads[8].wait()

    def norm_block(i, carry):
        here = rows_at(i, 64)
        hat, _ = normed_rows(after_self[here])
        rows[here] = (hat * gains[0:1] + gains[1:2]).astype(BF)
        return carry

    lax.fori_loop(0, n // 64, norm_block, 0)
    for copy in loads[4:8]:
        copy.wait()
    middle = layout.middle

    def tick(k):
        @pl.when(k < middle)
        def _():
            pump.step(jnp.int32(k))

    tick(jnp.int32(1))

    def quarter(q, carry):
        @pl.when(q % 2 == 1)
        def _():
            tick(2 + q // 2)

        grad_heads = dot_t(branch[...], wo[rows_at(q, width)]).astype(BF)
        whole_q_cols = cols(q, width)
        query_grad_block = []
        for p in range(width // 128):
            lane = slice(p * 128, p * 128 + 128)
            keys = stack_pair(memory[q, :, lane], texts)
            values = stack_pair(memory[q, :, width + p * 128 : width + p * 128 + 128], texts)
            here = pl.ds(pl.multiple_of(q * width + p * 128, 128), 128)
            grad = grad_heads[:, lane]
            ask = query[:, here]
            probs, left = pair_softmax(ask, keys)
            grad_probs = dot_t(grad, values)
            centred = pair_sum(grad_probs * probs, left)
            grad_scores = (probs * (grad_probs - centred)).astype(BF)
            query_grad[:, here] = (dot(grad_scores, keys) * scale).astype(BF)
            memory_grad[q, :, lane] = unstack(dot_c(grad_scores, ask) * scale).astype(BF)
            memory_grad[q, :, width + p * 128 : width + p * 128 + 128] = unstack(
                dot_c(probs.astype(BF), grad)
            ).astype(BF)
        return carry

    lax.fori_loop(0, 4, quarter, 0)
    stores = [pltpu.make_async_copy(memory_grad, o_memory, store.at[0])]
    stores[0].start()
    halves_q = Halves(whole_q, land_q, send, recv, 0)
    halves_o = Halves(whole_o, land_o, send, recv, 4 * (subs - 1))

    def weights(q, carry):

        def grad_o(j, carry):
            whole_o[q, :, cols(j, 512)] = dot_c(flat[:, cols(q, width)], branch[:, cols(j, 512)]).astype(BF)
            return carry

        lax.fori_loop(0, m // 512, grad_o, 0)

        def grad_q(j, carry):
            whole_q[q, rows_at(j, 256)] = dot_c(rows[:, cols(j, 256)], query_grad[:, cols(q, width)]).astype(BF)
            return carry

        lax.fori_loop(0, m // 256, grad_q, 0)
        return carry

    lax.fori_loop(0, 4, weights, 0)
    for q in range(4):
        halves_q.start(q)
        halves_o.start(q)
    loads[9].wait()

    tick(4)

    def norm_grad(j, carry):
        here = rows_at(j, 256)
        total = jnp.zeros((n, 256), F32)
        for q in range(4):
            total = total + dot_t(query_grad[:, q * width : (q + 1) * width], wq[q, here])
        norm_self[:, cols(j, 256)] = total
        return carry

    lax.fori_loop(0, m // 256, norm_grad, 0)

    def self_block(i, carry):
        here = rows_at(i, 64)
        grad = norm_self[here]
        inner, terms = norm_back_block(grad, after_self[here], gains[0:1])
        total = cot[here] + inner
        cot[here] = total
        branch[here] = total.astype(BF)
        return carry[0] + fold(terms), carry[1] + fold(grad)

    gain_sum, bias_sum = lax.fori_loop(0, n // 64, self_block, (zero, zero))
    sums[16:24] = gain_sum
    sums[24:32] = bias_sum
    stores += [
        pltpu.make_async_copy(cot, o_out, store.at[1]),
        pltpu.make_async_copy(branch, o_branch, store.at[2]),
        pltpu.make_async_copy(sums, o_sums, store.at[3]),
    ]
    for copy in stores[1:]:
        copy.start()

    tick(5)
    for halves, piece in ((halves_q, piece_q), (halves_o, piece_o)):
        for q in range(4):

            def take(here, value, q=q, piece=piece):
                piece[q, here] = value.astype(BF)

            halves.total(q, take, 16)
    stores += [pltpu.make_async_copy(piece_q, o_wq, store.at[4]), pltpu.make_async_copy(piece_o, o_wo, store.at[5])]
    for copy in stores[4:]:
        copy.start()
    pump.drain()
    stores.append(pltpu.make_async_copy(land, o_land, store.at[6]))
    stores[-1].start()
    for q in range(4):
        halves_q.drain(q)
        halves_o.drain(q)
    for copy in stores:
        copy.wait()


def cross_back(layout, cot, norm, after_cross, after_self, gains, query, flat, memory, wq, wo, own, subs):
    n, m = cot.shape
    width = wq.shape[2]
    count = 8 * (subs - 1)
    held = (2, layout.window, layout.chunk, m)
    part_q, part_o = (4, m // subs, width), (4, width // subs, m)
    return pl.pallas_call(
        partial(cross_back_kernel, layout),
        name="cross_back",
        out_shape=[
            shape(n, m, kind=F32), shape(n, m), shape(32, m, kind=F32), shape(*memory.shape), shape(*part_q), shape(*part_o),
            shape(layout.feed_count // 2, layout.chunk, m), shape(*held),
        ],
        in_specs=[ANY] * 11,
        out_specs=[ANY] * 8,
        scratch_shapes=[
            pltpu.VMEM((n, m), F32), pltpu.VMEM((n, m), BF), pltpu.VMEM((n, m), F32), pltpu.VMEM((n, m), F32),
            pltpu.VMEM(gains.shape, F32), pltpu.VMEM((n, m), BF), pltpu.VMEM((n, m), BF), pltpu.VMEM(memory.shape, BF),
            pltpu.VMEM(wq.shape, BF), pltpu.VMEM(wo.shape, BF),
            pltpu.VMEM((n, m), BF), pltpu.VMEM((n, m), BF), pltpu.VMEM((n, m), BF), pltpu.VMEM(memory.shape, BF),
            pltpu.VMEM((32, m), F32), pltpu.VMEM((4, m, width), BF), pltpu.VMEM((4, width, m), BF),
            pltpu.VMEM((4, subs - 1, m // subs, width), BF), pltpu.VMEM((4, subs - 1, width // subs, m), BF),
            pltpu.VMEM(part_q, BF), pltpu.VMEM(part_o, BF),
            pltpu.VMEM((n, m), F32),
            *pump_scratch(layout, layout.middle),
            dma(11), dma(7), dma(count), dma(count),
        ],
        compiler_params=params(5),
    )(cot, norm, after_cross, after_self, gains, query, flat, memory, wq, wo, own)


def attend_pair_back(p, triple, place, blocks, heads, grad_heads, deltas, sums, grads, grad_keys, grad_values):
    n = triple.shape[1]
    width = heads * HEAD
    scale = HEAD ** (-0.5)
    lanes = head_lanes(n)
    key_lanes = head_lanes(blocks * n)

    here = pl.ds(pl.multiple_of(p * 128, 128), 128)
    key_cols = pl.ds(pl.multiple_of(width + p * 128, 128), 128)
    value_cols = pl.ds(pl.multiple_of(2 * width + p * 128, 128), 128)
    query = triple[place, :, here]
    grad = grad_heads[place, :, here]
    keys = triple[0:blocks, :, key_cols].reshape(blocks * n, 128)
    values = triple[0:blocks, :, value_cols].reshape(blocks * n, 128)
    stats = sums[place]
    means = deltas[place]
    found = []
    for h in range(2):
        mine = (lanes < HEAD) if h == 0 else (lanes >= HEAD)
        log_sum = jnp.sum(jnp.where(lanes == 2 * p + h, stats, 0.0), -1, keepdims=True)
        delta = jnp.sum(jnp.where(lanes == 2 * p + h, means, 0.0), -1, keepdims=True)
        scores = dot_t(jnp.where(mine, query, jnp.zeros_like(query)), keys)
        row = lax.broadcasted_iota(jnp.int32, scores.shape, 0)
        col = lax.broadcasted_iota(jnp.int32, scores.shape, 1)
        probs = jnp.where(
            col <= row + (blocks - 1) * n, jnp.exp2(scores * (scale * LOG2E) - log_sum), 0.0
        )
        grad_probs = dot_t(jnp.where(mine, grad, jnp.zeros_like(grad)), values)
        grad_scores = (probs * (grad_probs - delta)).astype(BF)
        found.append((dot(grad_scores, keys), dot_c(grad_scores, query), dot_c(probs.astype(BF), grad)))
    grads[place, :, here] = (jnp.where(lanes < HEAD, found[0][0], found[1][0]) * scale).astype(BF)
    grad_keys[0 : blocks * n, here] += jnp.where(key_lanes < HEAD, found[0][1], found[1][1]) * scale
    grad_values[0 : blocks * n, here] += jnp.where(key_lanes < HEAD, found[0][2], found[1][2])


def attend_back_kernel(
    layout,
    branch_in, triple_in, flat_in, sums_in, out_in, qkv_in, rows_in, frames_in, gains_in, grad_in, memory_in, text_in, kv_in,
    own_in, land_in, down_in,
    o_frames, o_sums, o_text, o_qkv, o_more, o_down, o_up, o_kv, o_land,
    branch, triple, flat, sums, out, qkv, rows, frames, gains, grad_out, memory, text, kv,
    land_m, stage_m,
    grad_heads, deltas, grads, grad_keys, grad_values, part, land, stage, whole_qkv, land_qkv, whole_out, land_out,
    whole_kv, land_kv, text_grad, sums_out, sum_m, own, held, ring, result, ring_send, ring_recv, ring_store,
    load, store, send, recv,
):
    t, x, y, d = neighbours()
    s = lax.axis_index("sub")
    subs = lax.axis_size("sub")
    names = (
        (branch_in, branch.at[t]), (out_in, out), (flat_in, flat), (triple_in, triple), (sums_in, sums),
        (memory_in, memory), (own_in, own.at[pl.ds(0, layout.feed_count)]), (land_in, held),
        *((qkv_in.at[i], qkv.at[:, pl.ds(i * qkv_in.shape[2], qkv_in.shape[2])]) for i in range(3)), (rows_in, rows),
        (text_in, text), (kv_in, kv), (frames_in, frames), (gains_in, gains), (grad_in, grad_out),
    )
    loads = [pltpu.make_async_copy(a, b, load.at[i]) for i, (a, b) in enumerate(names)]
    loads[7].start()
    for copy in loads[:7] + loads[8:]:
        copy.start()
    loads[7].wait()
    greet([{"tensor": x}, {"tensor": y}] + [{"sub": (s + k) % subs} for k in range(1, subs)] + group_ring())
    first, last = layout.middle, layout.later
    pump = Pump(
        own, held, ring, result, ring_send, ring_recv, ring_store, first, last, layout.count,
        sum_outputs(layout, (o_down, o_up), o_kv),
    )

    def tick(k):
        @pl.when(k + first < last)
        def _():
            pump.step(jnp.int32(k + first))

    n, m = grad_out.shape
    width = triple.shape[2]
    local = out.shape[0]
    heads = local // HEAD
    gather = Gather(branch.at[t], branch, send, recv, 0)
    scatter = Scatter(part, land, stage, send, recv, 6)
    scatter_m = Scatter(memory, land_m, stage_m, send, recv, 12)
    halves_qkv = Halves(whole_qkv, land_qkv, send, recv, 18)
    halves_out = Halves(whole_out, land_out, send, recv, 18 + subs - 1)
    halves_kv = Halves(whole_kv, land_kv, send, recv, 18 + 2 * (subs - 1))
    loads[0].wait()
    gather.start()
    for copy in loads[5:7]:
        copy.wait()
    scatter_m.diagonal()
    scatter_m.along_x()
    scatter_m.along_y()
    for copy in loads[1:5]:
        copy.wait()
    grad_keys[...] = jnp.zeros_like(grad_keys)
    grad_values[...] = jnp.zeros_like(grad_values)
    lanes = head_lanes(n)

    def turn(i, carry):
        far_y = i // 2
        far_x = i % 2
        place = (t // 2 + far_y - 2 * (t // 2) * far_y) * 2 + (t % 2 + far_x - 2 * (t % 2) * far_x)

        @pl.when(i == 1)
        def _():
            gather.relay_x()
            gather.relay_y()
            gather.have_x()

        @pl.when(i == 2)
        def _():
            gather.have_y()

        @pl.when(i == 3)
        def _():
            gather.have_d()

        grad_heads[place] = dot_t(branch[place], out[...]).astype(BF)

        def delta(p, stats):
            here = pl.ds(pl.multiple_of(p * 128, 128), 128)
            product = grad_heads[place, :, here].astype(F32) * flat[place, :, here].astype(F32)
            low = jnp.sum(jnp.where(lanes < HEAD, product, 0.0), -1, keepdims=True)
            high = jnp.sum(jnp.where(lanes < HEAD, 0.0, product), -1, keepdims=True)
            return jnp.where(lanes == 2 * p, low, jnp.where(lanes == 2 * p + 1, high, stats))

        deltas[place] = lax.fori_loop(0, heads // 2, delta, jnp.zeros((n, 128), F32))

        def pair(p, carry):
            turns = i * (heads // 2) + p

            @pl.when(turns % 2 == 0)
            def _():
                tick(turns // 2)

            for blocks in range(1, 5):

                @pl.when(place == blocks - 1)
                def _(blocks=blocks):
                    attend_pair_back(
                        p, triple, blocks - 1, blocks, heads, grad_heads, deltas, sums, grads, grad_keys, grad_values
                    )

            return carry

        lax.fori_loop(0, heads // 2, pair, 0)
        return carry

    lax.fori_loop(0, 4, turn, 0)
    for copy in loads[8:14]:
        copy.wait()

    def finish_grads(i, carry):
        grads[i, :, local : 2 * local] = grad_keys[rows_at(i, n)].astype(BF)
        grads[i, :, 2 * local :] = grad_values[rows_at(i, n)].astype(BF)
        return carry

    lax.fori_loop(0, 4, finish_grads, 0)

    def back(i, carry):
        far_y = 1 - i // 2
        far_x = 1 - i % 2
        place = (t // 2 + far_y - 2 * (t // 2) * far_y) * 2 + (t % 2 + far_x - 2 * (t % 2) * far_x)

        def step(j, carry):
            part[place, :, cols(j, 512)] = dot_t(grads[place], qkv[rows_at(j, 512)]).astype(BF)
            return carry

        lax.fori_loop(0, m // 512, step, 0)

        @pl.when(i % 2 == 0)
        def _():
            tick(6 + i // 2)

        @pl.when(i == 0)
        def _():
            scatter.diagonal()

        @pl.when(i == 1)
        def _():
            scatter.along_y()

        @pl.when(i == 2)
        def _():
            scatter.along_x()

        return carry

    lax.fori_loop(0, 4, back, 0)
    tick(8)
    scatter_m.relay()

    def take_m(here, total):
        sum_m[here] = total.astype(BF)

    scatter_m.finish(take_m, 16)
    text_grad[...] = dot_t(sum_m[...], kv[...])
    stores = [pltpu.make_async_copy(text_grad, o_text, store.at[0])]
    stores[0].start()

    def grad_kv(j, carry):
        whole_kv[0, rows_at(j, 384)] = dot_c(text[:, cols(j, 384)], sum_m[...]).astype(BF)
        return carry

    lax.fori_loop(0, m // 384, grad_kv, 0)
    halves_kv.start(0)

    def grad_wout(j, carry):
        whole_out[0, :, cols(j, 512)] = dot_c(
            flat[...].reshape(4 * n, local), branch[:, :, cols(j, 512)].reshape(4 * n, 512)
        ).astype(BF)
        return carry

    lax.fori_loop(0, m // 512, grad_wout, 0)
    halves_out.start(0)
    tick(9)
    chunk, half = layout.chunk, 2 * layout.quarter

    def take_kv(here, total):
        c = here.start // chunk
        own[layout.kv + c % half, :, cols(c // half, 2 * local)] = total.astype(BF)

    halves_kv.total(0, take_kv, chunk)
    scatter.relay()

    def grad_wqkv(j, carry):
        @pl.when(j % 2 == 0)
        def _():
            tick(10 + j // 2)

        turned = rows[:, :, cols(j, 256)].reshape(4 * n, 256)

        def inner(i, carry):
            whole_qkv[0, rows_at(j, 256), cols(i, 384)] = dot_c(
                turned, grads[:, :, cols(i, 384)].reshape(4 * n, 384)
            ).astype(BF)
            return carry

        lax.fori_loop(0, width // 384, inner, 0)
        return carry

    lax.fori_loop(0, m // 256, grad_wqkv, 0)
    halves_qkv.start(0)
    tick(13)

    def take_out(here, total):
        own[layout.out + here.start // chunk] = total.astype(BF)

    halves_out.total(0, take_out, chunk)

    def take(here, total):
        land_qkv[0, 0, here] = total.astype(BF)

    halves_qkv.total(0, take, 16)
    stores.append(pltpu.make_async_copy(land_qkv.at[0, 0], o_qkv, store.at[1]))
    stores.append(pltpu.make_async_copy(own.at[pl.ds(layout.kv, layout.qkv - layout.kv)], o_more, store.at[2]))
    for copy in stores[-2:]:
        copy.start()
    tick(14)
    for copy in loads[14:]:
        copy.wait()

    def take_norm(here, total):
        part[t, here] = total.astype(BF)

    scatter.finish(take_norm, 64)

    def frame_block(i, carry):
        here = rows_at(i, 64)
        grad = part[t, here].astype(F32)
        inner, terms = norm_back_block(grad, frames[here].astype(F32), gains[4:5])
        grad_out[here] = grad_out[here] + inner
        return carry[0] + fold(terms), carry[1] + fold(grad)

    zero = jnp.zeros((8, m), F32)
    gain_sum, bias_sum = lax.fori_loop(0, n // 64, frame_block, (zero, zero))
    tick(15)
    sums_out[0:8] = gain_sum
    sums_out[8:16] = bias_sum
    stores += [pltpu.make_async_copy(grad_out, o_frames, store.at[3]), pltpu.make_async_copy(sums_out, o_sums, store.at[4])]
    for copy in stores[-2:]:
        copy.start()
    pump.drain()
    stores.append(pltpu.make_async_copy(held, o_land, store.at[5]))
    stores[-1].start()
    gather.drain()
    for each in (scatter, scatter_m):
        each.drain()
    for each in (halves_qkv, halves_out, halves_kv):
        each.drain(0)
    for copy in stores:
        copy.wait()


def attend_back(
    layout, branch, triple, flat, sums, out, qkv, rows, frames, gains, grad, memory, text, kv, own, land, down, subs
):
    n, m = grad.shape
    width = triple.shape[2]
    local = out.shape[0]
    texts, kvw = text.shape[0], kv.shape[1]
    count = 18 + 3 * (subs - 1)
    v = pltpu.VMEM
    return pl.pallas_call(
        partial(attend_back_kernel, layout),
        name="attend_back",
        out_shape=[
            shape(n, m, kind=F32), shape(16, m, kind=F32), shape(texts, m, kind=F32), shape(m // subs, width),
            shape(layout.qkv - layout.kv, layout.chunk, m), shape(*down.shape), shape(*down.shape),
            shape(4 * layout.quarter, layout.chunk, kvw), shape(*land.shape),
        ],
        in_specs=[ANY] * 16,
        out_specs=[ANY] * 9,
        input_output_aliases={15: 5},
        scratch_shapes=[
            v((4, n, m), BF), v(triple.shape, BF), v(flat.shape, BF), v(sums.shape, F32), v(out.shape, BF), v((m, width), BF),
            v(rows.shape, BF), v(frames.shape, frames.dtype), v(gains.shape, F32), v((n, m), F32), v(memory.shape, BF),
            v(text.shape, BF), v(kv.shape, BF),
            v((6, texts // 2, kvw), BF), v((2, texts // 2, kvw), BF),
            v((4, n, local), BF), v((4, n, 128), F32), v((4, n, width), BF), v((4 * n, local), F32), v((4 * n, local), F32),
            v((4, n, m), BF), v((6, n // 2, m), BF), v((2, n // 2, m), BF),
            v((1, m, width), BF), v((1, subs - 1, m // subs, width), BF),
            v((1, local, m), BF), v((1, subs - 1, local // subs, m), BF),
            v((1, m, kvw), BF), v((1, subs - 1, m // subs, kvw), BF),
            v((texts, m), F32), v((16, m), F32), v((texts, kvw), BF),
            *pump_scratch(layout, layout.qkv),
            dma(17), dma(6), dma(count), dma(count),
        ],
        compiler_params=params(6),
    )(branch, triple, flat, sums, out, qkv, rows, frames, gains, grad, memory, text, kv, own, land, down)


def total_kernel(
    layout,
    feed_in, qkv_in, more_in, cross_q_in, cross_o_in, sums_a_in, sums_b_in, text_in, land_in, part_in, after_in,
    down_in, up_in, kv_in,
    o_qkv, o_cq, o_out, o_co, o_text, o_vectors, o_layer, o_down, o_up, o_kv,
    own, held, ring, result, ring_send, ring_recv, ring_store,
    cross_q, cross_o, land_q, land_o, stage_q, stage_o, part, land_p, stage_p, after,
    sums_a, sums_b, text, text_land, text_full, vectors, vectors_land, share, share_land, load, store, send, recv,
):
    t, x, y, d = neighbours()
    s, subs = lax.axis_index("sub"), lax.axis_size("sub")
    g, groups = lax.axis_index("group"), lax.axis_size("group")
    chunk, m, local = layout.chunk, layout.m, layout.local
    width, quarter = 3 * local, layout.quarter
    at_kv, at_out, at_qkv, at_cq, at_co = layout.kv, layout.out, layout.qkv, layout.cq, layout.co
    def outputs(c, block, slots, act):
        slot = c % RING

        def region(begin, end, copies):
            @pl.when(jnp.logical_and(c >= begin, c < end))
            def _():
                for i, (source, target) in enumerate(copies(c - begin)):
                    act(pltpu.make_async_copy(source, target, slots.at[slot, i]))

        def whole(output):
            return lambda r: [(block, output.at[r])]

        region(0, at_kv // 2, whole(o_down))
        region(at_kv // 2, at_kv, whole(o_up))
        region(
            at_qkv, at_cq,
            lambda r: [
                *((block.at[:, pl.ds(i * local, local)], o_qkv.at[i, r]) for i in range(3)),
                (block.at[:, pl.ds(width, local)], o_qkv.at[r // quarter, 3 * quarter + r % quarter]),
            ],
        )
        region(
            at_kv, at_out,
            lambda r: [
                (block.at[:, pl.ds(2 * i * local, 2 * local)], o_kv.at[2 * i * quarter + r]) for i in range(2)
            ],
        )
        region(at_out, at_qkv, whole(o_out))
        region(
            at_cq, at_co,
            lambda r: [(block.at[:, pl.ds(i * local, local)], o_cq.at[i * quarter + r]) for i in range(4)],
        )
        region(at_co, layout.count, whole(o_co))

    fresh = max(0, layout.later - LAG * (groups - 1))
    newer = max(fresh, at_kv)
    pairs = [
        (land_in, held),
        (more_in.at[pl.ds(newer - at_kv, at_qkv - newer)], own.at[pl.ds(newer, at_qkv - newer)]),
        (qkv_in.at[pl.ds(0, 3 * quarter)], own.at[pl.ds(at_qkv, 3 * quarter), :, pl.ds(0, width)]),
    ]
    for i in range(3):
        pairs.append(
            (
                qkv_in.at[pl.ds(3 * quarter, quarter), :, pl.ds(i * local, local)],
                own.at[pl.ds(at_qkv + i * quarter, quarter), :, pl.ds(width, local)],
            )
        )
    if fresh < at_kv:
        pairs.append((feed_in.at[pl.ds(fresh, at_kv - fresh)], own.at[pl.ds(fresh, at_kv - fresh)]))
    early = len(pairs)
    pairs += [
        (cross_q_in, cross_q), (cross_o_in, cross_o), (sums_a_in, sums_a), (sums_b_in, sums_b), (text_in, text),
        (part_in, part), (after_in, after),
    ]
    loads = [pltpu.make_async_copy(a, b, load.at[i]) for i, (a, b) in enumerate(pairs)]
    for copy in loads:
        copy.start()
    loads[0].wait()
    greet(
        [{"tensor": x}, {"tensor": y}, {"tensor": d}]
        + [{"sub": (s + k) % subs} for k in range(1, subs)]
        + [{"group": (g + k) % groups} for k in range(1, groups)]
    )
    begin, end = layout.later, layout.end
    pump = Pump(own, held, ring, result, ring_send, ring_recv, ring_store, begin, end, layout.count, outputs)

    def run(a, b):
        def step(k, carry):
            pump.step(k)
            return carry

        lax.fori_loop(a, b, step, 0)

    for copy in loads[1:early]:
        copy.wait()
    run(begin, begin + 1)
    for copy in loads[early:-2]:
        copy.wait()
    share_width = m // subs
    for i in range(6):
        source, at = (sums_a, i) if i < 4 else (sums_b, i - 4)
        row = jnp.sum(source[8 * at : 8 * at + 8], 0, keepdims=True)
        for j in range(subs):
            vectors[j, i : i + 1] = row[:, j * share_width : (j + 1) * share_width]
    strip = text.shape[0] // 4

    def remote(source, target, k, device):
        return pltpu.make_async_remote_copy(
            source, target, send.at[k], recv.at[k], device_id=device, device_id_type=MESH
        )

    square = (x, y, d)
    first = [remote(vectors, vectors_land.at[k], k, {"tensor": square[k]}) for k in range(3)]
    first += [
        remote(text.at[rows_at(square[k], strip)], text_land.at[k], 3 + k, {"tensor": square[k]}) for k in range(3)
    ]
    second = [
        remote(share.at[0, (s + k) % subs], share_land.at[k - 1], 5 + k, {"sub": (s + k) % subs}) for k in range(1, subs)
    ]
    base = 5 + subs
    second += [
        remote(text_full.at[rows_at(t, strip)], text_full.at[rows_at(t, strip)], base + k, {"tensor": square[k]}) for k in range(3)
    ]
    base += 3
    third = [
        remote(share.at[1, 0], share_land.at[subs - 2 + k], base + k - 1, {"group": (g + k) % groups})
        for k in range(1, groups)
    ]
    base += groups - 1
    scatter_q = Scatter(cross_q, land_q, stage_q, send, recv, base)
    scatter_o = Scatter(cross_o, land_o, stage_o, send, recv, base + 6)
    for copy in first:
        copy.start()
    scatter_p = Scatter(part, land_p, stage_p, send, recv, base + 12)
    for each in (scatter_q, scatter_o):
        each.diagonal()
        each.along_x()
        each.along_y()

    run(begin + 1, begin + 2)
    for copy in first:
        copy.wait_recv()
    for j in range(subs):
        share[0, j] = vectors[j] + vectors_land[0, j] + vectors_land[1, j] + vectors_land[2, j]
    text_full[rows_at(t, strip)] = text[rows_at(t, strip)] + text_land[0] + text_land[1] + text_land[2]
    for copy in first:
        copy.wait_send()
    for copy in second:
        copy.start()
    run(begin + 2, begin + 3)
    for copy in second:
        copy.wait_recv()
    total = share[0, s]
    for k in range(1, subs):
        total = total + share_land[k - 1]
    share[1, 0] = total
    text_store = pltpu.make_async_copy(text_full, o_text, store.at[0])
    text_store.start()
    for copy in third:
        copy.start()
    scatter_q.relay()
    scatter_o.relay()
    loads[-2].wait()
    loads[-1].wait()
    scatter_p.diagonal()
    scatter_p.along_x()
    scatter_p.along_y()
    run(begin + 3, at_cq)

    def take_q(rows, value):
        row = rows.start
        c = row // chunk
        own[at_cq + c % quarter, :, cols(c // quarter, local)] = value.astype(BF)

    scatter_q.finish(take_q, chunk)
    run(at_cq, at_co)
    step = min(chunk, scatter_o.half)

    def take_o(rows, value):
        own[at_co + rows.start // chunk, rows_at(rows.start % chunk // step, step)] = value.astype(BF)

    scatter_o.finish(take_o, step)
    run(at_co, layout.count)
    scatter_p.relay()
    run(layout.count, end)

    def take_layer(rows, value):
        after[rows] = after[rows] + value

    scatter_p.finish(take_layer, 64)
    layer_store = pltpu.make_async_copy(after, o_layer, store.at[2])
    layer_store.start()
    for copy in third:
        copy.wait_recv()
    total = share[1, 0]
    for k in range(1, groups):
        total = total + share_land[subs - 2 + k]
    share[2, 0] = total
    vector_store = pltpu.make_async_copy(share.at[2, 0], o_vectors, store.at[1])
    vector_store.start()
    for copy in second + third:
        copy.wait_send()
    for each in (scatter_q, scatter_o, scatter_p):
        each.drain()
    pump.drain()
    layer_store.wait()
    text_store.wait()
    vector_store.wait()


def total(layout, pieces, qkv, more, cross_q, cross_o, sums_a, sums_b, text, land, part, after, down, up, kv, subs, groups):
    m, chunk = layout.m, layout.chunk
    n = after.shape[0]
    v = pltpu.VMEM
    sems = 7 + subs + groups + 18
    qkv = qkv.reshape(-1, chunk, qkv.shape[1])
    piece_q, piece_o = cross_q.shape[1:], cross_o.shape[1:]
    out_shape = shape(layout.qkv - layout.out, chunk, m)
    return pl.pallas_call(
        partial(total_kernel, layout),
        name="total",
        out_shape=[
            shape(3, *qkv.shape[:2], layout.local), shape(layout.piece // chunk, chunk, layout.local), out_shape, out_shape,
            shape(*text.shape, kind=F32), shape(8, m // subs, kind=F32), shape(n, m, kind=F32),
            shape(*down.shape), shape(*up.shape), shape(*kv.shape),
        ],
        in_specs=[ANY] * 14,
        out_specs=[ANY] * 10,
        input_output_aliases={11: 7, 12: 8, 13: 9},
        scratch_shapes=[
            *pump_scratch(layout, layout.count),
            v(cross_q.shape, BF), v(cross_o.shape, BF),
            v((6, piece_q[0] // 2, piece_q[1]), BF), v((6, piece_o[0] // 2, piece_o[1]), BF),
            v((2, piece_q[0] // 2, piece_q[1]), BF), v((2, piece_o[0] // 2, piece_o[1]), BF),
            v((4, n, m), BF), v((6, n // 2, m), BF), v((2, n // 2, m), BF), v((n, m), F32),
            v(sums_a.shape, F32), v(sums_b.shape, F32), v(text.shape, F32),
            v((3, text.shape[0] // 4, m), F32), v(text.shape, F32), v((subs, 8, m // subs), F32), v((3, subs, 8, m // subs), F32),
            v((3, subs, 8, m // subs), F32), v((subs - 1 + groups - 1, 8, m // subs), F32),
            dma(14), dma(3), dma(sems), dma(sems),
        ],
        compiler_params=params(7),
    )(pieces, qkv, more, cross_q, cross_o, sums_a, sums_b, text, land, part, after, down, up, kv)


def local(
    frames, text_states, selfgain, selfbias, selfqkv, selfout, crossgain, crossbias, crossquery, crosskv, crossout,
    feedgain, feedbias, feedup, feeddown, cotangent,
):
    subs, groups = lax.axis_size("sub"), lax.axis_size("group")
    m = frames.shape[2]
    width = selfout.shape[0]
    qkv = selfqkv.transpose(1, 0, 2)
    kv = crosskv.reshape(m, 2 * width)
    gains = jnp.concatenate([crossgain, crossbias, feedgain, feedbias, selfgain, selfbias]).reshape(6, m)
    rows, triple, memory = enter(frames[0], gains, qkv, text_states[0], kv)
    flat, sums, after_self, wq, wo = attend(triple, selfout, frames[0], crossquery, crossout, subs)
    wo = wo.reshape(4 * width, m)
    query, cross_flat, after_cross, feed_rows, grads = cross(after_self, gains, wq, wo, memory, cotangent[0])
    layout = Layout(m, width, subs, groups)
    part, norm_grad, pieces = feed(feed_rows, grads, feedup, feeddown, subs)
    pieces = pieces.reshape(-1, layout.chunk, m)
    grad_out, branch, sums_a, memory_grad, piece_q, piece_o, down, land = cross_back(
        layout, cotangent[0], norm_grad, after_cross, after_self, gains, query, cross_flat, memory, wq, wo, pieces, subs
    )
    frame_grad, sums_b, text_part, grad_qkv, more, down, up, full_kv, land = attend_back(
        layout, branch, triple, flat, sums, selfout, qkv, rows, frames[0], gains, grad_out, memory_grad,
        text_states[0], kv, pieces, land, down, subs,
    )
    full_qkv, full_cq, full_out, full_co, text_grad, vectors, layer_output, down, up, full_kv = total(
        layout, pieces, grad_qkv, more, piece_q, piece_o, sums_a, sums_b, text_part, land, part, after_cross,
        down, up, full_kv, subs, groups,
    )
    return (
        layer_output[None],
        frame_grad[None],
        text_grad[None],
        vectors[4],
        vectors[5],
        full_qkv.astype(F32).reshape(3, -1, width).transpose(1, 0, 2),
        full_out.astype(F32).reshape(-1, m),
        vectors[2],
        vectors[3],
        full_cq.astype(F32).reshape(-1, width),
        full_kv.astype(F32).reshape(-1, 2, width),
        full_co.astype(F32).reshape(-1, m),
        vectors[0],
        vectors[1],
        up.astype(F32).reshape(-1, m),
        down.astype(F32).reshape(-1, m),
    )


def solution(mesh):
    clips = P(("sub", "group"), "tensor", None)
    whole = P(("sub", "group"), None, None)
    narrow, wide = P("tensor", None), P(None, "tensor")
    third = P(None, None, "tensor")
    vector = P("sub")
    return jax.shard_map(
        local,
        mesh=mesh,
        in_specs=(
            clips, whole, P(), P(), third, narrow, P(), P(), wide, third, narrow, P(), P(), wide, narrow, clips,
        ),
        out_specs=(
            clips, clips, whole, vector, vector, P("sub", None, "tensor"), P(("tensor", "sub"), None), vector, vector,
            P("sub", "tensor"), P("sub", None, "tensor"), P(("tensor", "sub"), None), vector, vector,
            P("sub", "tensor"), P(("tensor", "sub"), None),
        ),
        check_vma=False,
    )
```

```python
from functools import partial

import jax
import jax.numpy as jnp
from jax import lax
from jax.experimental import pallas as pl
from jax.experimental.pallas import tpu as pltpu
from jax.sharding import PartitionSpec as P

HEAD = 64
EPSILON = 1e-05
NEG_BIG = -1e30
LOG2E = 1.4426950408889634
MESH = pl.DeviceIdType.MESH
F32 = jnp.float32
BF = jnp.bfloat16
ANY = pl.BlockSpec(memory_space=pl.ANY)
VMEM_LIMIT = 63 << 20


def neighbours():
    t = lax.axis_index("tensor")
    return t, t + 1 - 2 * (t % 2), (t + 2) % 4, 3 - t


def greet(targets):
    barrier = pltpu.get_barrier_semaphore()
    for target in targets:
        pl.semaphore_signal(barrier, inc=1, device_id=target, device_id_type=MESH)
    pl.semaphore_wait(barrier, len(targets))


def dot(a, b):
    return lax.dot_general(a, b, (((1,), (0,)), ((), ())), preferred_element_type=F32)


def dot_t(a, b):
    return lax.dot_general(a, b, (((1,), (1,)), ((), ())), preferred_element_type=F32)


def dot_c(a, b):
    return lax.dot_general(a, b, (((0,), (0,)), ((), ())), preferred_element_type=F32)


def cols(j, width):
    return pl.ds(pl.multiple_of(j * width, width), width)


def rows_at(j, height):
    return pl.ds(pl.multiple_of(j * height, height), height)


def split(count):
    first = (count // 2 + 15) // 16 * 16
    return pl.ds(0, first), pl.ds(first, count - first)


class Gather:
    def __init__(self, own, dst, send, recv, base, halves=None):
        self.own, self.dst, self.send, self.recv, self.base = own, dst, send, recv, base
        self.halves = halves or split(own.shape[0])

    def copy(self, k):
        t, x, y, _ = neighbours()
        first, second = self.halves
        half = (first, second, second, first, first, second)[k]
        place = (t, t, t, t, x, y)[k]
        target = (x, y, x, y, y, x)[k]
        source = self.own.at[half] if k < 4 else self.dst.at[place, half]
        return pltpu.make_async_remote_copy(
            source,
            self.dst.at[place, half],
            self.send.at[self.base + k],
            self.recv.at[self.base + k],
            device_id={"tensor": target},
            device_id_type=MESH,
        )

    def start(self):
        for k in range(4):
            self.copy(k).start()

    def relay_x(self):
        self.copy(0).wait_recv()
        self.copy(4).start()

    def relay_y(self):
        self.copy(1).wait_recv()
        self.copy(5).start()

    def have_x(self):
        self.copy(2).wait_recv()

    def have_y(self):
        self.copy(3).wait_recv()

    def have_d(self):
        self.copy(4).wait_recv()
        self.copy(5).wait_recv()

    def drain(self):
        for k in range(6):
            self.copy(k).wait_send()


class Scatter:
    def __init__(self, part, land, stage, send, recv, base):
        self.part, self.land, self.stage = part, land, stage
        self.send, self.recv, self.base = send, recv, base
        self.half = part.shape[1] // 2

    def copy(self, k):
        t, x, y, d = neighbours()
        low, high = pl.ds(0, self.half), pl.ds(self.half, self.half)
        source = (
            self.part.at[d, low],
            self.part.at[d, high],
            self.part.at[x, low],
            self.stage.at[1],
            self.part.at[y, high],
            self.stage.at[0],
        )[k]
        target = (x, y, x, x, y, y)[k]
        return pltpu.make_async_remote_copy(
            source,
            self.land.at[k],
            self.send.at[self.base + k],
            self.recv.at[self.base + k],
            device_id={"tensor": target},
            device_id_type=MESH,
        )

    def diagonal(self):
        self.copy(0).start()
        self.copy(1).start()

    def along_x(self):
        self.copy(2).start()

    def along_y(self):
        self.copy(4).start()

    def relay(self):
        t, x, y, d = neighbours()
        low, high = pl.ds(0, self.half), pl.ds(self.half, self.half)
        self.copy(0).wait_recv()
        self.stage[0] = (self.part[y, low].astype(F32) + self.land[0].astype(F32)).astype(BF)
        self.copy(5).start()
        self.copy(1).wait_recv()
        self.stage[1] = (self.part[x, high].astype(F32) + self.land[1].astype(F32)).astype(BF)
        self.copy(3).start()

    def finish(self, take, step):
        t, x, y, d = neighbours()
        for k in (2, 4, 5, 3):
            self.copy(k).wait_recv()
        for base, a, b in ((0, 2, 5), (self.half, 4, 3)):

            def block(i, carry, base=base, a=a, b=b):
                here = rows_at(i, step)
                rows = pl.ds(pl.multiple_of(base + i * step, step), step)
                take(
                    rows,
                    self.part[t, rows].astype(F32)
                    + self.land[a, here].astype(F32)
                    + self.land[b, here].astype(F32),
                )
                return carry

            lax.fori_loop(0, self.half // step, block, 0)

    def drain(self):
        for k in range(6):
            self.copy(k).wait_send()


def normed_rows(values):
    centre = values - jnp.mean(values, -1, keepdims=True)
    inverse = lax.rsqrt(jnp.mean(centre * centre, -1, keepdims=True) + EPSILON)
    return centre * inverse, inverse


def params(cid, **more):
    return pltpu.CompilerParams(
        collective_id=cid, has_side_effects=True, vmem_limit_bytes=VMEM_LIMIT, **more
    )


def dma(count):
    return pltpu.SemaphoreType.DMA((count,))


def shape(*dims, kind=BF):
    return jax.ShapeDtypeStruct(dims, kind)


LAG = 2
RING = 4


def either(condition, other):
    return jnp.logical_and(condition, other)


class Pump:
    def __init__(self, own, land, ring, result, send, recv, store, first, last, count, outputs):
        self.own, self.land, self.ring, self.result = own, land, ring, result
        self.send, self.recv, self.store = send, recv, store
        self.first, self.last, self.count, self.outputs = first, last, count, outputs
        self.window = land.shape[1]
        self.g, self.n = lax.axis_index("group"), lax.axis_size("group")

    def copy(self, way, c):
        target = (self.g + 1) % self.n if way == 0 else (self.g + self.n - 1) % self.n
        return pltpu.make_async_remote_copy(
            self.ring.at[way, c % RING],
            self.land.at[way, c % self.window],
            self.send.at[way, c % RING],
            self.recv.at[way, c % self.window],
            device_id={"group": target},
            device_id_type=MESH,
        )

    def flow(self, way, k):
        place = self.g if way == 0 else self.n - 1 - self.g
        c = k - LAG * place

        @pl.when(either(c >= 0, c < self.count))
        def _():
            @pl.when(either(place > 0, k - LAG >= self.first))
            def _():
                self.copy(way, c).wait_recv()

            @pl.when(place < self.n - 1)
            def _():
                @pl.when(either(c >= RING, k - RING >= self.first))
                def _():
                    self.copy(way, c - RING).wait_send()

                @pl.when(place > 0)
                def _():
                    self.fill(self.ring.at[way, c % RING], (self.own.at[c], self.land.at[way, c % self.window]))

                @pl.when(place == 0)
                def _():
                    self.fill(self.ring.at[way, c % RING], (self.own.at[c],))

                self.copy(way, c).start()

    def fill(self, target, terms):
        def block(i, carry):
            here = rows_at(i, 48)
            value = terms[0][here].astype(F32)
            for term in terms[1:]:
                value = value + term[here].astype(F32)
            target[here] = value.astype(BF)
            return carry

        lax.fori_loop(0, target.shape[0] // 48, block, 0)

    def finished(self, k):
        far = jnp.maximum(self.g, self.n - 1 - self.g)
        return k - LAG * far

    def step(self, k):
        self.flow(0, k)
        self.flow(1, k)
        f = self.finished(k)

        @pl.when(either(f >= 0, f < self.count))
        def _():
            @pl.when(either(f >= RING, k - RING >= self.first))
            def _():
                self.outputs(f - RING, self.result.at[f % RING], self.store, lambda copy: copy.wait())

            slot, held = f % RING, f % self.window
            mine, target = self.own.at[f], self.result.at[slot]

            @pl.when(either(self.g > 0, self.g < self.n - 1))
            def _():
                self.fill(target, (mine, self.land.at[0, held], self.land.at[1, held]))

            @pl.when(self.g == 0)
            def _():
                self.fill(target, (mine, self.land.at[1, held]))

            @pl.when(self.g == self.n - 1)
            def _():
                self.fill(target, (mine, self.land.at[0, held]))

            self.outputs(f, self.result.at[slot], self.store, lambda copy: copy.start())

    def drain(self):
        for way in range(2):
            place = self.g if way == 0 else self.n - 1 - self.g
            top = jnp.minimum(self.last - LAG * place, self.count)
            for j in range(1, RING + 1):
                c = top - j

                @pl.when(either(place < self.n - 1, either(c >= 0, c + LAG * place >= self.first)))
                def _(way=way, c=c):
                    self.copy(way, c).wait_send()

            for k in range(max(self.first, self.last - LAG), self.last):
                c = k - LAG * (place - 1)

                @pl.when(either(place > 0, either(c >= 0, c < self.count)))
                def _(way=way, c=c):
                    self.copy(way, c).wait_recv()

        far = jnp.maximum(self.g, self.n - 1 - self.g)
        top = jnp.minimum(self.last - LAG * far, self.count)
        for j in range(1, RING + 1):
            f = top - j

            @pl.when(either(f >= 0, f + LAG * far >= self.first))
            def _(f=f):
                self.outputs(f, self.result.at[f % RING], self.store, lambda copy: copy.wait())


KV_TICKS, OUT_TICKS = 10, 14


class Layout:
    def __init__(self, m, local, subs, groups):
        piece = m // subs
        self.m, self.piece, self.local = m, piece, local
        self.out_rows = local // subs
        self.chunk = 96 if piece % 384 == 0 and self.out_rows % 96 == 0 else 48
        quarter = piece // 4 // self.chunk
        self.quarter = quarter
        self.feed_count = 2 * piece // self.chunk
        self.kv = self.feed_count
        self.out = self.kv + 2 * quarter
        self.qkv = self.out + self.out_rows // self.chunk
        self.cq = self.qkv + 3 * quarter
        self.co = self.cq + quarter
        self.count = self.co + self.out_rows // self.chunk
        self.window = LAG * groups
        self.end = self.count + LAG * (groups - 1)
        self.middle = min(6, self.feed_count // 2 - 2)
        self.later = self.feed_count
        if self.middle + KV_TICKS <= self.kv and self.middle + OUT_TICKS <= self.out:
            self.later = self.middle + OUT_TICKS + 2


def sum_outputs(layout, halves, text=None):
    def outputs(c, block, store, act):
        count = layout.feed_count // 2
        for i, half in enumerate(halves):

            @pl.when(either(c >= i * count, c < (i + 1) * count))
            def _(i=i, half=half):
                act(pltpu.make_async_copy(block, half.at[c - i * count], store.at[c % RING, 0]))

        if text is not None:

            @pl.when(either(c >= layout.kv, c < layout.out))
            def _():
                for i in range(2):
                    lanes = pl.ds(2 * i * layout.local, 2 * layout.local)
                    target = text.at[2 * i * layout.quarter + c - layout.kv]
                    act(pltpu.make_async_copy(block.at[:, lanes], target, store.at[c % RING, i]))

    return outputs


def pump_scratch(layout, count):
    chunk, m = layout.chunk, layout.m
    return [
        pltpu.VMEM((count, chunk, m), BF),
        pltpu.VMEM((2, layout.window, chunk, m), BF),
        pltpu.VMEM((2, RING, chunk, m), BF),
        pltpu.VMEM((RING, chunk, m), BF),
        pltpu.SemaphoreType.DMA((2, RING)),
        pltpu.SemaphoreType.DMA((2, layout.window)),
        pltpu.SemaphoreType.DMA((RING, 4)),
    ]


def group_ring():
    g, n = lax.axis_index("group"), lax.axis_size("group")
    return [{"group": (g + 1) % n}, {"group": (g + n - 1) % n}]


def enter_kernel(
    frames, gains, qkv, text, kv, o_rows, o_triple, o_memory,
    v_frames, v_gains, v_qkv, v_text, v_kv, rows, triple, memory, load, store, send, recv,
):
    t, x, y, d = neighbours()
    loads = [
        pltpu.make_async_copy(a, b, load.at[i])
        for i, (a, b) in enumerate(
            (
                (frames, v_frames), (gains, v_gains), (text, v_text), (kv, v_kv),
                *((qkv.at[i], v_qkv.at[:, pl.ds(i * qkv.shape[2], qkv.shape[2])]) for i in range(3)),
            )
        )
    ]
    for copy in loads:
        copy.start()
    greet([{"tensor": x}, {"tensor": y}])
    for copy in loads[:2]:
        copy.wait()
    count, width = v_qkv.shape
    block = 384

    def norm_block(i, carry):
        here = rows_at(i, 64)
        hat, _ = normed_rows(v_frames[here].astype(F32))
        rows[t, here] = (hat * v_gains[4:5] + v_gains[5:6]).astype(BF)
        return carry

    lax.fori_loop(0, v_frames.shape[0] // 64, norm_block, 0)
    gather = Gather(rows.at[t], rows, send, recv, 0)
    gather.start()
    texts = Gather(memory.at[t], memory, send, recv, 6)

    def project(place):
        def step(j, carry):
            triple[place, :, cols(j, block)] = dot(rows[place], v_qkv[:, cols(j, block)]).astype(BF)
            return carry

        lax.fori_loop(0, width // block, step, 0)

    def put(k, place):
        a = pltpu.make_async_copy(rows.at[place], o_rows.at[place], store.at[2 * k])
        b = pltpu.make_async_copy(triple.at[place], o_triple.at[place], store.at[2 * k + 1])
        a.start()
        b.start()
        return [a, b]

    loads[2].wait()
    loads[3].wait()

    def texts_step(j, carry):
        memory[t, :, cols(j, block)] = dot(v_text[...], v_kv[:, cols(j, block)]).astype(BF)
        return carry

    lax.fori_loop(0, v_kv.shape[1] // block, texts_step, 0)
    texts.start()
    for copy in loads[4:]:
        copy.wait()
    project(t)
    stores = put(0, t)
    gather.relay_x()
    gather.relay_y()
    gather.have_x()
    project(x)
    stores += put(1, x)
    gather.have_y()
    project(y)
    stores += put(2, y)
    texts.relay_x()
    texts.relay_y()
    texts.have_x()
    texts.have_y()
    gather.have_d()
    project(d)
    stores += put(3, d)
    texts.have_d()
    last = pltpu.make_async_copy(memory, o_memory, store.at[8])
    last.start()
    gather.drain()
    texts.drain()
    for copy in stores:
        copy.wait()
    last.wait()


def enter(frames, gains, qkv, text, kv):
    n, m = frames.shape
    width, texts, kvw = 3 * qkv.shape[2], text.shape[0], kv.shape[1]
    return pl.pallas_call(
        enter_kernel,
        name="enter",
        out_shape=[shape(4, n, m), shape(4, n, width), shape(4, texts, kvw)],
        in_specs=[ANY] * 5,
        out_specs=[ANY] * 3,
        scratch_shapes=[
            pltpu.VMEM((n, m), frames.dtype), pltpu.VMEM(gains.shape, F32),
            pltpu.VMEM((m, width), BF), pltpu.VMEM(text.shape, BF), pltpu.VMEM(kv.shape, BF),
            pltpu.VMEM((4, n, m), BF), pltpu.VMEM((4, n, width), BF), pltpu.VMEM((4, texts, kvw), BF),
            dma(7), dma(9), dma(12), dma(12),
        ],
        compiler_params=params(1),
    )(frames, gains, qkv, text, kv)


def head_lanes(rows):
    return lax.broadcasted_iota(jnp.int32, (rows, 128), 1)


def attend_rows(triple, place, blocks, heads, flat, sums):
    n = triple.shape[1]
    width = heads * HEAD
    scale = HEAD ** (-0.5) * LOG2E
    lanes = head_lanes(n)

    def pair(p, stats):
        here = pl.ds(pl.multiple_of(p * 128, 128), 128)
        key_cols = pl.ds(pl.multiple_of(width + p * 128, 128), 128)
        value_cols = pl.ds(pl.multiple_of(2 * width + p * 128, 128), 128)
        query = triple[place, :, here]
        keys = triple[0:blocks, :, key_cols].reshape(blocks * n, 128)
        values = triple[0:blocks, :, value_cols].reshape(blocks * n, 128)
        outs = []
        for h in range(2):
            mine = (lanes < HEAD) if h == 0 else (lanes >= HEAD)
            scores = dot_t(jnp.where(mine, query, jnp.zeros_like(query)), keys)
            row = lax.broadcasted_iota(jnp.int32, scores.shape, 0)
            col = lax.broadcasted_iota(jnp.int32, scores.shape, 1)
            scores = jnp.where(col <= row + (blocks - 1) * n, scores, NEG_BIG)
            peak = jnp.max(scores, -1, keepdims=True) * scale
            exponent = jnp.exp2(scores * scale - peak)
            total = jnp.sum(exponent, -1, keepdims=True)
            outs.append(dot(exponent.astype(BF), values) / total)
            stats = jnp.where(lanes == 2 * p + h, peak + jnp.log2(total), stats)
        flat[place, :, here] = jnp.where(lanes < HEAD, outs[0], outs[1]).astype(BF)
        return stats

    sums[place] = lax.fori_loop(0, heads // 2, pair, jnp.zeros((n, 128), F32))


def attend_kernel(
    triple_in, out_in, frames_in, wq, wo, o_flat, o_sums, o_after, o_wq, o_wo,
    triple, v_out, v_frames, flat, sums, after, part, land, stage, v_wq, v_wo, load, store, send, recv, side,
):
    t, x, y, d = neighbours()
    s = lax.axis_index("sub")
    subs = lax.axis_size("sub")
    g, groups = lax.axis_index("group"), lax.axis_size("group")
    n = triple.shape[1]
    m = v_out.shape[1]
    heads = v_out.shape[0] // HEAD
    loads = [
        pltpu.make_async_copy(a, b, load.at[i])
        for i, (a, b) in enumerate(
            ((triple_in, triple), (out_in, v_out), (frames_in, v_frames), (wq, v_wq), (wo, v_wo))
        )
    ]
    for copy in loads:
        copy.start()
    greet(
        [{"tensor": x}, {"tensor": y}]
        + [{"sub": (s + k) % subs} for k in range(1, subs)]
        + [{"group": (g + k) % groups} for k in range(1, groups)]
    )
    scatter = Scatter(part, land, stage, send, recv, 0)
    gathers = []
    for i, (weight, full) in enumerate(((wq, o_wq), (wo, o_wo))):
        piece = weight.shape[0] // subs
        strips = groups if i == 0 and piece % (32 * groups) == 0 else 1
        strip = piece // strips
        first, second = split(strip)
        offset = pl.multiple_of(s * piece, piece)
        begin = pl.multiple_of(offset + (g * strip if strips > 1 else 0), strip)
        halves = (
            pl.ds(begin, first.size),
            pl.ds(pl.multiple_of(begin + first.size, 16), second.size),
        )
        gathers.append((Gather(weight, full, send, recv, 6 + 6 * i, halves), full, pl.ds(offset, piece)))
        if i == 0:
            mine = pl.ds(begin, strip)
            spread = [(j, k) for j in range(3) for k in range(1, groups)] if strips > 1 else []

    def shared(i, j, k):
        _, full, piece = gathers[i]
        place = (x, y, d)[j]
        slot = (i * 3 + j) * (subs - 1) + k - 1
        return pltpu.make_async_remote_copy(
            full.at[place, piece], full.at[place, piece],
            send.at[18 + slot], recv.at[18 + slot],
            device_id={"sub": (s + k) % subs}, device_id_type=MESH,
        )

    def stripped(j, k):
        place = (x, y, d)[j]
        slot = 18 + 6 * (subs - 1) + j * (groups - 1) + k - 1
        return pltpu.make_async_remote_copy(
            o_wq.at[place, mine], o_wq.at[place, mine], send.at[slot], recv.at[slot],
            device_id={"group": (g + k) % groups}, device_id_type=MESH,
        )

    (query_gather, _, _), (out_gather, _, _) = gathers
    query_gather.start()
    for copy in loads[:2]:
        copy.wait()

    def one(i, carry):
        far_y = 1 - i // 2
        far_x = 1 - i % 2
        place = (t // 2 + far_y - 2 * (t // 2) * far_y) * 2 + (t % 2 + far_x - 2 * (t % 2) * far_x)

        @pl.when(i == 1)
        def _():
            query_gather.relay_x()
            query_gather.relay_y()
            out_gather.start()

        @pl.when(i == 2)
        def _():
            query_gather.have_x()
            query_gather.have_y()
            query_gather.have_d()
            for j, k in spread:
                stripped(j, k).start()

        for blocks in range(1, 5):

            @pl.when(place == blocks - 1)
            def _(blocks=blocks):
                attend_rows(triple, blocks - 1, blocks, heads, flat, sums)

        def out_step(j, carry):
            part[place, :, cols(j, 512)] = dot(flat[place], v_out[:, cols(j, 512)]).astype(BF)
            return carry

        lax.fori_loop(0, m // 512, out_step, 0)

        @pl.when(i == 0)
        def _():
            scatter.diagonal()

        @pl.when(i == 1)
        def _():
            scatter.along_y()

        @pl.when(i == 2)
        def _():
            scatter.along_x()

        return carry

    lax.fori_loop(0, 4, one, 0)
    out_gather.relay_x()
    out_gather.relay_y()
    stores = [
        pltpu.make_async_copy(flat, o_flat, store.at[0]),
        pltpu.make_async_copy(sums, o_sums, store.at[1]),
    ]
    loads[3].wait()
    loads[4].wait()
    stores += [
        pltpu.make_async_copy(v_wq, o_wq.at[t], store.at[2]),
        pltpu.make_async_copy(v_wo, o_wo.at[t], store.at[3]),
    ]
    for copy in stores:
        copy.start()
    scatter.relay()
    loads[2].wait()

    def take(rows, total):
        after[rows] = v_frames[rows].astype(F32) + total

    scatter.finish(take, 64)
    last = pltpu.make_async_copy(after, o_after, store.at[4])
    last.start()
    out_gather.have_x()
    out_gather.have_y()
    out_gather.have_d()
    for j in range(3):
        for k in range(1, subs):
            shared(1, j, k).start()
    for j, k in spread:
        stripped(j, k).wait_recv()
    for j in range(3):
        for k in range(1, subs):
            shared(0, j, k).start()
    scatter.drain()
    for j, k in spread:
        stripped(j, k).wait_send()
    for i, (gather, _, _) in enumerate(gathers):
        gather.drain()
        for j in range(3):
            for k in range(1, subs):
                shared(i, j, k).wait()
    for copy in stores:
        copy.wait()
    last.wait()


def attend(triple, out, frames, wq, wo, subs, groups):
    _, n, width = triple.shape
    local, m = out.shape
    extra = 18 + 6 * (subs - 1) + 3 * (groups - 1)
    return pl.pallas_call(
        attend_kernel,
        name="attend",
        out_shape=[
            shape(4, n, local), shape(4, n, 128, kind=F32), shape(n, m, kind=F32),
            shape(4, *wq.shape), shape(4, *wo.shape),
        ],
        in_specs=[ANY] * 5,
        out_specs=[ANY] * 5,
        scratch_shapes=[
            pltpu.VMEM((4, n, width), BF), pltpu.VMEM((local, m), BF), pltpu.VMEM((n, m), frames.dtype),
            pltpu.VMEM((4, n, local), BF), pltpu.VMEM((4, n, 128), F32), pltpu.VMEM((n, m), F32),
            pltpu.VMEM((4, n, m), BF), pltpu.VMEM((6, n // 2, m), BF), pltpu.VMEM((2, n // 2, m), BF),
            pltpu.VMEM(wq.shape, BF), pltpu.VMEM(wo.shape, BF),
            dma(5), dma(5), dma(extra), dma(extra), dma(1),
        ],
        compiler_params=params(2),
    )(triple, out, frames, wq, wo)


def stack_pair(block, rows):
    lanes = head_lanes(rows)
    zero = jnp.zeros_like(block)
    return jnp.concatenate([jnp.where(lanes < HEAD, block, zero), jnp.where(lanes >= HEAD, block, zero)], 0)


def pair_softmax(query, keys):
    scale = HEAD ** (-0.5) * LOG2E
    scores = dot_t(query, keys)
    left = head_lanes(scores.shape[0]) < HEAD
    low = jnp.max(jnp.where(left, scores, -jnp.inf), -1, keepdims=True)
    high = jnp.max(jnp.where(left, -jnp.inf, scores), -1, keepdims=True)
    exponent = jnp.exp2((scores - jnp.where(left, low, high)) * scale)
    total = pair_sum(exponent, left)
    return exponent / total, left


def pair_sum(values, left):
    low = jnp.sum(jnp.where(left, values, 0.0), -1, keepdims=True)
    high = jnp.sum(jnp.where(left, 0.0, values), -1, keepdims=True)
    return jnp.where(left, low, high)


def cross_kernel(
    after_in, gains_in, wq_in, wo_in, memory_in, cot_in,
    o_query, o_flat, o_after, o_rows, o_grads,
    after, gains, wq, wo, memory, cot, rows, query, flat, result, feed, grads, load, store, send, recv,
):
    t, x, y, d = neighbours()
    loads = [
        pltpu.make_async_copy(a, b, load.at[i])
        for i, (a, b) in enumerate(
            ((cot_in, cot), (after_in, after), (gains_in, gains), (wq_in, wq), (memory_in, memory), (wo_in, wo))
        )
    ]
    for copy in loads:
        copy.start()
    greet([{"tensor": x}, {"tensor": y}])
    n, m = after.shape
    width = wq.shape[2]
    texts = memory.shape[1]
    loads[0].wait()

    def round_block(i, carry):
        here = rows_at(i, 64)
        grads[t, here] = cot[here].astype(BF)
        return carry

    lax.fori_loop(0, n // 64, round_block, 0)
    gather = Gather(grads.at[t], grads, send, recv, 0)
    gather.start()
    loads[1].wait()
    loads[2].wait()

    def norm_block(i, carry):
        here = rows_at(i, 64)
        hat, _ = normed_rows(after[here])
        rows[here] = (hat * gains[0:1] + gains[1:2]).astype(BF)
        return carry

    lax.fori_loop(0, n // 64, norm_block, 0)
    loads[3].wait()
    loads[4].wait()

    def quarter(q, carry):
        query[:, cols(q, width)] = dot(rows[...], wq[q]).astype(BF)

        def pair(p, carry):
            keys = stack_pair(memory[q, :, cols(p, 128)], texts)
            values = stack_pair(memory[q, :, pl.ds(pl.multiple_of(width + p * 128, 128), 128)], texts)
            here = pl.ds(pl.multiple_of(q * width + p * 128, 128), 128)
            probs, _ = pair_softmax(query[:, here], keys)
            flat[:, here] = dot(probs.astype(BF), values).astype(BF)
            return carry

        lax.fori_loop(0, width // 128, pair, 0)
        return carry

    lax.fori_loop(0, 4, quarter, 0)
    gather.relay_x()
    gather.relay_y()
    stores = [pltpu.make_async_copy(query, o_query, store.at[0]), pltpu.make_async_copy(flat, o_flat, store.at[1])]
    loads[5].wait()

    def out_step(j, carry):
        result[:, cols(j, 512)] = after[:, cols(j, 512)] + dot(flat[...], wo[:, cols(j, 512)])
        return carry

    lax.fori_loop(0, m // 512, out_step, 0)

    def feed_block(i, carry):
        here = rows_at(i, 64)
        hat, _ = normed_rows(result[here])
        feed[here] = (hat * gains[2:3] + gains[3:4]).astype(BF)
        return carry

    lax.fori_loop(0, n // 64, feed_block, 0)
    stores += [pltpu.make_async_copy(result, o_after, store.at[2]), pltpu.make_async_copy(feed, o_rows, store.at[3])]
    for copy in stores:
        copy.start()
    gather.have_x()
    gather.have_y()
    gather.have_d()
    last = pltpu.make_async_copy(grads, o_grads, store.at[4])
    last.start()
    gather.drain()
    for copy in stores:
        copy.wait()
    last.wait()


def cross(after, gains, wq, wo, memory, cot):
    n, m = after.shape
    return pl.pallas_call(
        cross_kernel,
        name="cross",
        out_shape=[shape(n, m), shape(n, m), shape(n, m, kind=F32), shape(n, m), shape(4, n, m)],
        in_specs=[ANY] * 6,
        out_specs=[ANY] * 5,
        scratch_shapes=[
            pltpu.VMEM((n, m), F32), pltpu.VMEM(gains.shape, F32), pltpu.VMEM(wq.shape, BF), pltpu.VMEM(wo.shape, BF),
            pltpu.VMEM(memory.shape, BF), pltpu.VMEM((n, m), F32), pltpu.VMEM((n, m), BF), pltpu.VMEM((n, m), BF),
            pltpu.VMEM((n, m), BF), pltpu.VMEM((n, m), F32), pltpu.VMEM((n, m), BF), pltpu.VMEM((4, n, m), BF),
            dma(6), dma(5), dma(6), dma(6),
        ],
        compiler_params=params(3),
    )(after, gains, wq, wo, memory, cot)


def gelu_both(pre):
    size = jnp.abs(pre) * 0.7071067811865476
    rate = 1.0 / (1.0 + 0.3275911 * size)
    bell = jnp.exp2(pre * pre * (-0.5 * LOG2E))
    series = rate * (
        0.254829592
        + rate * (-0.284496736 + rate * (1.421413741 + rate * (-1.453152027 + rate * 1.061405429)))
    )
    tail = 0.5 * series * bell
    gate = jnp.where(pre >= 0, 1.0 - tail, tail)
    return pre * gate, gate + pre * (0.3989422804014327 * bell)


class Halves:
    def __init__(self, whole, land, send, recv, base):
        self.whole, self.land, self.send, self.recv, self.base = whole, land, send, recv, base
        self.subs = lax.axis_size("sub")
        self.piece = whole.shape[1] // self.subs

    def copies(self, w):
        s = lax.axis_index("sub")
        made = []
        for k in range(1, self.subs):
            target = (s + k) % self.subs
            slot = w * (self.subs - 1) + k - 1
            made.append(
                pltpu.make_async_remote_copy(
                    self.whole.at[w, rows_at(target, self.piece)],
                    self.land.at[w, k - 1],
                    self.send.at[self.base + slot],
                    self.recv.at[self.base + slot],
                    device_id={"sub": target},
                    device_id_type=MESH,
                )
            )
        return made

    def start(self, w):
        for copy in self.copies(w):
            copy.start()

    def total(self, w, take, step):
        s = lax.axis_index("sub")
        for copy in self.copies(w):
            copy.wait_recv()

        def block(i, carry):
            here = rows_at(i, step)
            value = self.whole[w, pl.ds(pl.multiple_of(s * self.piece + i * step, step), step)].astype(F32)
            for k in range(1, self.subs):
                value = value + self.land[w, k - 1, here].astype(F32)
            take(here, value)
            return carry

        lax.fori_loop(0, self.piece // step, block, 0)

    def drain(self, w):
        for copy in self.copies(w):
            copy.wait_send()


def weight_grad(left, right, whole, w, halves, block):
    s = lax.axis_index("sub")
    subs = lax.axis_size("sub")
    total_rows = left.shape[0] * left.shape[1]
    count = whole.shape[1] // block
    begin = ((s + 1) % subs) * halves.piece // block

    def one(j, carry):
        b = (begin + j) % count
        turned = left[:, :, cols(b, block)].reshape(total_rows, block)

        def inner(i, carry):
            other = right[:, :, cols(i, 512)].reshape(total_rows, 512)
            whole[w, rows_at(b, block), cols(i, 512)] = dot_c(turned, other).astype(BF)
            return carry

        lax.fori_loop(0, whole.shape[2] // 512, inner, 0)
        return carry

    if subs == 2:
        lax.fori_loop(0, count // 2, one, 0)
        halves.start(w)
        lax.fori_loop(count // 2, count, one, 0)
    else:
        lax.fori_loop(0, count, one, 0)
        halves.start(w)


def feed_kernel(
    rows_in, grads_in, up_in, down_in, o_part, o_norm, o_pieces,
    rows, grads, up, down, act, pre_grad, part_out, part_norm, land_norm, stage_norm,
    whole, land_whole, load, store, send, recv,
):
    t, x, y, d = neighbours()
    s = lax.axis_index("sub")
    subs = lax.axis_size("sub")
    loads = [
        pltpu.make_async_copy(a, b, load.at[i])
        for i, (a, b) in enumerate(
            ((rows_in, rows.at[t]), (up_in, up), (grads_in, grads), (down_in, down))
        )
    ]
    for copy in loads:
        copy.start()
    greet([{"tensor": x}, {"tensor": y}] + [{"sub": (s + k) % subs} for k in range(1, subs)])
    _, n, m = rows.shape
    hidden = up.shape[1]
    loads[0].wait()
    gather = Gather(rows.at[t], rows, send, recv, 0)
    gather.start()
    back = Scatter(part_norm, land_norm, stage_norm, send, recv, 6)
    halves = Halves(whole, land_whole, send, recv, 12)
    for copy in loads[1:4]:
        copy.wait()

    def work(place):
        def step(j, carry):
            here = cols(j, 256)
            value, slope = gelu_both(dot(rows[place], up[:, here]))
            act[place, :, here] = value.astype(BF)
            pre_grad[place, :, here] = (dot_t(grads[place], down[here]) * slope).astype(BF)
            return carry

        lax.fori_loop(0, hidden // 256, step, 0)

        def out_step(j, carry):
            part_norm[place, :, cols(j, 512)] = dot_t(pre_grad[place], up[rows_at(j, 512)]).astype(BF)
            part_out[place, :, cols(j, 512)] = dot(act[place], down[:, cols(j, 512)]).astype(BF)
            return carry

        lax.fori_loop(0, m // 512, out_step, 0)

    def turn(i, carry):
        far_y = i // 2
        far_x = i % 2
        place = (t // 2 + far_y - 2 * (t // 2) * far_y) * 2 + (t % 2 + far_x - 2 * (t % 2) * far_x)

        @pl.when(i == 1)
        def _():
            gather.relay_x()
            gather.relay_y()
            gather.have_x()

        @pl.when(i == 2)
        def _():
            gather.have_y()

        @pl.when(i == 3)
        def _():
            gather.have_d()

        work(place)

        @pl.when(i == 1)
        def _():
            back.along_x()

        @pl.when(i == 2)
        def _():
            back.along_y()

        @pl.when(i == 3)
        def _():
            back.diagonal()

        return carry

    lax.fori_loop(0, 4, turn, 0)
    stores = [pltpu.make_async_copy(part_out, o_part, store.at[1])]
    stores[0].start()
    weight_grad(act, grads, whole, 0, halves, 256)
    back.relay()
    weight_grad(rows, pre_grad, whole, 1, halves, 256)
    pieces = land_whole
    for w in range(2):

        def take(here, value, w=w):
            pieces[w, 0, here] = value.astype(BF)

        halves.total(w, take, 64)
    stores.append(pltpu.make_async_copy(pieces.at[:, 0], o_pieces, store.at[0]))
    stores[1].start()
    norm_total = part_norm


    def take_norm(here, total):
        norm_total[t, here] = total.astype(BF)

    back.finish(take_norm, 64)
    stores.append(pltpu.make_async_copy(norm_total.at[t], o_norm, store.at[2]))
    stores[2].start()
    gather.drain()
    back.drain()
    for w in range(2):
        halves.drain(w)
    for copy in stores:
        copy.wait()


def feed(rows, grads, up, down, subs):
    n, m = rows.shape
    hidden = up.shape[1]
    count = 12 + 2 * (subs - 1)
    return pl.pallas_call(
        feed_kernel,
        name="feed",
        out_shape=[shape(4, n, m), shape(n, m), shape(2, m // subs, hidden)],
        in_specs=[ANY] * 4,
        out_specs=[ANY] * 3,
        scratch_shapes=[
            pltpu.VMEM((4, n, m), BF), pltpu.VMEM((4, n, m), BF), pltpu.VMEM((m, hidden), BF), pltpu.VMEM((hidden, m), BF),
            pltpu.VMEM((4, n, hidden), BF), pltpu.VMEM((4, n, hidden), BF),
            pltpu.VMEM((4, n, m), BF), pltpu.VMEM((4, n, m), BF),
            pltpu.VMEM((6, n // 2, m), BF), pltpu.VMEM((2, n // 2, m), BF),
            pltpu.VMEM((2, m, hidden), BF), pltpu.VMEM((2, subs - 1, m // subs, hidden), BF),
            dma(4), dma(3), dma(count), dma(count),
        ],
        compiler_params=params(4),
    )(rows, grads, up, down)


def norm_back_block(grad, source, gain):
    hat, inverse = normed_rows(source)
    scaled = grad * gain
    inner = scaled - jnp.mean(scaled, -1, keepdims=True) - hat * jnp.mean(scaled * hat, -1, keepdims=True)
    return inverse * inner, grad * hat


def fold(block):
    total = block[0:8]
    for i in range(1, block.shape[0] // 8):
        total = total + block[8 * i : 8 * i + 8]
    return total


def unstack(block):
    lanes = head_lanes(block.shape[0] // 2)
    return jnp.where(lanes < HEAD, block[: block.shape[0] // 2], block[block.shape[0] // 2 :])


def cross_back_kernel(
    layout,
    cot_in, norm_in, cross_in, self_in, gains_in, query_in, flat_in, memory_in, wq_in, wo_in, own_in,
    o_out, o_branch, o_sums, o_memory, o_wq, o_wo, o_down, o_land,
    cot, norm, after_cross, after_self, gains, query, flat, memory, wq, wo,
    branch, rows, query_grad, memory_grad, sums, whole_q, whole_o, land_q, land_o, piece_q, piece_o,
    norm_self, own, land, ring, result, ring_send, ring_recv, ring_store,
    load, store, send, recv,
):
    s = lax.axis_index("sub")
    subs = lax.axis_size("sub")
    loads = [
        pltpu.make_async_copy(a, b, load.at[i])
        for i, (a, b) in enumerate(
            (
                (cot_in, cot), (norm_in, norm), (cross_in, after_cross), (gains_in, gains), (wo_in, wo),
                (query_in, query), (flat_in, flat), (memory_in, memory), (self_in, after_self), (wq_in, wq),
                (own_in.at[pl.ds(0, layout.middle)], own),
            )
        )
    ]
    for copy in loads[10:] + loads[:10]:
        copy.start()
    greet([{"sub": (s + k) % subs} for k in range(1, subs)] + group_ring())
    pump = Pump(
        own, land, ring, result, ring_send, ring_recv, ring_store, 0, layout.middle, layout.count,
        sum_outputs(layout, (o_down,)),
    )
    n, m = cot.shape
    width = wq.shape[2]
    texts = memory.shape[1]
    loads[10].wait()
    pump.step(jnp.int32(0))
    for copy in loads[:4]:
        copy.wait()
    scale = HEAD ** (-0.5)

    def feed_block(i, carry):
        here = rows_at(i, 64)
        grad = norm[here].astype(F32)
        inner, terms = norm_back_block(grad, after_cross[here], gains[2:3])
        total = cot[here] + inner
        cot[here] = total
        branch[here] = total.astype(BF)
        return carry[0] + fold(terms), carry[1] + fold(grad)

    zero = jnp.zeros((8, m), F32)
    gain_sum, bias_sum = lax.fori_loop(0, n // 64, feed_block, (zero, zero))
    sums[0:8] = gain_sum
    sums[8:16] = bias_sum
    loads[8].wait()

    def norm_block(i, carry):
        here = rows_at(i, 64)
        hat, _ = normed_rows(after_self[here])
        rows[here] = (hat * gains[0:1] + gains[1:2]).astype(BF)
        return carry

    lax.fori_loop(0, n // 64, norm_block, 0)
    for copy in loads[4:8]:
        copy.wait()
    middle = layout.middle

    def tick(k):
        @pl.when(k < middle)
        def _():
            pump.step(jnp.int32(k))

    tick(jnp.int32(1))

    def quarter(q, carry):
        @pl.when(q % 2 == 1)
        def _():
            tick(2 + q // 2)

        grad_heads = dot_t(branch[...], wo[rows_at(q, width)]).astype(BF)
        whole_q_cols = cols(q, width)
        query_grad_block = []
        for p in range(width // 128):
            lane = slice(p * 128, p * 128 + 128)
            keys = stack_pair(memory[q, :, lane], texts)
            values = stack_pair(memory[q, :, width + p * 128 : width + p * 128 + 128], texts)
            here = pl.ds(pl.multiple_of(q * width + p * 128, 128), 128)
            grad = grad_heads[:, lane]
            ask = query[:, here]
            probs, left = pair_softmax(ask, keys)
            grad_probs = dot_t(grad, values)
            centred = pair_sum(grad_probs * probs, left)
            grad_scores = (probs * (grad_probs - centred)).astype(BF)
            query_grad[:, here] = (dot(grad_scores, keys) * scale).astype(BF)
            memory_grad[q, :, lane] = unstack(dot_c(grad_scores, ask) * scale).astype(BF)
            memory_grad[q, :, width + p * 128 : width + p * 128 + 128] = unstack(
                dot_c(probs.astype(BF), grad)
            ).astype(BF)
        return carry

    lax.fori_loop(0, 4, quarter, 0)
    stores = [pltpu.make_async_copy(memory_grad, o_memory, store.at[0])]
    stores[0].start()
    halves_q = Halves(whole_q, land_q, send, recv, 0)
    halves_o = Halves(whole_o, land_o, send, recv, 4 * (subs - 1))

    def weights(q, carry):

        def grad_o(j, carry):
            whole_o[q, :, cols(j, 512)] = dot_c(flat[:, cols(q, width)], branch[:, cols(j, 512)]).astype(BF)
            return carry

        lax.fori_loop(0, m // 512, grad_o, 0)

        def grad_q(j, carry):
            whole_q[q, rows_at(j, 256)] = dot_c(rows[:, cols(j, 256)], query_grad[:, cols(q, width)]).astype(BF)
            return carry

        lax.fori_loop(0, m // 256, grad_q, 0)
        return carry

    lax.fori_loop(0, 4, weights, 0)
    for q in range(4):
        halves_q.start(q)
        halves_o.start(q)
    loads[9].wait()

    tick(4)

    def norm_grad(j, carry):
        here = rows_at(j, 256)
        total = jnp.zeros((n, 256), F32)
        for q in range(4):
            total = total + dot_t(query_grad[:, q * width : (q + 1) * width], wq[q, here])
        norm_self[:, cols(j, 256)] = total
        return carry

    lax.fori_loop(0, m // 256, norm_grad, 0)

    def self_block(i, carry):
        here = rows_at(i, 64)
        grad = norm_self[here]
        inner, terms = norm_back_block(grad, after_self[here], gains[0:1])
        total = cot[here] + inner
        cot[here] = total
        branch[here] = total.astype(BF)
        return carry[0] + fold(terms), carry[1] + fold(grad)

    gain_sum, bias_sum = lax.fori_loop(0, n // 64, self_block, (zero, zero))
    sums[16:24] = gain_sum
    sums[24:32] = bias_sum
    stores += [
        pltpu.make_async_copy(cot, o_out, store.at[1]),
        pltpu.make_async_copy(branch, o_branch, store.at[2]),
        pltpu.make_async_copy(sums, o_sums, store.at[3]),
    ]
    for copy in stores[1:]:
        copy.start()

    tick(5)
    for halves, piece in ((halves_q, piece_q), (halves_o, piece_o)):
        for q in range(4):

            def take(here, value, q=q, piece=piece):
                piece[q, here] = value.astype(BF)

            halves.total(q, take, 16)
    stores += [pltpu.make_async_copy(piece_q, o_wq, store.at[4]), pltpu.make_async_copy(piece_o, o_wo, store.at[5])]
    for copy in stores[4:]:
        copy.start()
    pump.drain()
    stores.append(pltpu.make_async_copy(land, o_land, store.at[6]))
    stores[-1].start()
    for q in range(4):
        halves_q.drain(q)
        halves_o.drain(q)
    for copy in stores:
        copy.wait()


def cross_back(layout, cot, norm, after_cross, after_self, gains, query, flat, memory, wq, wo, own, subs):
    n, m = cot.shape
    width = wq.shape[2]
    count = 8 * (subs - 1)
    held = (2, layout.window, layout.chunk, m)
    part_q, part_o = (4, m // subs, width), (4, width // subs, m)
    return pl.pallas_call(
        partial(cross_back_kernel, layout),
        name="cross_back",
        out_shape=[
            shape(n, m, kind=F32), shape(n, m), shape(32, m, kind=F32), shape(*memory.shape), shape(*part_q), shape(*part_o),
            shape(layout.feed_count // 2, layout.chunk, m), shape(*held),
        ],
        in_specs=[ANY] * 11,
        out_specs=[ANY] * 8,
        scratch_shapes=[
            pltpu.VMEM((n, m), F32), pltpu.VMEM((n, m), BF), pltpu.VMEM((n, m), F32), pltpu.VMEM((n, m), F32),
            pltpu.VMEM(gains.shape, F32), pltpu.VMEM((n, m), BF), pltpu.VMEM((n, m), BF), pltpu.VMEM(memory.shape, BF),
            pltpu.VMEM(wq.shape, BF), pltpu.VMEM(wo.shape, BF),
            pltpu.VMEM((n, m), BF), pltpu.VMEM((n, m), BF), pltpu.VMEM((n, m), BF), pltpu.VMEM(memory.shape, BF),
            pltpu.VMEM((32, m), F32), pltpu.VMEM((4, m, width), BF), pltpu.VMEM((4, width, m), BF),
            pltpu.VMEM((4, subs - 1, m // subs, width), BF), pltpu.VMEM((4, subs - 1, width // subs, m), BF),
            pltpu.VMEM(part_q, BF), pltpu.VMEM(part_o, BF),
            pltpu.VMEM((n, m), F32),
            *pump_scratch(layout, layout.middle),
            dma(11), dma(7), dma(count), dma(count),
        ],
        compiler_params=params(5),
    )(cot, norm, after_cross, after_self, gains, query, flat, memory, wq, wo, own)


def attend_pair_back(p, triple, place, blocks, heads, grad_heads, deltas, sums, grads, grad_keys, grad_values):
    n = triple.shape[1]
    width = heads * HEAD
    scale = HEAD ** (-0.5)
    lanes = head_lanes(n)
    key_lanes = head_lanes(blocks * n)

    here = pl.ds(pl.multiple_of(p * 128, 128), 128)
    key_cols = pl.ds(pl.multiple_of(width + p * 128, 128), 128)
    value_cols = pl.ds(pl.multiple_of(2 * width + p * 128, 128), 128)
    query = triple[place, :, here]
    grad = grad_heads[place, :, here]
    keys = triple[0:blocks, :, key_cols].reshape(blocks * n, 128)
    values = triple[0:blocks, :, value_cols].reshape(blocks * n, 128)
    stats = sums[place]
    means = deltas[place]
    found = []
    for h in range(2):
        mine = (lanes < HEAD) if h == 0 else (lanes >= HEAD)
        log_sum = jnp.sum(jnp.where(lanes == 2 * p + h, stats, 0.0), -1, keepdims=True)
        delta = jnp.sum(jnp.where(lanes == 2 * p + h, means, 0.0), -1, keepdims=True)
        scores = dot_t(jnp.where(mine, query, jnp.zeros_like(query)), keys)
        row = lax.broadcasted_iota(jnp.int32, scores.shape, 0)
        col = lax.broadcasted_iota(jnp.int32, scores.shape, 1)
        probs = jnp.where(
            col <= row + (blocks - 1) * n, jnp.exp2(scores * (scale * LOG2E) - log_sum), 0.0
        )
        grad_probs = dot_t(jnp.where(mine, grad, jnp.zeros_like(grad)), values)
        grad_scores = (probs * (grad_probs - delta)).astype(BF)
        found.append((dot(grad_scores, keys), dot_c(grad_scores, query), dot_c(probs.astype(BF), grad)))
    grads[place, :, here] = (jnp.where(lanes < HEAD, found[0][0], found[1][0]) * scale).astype(BF)
    grad_keys[0 : blocks * n, here] += jnp.where(key_lanes < HEAD, found[0][1], found[1][1]) * scale
    grad_values[0 : blocks * n, here] += jnp.where(key_lanes < HEAD, found[0][2], found[1][2])


def attend_back_kernel(
    layout,
    branch_in, triple_in, flat_in, sums_in, out_in, qkv_in, rows_in, frames_in, gains_in, grad_in, memory_in, text_in, kv_in,
    own_in, land_in, down_in,
    o_frames, o_sums, o_text, o_qkv, o_more, o_down, o_up, o_kv, o_land,
    branch, triple, flat, sums, out, qkv, rows, frames, gains, grad_out, memory, text, kv,
    land_m, stage_m,
    grad_heads, deltas, grads, grad_keys, grad_values, part, land, stage, whole_qkv, land_qkv, whole_out, land_out,
    whole_kv, land_kv, text_grad, sums_out, sum_m, own, held, ring, result, ring_send, ring_recv, ring_store,
    load, store, send, recv,
):
    t, x, y, d = neighbours()
    s = lax.axis_index("sub")
    subs = lax.axis_size("sub")
    names = (
        (branch_in, branch.at[t]), (out_in, out), (flat_in, flat), (triple_in, triple), (sums_in, sums),
        (memory_in, memory), (own_in, own.at[pl.ds(0, layout.feed_count)]), (land_in, held),
        *((qkv_in.at[i], qkv.at[:, pl.ds(i * qkv_in.shape[2], qkv_in.shape[2])]) for i in range(3)), (rows_in, rows),
        (text_in, text), (kv_in, kv), (frames_in, frames), (gains_in, gains), (grad_in, grad_out),
    )
    loads = [pltpu.make_async_copy(a, b, load.at[i]) for i, (a, b) in enumerate(names)]
    loads[7].start()
    for copy in loads[:7] + loads[8:]:
        copy.start()
    loads[7].wait()
    greet([{"tensor": x}, {"tensor": y}] + [{"sub": (s + k) % subs} for k in range(1, subs)] + group_ring())
    first, last = layout.middle, layout.later
    pump = Pump(
        own, held, ring, result, ring_send, ring_recv, ring_store, first, last, layout.count,
        sum_outputs(layout, (o_down, o_up), o_kv),
    )

    def tick(k):
        @pl.when(k + first < last)
        def _():
            pump.step(jnp.int32(k + first))

    n, m = grad_out.shape
    width = triple.shape[2]
    local = out.shape[0]
    heads = local // HEAD
    gather = Gather(branch.at[t], branch, send, recv, 0)
    scatter = Scatter(part, land, stage, send, recv, 6)
    scatter_m = Scatter(memory, land_m, stage_m, send, recv, 12)
    halves_qkv = Halves(whole_qkv, land_qkv, send, recv, 18)
    halves_out = Halves(whole_out, land_out, send, recv, 18 + subs - 1)
    halves_kv = Halves(whole_kv, land_kv, send, recv, 18 + 2 * (subs - 1))
    loads[0].wait()
    gather.start()
    for copy in loads[5:7]:
        copy.wait()
    scatter_m.diagonal()
    scatter_m.along_x()
    scatter_m.along_y()
    for copy in loads[1:5]:
        copy.wait()
    grad_keys[...] = jnp.zeros_like(grad_keys)
    grad_values[...] = jnp.zeros_like(grad_values)
    lanes = head_lanes(n)

    def turn(i, carry):
        far_y = i // 2
        far_x = i % 2
        place = (t // 2 + far_y - 2 * (t // 2) * far_y) * 2 + (t % 2 + far_x - 2 * (t % 2) * far_x)

        @pl.when(i == 1)
        def _():
            gather.relay_x()
            gather.relay_y()
            gather.have_x()

        @pl.when(i == 2)
        def _():
            gather.have_y()

        @pl.when(i == 3)
        def _():
            gather.have_d()

        grad_heads[place] = dot_t(branch[place], out[...]).astype(BF)

        def delta(p, stats):
            here = pl.ds(pl.multiple_of(p * 128, 128), 128)
            product = grad_heads[place, :, here].astype(F32) * flat[place, :, here].astype(F32)
            low = jnp.sum(jnp.where(lanes < HEAD, product, 0.0), -1, keepdims=True)
            high = jnp.sum(jnp.where(lanes < HEAD, 0.0, product), -1, keepdims=True)
            return jnp.where(lanes == 2 * p, low, jnp.where(lanes == 2 * p + 1, high, stats))

        deltas[place] = lax.fori_loop(0, heads // 2, delta, jnp.zeros((n, 128), F32))

        def pair(p, carry):
            turns = i * (heads // 2) + p

            @pl.when(turns % 2 == 0)
            def _():
                tick(turns // 2)

            for blocks in range(1, 5):

                @pl.when(place == blocks - 1)
                def _(blocks=blocks):
                    attend_pair_back(
                        p, triple, blocks - 1, blocks, heads, grad_heads, deltas, sums, grads, grad_keys, grad_values
                    )

            return carry

        lax.fori_loop(0, heads // 2, pair, 0)
        return carry

    lax.fori_loop(0, 4, turn, 0)
    for copy in loads[8:14]:
        copy.wait()

    def finish_grads(i, carry):
        grads[i, :, local : 2 * local] = grad_keys[rows_at(i, n)].astype(BF)
        grads[i, :, 2 * local :] = grad_values[rows_at(i, n)].astype(BF)
        return carry

    lax.fori_loop(0, 4, finish_grads, 0)

    def back(i, carry):
        far_y = 1 - i // 2
        far_x = 1 - i % 2
        place = (t // 2 + far_y - 2 * (t // 2) * far_y) * 2 + (t % 2 + far_x - 2 * (t % 2) * far_x)

        def step(j, carry):
            part[place, :, cols(j, 512)] = dot_t(grads[place], qkv[rows_at(j, 512)]).astype(BF)
            return carry

        lax.fori_loop(0, m // 512, step, 0)

        @pl.when(i % 2 == 0)
        def _():
            tick(6 + i // 2)

        @pl.when(i == 0)
        def _():
            scatter.diagonal()

        @pl.when(i == 1)
        def _():
            scatter.along_y()

        @pl.when(i == 2)
        def _():
            scatter.along_x()

        return carry

    lax.fori_loop(0, 4, back, 0)
    tick(8)
    scatter_m.relay()

    def take_m(here, total):
        sum_m[here] = total.astype(BF)

    scatter_m.finish(take_m, 16)
    text_grad[...] = dot_t(sum_m[...], kv[...])
    stores = [pltpu.make_async_copy(text_grad, o_text, store.at[0])]
    stores[0].start()

    def grad_kv(j, carry):
        whole_kv[0, rows_at(j, 384)] = dot_c(text[:, cols(j, 384)], sum_m[...]).astype(BF)
        return carry

    lax.fori_loop(0, m // 384, grad_kv, 0)
    halves_kv.start(0)

    def grad_wout(j, carry):
        whole_out[0, :, cols(j, 512)] = dot_c(
            flat[...].reshape(4 * n, local), branch[:, :, cols(j, 512)].reshape(4 * n, 512)
        ).astype(BF)
        return carry

    lax.fori_loop(0, m // 512, grad_wout, 0)
    halves_out.start(0)
    tick(9)
    chunk, half = layout.chunk, 2 * layout.quarter

    def take_kv(here, total):
        c = here.start // chunk
        own[layout.kv + c % half, :, cols(c // half, 2 * local)] = total.astype(BF)

    halves_kv.total(0, take_kv, chunk)
    scatter.relay()

    def grad_wqkv(j, carry):
        @pl.when(j % 2 == 0)
        def _():
            tick(10 + j // 2)

        turned = rows[:, :, cols(j, 256)].reshape(4 * n, 256)

        def inner(i, carry):
            whole_qkv[0, rows_at(j, 256), cols(i, 384)] = dot_c(
                turned, grads[:, :, cols(i, 384)].reshape(4 * n, 384)
            ).astype(BF)
            return carry

        lax.fori_loop(0, width // 384, inner, 0)
        return carry

    lax.fori_loop(0, m // 256, grad_wqkv, 0)
    halves_qkv.start(0)
    tick(13)

    def take_out(here, total):
        own[layout.out + here.start // chunk] = total.astype(BF)

    halves_out.total(0, take_out, chunk)

    def take(here, total):
        land_qkv[0, 0, here] = total.astype(BF)

    halves_qkv.total(0, take, 16)
    stores.append(pltpu.make_async_copy(land_qkv.at[0, 0], o_qkv, store.at[1]))
    stores.append(pltpu.make_async_copy(own.at[pl.ds(layout.kv, layout.qkv - layout.kv)], o_more, store.at[2]))
    for copy in stores[-2:]:
        copy.start()
    tick(14)
    for copy in loads[14:]:
        copy.wait()

    def take_norm(here, total):
        part[t, here] = total.astype(BF)

    scatter.finish(take_norm, 64)

    def frame_block(i, carry):
        here = rows_at(i, 64)
        grad = part[t, here].astype(F32)
        inner, terms = norm_back_block(grad, frames[here].astype(F32), gains[4:5])
        grad_out[here] = grad_out[here] + inner
        return carry[0] + fold(terms), carry[1] + fold(grad)

    zero = jnp.zeros((8, m), F32)
    gain_sum, bias_sum = lax.fori_loop(0, n // 64, frame_block, (zero, zero))
    tick(15)
    sums_out[0:8] = gain_sum
    sums_out[8:16] = bias_sum
    stores += [pltpu.make_async_copy(grad_out, o_frames, store.at[3]), pltpu.make_async_copy(sums_out, o_sums, store.at[4])]
    for copy in stores[-2:]:
        copy.start()
    pump.drain()
    stores.append(pltpu.make_async_copy(held, o_land, store.at[5]))
    stores[-1].start()
    gather.drain()
    for each in (scatter, scatter_m):
        each.drain()
    for each in (halves_qkv, halves_out, halves_kv):
        each.drain(0)
    for copy in stores:
        copy.wait()


def attend_back(
    layout, branch, triple, flat, sums, out, qkv, rows, frames, gains, grad, memory, text, kv, own, land, down, subs
):
    n, m = grad.shape
    width = triple.shape[2]
    local = out.shape[0]
    texts, kvw = text.shape[0], kv.shape[1]
    count = 18 + 3 * (subs - 1)
    v = pltpu.VMEM
    return pl.pallas_call(
        partial(attend_back_kernel, layout),
        name="attend_back",
        out_shape=[
            shape(n, m, kind=F32), shape(16, m, kind=F32), shape(texts, m, kind=F32), shape(m // subs, width),
            shape(layout.qkv - layout.kv, layout.chunk, m), shape(*down.shape), shape(*down.shape),
            shape(4 * layout.quarter, layout.chunk, kvw), shape(*land.shape),
        ],
        in_specs=[ANY] * 16,
        out_specs=[ANY] * 9,
        input_output_aliases={15: 5},
        scratch_shapes=[
            v((4, n, m), BF), v(triple.shape, BF), v(flat.shape, BF), v(sums.shape, F32), v(out.shape, BF), v((m, width), BF),
            v(rows.shape, BF), v(frames.shape, frames.dtype), v(gains.shape, F32), v((n, m), F32), v(memory.shape, BF),
            v(text.shape, BF), v(kv.shape, BF),
            v((6, texts // 2, kvw), BF), v((2, texts // 2, kvw), BF),
            v((4, n, local), BF), v((4, n, 128), F32), v((4, n, width), BF), v((4 * n, local), F32), v((4 * n, local), F32),
            v((4, n, m), BF), v((6, n // 2, m), BF), v((2, n // 2, m), BF),
            v((1, m, width), BF), v((1, subs - 1, m // subs, width), BF),
            v((1, local, m), BF), v((1, subs - 1, local // subs, m), BF),
            v((1, m, kvw), BF), v((1, subs - 1, m // subs, kvw), BF),
            v((texts, m), F32), v((16, m), F32), v((texts, kvw), BF),
            *pump_scratch(layout, layout.qkv),
            dma(17), dma(6), dma(count), dma(count),
        ],
        compiler_params=params(6),
    )(branch, triple, flat, sums, out, qkv, rows, frames, gains, grad, memory, text, kv, own, land, down)


def total_kernel(
    layout,
    feed_in, qkv_in, more_in, cross_q_in, cross_o_in, sums_a_in, sums_b_in, text_in, land_in, part_in, after_in,
    down_in, up_in, kv_in,
    o_qkv, o_cq, o_out, o_co, o_text, o_vectors, o_layer, o_down, o_up, o_kv,
    own, held, ring, result, ring_send, ring_recv, ring_store,
    cross_q, cross_o, land_q, land_o, stage_q, stage_o, part, land_p, stage_p, after,
    sums_a, sums_b, text, text_land, text_full, vectors, vectors_land, share, share_land, load, store, send, recv,
):
    t, x, y, d = neighbours()
    s, subs = lax.axis_index("sub"), lax.axis_size("sub")
    g, groups = lax.axis_index("group"), lax.axis_size("group")
    chunk, m, local = layout.chunk, layout.m, layout.local
    width, quarter = 3 * local, layout.quarter
    at_kv, at_out, at_qkv, at_cq, at_co = layout.kv, layout.out, layout.qkv, layout.cq, layout.co
    def outputs(c, block, slots, act):
        slot = c % RING

        def region(begin, end, copies):
            @pl.when(jnp.logical_and(c >= begin, c < end))
            def _():
                for i, (source, target) in enumerate(copies(c - begin)):
                    act(pltpu.make_async_copy(source, target, slots.at[slot, i]))

        def whole(output):
            return lambda r: [(block, output.at[r])]

        region(0, at_kv // 2, whole(o_down))
        region(at_kv // 2, at_kv, whole(o_up))
        region(
            at_qkv, at_cq,
            lambda r: [
                *((block.at[:, pl.ds(i * local, local)], o_qkv.at[i, r]) for i in range(3)),
                (block.at[:, pl.ds(width, local)], o_qkv.at[r // quarter, 3 * quarter + r % quarter]),
            ],
        )
        region(
            at_kv, at_out,
            lambda r: [
                (block.at[:, pl.ds(2 * i * local, 2 * local)], o_kv.at[2 * i * quarter + r]) for i in range(2)
            ],
        )
        region(at_out, at_qkv, whole(o_out))
        region(
            at_cq, at_co,
            lambda r: [(block.at[:, pl.ds(i * local, local)], o_cq.at[i * quarter + r]) for i in range(4)],
        )
        region(at_co, layout.count, whole(o_co))

    fresh = max(0, layout.later - LAG * (groups - 1))
    newer = max(fresh, at_kv)
    pairs = [
        (land_in, held),
        (more_in.at[pl.ds(newer - at_kv, at_qkv - newer)], own.at[pl.ds(newer, at_qkv - newer)]),
        (qkv_in.at[pl.ds(0, 3 * quarter)], own.at[pl.ds(at_qkv, 3 * quarter), :, pl.ds(0, width)]),
    ]
    for i in range(3):
        pairs.append(
            (
                qkv_in.at[pl.ds(3 * quarter, quarter), :, pl.ds(i * local, local)],
                own.at[pl.ds(at_qkv + i * quarter, quarter), :, pl.ds(width, local)],
            )
        )
    if fresh < at_kv:
        pairs.append((feed_in.at[pl.ds(fresh, at_kv - fresh)], own.at[pl.ds(fresh, at_kv - fresh)]))
    early = len(pairs)
    pairs += [
        (cross_q_in, cross_q), (cross_o_in, cross_o), (sums_a_in, sums_a), (sums_b_in, sums_b), (text_in, text),
        (part_in, part), (after_in, after),
    ]
    loads = [pltpu.make_async_copy(a, b, load.at[i]) for i, (a, b) in enumerate(pairs)]
    for copy in loads:
        copy.start()
    loads[0].wait()
    greet(
        [{"tensor": x}, {"tensor": y}, {"tensor": d}]
        + [{"sub": (s + k) % subs} for k in range(1, subs)]
        + [{"group": (g + k) % groups} for k in range(1, groups)]
    )
    begin, end = layout.later, layout.end
    pump = Pump(own, held, ring, result, ring_send, ring_recv, ring_store, begin, end, layout.count, outputs)

    def run(a, b):
        def step(k, carry):
            pump.step(k)
            return carry

        lax.fori_loop(a, b, step, 0)

    for copy in loads[1:early]:
        copy.wait()
    run(begin, begin + 1)
    for copy in loads[early:-2]:
        copy.wait()
    share_width = m // subs
    for i in range(6):
        source, at = (sums_a, i) if i < 4 else (sums_b, i - 4)
        row = jnp.sum(source[8 * at : 8 * at + 8], 0, keepdims=True)
        for j in range(subs):
            vectors[j, i : i + 1] = row[:, j * share_width : (j + 1) * share_width]
    strip = text.shape[0] // 4

    def remote(source, target, k, device):
        return pltpu.make_async_remote_copy(
            source, target, send.at[k], recv.at[k], device_id=device, device_id_type=MESH
        )

    square = (x, y, d)
    first = [remote(vectors, vectors_land.at[k], k, {"tensor": square[k]}) for k in range(3)]
    first += [
        remote(text.at[rows_at(square[k], strip)], text_land.at[k], 3 + k, {"tensor": square[k]}) for k in range(3)
    ]
    second = [
        remote(share.at[0, (s + k) % subs], share_land.at[k - 1], 5 + k, {"sub": (s + k) % subs}) for k in range(1, subs)
    ]
    base = 5 + subs
    second += [
        remote(text_full.at[rows_at(t, strip)], text_full.at[rows_at(t, strip)], base + k, {"tensor": square[k]}) for k in range(3)
    ]
    base += 3
    third = [
        remote(share.at[1, 0], share_land.at[subs - 2 + k], base + k - 1, {"group": (g + k) % groups})
        for k in range(1, groups)
    ]
    base += groups - 1
    scatter_q = Scatter(cross_q, land_q, stage_q, send, recv, base)
    scatter_o = Scatter(cross_o, land_o, stage_o, send, recv, base + 6)
    for copy in first:
        copy.start()
    scatter_p = Scatter(part, land_p, stage_p, send, recv, base + 12)
    for each in (scatter_q, scatter_o):
        each.diagonal()
        each.along_x()
        each.along_y()

    run(begin + 1, begin + 2)
    for copy in first:
        copy.wait_recv()
    for j in range(subs):
        share[0, j] = vectors[j] + vectors_land[0, j] + vectors_land[1, j] + vectors_land[2, j]
    text_full[rows_at(t, strip)] = text[rows_at(t, strip)] + text_land[0] + text_land[1] + text_land[2]
    for copy in first:
        copy.wait_send()
    for copy in second:
        copy.start()
    run(begin + 2, begin + 3)
    for copy in second:
        copy.wait_recv()
    total = share[0, s]
    for k in range(1, subs):
        total = total + share_land[k - 1]
    share[1, 0] = total
    text_store = pltpu.make_async_copy(text_full, o_text, store.at[0])
    text_store.start()
    for copy in third:
        copy.start()
    scatter_q.relay()
    scatter_o.relay()
    loads[-2].wait()
    loads[-1].wait()
    scatter_p.diagonal()
    scatter_p.along_x()
    scatter_p.along_y()
    run(begin + 3, at_cq)

    def take_q(rows, value):
        row = rows.start
        c = row // chunk
        own[at_cq + c % quarter, :, cols(c // quarter, local)] = value.astype(BF)

    scatter_q.finish(take_q, chunk)
    run(at_cq, at_co)
    step = min(chunk, scatter_o.half)

    def take_o(rows, value):
        own[at_co + rows.start // chunk, rows_at(rows.start % chunk // step, step)] = value.astype(BF)

    scatter_o.finish(take_o, step)
    run(at_co, layout.count)
    scatter_p.relay()
    run(layout.count, end)

    def take_layer(rows, value):
        after[rows] = after[rows] + value

    scatter_p.finish(take_layer, 64)
    layer_store = pltpu.make_async_copy(after, o_layer, store.at[2])
    layer_store.start()
    for copy in third:
        copy.wait_recv()
    total = share[1, 0]
    for k in range(1, groups):
        total = total + share_land[subs - 2 + k]
    share[2, 0] = total
    vector_store = pltpu.make_async_copy(share.at[2, 0], o_vectors, store.at[1])
    vector_store.start()
    for copy in second + third:
        copy.wait_send()
    for each in (scatter_q, scatter_o, scatter_p):
        each.drain()
    pump.drain()
    layer_store.wait()
    text_store.wait()
    vector_store.wait()


def total(layout, pieces, qkv, more, cross_q, cross_o, sums_a, sums_b, text, land, part, after, down, up, kv, subs, groups):
    m, chunk = layout.m, layout.chunk
    n = after.shape[0]
    v = pltpu.VMEM
    sems = 7 + subs + groups + 18
    qkv = qkv.reshape(-1, chunk, qkv.shape[1])
    piece_q, piece_o = cross_q.shape[1:], cross_o.shape[1:]
    out_shape = shape(layout.qkv - layout.out, chunk, m)
    return pl.pallas_call(
        partial(total_kernel, layout),
        name="total",
        out_shape=[
            shape(3, *qkv.shape[:2], layout.local), shape(layout.piece // chunk, chunk, layout.local), out_shape, out_shape,
            shape(*text.shape, kind=F32), shape(8, m // subs, kind=F32), shape(n, m, kind=F32),
            shape(*down.shape), shape(*up.shape), shape(*kv.shape),
        ],
        in_specs=[ANY] * 14,
        out_specs=[ANY] * 10,
        input_output_aliases={11: 7, 12: 8, 13: 9},
        scratch_shapes=[
            *pump_scratch(layout, layout.count),
            v(cross_q.shape, BF), v(cross_o.shape, BF),
            v((6, piece_q[0] // 2, piece_q[1]), BF), v((6, piece_o[0] // 2, piece_o[1]), BF),
            v((2, piece_q[0] // 2, piece_q[1]), BF), v((2, piece_o[0] // 2, piece_o[1]), BF),
            v((4, n, m), BF), v((6, n // 2, m), BF), v((2, n // 2, m), BF), v((n, m), F32),
            v(sums_a.shape, F32), v(sums_b.shape, F32), v(text.shape, F32),
            v((3, text.shape[0] // 4, m), F32), v(text.shape, F32), v((subs, 8, m // subs), F32), v((3, subs, 8, m // subs), F32),
            v((3, subs, 8, m // subs), F32), v((subs - 1 + groups - 1, 8, m // subs), F32),
            dma(14), dma(3), dma(sems), dma(sems),
        ],
        compiler_params=params(7),
    )(pieces, qkv, more, cross_q, cross_o, sums_a, sums_b, text, land, part, after, down, up, kv)


def local(
    frames, text_states, selfgain, selfbias, selfqkv, selfout, crossgain, crossbias, crossquery, crosskv, crossout,
    feedgain, feedbias, feedup, feeddown, cotangent,
):
    subs, groups = lax.axis_size("sub"), lax.axis_size("group")
    m = frames.shape[2]
    width = selfout.shape[0]
    qkv = selfqkv.transpose(1, 0, 2)
    kv = crosskv.reshape(m, 2 * width)
    gains = jnp.concatenate([crossgain, crossbias, feedgain, feedbias, selfgain, selfbias]).reshape(6, m)
    rows, triple, memory = enter(frames[0], gains, qkv, text_states[0], kv)
    flat, sums, after_self, wq, wo = attend(triple, selfout, frames[0], crossquery, crossout, subs, groups)
    wo = wo.reshape(4 * width, m)
    query, cross_flat, after_cross, feed_rows, grads = cross(after_self, gains, wq, wo, memory, cotangent[0])
    layout = Layout(m, width, subs, groups)
    part, norm_grad, pieces = feed(feed_rows, grads, feedup, feeddown, subs)
    pieces = pieces.reshape(-1, layout.chunk, m)
    grad_out, branch, sums_a, memory_grad, piece_q, piece_o, down, land = cross_back(
        layout, cotangent[0], norm_grad, after_cross, after_self, gains, query, cross_flat, memory, wq, wo, pieces, subs
    )
    frame_grad, sums_b, text_part, grad_qkv, more, down, up, full_kv, land = attend_back(
        layout, branch, triple, flat, sums, selfout, qkv, rows, frames[0], gains, grad_out, memory_grad,
        text_states[0], kv, pieces, land, down, subs,
    )
    full_qkv, full_cq, full_out, full_co, text_grad, vectors, layer_output, down, up, full_kv = total(
        layout, pieces, grad_qkv, more, piece_q, piece_o, sums_a, sums_b, text_part, land, part, after_cross,
        down, up, full_kv, subs, groups,
    )
    return (
        layer_output[None],
        frame_grad[None],
        text_grad[None],
        vectors[4],
        vectors[5],
        full_qkv.astype(F32).reshape(3, -1, width).transpose(1, 0, 2),
        full_out.astype(F32).reshape(-1, m),
        vectors[2],
        vectors[3],
        full_cq.astype(F32).reshape(-1, width),
        full_kv.astype(F32).reshape(-1, 2, width),
        full_co.astype(F32).reshape(-1, m),
        vectors[0],
        vectors[1],
        up.astype(F32).reshape(-1, m),
        down.astype(F32).reshape(-1, m),
    )


def solution(mesh):
    clips = P(("sub", "group"), "tensor", None)
    whole = P(("sub", "group"), None, None)
    narrow, wide = P("tensor", None), P(None, "tensor")
    third = P(None, None, "tensor")
    vector = P("sub")
    return jax.shard_map(
        local,
        mesh=mesh,
        in_specs=(
            clips, whole, P(), P(), third, narrow, P(), P(), wide, third, narrow, P(), P(), wide, narrow, clips,
        ),
        out_specs=(
            clips, clips, whole, vector, vector, P("sub", None, "tensor"), P(("tensor", "sub"), None), vector, vector,
            P("sub", "tensor"), P("sub", None, "tensor"), P(("tensor", "sub"), None), vector, vector,
            P("sub", "tensor"), P(("tensor", "sub"), None),
        ),
        check_vma=False,
    )
```

```python
from functools import partial

import jax
import jax.numpy as jnp
from jax import lax
from jax.experimental import pallas as pl
from jax.experimental.pallas import tpu as pltpu
from jax.sharding import PartitionSpec as P

HEAD = 64
EPSILON = 1e-05
NEG_BIG = -1e30
LOG2E = 1.4426950408889634
MESH = pl.DeviceIdType.MESH
F32 = jnp.float32
BF = jnp.bfloat16
ANY = pl.BlockSpec(memory_space=pl.ANY)
VMEM_LIMIT = 63 << 20


def neighbours():
    t = lax.axis_index("tensor")
    return t, t + 1 - 2 * (t % 2), (t + 2) % 4, 3 - t


def greet(targets):
    barrier = pltpu.get_barrier_semaphore()
    for target in targets:
        pl.semaphore_signal(barrier, inc=1, device_id=target, device_id_type=MESH)
    pl.semaphore_wait(barrier, len(targets))


def dot(a, b):
    return lax.dot_general(a, b, (((1,), (0,)), ((), ())), preferred_element_type=F32)


def dot_t(a, b):
    return lax.dot_general(a, b, (((1,), (1,)), ((), ())), preferred_element_type=F32)


def dot_c(a, b):
    return lax.dot_general(a, b, (((0,), (0,)), ((), ())), preferred_element_type=F32)


def cols(j, width):
    return pl.ds(pl.multiple_of(j * width, width), width)


def rows_at(j, height):
    return pl.ds(pl.multiple_of(j * height, height), height)


def split(count):
    first = (count // 2 + 15) // 16 * 16
    return pl.ds(0, first), pl.ds(first, count - first)


class Gather:
    def __init__(self, own, dst, send, recv, base, halves=None):
        self.own, self.dst, self.send, self.recv, self.base = own, dst, send, recv, base
        self.halves = halves or split(own.shape[0])

    def copy(self, k):
        t, x, y, _ = neighbours()
        first, second = self.halves
        half = (first, second, second, first, first, second)[k]
        place = (t, t, t, t, x, y)[k]
        target = (x, y, x, y, y, x)[k]
        source = self.own.at[half] if k < 4 else self.dst.at[place, half]
        return pltpu.make_async_remote_copy(
            source,
            self.dst.at[place, half],
            self.send.at[self.base + k],
            self.recv.at[self.base + k],
            device_id={"tensor": target},
            device_id_type=MESH,
        )

    def start(self):
        for k in range(4):
            self.copy(k).start()

    def relay_x(self):
        self.copy(0).wait_recv()
        self.copy(4).start()

    def relay_y(self):
        self.copy(1).wait_recv()
        self.copy(5).start()

    def have_x(self):
        self.copy(2).wait_recv()

    def have_y(self):
        self.copy(3).wait_recv()

    def have_d(self):
        self.copy(4).wait_recv()
        self.copy(5).wait_recv()

    def drain(self):
        for k in range(6):
            self.copy(k).wait_send()


class Scatter:
    def __init__(self, part, land, stage, send, recv, base):
        self.part, self.land, self.stage = part, land, stage
        self.send, self.recv, self.base = send, recv, base
        self.half = part.shape[1] // 2

    def copy(self, k):
        t, x, y, d = neighbours()
        low, high = pl.ds(0, self.half), pl.ds(self.half, self.half)
        source = (
            self.part.at[d, low],
            self.part.at[d, high],
            self.part.at[x, low],
            self.stage.at[1],
            self.part.at[y, high],
            self.stage.at[0],
        )[k]
        target = (x, y, x, x, y, y)[k]
        return pltpu.make_async_remote_copy(
            source,
            self.land.at[k],
            self.send.at[self.base + k],
            self.recv.at[self.base + k],
            device_id={"tensor": target},
            device_id_type=MESH,
        )

    def diagonal(self):
        self.copy(0).start()
        self.copy(1).start()

    def along_x(self):
        self.copy(2).start()

    def along_y(self):
        self.copy(4).start()

    def relay(self):
        t, x, y, d = neighbours()
        low, high = pl.ds(0, self.half), pl.ds(self.half, self.half)
        self.copy(0).wait_recv()
        self.stage[0] = (self.part[y, low].astype(F32) + self.land[0].astype(F32)).astype(BF)
        self.copy(5).start()
        self.copy(1).wait_recv()
        self.stage[1] = (self.part[x, high].astype(F32) + self.land[1].astype(F32)).astype(BF)
        self.copy(3).start()

    def finish(self, take, step):
        t, x, y, d = neighbours()
        for k in (2, 4, 5, 3):
            self.copy(k).wait_recv()
        for base, a, b in ((0, 2, 5), (self.half, 4, 3)):

            def block(i, carry, base=base, a=a, b=b):
                here = rows_at(i, step)
                rows = pl.ds(pl.multiple_of(base + i * step, step), step)
                take(
                    rows,
                    self.part[t, rows].astype(F32)
                    + self.land[a, here].astype(F32)
                    + self.land[b, here].astype(F32),
                )
                return carry

            lax.fori_loop(0, self.half // step, block, 0)

    def drain(self):
        for k in range(6):
            self.copy(k).wait_send()


def normed_rows(values):
    centre = values - jnp.mean(values, -1, keepdims=True)
    inverse = lax.rsqrt(jnp.mean(centre * centre, -1, keepdims=True) + EPSILON)
    return centre * inverse, inverse


def params(cid, **more):
    return pltpu.CompilerParams(
        collective_id=cid, has_side_effects=True, vmem_limit_bytes=VMEM_LIMIT, **more
    )


def dma(count):
    return pltpu.SemaphoreType.DMA((count,))


def shape(*dims, kind=BF):
    return jax.ShapeDtypeStruct(dims, kind)


LAG = 2
RING = 4


def either(condition, other):
    return jnp.logical_and(condition, other)


class Pump:
    def __init__(self, own, land, ring, result, send, recv, store, first, last, count, outputs):
        self.own, self.land, self.ring, self.result = own, land, ring, result
        self.send, self.recv, self.store = send, recv, store
        self.first, self.last, self.count, self.outputs = first, last, count, outputs
        self.window = land.shape[1]
        self.g, self.n = lax.axis_index("group"), lax.axis_size("group")

    def copy(self, way, c):
        target = (self.g + 1) % self.n if way == 0 else (self.g + self.n - 1) % self.n
        return pltpu.make_async_remote_copy(
            self.ring.at[way, c % RING],
            self.land.at[way, c % self.window],
            self.send.at[way, c % RING],
            self.recv.at[way, c % self.window],
            device_id={"group": target},
            device_id_type=MESH,
        )

    def flow(self, way, k):
        place = self.g if way == 0 else self.n - 1 - self.g
        c = k - LAG * place

        @pl.when(either(c >= 0, c < self.count))
        def _():
            @pl.when(either(place > 0, k - LAG >= self.first))
            def _():
                self.copy(way, c).wait_recv()

            @pl.when(place < self.n - 1)
            def _():
                @pl.when(either(c >= RING, k - RING >= self.first))
                def _():
                    self.copy(way, c - RING).wait_send()

                @pl.when(place > 0)
                def _():
                    self.fill(self.ring.at[way, c % RING], (self.own.at[c], self.land.at[way, c % self.window]))

                @pl.when(place == 0)
                def _():
                    self.fill(self.ring.at[way, c % RING], (self.own.at[c],))

                self.copy(way, c).start()

    def fill(self, target, terms):
        def block(i, carry):
            here = rows_at(i, 48)
            value = terms[0][here].astype(F32)
            for term in terms[1:]:
                value = value + term[here].astype(F32)
            target[here] = value.astype(BF)
            return carry

        lax.fori_loop(0, target.shape[0] // 48, block, 0)

    def finished(self, k):
        far = jnp.maximum(self.g, self.n - 1 - self.g)
        return k - LAG * far

    def step(self, k):
        self.flow(0, k)
        self.flow(1, k)
        f = self.finished(k)

        @pl.when(either(f >= 0, f < self.count))
        def _():
            @pl.when(either(f >= RING, k - RING >= self.first))
            def _():
                self.outputs(f - RING, self.result.at[f % RING], self.store, lambda copy: copy.wait())

            slot, held = f % RING, f % self.window
            mine, target = self.own.at[f], self.result.at[slot]

            @pl.when(either(self.g > 0, self.g < self.n - 1))
            def _():
                self.fill(target, (mine, self.land.at[0, held], self.land.at[1, held]))

            @pl.when(self.g == 0)
            def _():
                self.fill(target, (mine, self.land.at[1, held]))

            @pl.when(self.g == self.n - 1)
            def _():
                self.fill(target, (mine, self.land.at[0, held]))

            self.outputs(f, self.result.at[slot], self.store, lambda copy: copy.start())

    def drain(self):
        for way in range(2):
            place = self.g if way == 0 else self.n - 1 - self.g
            top = jnp.minimum(self.last - LAG * place, self.count)
            for j in range(1, RING + 1):
                c = top - j

                @pl.when(either(place < self.n - 1, either(c >= 0, c + LAG * place >= self.first)))
                def _(way=way, c=c):
                    self.copy(way, c).wait_send()

            for k in range(max(self.first, self.last - LAG), self.last):
                c = k - LAG * (place - 1)

                @pl.when(either(place > 0, either(c >= 0, c < self.count)))
                def _(way=way, c=c):
                    self.copy(way, c).wait_recv()

        far = jnp.maximum(self.g, self.n - 1 - self.g)
        top = jnp.minimum(self.last - LAG * far, self.count)
        for j in range(1, RING + 1):
            f = top - j

            @pl.when(either(f >= 0, f + LAG * far >= self.first))
            def _(f=f):
                self.outputs(f, self.result.at[f % RING], self.store, lambda copy: copy.wait())


KV_TICKS, OUT_TICKS = 10, 14


class Layout:
    def __init__(self, m, local, subs, groups):
        piece = m // subs
        self.m, self.piece, self.local = m, piece, local
        self.out_rows = local // subs
        self.chunk = 96 if piece % 384 == 0 and self.out_rows % 96 == 0 else 48
        quarter = piece // 4 // self.chunk
        self.quarter = quarter
        self.feed_count = 2 * piece // self.chunk
        self.kv = self.feed_count
        self.out = self.kv + 2 * quarter
        self.qkv = self.out + self.out_rows // self.chunk
        self.cq = self.qkv + 3 * quarter
        self.co = self.cq + quarter
        self.count = self.co + self.out_rows // self.chunk
        self.window = LAG * groups
        self.end = self.count + LAG * (groups - 1)
        self.middle = min(6, self.feed_count // 2 - 2)
        self.later = self.feed_count
        if self.middle + KV_TICKS <= self.kv and self.middle + OUT_TICKS <= self.out:
            self.later = self.middle + OUT_TICKS + 2


def sum_outputs(layout, halves, text=None):
    def outputs(c, block, store, act):
        count = layout.feed_count // 2
        for i, half in enumerate(halves):

            @pl.when(either(c >= i * count, c < (i + 1) * count))
            def _(i=i, half=half):
                act(pltpu.make_async_copy(block, half.at[c - i * count], store.at[c % RING, 0]))

        if text is not None:

            @pl.when(either(c >= layout.kv, c < layout.out))
            def _():
                for i in range(2):
                    lanes = pl.ds(2 * i * layout.local, 2 * layout.local)
                    target = text.at[2 * i * layout.quarter + c - layout.kv]
                    act(pltpu.make_async_copy(block.at[:, lanes], target, store.at[c % RING, i]))

    return outputs


def pump_scratch(layout, count):
    chunk, m = layout.chunk, layout.m
    return [
        pltpu.VMEM((count, chunk, m), BF),
        pltpu.VMEM((2, layout.window, chunk, m), BF),
        pltpu.VMEM((2, RING, chunk, m), BF),
        pltpu.VMEM((RING, chunk, m), BF),
        pltpu.SemaphoreType.DMA((2, RING)),
        pltpu.SemaphoreType.DMA((2, layout.window)),
        pltpu.SemaphoreType.DMA((RING, 4)),
    ]


def group_ring():
    g, n = lax.axis_index("group"), lax.axis_size("group")
    return [{"group": (g + 1) % n}, {"group": (g + n - 1) % n}]


def enter_kernel(
    frames, gains, qkv, text, kv, o_rows, o_triple, o_memory,
    v_frames, v_gains, v_qkv, v_text, v_kv, rows, triple, memory, load, store, send, recv,
):
    t, x, y, d = neighbours()
    loads = [
        pltpu.make_async_copy(a, b, load.at[i])
        for i, (a, b) in enumerate(
            (
                (frames, v_frames), (gains, v_gains), (text, v_text), (kv, v_kv),
                *((qkv.at[i], v_qkv.at[:, pl.ds(i * qkv.shape[2], qkv.shape[2])]) for i in range(3)),
            )
        )
    ]
    for copy in loads:
        copy.start()
    greet([{"tensor": x}, {"tensor": y}])
    for copy in loads[:2]:
        copy.wait()
    count, width = v_qkv.shape
    block = 384

    def norm_block(i, carry):
        here = rows_at(i, 64)
        hat, _ = normed_rows(v_frames[here].astype(F32))
        rows[t, here] = (hat * v_gains[4:5] + v_gains[5:6]).astype(BF)
        return carry

    lax.fori_loop(0, v_frames.shape[0] // 64, norm_block, 0)
    gather = Gather(rows.at[t], rows, send, recv, 0)
    gather.start()
    texts = Gather(memory.at[t], memory, send, recv, 6)

    def project(place):
        def step(j, carry):
            triple[place, :, cols(j, block)] = dot(rows[place], v_qkv[:, cols(j, block)]).astype(BF)
            return carry

        lax.fori_loop(0, width // block, step, 0)

    def put(k, place):
        a = pltpu.make_async_copy(rows.at[place], o_rows.at[place], store.at[2 * k])
        b = pltpu.make_async_copy(triple.at[place], o_triple.at[place], store.at[2 * k + 1])
        a.start()
        b.start()
        return [a, b]

    loads[2].wait()
    loads[3].wait()

    def texts_step(j, carry):
        memory[t, :, cols(j, block)] = dot(v_text[...], v_kv[:, cols(j, block)]).astype(BF)
        return carry

    lax.fori_loop(0, v_kv.shape[1] // block, texts_step, 0)
    texts.start()
    for copy in loads[4:]:
        copy.wait()
    project(t)
    stores = put(0, t)
    gather.relay_x()
    gather.relay_y()
    gather.have_x()
    project(x)
    stores += put(1, x)
    gather.have_y()
    project(y)
    stores += put(2, y)
    texts.relay_x()
    texts.relay_y()
    texts.have_x()
    texts.have_y()
    gather.have_d()
    project(d)
    stores += put(3, d)
    texts.have_d()
    last = pltpu.make_async_copy(memory, o_memory, store.at[8])
    last.start()
    gather.drain()
    texts.drain()
    for copy in stores:
        copy.wait()
    last.wait()


def enter(frames, gains, qkv, text, kv):
    n, m = frames.shape
    width, texts, kvw = 3 * qkv.shape[2], text.shape[0], kv.shape[1]
    return pl.pallas_call(
        enter_kernel,
        name="enter",
        out_shape=[shape(4, n, m), shape(4, n, width), shape(4, texts, kvw)],
        in_specs=[ANY] * 5,
        out_specs=[ANY] * 3,
        scratch_shapes=[
            pltpu.VMEM((n, m), frames.dtype), pltpu.VMEM(gains.shape, F32),
            pltpu.VMEM((m, width), BF), pltpu.VMEM(text.shape, BF), pltpu.VMEM(kv.shape, BF),
            pltpu.VMEM((4, n, m), BF), pltpu.VMEM((4, n, width), BF), pltpu.VMEM((4, texts, kvw), BF),
            dma(7), dma(9), dma(12), dma(12),
        ],
        compiler_params=params(1),
    )(frames, gains, qkv, text, kv)


def head_lanes(rows):
    return lax.broadcasted_iota(jnp.int32, (rows, 128), 1)


def attend_rows(triple, place, blocks, heads, flat, sums):
    n = triple.shape[1]
    width = heads * HEAD
    scale = HEAD ** (-0.5) * LOG2E
    lanes = head_lanes(n)

    def pair(p, stats):
        here = pl.ds(pl.multiple_of(p * 128, 128), 128)
        key_cols = pl.ds(pl.multiple_of(width + p * 128, 128), 128)
        value_cols = pl.ds(pl.multiple_of(2 * width + p * 128, 128), 128)
        query = triple[place, :, here]
        keys = triple[0:blocks, :, key_cols].reshape(blocks * n, 128)
        values = triple[0:blocks, :, value_cols].reshape(blocks * n, 128)
        outs = []
        for h in range(2):
            mine = (lanes < HEAD) if h == 0 else (lanes >= HEAD)
            scores = dot_t(jnp.where(mine, query, jnp.zeros_like(query)), keys)
            row = lax.broadcasted_iota(jnp.int32, scores.shape, 0)
            col = lax.broadcasted_iota(jnp.int32, scores.shape, 1)
            scores = jnp.where(col <= row + (blocks - 1) * n, scores, NEG_BIG)
            peak = jnp.max(scores, -1, keepdims=True) * scale
            exponent = jnp.exp2(scores * scale - peak)
            total = jnp.sum(exponent, -1, keepdims=True)
            outs.append(dot(exponent.astype(BF), values) / total)
            stats = jnp.where(lanes == 2 * p + h, peak + jnp.log2(total), stats)
        flat[place, :, here] = jnp.where(lanes < HEAD, outs[0], outs[1]).astype(BF)
        return stats

    sums[place] = lax.fori_loop(0, heads // 2, pair, jnp.zeros((n, 128), F32))


def attend_kernel(
    triple_in, out_in, frames_in, wq, wo, o_flat, o_sums, o_after, o_wq, o_wo,
    triple, v_out, v_frames, flat, sums, after, part, land, stage, v_wq, v_wo, load, store, send, recv, side,
):
    t, x, y, d = neighbours()
    s = lax.axis_index("sub")
    subs = lax.axis_size("sub")
    g, groups = lax.axis_index("group"), lax.axis_size("group")
    n = triple.shape[1]
    m = v_out.shape[1]
    heads = v_out.shape[0] // HEAD
    loads = [
        pltpu.make_async_copy(a, b, load.at[i])
        for i, (a, b) in enumerate(
            ((triple_in, triple), (out_in, v_out), (frames_in, v_frames), (wq, v_wq), (wo, v_wo))
        )
    ]
    for copy in loads:
        copy.start()
    greet(
        [{"tensor": x}, {"tensor": y}]
        + [{"sub": (s + k) % subs} for k in range(1, subs)]
        + [{"group": (g + k) % groups} for k in range(1, groups)]
    )
    scatter = Scatter(part, land, stage, send, recv, 0)
    gathers = []
    for i, (weight, full) in enumerate(((wq, o_wq), (wo, o_wo))):
        piece = weight.shape[0] // subs
        strips = groups if i == 0 and piece % (32 * groups) == 0 else 1
        strip = piece // strips
        first, second = split(strip)
        offset = pl.multiple_of(s * piece, piece)
        begin = pl.multiple_of(offset + (g * strip if strips > 1 else 0), strip)
        halves = (
            pl.ds(begin, first.size),
            pl.ds(pl.multiple_of(begin + first.size, 16), second.size),
        )
        gathers.append((Gather(weight, full, send, recv, 6 + 6 * i, halves), full, pl.ds(offset, piece)))
        if i == 0:
            mine = pl.ds(begin, strip)
            spread = [(j, k) for j in range(3) for k in range(1, groups)] if strips > 1 else []

    def shared(i, j, k):
        _, full, piece = gathers[i]
        place = (x, y, d)[j]
        slot = (i * 3 + j) * (subs - 1) + k - 1
        return pltpu.make_async_remote_copy(
            full.at[place, piece], full.at[place, piece],
            send.at[18 + slot], recv.at[18 + slot],
            device_id={"sub": (s + k) % subs}, device_id_type=MESH,
        )

    def stripped(j, k):
        place = (x, y, d)[j]
        slot = 18 + 6 * (subs - 1) + j * (groups - 1) + k - 1
        return pltpu.make_async_remote_copy(
            o_wq.at[place, mine], o_wq.at[place, mine], send.at[slot], recv.at[slot],
            device_id={"group": (g + k) % groups}, device_id_type=MESH,
        )

    (query_gather, _, _), (out_gather, _, _) = gathers
    query_gather.start()
    for copy in loads[:2]:
        copy.wait()

    def one(i, carry):
        far_y = 1 - i // 2
        far_x = 1 - i % 2
        place = (t // 2 + far_y - 2 * (t // 2) * far_y) * 2 + (t % 2 + far_x - 2 * (t % 2) * far_x)

        @pl.when(i == 1)
        def _():
            query_gather.relay_x()
            query_gather.relay_y()
            out_gather.start()

        @pl.when(i == 2)
        def _():
            query_gather.have_x()
            query_gather.have_y()
            query_gather.have_d()
            for j, k in spread:
                stripped(j, k).start()

        for blocks in range(1, 5):

            @pl.when(place == blocks - 1)
            def _(blocks=blocks):
                attend_rows(triple, blocks - 1, blocks, heads, flat, sums)

        def out_step(j, carry):
            part[place, :, cols(j, 512)] = dot(flat[place], v_out[:, cols(j, 512)]).astype(BF)
            return carry

        lax.fori_loop(0, m // 512, out_step, 0)

        @pl.when(i == 0)
        def _():
            scatter.diagonal()

        @pl.when(i == 1)
        def _():
            scatter.along_y()

        @pl.when(i == 2)
        def _():
            scatter.along_x()

        return carry

    lax.fori_loop(0, 4, one, 0)
    out_gather.relay_x()
    out_gather.relay_y()
    stores = [
        pltpu.make_async_copy(flat, o_flat, store.at[0]),
        pltpu.make_async_copy(sums, o_sums, store.at[1]),
    ]
    loads[3].wait()
    loads[4].wait()
    stores += [
        pltpu.make_async_copy(v_wq, o_wq.at[t], store.at[2]),
        pltpu.make_async_copy(v_wo, o_wo.at[t], store.at[3]),
    ]
    for copy in stores:
        copy.start()
    scatter.relay()
    loads[2].wait()

    def take(rows, total):
        after[rows] = v_frames[rows].astype(F32) + total

    scatter.finish(take, 64)
    last = pltpu.make_async_copy(after, o_after, store.at[4])
    last.start()
    out_gather.have_x()
    out_gather.have_y()
    out_gather.have_d()
    for j in range(3):
        for k in range(1, subs):
            shared(1, j, k).start()
    for j, k in spread:
        stripped(j, k).wait_recv()
    for j in range(3):
        for k in range(1, subs):
            shared(0, j, k).start()
    scatter.drain()
    for j, k in spread:
        stripped(j, k).wait_send()
    for i, (gather, _, _) in enumerate(gathers):
        gather.drain()
        for j in range(3):
            for k in range(1, subs):
                shared(i, j, k).wait()
    for copy in stores:
        copy.wait()
    last.wait()


def attend(triple, out, frames, wq, wo, subs, groups):
    _, n, width = triple.shape
    local, m = out.shape
    extra = 18 + 6 * (subs - 1) + 3 * (groups - 1)
    return pl.pallas_call(
        attend_kernel,
        name="attend",
        out_shape=[
            shape(4, n, local), shape(4, n, 128, kind=F32), shape(n, m, kind=F32),
            shape(4, *wq.shape), shape(4, *wo.shape),
        ],
        in_specs=[ANY] * 5,
        out_specs=[ANY] * 5,
        scratch_shapes=[
            pltpu.VMEM((4, n, width), BF), pltpu.VMEM((local, m), BF), pltpu.VMEM((n, m), frames.dtype),
            pltpu.VMEM((4, n, local), BF), pltpu.VMEM((4, n, 128), F32), pltpu.VMEM((n, m), F32),
            pltpu.VMEM((4, n, m), BF), pltpu.VMEM((6, n // 2, m), BF), pltpu.VMEM((2, n // 2, m), BF),
            pltpu.VMEM(wq.shape, BF), pltpu.VMEM(wo.shape, BF),
            dma(5), dma(5), dma(extra), dma(extra), dma(1),
        ],
        compiler_params=params(2),
    )(triple, out, frames, wq, wo)


def stack_pair(block, rows):
    lanes = head_lanes(rows)
    zero = jnp.zeros_like(block)
    return jnp.concatenate([jnp.where(lanes < HEAD, block, zero), jnp.where(lanes >= HEAD, block, zero)], 0)


def pair_softmax(query, keys):
    scale = HEAD ** (-0.5) * LOG2E
    scores = dot_t(query, keys)
    left = head_lanes(scores.shape[0]) < HEAD
    low = jnp.max(jnp.where(left, scores, -jnp.inf), -1, keepdims=True)
    high = jnp.max(jnp.where(left, -jnp.inf, scores), -1, keepdims=True)
    exponent = jnp.exp2((scores - jnp.where(left, low, high)) * scale)
    total = pair_sum(exponent, left)
    return exponent / total, left


def pair_sum(values, left):
    low = jnp.sum(jnp.where(left, values, 0.0), -1, keepdims=True)
    high = jnp.sum(jnp.where(left, 0.0, values), -1, keepdims=True)
    return jnp.where(left, low, high)


def cross_kernel(
    after_in, gains_in, wq_in, wo_in, memory_in, cot_in,
    o_query, o_flat, o_after, o_rows, o_grads,
    after, gains, wq, wo, memory, cot, rows, query, flat, result, feed, grads, load, store, send, recv,
):
    t, x, y, d = neighbours()
    loads = [
        pltpu.make_async_copy(a, b, load.at[i])
        for i, (a, b) in enumerate(
            ((cot_in, cot), (after_in, after), (gains_in, gains), (wq_in, wq), (memory_in, memory), (wo_in, wo))
        )
    ]
    for copy in loads:
        copy.start()
    greet([{"tensor": x}, {"tensor": y}])
    n, m = after.shape
    width = wq.shape[2]
    texts = memory.shape[1]
    loads[0].wait()

    def round_block(i, carry):
        here = rows_at(i, 64)
        grads[t, here] = cot[here].astype(BF)
        return carry

    lax.fori_loop(0, n // 64, round_block, 0)
    gather = Gather(grads.at[t], grads, send, recv, 0)
    gather.start()
    loads[1].wait()
    loads[2].wait()

    def norm_block(i, carry):
        here = rows_at(i, 64)
        hat, _ = normed_rows(after[here])
        rows[here] = (hat * gains[0:1] + gains[1:2]).astype(BF)
        return carry

    lax.fori_loop(0, n // 64, norm_block, 0)
    loads[3].wait()
    loads[4].wait()

    def quarter(q, carry):
        query[:, cols(q, width)] = dot(rows[...], wq[q]).astype(BF)

        def pair(p, carry):
            keys = stack_pair(memory[q, :, cols(p, 128)], texts)
            values = stack_pair(memory[q, :, pl.ds(pl.multiple_of(width + p * 128, 128), 128)], texts)
            here = pl.ds(pl.multiple_of(q * width + p * 128, 128), 128)
            probs, _ = pair_softmax(query[:, here], keys)
            flat[:, here] = dot(probs.astype(BF), values).astype(BF)
            return carry

        lax.fori_loop(0, width // 128, pair, 0)
        return carry

    lax.fori_loop(0, 4, quarter, 0)
    gather.relay_x()
    gather.relay_y()
    stores = [pltpu.make_async_copy(query, o_query, store.at[0]), pltpu.make_async_copy(flat, o_flat, store.at[1])]
    loads[5].wait()

    def out_step(j, carry):
        result[:, cols(j, 512)] = after[:, cols(j, 512)] + dot(flat[...], wo[:, cols(j, 512)])
        return carry

    lax.fori_loop(0, m // 512, out_step, 0)

    def feed_block(i, carry):
        here = rows_at(i, 64)
        hat, _ = normed_rows(result[here])
        feed[here] = (hat * gains[2:3] + gains[3:4]).astype(BF)
        return carry

    lax.fori_loop(0, n // 64, feed_block, 0)
    stores += [pltpu.make_async_copy(result, o_after, store.at[2]), pltpu.make_async_copy(feed, o_rows, store.at[3])]
    for copy in stores:
        copy.start()
    gather.have_x()
    gather.have_y()
    gather.have_d()
    last = pltpu.make_async_copy(grads, o_grads, store.at[4])
    last.start()
    gather.drain()
    for copy in stores:
        copy.wait()
    last.wait()


def cross(after, gains, wq, wo, memory, cot):
    n, m = after.shape
    return pl.pallas_call(
        cross_kernel,
        name="cross",
        out_shape=[shape(n, m), shape(n, m), shape(n, m, kind=F32), shape(n, m), shape(4, n, m)],
        in_specs=[ANY] * 6,
        out_specs=[ANY] * 5,
        scratch_shapes=[
            pltpu.VMEM((n, m), F32), pltpu.VMEM(gains.shape, F32), pltpu.VMEM(wq.shape, BF), pltpu.VMEM(wo.shape, BF),
            pltpu.VMEM(memory.shape, BF), pltpu.VMEM((n, m), F32), pltpu.VMEM((n, m), BF), pltpu.VMEM((n, m), BF),
            pltpu.VMEM((n, m), BF), pltpu.VMEM((n, m), F32), pltpu.VMEM((n, m), BF), pltpu.VMEM((4, n, m), BF),
            dma(6), dma(5), dma(6), dma(6),
        ],
        compiler_params=params(3),
    )(after, gains, wq, wo, memory, cot)


def gelu_both(pre):
    size = jnp.abs(pre) * 0.7071067811865476
    rate = 1.0 / (1.0 + 0.3275911 * size)
    bell = jnp.exp2(pre * pre * (-0.5 * LOG2E))
    series = rate * (
        0.254829592
        + rate * (-0.284496736 + rate * (1.421413741 + rate * (-1.453152027 + rate * 1.061405429)))
    )
    tail = 0.5 * series * bell
    gate = jnp.where(pre >= 0, 1.0 - tail, tail)
    return pre * gate, gate + pre * (0.3989422804014327 * bell)


class Halves:
    def __init__(self, whole, land, send, recv, base):
        self.whole, self.land, self.send, self.recv, self.base = whole, land, send, recv, base
        self.subs = lax.axis_size("sub")
        self.piece = whole.shape[1] // self.subs

    def copies(self, w):
        s = lax.axis_index("sub")
        made = []
        for k in range(1, self.subs):
            target = (s + k) % self.subs
            slot = w * (self.subs - 1) + k - 1
            made.append(
                pltpu.make_async_remote_copy(
                    self.whole.at[w, rows_at(target, self.piece)],
                    self.land.at[w, k - 1],
                    self.send.at[self.base + slot],
                    self.recv.at[self.base + slot],
                    device_id={"sub": target},
                    device_id_type=MESH,
                )
            )
        return made

    def start(self, w):
        for copy in self.copies(w):
            copy.start()

    def total(self, w, take, step):
        s = lax.axis_index("sub")
        for copy in self.copies(w):
            copy.wait_recv()

        def block(i, carry):
            here = rows_at(i, step)
            value = self.whole[w, pl.ds(pl.multiple_of(s * self.piece + i * step, step), step)].astype(F32)
            for k in range(1, self.subs):
                value = value + self.land[w, k - 1, here].astype(F32)
            take(here, value)
            return carry

        lax.fori_loop(0, self.piece // step, block, 0)

    def drain(self, w):
        for copy in self.copies(w):
            copy.wait_send()


def weight_grad(left, right, whole, w, halves, block):
    s = lax.axis_index("sub")
    subs = lax.axis_size("sub")
    total_rows = left.shape[0] * left.shape[1]
    count = whole.shape[1] // block
    begin = ((s + 1) % subs) * halves.piece // block

    def one(j, carry):
        b = (begin + j) % count
        turned = left[:, :, cols(b, block)].reshape(total_rows, block)

        def inner(i, carry):
            other = right[:, :, cols(i, 512)].reshape(total_rows, 512)
            whole[w, rows_at(b, block), cols(i, 512)] = dot_c(turned, other).astype(BF)
            return carry

        lax.fori_loop(0, whole.shape[2] // 512, inner, 0)
        return carry

    if subs == 2:
        lax.fori_loop(0, count // 2, one, 0)
        halves.start(w)
        lax.fori_loop(count // 2, count, one, 0)
    else:
        lax.fori_loop(0, count, one, 0)
        halves.start(w)


def feed_kernel(
    rows_in, grads_in, up_in, down_in, o_part, o_norm, o_pieces,
    rows, grads, up, down, act, pre_grad, part_out, part_norm, land_norm, stage_norm,
    whole, land_whole, load, store, send, recv,
):
    t, x, y, d = neighbours()
    s = lax.axis_index("sub")
    subs = lax.axis_size("sub")
    loads = [
        pltpu.make_async_copy(a, b, load.at[i])
        for i, (a, b) in enumerate(
            ((rows_in, rows.at[t]), (up_in, up), (grads_in, grads), (down_in, down))
        )
    ]
    for copy in loads:
        copy.start()
    greet([{"tensor": x}, {"tensor": y}] + [{"sub": (s + k) % subs} for k in range(1, subs)])
    _, n, m = rows.shape
    hidden = up.shape[1]
    loads[0].wait()
    gather = Gather(rows.at[t], rows, send, recv, 0)
    gather.start()
    back = Scatter(part_norm, land_norm, stage_norm, send, recv, 6)
    halves = Halves(whole, land_whole, send, recv, 12)
    for copy in loads[1:4]:
        copy.wait()

    def work(place):
        def step(j, carry):
            here = cols(j, 256)
            value, slope = gelu_both(dot(rows[place], up[:, here]))
            act[place, :, here] = value.astype(BF)
            pre_grad[place, :, here] = (dot_t(grads[place], down[here]) * slope).astype(BF)
            return carry

        lax.fori_loop(0, hidden // 256, step, 0)

        def out_step(j, carry):
            part_norm[place, :, cols(j, 512)] = dot_t(pre_grad[place], up[rows_at(j, 512)]).astype(BF)
            part_out[place, :, cols(j, 512)] = dot(act[place], down[:, cols(j, 512)]).astype(BF)
            return carry

        lax.fori_loop(0, m // 512, out_step, 0)

    def turn(i, carry):
        far_y = i // 2
        far_x = i % 2
        place = (t // 2 + far_y - 2 * (t // 2) * far_y) * 2 + (t % 2 + far_x - 2 * (t % 2) * far_x)

        @pl.when(i == 1)
        def _():
            gather.relay_x()
            gather.relay_y()
            gather.have_x()

        @pl.when(i == 2)
        def _():
            gather.have_y()

        @pl.when(i == 3)
        def _():
            gather.have_d()

        work(place)

        @pl.when(i == 1)
        def _():
            back.along_x()

        @pl.when(i == 2)
        def _():
            back.along_y()

        @pl.when(i == 3)
        def _():
            back.diagonal()

        return carry

    lax.fori_loop(0, 4, turn, 0)
    stores = [pltpu.make_async_copy(part_out, o_part, store.at[1])]
    stores[0].start()
    weight_grad(act, grads, whole, 0, halves, 256)
    back.relay()
    weight_grad(rows, pre_grad, whole, 1, halves, 256)
    pieces = land_whole
    for w in range(2):

        def take(here, value, w=w):
            pieces[w, 0, here] = value.astype(BF)

        halves.total(w, take, 64)
    stores.append(pltpu.make_async_copy(pieces.at[:, 0], o_pieces, store.at[0]))
    stores[1].start()
    norm_total = part_norm


    def take_norm(here, total):
        norm_total[t, here] = total.astype(BF)

    back.finish(take_norm, 64)
    stores.append(pltpu.make_async_copy(norm_total.at[t], o_norm, store.at[2]))
    stores[2].start()
    gather.drain()
    back.drain()
    for w in range(2):
        halves.drain(w)
    for copy in stores:
        copy.wait()


def feed(rows, grads, up, down, subs):
    n, m = rows.shape
    hidden = up.shape[1]
    count = 12 + 2 * (subs - 1)
    return pl.pallas_call(
        feed_kernel,
        name="feed",
        out_shape=[shape(4, n, m), shape(n, m), shape(2, m // subs, hidden)],
        in_specs=[ANY] * 4,
        out_specs=[ANY] * 3,
        scratch_shapes=[
            pltpu.VMEM((4, n, m), BF), pltpu.VMEM((4, n, m), BF), pltpu.VMEM((m, hidden), BF), pltpu.VMEM((hidden, m), BF),
            pltpu.VMEM((4, n, hidden), BF), pltpu.VMEM((4, n, hidden), BF),
            pltpu.VMEM((4, n, m), BF), pltpu.VMEM((4, n, m), BF),
            pltpu.VMEM((6, n // 2, m), BF), pltpu.VMEM((2, n // 2, m), BF),
            pltpu.VMEM((2, m, hidden), BF), pltpu.VMEM((2, subs - 1, m // subs, hidden), BF),
            dma(4), dma(3), dma(count), dma(count),
        ],
        compiler_params=params(4),
    )(rows, grads, up, down)


def norm_back_block(grad, source, gain):
    hat, inverse = normed_rows(source)
    scaled = grad * gain
    inner = scaled - jnp.mean(scaled, -1, keepdims=True) - hat * jnp.mean(scaled * hat, -1, keepdims=True)
    return inverse * inner, grad * hat


def fold(block):
    total = block[0:8]
    for i in range(1, block.shape[0] // 8):
        total = total + block[8 * i : 8 * i + 8]
    return total


def unstack(block):
    lanes = head_lanes(block.shape[0] // 2)
    return jnp.where(lanes < HEAD, block[: block.shape[0] // 2], block[block.shape[0] // 2 :])


def cross_back_kernel(
    layout,
    cot_in, norm_in, cross_in, self_in, gains_in, query_in, flat_in, memory_in, wq_in, wo_in, own_in,
    o_out, o_branch, o_sums, o_memory, o_wq, o_wo, o_down, o_land,
    cot, norm, after_cross, after_self, gains, query, flat, memory, wq, wo,
    branch, rows, query_grad, memory_grad, sums, whole_q, whole_o, land_q, land_o, piece_q, piece_o,
    norm_self, own, land, ring, result, ring_send, ring_recv, ring_store,
    load, store, send, recv,
):
    s = lax.axis_index("sub")
    subs = lax.axis_size("sub")
    loads = [
        pltpu.make_async_copy(a, b, load.at[i])
        for i, (a, b) in enumerate(
            (
                (cot_in, cot), (norm_in, norm), (cross_in, after_cross), (gains_in, gains), (wo_in, wo),
                (query_in, query), (flat_in, flat), (memory_in, memory), (self_in, after_self), (wq_in, wq),
                (own_in.at[pl.ds(0, layout.middle)], own),
            )
        )
    ]
    for copy in loads[10:] + loads[:10]:
        copy.start()
    greet([{"sub": (s + k) % subs} for k in range(1, subs)] + group_ring())
    pump = Pump(
        own, land, ring, result, ring_send, ring_recv, ring_store, 0, layout.middle, layout.count,
        sum_outputs(layout, (o_down,)),
    )
    n, m = cot.shape
    width = wq.shape[2]
    texts = memory.shape[1]
    loads[10].wait()
    pump.step(jnp.int32(0))
    for copy in loads[:4]:
        copy.wait()
    scale = HEAD ** (-0.5)

    def feed_block(i, carry):
        here = rows_at(i, 64)
        grad = norm[here].astype(F32)
        inner, terms = norm_back_block(grad, after_cross[here], gains[2:3])
        total = cot[here] + inner
        cot[here] = total
        branch[here] = total.astype(BF)
        return carry[0] + fold(terms), carry[1] + fold(grad)

    zero = jnp.zeros((8, m), F32)
    gain_sum, bias_sum = lax.fori_loop(0, n // 64, feed_block, (zero, zero))
    sums[0:8] = gain_sum
    sums[8:16] = bias_sum
    loads[8].wait()

    def norm_block(i, carry):
        here = rows_at(i, 64)
        hat, _ = normed_rows(after_self[here])
        rows[here] = (hat * gains[0:1] + gains[1:2]).astype(BF)
        return carry

    lax.fori_loop(0, n // 64, norm_block, 0)
    for copy in loads[4:8]:
        copy.wait()
    middle = layout.middle

    def tick(k):
        @pl.when(k < middle)
        def _():
            pump.step(jnp.int32(k))

    tick(jnp.int32(1))

    def quarter(q, carry):
        @pl.when(q % 2 == 1)
        def _():
            tick(2 + q // 2)

        grad_heads = dot_t(branch[...], wo[rows_at(q, width)]).astype(BF)
        whole_q_cols = cols(q, width)
        query_grad_block = []
        for p in range(width // 128):
            lane = slice(p * 128, p * 128 + 128)
            keys = stack_pair(memory[q, :, lane], texts)
            values = stack_pair(memory[q, :, width + p * 128 : width + p * 128 + 128], texts)
            here = pl.ds(pl.multiple_of(q * width + p * 128, 128), 128)
            grad = grad_heads[:, lane]
            ask = query[:, here]
            probs, left = pair_softmax(ask, keys)
            grad_probs = dot_t(grad, values)
            centred = pair_sum(grad_probs * probs, left)
            grad_scores = (probs * (grad_probs - centred)).astype(BF)
            query_grad[:, here] = (dot(grad_scores, keys) * scale).astype(BF)
            memory_grad[q, :, lane] = unstack(dot_c(grad_scores, ask) * scale).astype(BF)
            memory_grad[q, :, width + p * 128 : width + p * 128 + 128] = unstack(
                dot_c(probs.astype(BF), grad)
            ).astype(BF)
        return carry

    lax.fori_loop(0, 4, quarter, 0)
    stores = [pltpu.make_async_copy(memory_grad, o_memory, store.at[0])]
    stores[0].start()
    halves_q = Halves(whole_q, land_q, send, recv, 0)
    halves_o = Halves(whole_o, land_o, send, recv, 4 * (subs - 1))

    def weights(q, carry):

        def grad_o(j, carry):
            whole_o[q, :, cols(j, 512)] = dot_c(flat[:, cols(q, width)], branch[:, cols(j, 512)]).astype(BF)
            return carry

        lax.fori_loop(0, m // 512, grad_o, 0)

        def grad_q(j, carry):
            whole_q[q, rows_at(j, 256)] = dot_c(rows[:, cols(j, 256)], query_grad[:, cols(q, width)]).astype(BF)
            return carry

        lax.fori_loop(0, m // 256, grad_q, 0)
        return carry

    lax.fori_loop(0, 4, weights, 0)
    for q in range(4):
        halves_q.start(q)
        halves_o.start(q)
    loads[9].wait()

    tick(4)

    def norm_grad(j, carry):
        here = rows_at(j, 256)
        total = jnp.zeros((n, 256), F32)
        for q in range(4):
            total = total + dot_t(query_grad[:, q * width : (q + 1) * width], wq[q, here])
        norm_self[:, cols(j, 256)] = total
        return carry

    lax.fori_loop(0, m // 256, norm_grad, 0)

    def self_block(i, carry):
        here = rows_at(i, 64)
        grad = norm_self[here]
        inner, terms = norm_back_block(grad, after_self[here], gains[0:1])
        total = cot[here] + inner
        cot[here] = total
        branch[here] = total.astype(BF)
        return carry[0] + fold(terms), carry[1] + fold(grad)

    gain_sum, bias_sum = lax.fori_loop(0, n // 64, self_block, (zero, zero))
    sums[16:24] = gain_sum
    sums[24:32] = bias_sum
    stores += [
        pltpu.make_async_copy(cot, o_out, store.at[1]),
        pltpu.make_async_copy(branch, o_branch, store.at[2]),
        pltpu.make_async_copy(sums, o_sums, store.at[3]),
    ]
    for copy in stores[1:]:
        copy.start()

    tick(5)
    for halves, piece in ((halves_q, piece_q), (halves_o, piece_o)):
        for q in range(4):

            def take(here, value, q=q, piece=piece):
                piece[q, here] = value.astype(BF)

            halves.total(q, take, 16)
    stores += [pltpu.make_async_copy(piece_q, o_wq, store.at[4]), pltpu.make_async_copy(piece_o, o_wo, store.at[5])]
    for copy in stores[4:]:
        copy.start()
    pump.drain()
    stores.append(pltpu.make_async_copy(land, o_land, store.at[6]))
    stores[-1].start()
    for q in range(4):
        halves_q.drain(q)
        halves_o.drain(q)
    for copy in stores:
        copy.wait()


def cross_back(layout, cot, norm, after_cross, after_self, gains, query, flat, memory, wq, wo, own, subs):
    n, m = cot.shape
    width = wq.shape[2]
    count = 8 * (subs - 1)
    held = (2, layout.window, layout.chunk, m)
    part_q, part_o = (4, m // subs, width), (4, width // subs, m)
    return pl.pallas_call(
        partial(cross_back_kernel, layout),
        name="cross_back",
        out_shape=[
            shape(n, m, kind=F32), shape(n, m), shape(32, m, kind=F32), shape(*memory.shape), shape(*part_q), shape(*part_o),
            shape(layout.feed_count // 2, layout.chunk, m), shape(*held),
        ],
        in_specs=[ANY] * 11,
        out_specs=[ANY] * 8,
        scratch_shapes=[
            pltpu.VMEM((n, m), F32), pltpu.VMEM((n, m), BF), pltpu.VMEM((n, m), F32), pltpu.VMEM((n, m), F32),
            pltpu.VMEM(gains.shape, F32), pltpu.VMEM((n, m), BF), pltpu.VMEM((n, m), BF), pltpu.VMEM(memory.shape, BF),
            pltpu.VMEM(wq.shape, BF), pltpu.VMEM(wo.shape, BF),
            pltpu.VMEM((n, m), BF), pltpu.VMEM((n, m), BF), pltpu.VMEM((n, m), BF), pltpu.VMEM(memory.shape, BF),
            pltpu.VMEM((32, m), F32), pltpu.VMEM((4, m, width), BF), pltpu.VMEM((4, width, m), BF),
            pltpu.VMEM((4, subs - 1, m // subs, width), BF), pltpu.VMEM((4, subs - 1, width // subs, m), BF),
            pltpu.VMEM(part_q, BF), pltpu.VMEM(part_o, BF),
            pltpu.VMEM((n, m), F32),
            *pump_scratch(layout, layout.middle),
            dma(11), dma(7), dma(count), dma(count),
        ],
        compiler_params=params(5),
    )(cot, norm, after_cross, after_self, gains, query, flat, memory, wq, wo, own)


def attend_pair_back(p, triple, place, blocks, heads, grad_heads, deltas, sums, grads, grad_keys, grad_values):
    n = triple.shape[1]
    width = heads * HEAD
    scale = HEAD ** (-0.5)
    lanes = head_lanes(n)
    key_lanes = head_lanes(blocks * n)

    here = pl.ds(pl.multiple_of(p * 128, 128), 128)
    key_cols = pl.ds(pl.multiple_of(width + p * 128, 128), 128)
    value_cols = pl.ds(pl.multiple_of(2 * width + p * 128, 128), 128)
    query = triple[place, :, here]
    grad = grad_heads[place, :, here]
    keys = triple[0:blocks, :, key_cols].reshape(blocks * n, 128)
    values = triple[0:blocks, :, value_cols].reshape(blocks * n, 128)
    stats = sums[place]
    means = deltas[place]
    found = []
    for h in range(2):
        mine = (lanes < HEAD) if h == 0 else (lanes >= HEAD)
        log_sum = jnp.sum(jnp.where(lanes == 2 * p + h, stats, 0.0), -1, keepdims=True)
        delta = jnp.sum(jnp.where(lanes == 2 * p + h, means, 0.0), -1, keepdims=True)
        scores = dot_t(jnp.where(mine, query, jnp.zeros_like(query)), keys)
        row = lax.broadcasted_iota(jnp.int32, scores.shape, 0)
        col = lax.broadcasted_iota(jnp.int32, scores.shape, 1)
        probs = jnp.where(
            col <= row + (blocks - 1) * n, jnp.exp2(scores * (scale * LOG2E) - log_sum), 0.0
        )
        grad_probs = dot_t(jnp.where(mine, grad, jnp.zeros_like(grad)), values)
        grad_scores = (probs * (grad_probs - delta)).astype(BF)
        found.append((dot(grad_scores, keys), dot_c(grad_scores, query), dot_c(probs.astype(BF), grad)))
    grads[place, :, here] = (jnp.where(lanes < HEAD, found[0][0], found[1][0]) * scale).astype(BF)
    grad_keys[0 : blocks * n, here] += jnp.where(key_lanes < HEAD, found[0][1], found[1][1]) * scale
    grad_values[0 : blocks * n, here] += jnp.where(key_lanes < HEAD, found[0][2], found[1][2])


def attend_back_kernel(
    layout,
    branch_in, triple_in, flat_in, sums_in, out_in, qkv_in, rows_in, frames_in, gains_in, grad_in, memory_in, text_in, kv_in,
    own_in, land_in, down_in,
    o_frames, o_sums, o_text, o_qkv, o_more, o_down, o_up, o_kv, o_land,
    branch, triple, flat, sums, out, qkv, rows, frames, gains, grad_out, memory, text, kv,
    land_m, stage_m,
    grad_heads, deltas, grads, grad_keys, grad_values, part, land, stage, whole_qkv, land_qkv, whole_out, land_out,
    whole_kv, land_kv, text_grad, sums_out, sum_m, own, held, ring, result, ring_send, ring_recv, ring_store,
    load, store, send, recv,
):
    t, x, y, d = neighbours()
    s = lax.axis_index("sub")
    subs = lax.axis_size("sub")
    names = (
        (branch_in, branch.at[t]), (out_in, out), (flat_in, flat), (triple_in, triple), (sums_in, sums),
        (memory_in, memory), (own_in, own.at[pl.ds(0, layout.feed_count)]), (land_in, held),
        *((qkv_in.at[i], qkv.at[:, pl.ds(i * qkv_in.shape[2], qkv_in.shape[2])]) for i in range(3)), (rows_in, rows),
        (text_in, text), (kv_in, kv), (frames_in, frames), (gains_in, gains), (grad_in, grad_out),
    )
    loads = [pltpu.make_async_copy(a, b, load.at[i]) for i, (a, b) in enumerate(names)]
    loads[7].start()
    for copy in loads[:7] + loads[8:]:
        copy.start()
    loads[7].wait()
    greet([{"tensor": x}, {"tensor": y}] + [{"sub": (s + k) % subs} for k in range(1, subs)] + group_ring())
    first, last = layout.middle, layout.later
    pump = Pump(
        own, held, ring, result, ring_send, ring_recv, ring_store, first, last, layout.count,
        sum_outputs(layout, (o_down, o_up), o_kv),
    )

    def tick(k):
        @pl.when(k + first < last)
        def _():
            pump.step(jnp.int32(k + first))

    n, m = grad_out.shape
    width = triple.shape[2]
    local = out.shape[0]
    heads = local // HEAD
    gather = Gather(branch.at[t], branch, send, recv, 0)
    scatter = Scatter(part, land, stage, send, recv, 6)
    scatter_m = Scatter(memory, land_m, stage_m, send, recv, 12)
    halves_qkv = Halves(whole_qkv, land_qkv, send, recv, 18)
    halves_out = Halves(whole_out, land_out, send, recv, 18 + subs - 1)
    halves_kv = Halves(whole_kv, land_kv, send, recv, 18 + 2 * (subs - 1))
    loads[0].wait()
    gather.start()
    for copy in loads[5:7]:
        copy.wait()
    scatter_m.diagonal()
    scatter_m.along_x()
    scatter_m.along_y()
    for copy in loads[1:5]:
        copy.wait()
    grad_keys[...] = jnp.zeros_like(grad_keys)
    grad_values[...] = jnp.zeros_like(grad_values)
    lanes = head_lanes(n)

    def turn(i, carry):
        far_y = i // 2
        far_x = i % 2
        place = (t // 2 + far_y - 2 * (t // 2) * far_y) * 2 + (t % 2 + far_x - 2 * (t % 2) * far_x)

        @pl.when(i == 1)
        def _():
            gather.relay_x()
            gather.relay_y()
            gather.have_x()

        @pl.when(i == 2)
        def _():
            gather.have_y()
            scatter_m.relay()

        @pl.when(i == 3)
        def _():
            gather.have_d()

        grad_heads[place] = dot_t(branch[place], out[...]).astype(BF)

        def delta(p, stats):
            here = pl.ds(pl.multiple_of(p * 128, 128), 128)
            product = grad_heads[place, :, here].astype(F32) * flat[place, :, here].astype(F32)
            low = jnp.sum(jnp.where(lanes < HEAD, product, 0.0), -1, keepdims=True)
            high = jnp.sum(jnp.where(lanes < HEAD, 0.0, product), -1, keepdims=True)
            return jnp.where(lanes == 2 * p, low, jnp.where(lanes == 2 * p + 1, high, stats))

        deltas[place] = lax.fori_loop(0, heads // 2, delta, jnp.zeros((n, 128), F32))

        def pair(p, carry):
            turns = i * (heads // 2) + p

            @pl.when(turns % 2 == 0)
            def _():
                tick(turns // 2)

            for blocks in range(1, 5):

                @pl.when(place == blocks - 1)
                def _(blocks=blocks):
                    attend_pair_back(
                        p, triple, blocks - 1, blocks, heads, grad_heads, deltas, sums, grads, grad_keys, grad_values
                    )

            return carry

        lax.fori_loop(0, heads // 2, pair, 0)
        return carry

    lax.fori_loop(0, 4, turn, 0)
    for copy in loads[8:14]:
        copy.wait()

    def finish_grads(i, carry):
        grads[i, :, local : 2 * local] = grad_keys[rows_at(i, n)].astype(BF)
        grads[i, :, 2 * local :] = grad_values[rows_at(i, n)].astype(BF)
        return carry

    lax.fori_loop(0, 4, finish_grads, 0)

    def back(i, carry):
        far_y = 1 - i // 2
        far_x = 1 - i % 2
        place = (t // 2 + far_y - 2 * (t // 2) * far_y) * 2 + (t % 2 + far_x - 2 * (t % 2) * far_x)

        def step(j, carry):
            part[place, :, cols(j, 512)] = dot_t(grads[place], qkv[rows_at(j, 512)]).astype(BF)
            return carry

        lax.fori_loop(0, m // 512, step, 0)

        @pl.when(i % 2 == 0)
        def _():
            tick(6 + i // 2)

        @pl.when(i == 0)
        def _():
            scatter.diagonal()

        @pl.when(i == 1)
        def _():
            scatter.along_y()

        @pl.when(i == 2)
        def _():
            scatter.along_x()

        return carry

    lax.fori_loop(0, 4, back, 0)
    tick(8)

    def take_m(here, total):
        sum_m[here] = total.astype(BF)

    scatter_m.finish(take_m, 16)
    text_grad[...] = dot_t(sum_m[...], kv[...])
    stores = [pltpu.make_async_copy(text_grad, o_text, store.at[0])]
    stores[0].start()

    def grad_kv(j, carry):
        whole_kv[0, rows_at(j, 384)] = dot_c(text[:, cols(j, 384)], sum_m[...]).astype(BF)
        return carry

    lax.fori_loop(0, m // 384, grad_kv, 0)
    halves_kv.start(0)

    def grad_wout(j, carry):
        whole_out[0, :, cols(j, 512)] = dot_c(
            flat[...].reshape(4 * n, local), branch[:, :, cols(j, 512)].reshape(4 * n, 512)
        ).astype(BF)
        return carry

    lax.fori_loop(0, m // 512, grad_wout, 0)
    halves_out.start(0)
    tick(9)
    chunk, half = layout.chunk, 2 * layout.quarter

    def take_kv(here, total):
        c = here.start // chunk
        own[layout.kv + c % half, :, cols(c // half, 2 * local)] = total.astype(BF)

    halves_kv.total(0, take_kv, chunk)
    scatter.relay()

    def grad_wqkv(j, carry):
        @pl.when(j % 2 == 0)
        def _():
            tick(10 + j // 2)

        turned = rows[:, :, cols(j, 256)].reshape(4 * n, 256)

        def inner(i, carry):
            whole_qkv[0, rows_at(j, 256), cols(i, 384)] = dot_c(
                turned, grads[:, :, cols(i, 384)].reshape(4 * n, 384)
            ).astype(BF)
            return carry

        lax.fori_loop(0, width // 384, inner, 0)
        return carry

    lax.fori_loop(0, m // 256, grad_wqkv, 0)
    halves_qkv.start(0)
    tick(13)

    def take_out(here, total):
        own[layout.out + here.start // chunk] = total.astype(BF)

    halves_out.total(0, take_out, chunk)

    def take(here, total):
        land_qkv[0, 0, here] = total.astype(BF)

    halves_qkv.total(0, take, 16)
    stores.append(pltpu.make_async_copy(land_qkv.at[0, 0], o_qkv, store.at[1]))
    stores.append(pltpu.make_async_copy(own.at[pl.ds(layout.kv, layout.qkv - layout.kv)], o_more, store.at[2]))
    for copy in stores[-2:]:
        copy.start()
    tick(14)
    for copy in loads[14:]:
        copy.wait()

    def take_norm(here, total):
        part[t, here] = total.astype(BF)

    scatter.finish(take_norm, 64)

    def frame_block(i, carry):
        here = rows_at(i, 64)
        grad = part[t, here].astype(F32)
        inner, terms = norm_back_block(grad, frames[here].astype(F32), gains[4:5])
        grad_out[here] = grad_out[here] + inner
        return carry[0] + fold(terms), carry[1] + fold(grad)

    zero = jnp.zeros((8, m), F32)
    gain_sum, bias_sum = lax.fori_loop(0, n // 64, frame_block, (zero, zero))
    tick(15)
    sums_out[0:8] = gain_sum
    sums_out[8:16] = bias_sum
    stores += [pltpu.make_async_copy(grad_out, o_frames, store.at[3]), pltpu.make_async_copy(sums_out, o_sums, store.at[4])]
    for copy in stores[-2:]:
        copy.start()
    pump.drain()
    stores.append(pltpu.make_async_copy(held, o_land, store.at[5]))
    stores[-1].start()
    gather.drain()
    for each in (scatter, scatter_m):
        each.drain()
    for each in (halves_qkv, halves_out, halves_kv):
        each.drain(0)
    for copy in stores:
        copy.wait()


def attend_back(
    layout, branch, triple, flat, sums, out, qkv, rows, frames, gains, grad, memory, text, kv, own, land, down, subs
):
    n, m = grad.shape
    width = triple.shape[2]
    local = out.shape[0]
    texts, kvw = text.shape[0], kv.shape[1]
    count = 18 + 3 * (subs - 1)
    v = pltpu.VMEM
    return pl.pallas_call(
        partial(attend_back_kernel, layout),
        name="attend_back",
        out_shape=[
            shape(n, m, kind=F32), shape(16, m, kind=F32), shape(texts, m, kind=F32), shape(m // subs, width),
            shape(layout.qkv - layout.kv, layout.chunk, m), shape(*down.shape), shape(*down.shape),
            shape(4 * layout.quarter, layout.chunk, kvw), shape(*land.shape),
        ],
        in_specs=[ANY] * 16,
        out_specs=[ANY] * 9,
        input_output_aliases={15: 5},
        scratch_shapes=[
            v((4, n, m), BF), v(triple.shape, BF), v(flat.shape, BF), v(sums.shape, F32), v(out.shape, BF), v((m, width), BF),
            v(rows.shape, BF), v(frames.shape, frames.dtype), v(gains.shape, F32), v((n, m), F32), v(memory.shape, BF),
            v(text.shape, BF), v(kv.shape, BF),
            v((6, texts // 2, kvw), BF), v((2, texts // 2, kvw), BF),
            v((4, n, local), BF), v((4, n, 128), F32), v((4, n, width), BF), v((4 * n, local), F32), v((4 * n, local), F32),
            v((4, n, m), BF), v((6, n // 2, m), BF), v((2, n // 2, m), BF),
            v((1, m, width), BF), v((1, subs - 1, m // subs, width), BF),
            v((1, local, m), BF), v((1, subs - 1, local // subs, m), BF),
            v((1, m, kvw), BF), v((1, subs - 1, m // subs, kvw), BF),
            v((texts, m), F32), v((16, m), F32), v((texts, kvw), BF),
            *pump_scratch(layout, layout.qkv),
            dma(17), dma(6), dma(count), dma(count),
        ],
        compiler_params=params(6),
    )(branch, triple, flat, sums, out, qkv, rows, frames, gains, grad, memory, text, kv, own, land, down)


def total_kernel(
    layout,
    feed_in, qkv_in, more_in, cross_q_in, cross_o_in, sums_a_in, sums_b_in, text_in, land_in, part_in, after_in,
    down_in, up_in, kv_in,
    o_qkv, o_cq, o_out, o_co, o_text, o_vectors, o_layer, o_down, o_up, o_kv,
    own, held, ring, result, ring_send, ring_recv, ring_store,
    cross_q, cross_o, land_q, land_o, stage_q, stage_o, part, land_p, stage_p, after,
    sums_a, sums_b, text, text_land, text_full, vectors, vectors_land, share, share_land, load, store, send, recv,
):
    t, x, y, d = neighbours()
    s, subs = lax.axis_index("sub"), lax.axis_size("sub")
    g, groups = lax.axis_index("group"), lax.axis_size("group")
    chunk, m, local = layout.chunk, layout.m, layout.local
    width, quarter = 3 * local, layout.quarter
    at_kv, at_out, at_qkv, at_cq, at_co = layout.kv, layout.out, layout.qkv, layout.cq, layout.co
    def outputs(c, block, slots, act):
        slot = c % RING

        def region(begin, end, copies):
            @pl.when(jnp.logical_and(c >= begin, c < end))
            def _():
                for i, (source, target) in enumerate(copies(c - begin)):
                    act(pltpu.make_async_copy(source, target, slots.at[slot, i]))

        def whole(output):
            return lambda r: [(block, output.at[r])]

        region(0, at_kv // 2, whole(o_down))
        region(at_kv // 2, at_kv, whole(o_up))
        region(
            at_qkv, at_cq,
            lambda r: [
                *((block.at[:, pl.ds(i * local, local)], o_qkv.at[i, r]) for i in range(3)),
                (block.at[:, pl.ds(width, local)], o_qkv.at[r // quarter, 3 * quarter + r % quarter]),
            ],
        )
        region(
            at_kv, at_out,
            lambda r: [
                (block.at[:, pl.ds(2 * i * local, 2 * local)], o_kv.at[2 * i * quarter + r]) for i in range(2)
            ],
        )
        region(at_out, at_qkv, whole(o_out))
        region(
            at_cq, at_co,
            lambda r: [(block.at[:, pl.ds(i * local, local)], o_cq.at[i * quarter + r]) for i in range(4)],
        )
        region(at_co, layout.count, whole(o_co))

    fresh = max(0, layout.later - LAG * (groups - 1))
    newer = max(fresh, at_kv)
    pairs = [
        (land_in, held),
        (more_in.at[pl.ds(newer - at_kv, at_qkv - newer)], own.at[pl.ds(newer, at_qkv - newer)]),
        (qkv_in.at[pl.ds(0, 3 * quarter)], own.at[pl.ds(at_qkv, 3 * quarter), :, pl.ds(0, width)]),
    ]
    for i in range(3):
        pairs.append(
            (
                qkv_in.at[pl.ds(3 * quarter, quarter), :, pl.ds(i * local, local)],
                own.at[pl.ds(at_qkv + i * quarter, quarter), :, pl.ds(width, local)],
            )
        )
    if fresh < at_kv:
        pairs.append((feed_in.at[pl.ds(fresh, at_kv - fresh)], own.at[pl.ds(fresh, at_kv - fresh)]))
    early = len(pairs)
    pairs += [
        (cross_q_in, cross_q), (cross_o_in, cross_o), (sums_a_in, sums_a), (sums_b_in, sums_b), (text_in, text),
        (part_in, part), (after_in, after),
    ]
    loads = [pltpu.make_async_copy(a, b, load.at[i]) for i, (a, b) in enumerate(pairs)]
    for copy in loads:
        copy.start()
    loads[0].wait()
    greet(
        [{"tensor": x}, {"tensor": y}, {"tensor": d}]
        + [{"sub": (s + k) % subs} for k in range(1, subs)]
        + [{"group": (g + k) % groups} for k in range(1, groups)]
    )
    begin, end = layout.later, layout.end
    pump = Pump(own, held, ring, result, ring_send, ring_recv, ring_store, begin, end, layout.count, outputs)

    def run(a, b):
        def step(k, carry):
            pump.step(k)
            return carry

        lax.fori_loop(a, b, step, 0)

    for copy in loads[1:early]:
        copy.wait()
    run(begin, begin + 1)
    for copy in loads[early:-2]:
        copy.wait()
    share_width = m // subs
    for i in range(6):
        source, at = (sums_a, i) if i < 4 else (sums_b, i - 4)
        row = jnp.sum(source[8 * at : 8 * at + 8], 0, keepdims=True)
        for j in range(subs):
            vectors[j, i : i + 1] = row[:, j * share_width : (j + 1) * share_width]
    strip = text.shape[0] // 4

    def remote(source, target, k, device):
        return pltpu.make_async_remote_copy(
            source, target, send.at[k], recv.at[k], device_id=device, device_id_type=MESH
        )

    square = (x, y, d)
    first = [remote(vectors, vectors_land.at[k], k, {"tensor": square[k]}) for k in range(3)]
    first += [
        remote(text.at[rows_at(square[k], strip)], text_land.at[k], 3 + k, {"tensor": square[k]}) for k in range(3)
    ]
    second = [
        remote(share.at[0, (s + k) % subs], share_land.at[k - 1], 5 + k, {"sub": (s + k) % subs}) for k in range(1, subs)
    ]
    base = 5 + subs
    second += [
        remote(text_full.at[rows_at(t, strip)], text_full.at[rows_at(t, strip)], base + k, {"tensor": square[k]}) for k in range(3)
    ]
    base += 3
    third = [
        remote(share.at[1, 0], share_land.at[subs - 2 + k], base + k - 1, {"group": (g + k) % groups})
        for k in range(1, groups)
    ]
    base += groups - 1
    scatter_q = Scatter(cross_q, land_q, stage_q, send, recv, base)
    scatter_o = Scatter(cross_o, land_o, stage_o, send, recv, base + 6)
    for copy in first:
        copy.start()
    scatter_p = Scatter(part, land_p, stage_p, send, recv, base + 12)
    for each in (scatter_q, scatter_o):
        each.diagonal()
        each.along_x()
        each.along_y()

    run(begin + 1, begin + 2)
    for copy in first:
        copy.wait_recv()
    for j in range(subs):
        share[0, j] = vectors[j] + vectors_land[0, j] + vectors_land[1, j] + vectors_land[2, j]
    text_full[rows_at(t, strip)] = text[rows_at(t, strip)] + text_land[0] + text_land[1] + text_land[2]
    for copy in first:
        copy.wait_send()
    for copy in second:
        copy.start()
    run(begin + 2, begin + 3)
    scatter_q.relay()
    scatter_o.relay()
    loads[-2].wait()
    loads[-1].wait()
    scatter_p.diagonal()
    scatter_p.along_x()
    scatter_p.along_y()
    run(begin + 3, at_cq)

    def take_q(rows, value):
        row = rows.start
        c = row // chunk
        own[at_cq + c % quarter, :, cols(c // quarter, local)] = value.astype(BF)

    scatter_q.finish(take_q, chunk)
    run(at_cq, at_co)
    step = min(chunk, scatter_o.half)

    def take_o(rows, value):
        own[at_co + rows.start // chunk, rows_at(rows.start % chunk // step, step)] = value.astype(BF)

    scatter_o.finish(take_o, step)
    for copy in second:
        copy.wait_recv()
    total = share[0, s]
    for k in range(1, subs):
        total = total + share_land[k - 1]
    share[1, 0] = total
    text_store = pltpu.make_async_copy(text_full, o_text, store.at[0])
    text_store.start()
    for copy in third:
        copy.start()
    run(at_co, layout.count)
    scatter_p.relay()
    run(layout.count, end)

    def take_layer(rows, value):
        after[rows] = after[rows] + value

    scatter_p.finish(take_layer, 64)
    layer_store = pltpu.make_async_copy(after, o_layer, store.at[2])
    layer_store.start()
    for copy in third:
        copy.wait_recv()
    total = share[1, 0]
    for k in range(1, groups):
        total = total + share_land[subs - 2 + k]
    share[2, 0] = total
    vector_store = pltpu.make_async_copy(share.at[2, 0], o_vectors, store.at[1])
    vector_store.start()
    for copy in second + third:
        copy.wait_send()
    for each in (scatter_q, scatter_o, scatter_p):
        each.drain()
    pump.drain()
    layer_store.wait()
    text_store.wait()
    vector_store.wait()


def total(layout, pieces, qkv, more, cross_q, cross_o, sums_a, sums_b, text, land, part, after, down, up, kv, subs, groups):
    m, chunk = layout.m, layout.chunk
    n = after.shape[0]
    v = pltpu.VMEM
    sems = 7 + subs + groups + 18
    qkv = qkv.reshape(-1, chunk, qkv.shape[1])
    piece_q, piece_o = cross_q.shape[1:], cross_o.shape[1:]
    out_shape = shape(layout.qkv - layout.out, chunk, m)
    return pl.pallas_call(
        partial(total_kernel, layout),
        name="total",
        out_shape=[
            shape(3, *qkv.shape[:2], layout.local), shape(layout.piece // chunk, chunk, layout.local), out_shape, out_shape,
            shape(*text.shape, kind=F32), shape(8, m // subs, kind=F32), shape(n, m, kind=F32),
            shape(*down.shape), shape(*up.shape), shape(*kv.shape),
        ],
        in_specs=[ANY] * 14,
        out_specs=[ANY] * 10,
        input_output_aliases={11: 7, 12: 8, 13: 9},
        scratch_shapes=[
            *pump_scratch(layout, layout.count),
            v(cross_q.shape, BF), v(cross_o.shape, BF),
            v((6, piece_q[0] // 2, piece_q[1]), BF), v((6, piece_o[0] // 2, piece_o[1]), BF),
            v((2, piece_q[0] // 2, piece_q[1]), BF), v((2, piece_o[0] // 2, piece_o[1]), BF),
            v((4, n, m), BF), v((6, n // 2, m), BF), v((2, n // 2, m), BF), v((n, m), F32),
            v(sums_a.shape, F32), v(sums_b.shape, F32), v(text.shape, F32),
            v((3, text.shape[0] // 4, m), F32), v(text.shape, F32), v((subs, 8, m // subs), F32), v((3, subs, 8, m // subs), F32),
            v((3, subs, 8, m // subs), F32), v((subs - 1 + groups - 1, 8, m // subs), F32),
            dma(14), dma(3), dma(sems), dma(sems),
        ],
        compiler_params=params(7),
    )(pieces, qkv, more, cross_q, cross_o, sums_a, sums_b, text, land, part, after, down, up, kv)


def local(
    frames, text_states, selfgain, selfbias, selfqkv, selfout, crossgain, crossbias, crossquery, crosskv, crossout,
    feedgain, feedbias, feedup, feeddown, cotangent,
):
    subs, groups = lax.axis_size("sub"), lax.axis_size("group")
    m = frames.shape[2]
    width = selfout.shape[0]
    qkv = selfqkv.transpose(1, 0, 2)
    kv = crosskv.reshape(m, 2 * width)
    gains = jnp.concatenate([crossgain, crossbias, feedgain, feedbias, selfgain, selfbias]).reshape(6, m)
    rows, triple, memory = enter(frames[0], gains, qkv, text_states[0], kv)
    flat, sums, after_self, wq, wo = attend(triple, selfout, frames[0], crossquery, crossout, subs, groups)
    wo = wo.reshape(4 * width, m)
    query, cross_flat, after_cross, feed_rows, grads = cross(after_self, gains, wq, wo, memory, cotangent[0])
    layout = Layout(m, width, subs, groups)
    part, norm_grad, pieces = feed(feed_rows, grads, feedup, feeddown, subs)
    pieces = pieces.reshape(-1, layout.chunk, m)
    grad_out, branch, sums_a, memory_grad, piece_q, piece_o, down, land = cross_back(
        layout, cotangent[0], norm_grad, after_cross, after_self, gains, query, cross_flat, memory, wq, wo, pieces, subs
    )
    frame_grad, sums_b, text_part, grad_qkv, more, down, up, full_kv, land = attend_back(
        layout, branch, triple, flat, sums, selfout, qkv, rows, frames[0], gains, grad_out, memory_grad,
        text_states[0], kv, pieces, land, down, subs,
    )
    full_qkv, full_cq, full_out, full_co, text_grad, vectors, layer_output, down, up, full_kv = total(
        layout, pieces, grad_qkv, more, piece_q, piece_o, sums_a, sums_b, text_part, land, part, after_cross,
        down, up, full_kv, subs, groups,
    )
    return (
        layer_output[None],
        frame_grad[None],
        text_grad[None],
        vectors[4],
        vectors[5],
        full_qkv.astype(F32).reshape(3, -1, width).transpose(1, 0, 2),
        full_out.astype(F32).reshape(-1, m),
        vectors[2],
        vectors[3],
        full_cq.astype(F32).reshape(-1, width),
        full_kv.astype(F32).reshape(-1, 2, width),
        full_co.astype(F32).reshape(-1, m),
        vectors[0],
        vectors[1],
        up.astype(F32).reshape(-1, m),
        down.astype(F32).reshape(-1, m),
    )


def solution(mesh):
    clips = P(("sub", "group"), "tensor", None)
    whole = P(("sub", "group"), None, None)
    narrow, wide = P("tensor", None), P(None, "tensor")
    third = P(None, None, "tensor")
    vector = P("sub")
    return jax.shard_map(
        local,
        mesh=mesh,
        in_specs=(
            clips, whole, P(), P(), third, narrow, P(), P(), wide, third, narrow, P(), P(), wide, narrow, clips,
        ),
        out_specs=(
            clips, clips, whole, vector, vector, P("sub", None, "tensor"), P(("tensor", "sub"), None), vector, vector,
            P("sub", "tensor"), P("sub", None, "tensor"), P(("tensor", "sub"), None), vector, vector,
            P("sub", "tensor"), P(("tensor", "sub"), None),
        ),
        check_vma=False,
    )
```

```python
from functools import partial

import jax
import jax.numpy as jnp
from jax import lax
from jax.experimental import pallas as pl
from jax.experimental.pallas import tpu as pltpu
from jax.sharding import PartitionSpec as P

HEAD = 64
EPSILON = 1e-05
NEG_BIG = -1e30
LOG2E = 1.4426950408889634
MESH = pl.DeviceIdType.MESH
F32 = jnp.float32
BF = jnp.bfloat16
ANY = pl.BlockSpec(memory_space=pl.ANY)
VMEM_LIMIT = 63 << 20


def neighbours():
    t = lax.axis_index("tensor")
    return t, t + 1 - 2 * (t % 2), (t + 2) % 4, 3 - t


def greet(targets):
    barrier = pltpu.get_barrier_semaphore()
    for target in targets:
        pl.semaphore_signal(barrier, inc=1, device_id=target, device_id_type=MESH)
    pl.semaphore_wait(barrier, len(targets))


def dot(a, b):
    return lax.dot_general(a, b, (((1,), (0,)), ((), ())), preferred_element_type=F32)


def dot_t(a, b):
    return lax.dot_general(a, b, (((1,), (1,)), ((), ())), preferred_element_type=F32)


def dot_c(a, b):
    return lax.dot_general(a, b, (((0,), (0,)), ((), ())), preferred_element_type=F32)


def cols(j, width):
    return pl.ds(pl.multiple_of(j * width, width), width)


def rows_at(j, height):
    return pl.ds(pl.multiple_of(j * height, height), height)


def split(count):
    first = (count // 2 + 15) // 16 * 16
    return pl.ds(0, first), pl.ds(first, count - first)


class Gather:
    def __init__(self, own, dst, send, recv, base, halves=None):
        self.own, self.dst, self.send, self.recv, self.base = own, dst, send, recv, base
        self.halves = halves or split(own.shape[0])

    def copy(self, k):
        t, x, y, _ = neighbours()
        first, second = self.halves
        half = (first, second, second, first, first, second)[k]
        place = (t, t, t, t, x, y)[k]
        target = (x, y, x, y, y, x)[k]
        source = self.own.at[half] if k < 4 else self.dst.at[place, half]
        return pltpu.make_async_remote_copy(
            source,
            self.dst.at[place, half],
            self.send.at[self.base + k],
            self.recv.at[self.base + k],
            device_id={"tensor": target},
            device_id_type=MESH,
        )

    def start(self):
        for k in range(4):
            self.copy(k).start()

    def relay_x(self):
        self.copy(0).wait_recv()
        self.copy(4).start()

    def relay_y(self):
        self.copy(1).wait_recv()
        self.copy(5).start()

    def have_x(self):
        self.copy(2).wait_recv()

    def have_y(self):
        self.copy(3).wait_recv()

    def have_d(self):
        self.copy(4).wait_recv()
        self.copy(5).wait_recv()

    def drain(self):
        for k in range(6):
            self.copy(k).wait_send()


class Scatter:
    def __init__(self, part, land, stage, send, recv, base):
        self.part, self.land, self.stage = part, land, stage
        self.send, self.recv, self.base = send, recv, base
        self.half = part.shape[1] // 2

    def copy(self, k):
        t, x, y, d = neighbours()
        low, high = pl.ds(0, self.half), pl.ds(self.half, self.half)
        source = (
            self.part.at[d, low],
            self.part.at[d, high],
            self.part.at[x, low],
            self.stage.at[1],
            self.part.at[y, high],
            self.stage.at[0],
        )[k]
        target = (x, y, x, x, y, y)[k]
        return pltpu.make_async_remote_copy(
            source,
            self.land.at[k],
            self.send.at[self.base + k],
            self.recv.at[self.base + k],
            device_id={"tensor": target},
            device_id_type=MESH,
        )

    def diagonal(self):
        self.copy(0).start()
        self.copy(1).start()

    def along_x(self):
        self.copy(2).start()

    def along_y(self):
        self.copy(4).start()

    def relay(self):
        t, x, y, d = neighbours()
        low, high = pl.ds(0, self.half), pl.ds(self.half, self.half)
        self.copy(0).wait_recv()
        self.stage[0] = (self.part[y, low].astype(F32) + self.land[0].astype(F32)).astype(BF)
        self.copy(5).start()
        self.copy(1).wait_recv()
        self.stage[1] = (self.part[x, high].astype(F32) + self.land[1].astype(F32)).astype(BF)
        self.copy(3).start()

    def finish(self, take, step):
        t, x, y, d = neighbours()
        for k in (2, 4, 5, 3):
            self.copy(k).wait_recv()
        for base, a, b in ((0, 2, 5), (self.half, 4, 3)):

            def block(i, carry, base=base, a=a, b=b):
                here = rows_at(i, step)
                rows = pl.ds(pl.multiple_of(base + i * step, step), step)
                take(
                    rows,
                    self.part[t, rows].astype(F32)
                    + self.land[a, here].astype(F32)
                    + self.land[b, here].astype(F32),
                )
                return carry

            lax.fori_loop(0, self.half // step, block, 0)

    def drain(self):
        for k in range(6):
            self.copy(k).wait_send()


def normed_rows(values):
    centre = values - jnp.mean(values, -1, keepdims=True)
    inverse = lax.rsqrt(jnp.mean(centre * centre, -1, keepdims=True) + EPSILON)
    return centre * inverse, inverse


def params(cid, **more):
    return pltpu.CompilerParams(
        collective_id=cid, has_side_effects=True, vmem_limit_bytes=VMEM_LIMIT, **more
    )


def dma(count):
    return pltpu.SemaphoreType.DMA((count,))


def shape(*dims, kind=BF):
    return jax.ShapeDtypeStruct(dims, kind)


LAG = 2
RING = 4


def either(condition, other):
    return jnp.logical_and(condition, other)


class Pump:
    def __init__(self, own, land, ring, result, send, recv, store, first, last, count, outputs):
        self.own, self.land, self.ring, self.result = own, land, ring, result
        self.send, self.recv, self.store = send, recv, store
        self.first, self.last, self.count, self.outputs = first, last, count, outputs
        self.window = land.shape[1]
        self.g, self.n = lax.axis_index("group"), lax.axis_size("group")

    def copy(self, way, c):
        target = (self.g + 1) % self.n if way == 0 else (self.g + self.n - 1) % self.n
        return pltpu.make_async_remote_copy(
            self.ring.at[way, c % RING],
            self.land.at[way, c % self.window],
            self.send.at[way, c % RING],
            self.recv.at[way, c % self.window],
            device_id={"group": target},
            device_id_type=MESH,
        )

    def flow(self, way, k):
        place = self.g if way == 0 else self.n - 1 - self.g
        c = k - LAG * place

        @pl.when(either(c >= 0, c < self.count))
        def _():
            @pl.when(either(place > 0, k - LAG >= self.first))
            def _():
                self.copy(way, c).wait_recv()

            @pl.when(place < self.n - 1)
            def _():
                @pl.when(either(c >= RING, k - RING >= self.first))
                def _():
                    self.copy(way, c - RING).wait_send()

                @pl.when(place > 0)
                def _():
                    self.fill(self.ring.at[way, c % RING], (self.own.at[c], self.land.at[way, c % self.window]))

                @pl.when(place == 0)
                def _():
                    self.fill(self.ring.at[way, c % RING], (self.own.at[c],))

                self.copy(way, c).start()

    def fill(self, target, terms):
        def block(i, carry):
            here = rows_at(i, 48)
            value = terms[0][here].astype(F32)
            for term in terms[1:]:
                value = value + term[here].astype(F32)
            target[here] = value.astype(BF)
            return carry

        lax.fori_loop(0, target.shape[0] // 48, block, 0)

    def finished(self, k):
        far = jnp.maximum(self.g, self.n - 1 - self.g)
        return k - LAG * far

    def step(self, k):
        self.flow(0, k)
        self.flow(1, k)
        f = self.finished(k)

        @pl.when(either(f >= 0, f < self.count))
        def _():
            @pl.when(either(f >= RING, k - RING >= self.first))
            def _():
                self.outputs(f - RING, self.result.at[f % RING], self.store, lambda copy: copy.wait())

            slot, held = f % RING, f % self.window
            mine, target = self.own.at[f], self.result.at[slot]

            @pl.when(either(self.g > 0, self.g < self.n - 1))
            def _():
                self.fill(target, (mine, self.land.at[0, held], self.land.at[1, held]))

            @pl.when(self.g == 0)
            def _():
                self.fill(target, (mine, self.land.at[1, held]))

            @pl.when(self.g == self.n - 1)
            def _():
                self.fill(target, (mine, self.land.at[0, held]))

            self.outputs(f, self.result.at[slot], self.store, lambda copy: copy.start())

    def drain(self):
        for way in range(2):
            place = self.g if way == 0 else self.n - 1 - self.g
            top = jnp.minimum(self.last - LAG * place, self.count)
            for j in range(1, RING + 1):
                c = top - j

                @pl.when(either(place < self.n - 1, either(c >= 0, c + LAG * place >= self.first)))
                def _(way=way, c=c):
                    self.copy(way, c).wait_send()

            for k in range(max(self.first, self.last - LAG), self.last):
                c = k - LAG * (place - 1)

                @pl.when(either(place > 0, either(c >= 0, c < self.count)))
                def _(way=way, c=c):
                    self.copy(way, c).wait_recv()

        far = jnp.maximum(self.g, self.n - 1 - self.g)
        top = jnp.minimum(self.last - LAG * far, self.count)
        for j in range(1, RING + 1):
            f = top - j

            @pl.when(either(f >= 0, f + LAG * far >= self.first))
            def _(f=f):
                self.outputs(f, self.result.at[f % RING], self.store, lambda copy: copy.wait())


KV_TICKS, OUT_TICKS = 10, 14


class Layout:
    def __init__(self, m, local, subs, groups):
        piece = m // subs
        self.m, self.piece, self.local = m, piece, local
        self.out_rows = local // subs
        self.chunk = 96 if piece % 384 == 0 and self.out_rows % 96 == 0 else 48
        quarter = piece // 4 // self.chunk
        self.quarter = quarter
        self.feed_count = 2 * piece // self.chunk
        self.kv = self.feed_count
        self.out = self.kv + 2 * quarter
        self.qkv = self.out + self.out_rows // self.chunk
        self.cq = self.qkv + 3 * quarter
        self.co = self.cq + quarter
        self.count = self.co + self.out_rows // self.chunk
        self.window = LAG * groups
        self.end = self.count + LAG * (groups - 1)
        self.middle = min(6, self.feed_count // 2 - 2)
        self.later = self.feed_count
        if self.middle + KV_TICKS <= self.kv and self.middle + OUT_TICKS <= self.out:
            self.later = self.middle + OUT_TICKS + 2


def sum_outputs(layout, halves, text=None):
    def outputs(c, block, store, act):
        count = layout.feed_count // 2
        for i, half in enumerate(halves):

            @pl.when(either(c >= i * count, c < (i + 1) * count))
            def _(i=i, half=half):
                act(pltpu.make_async_copy(block, half.at[c - i * count], store.at[c % RING, 0]))

        if text is not None:

            @pl.when(either(c >= layout.kv, c < layout.out))
            def _():
                for i in range(2):
                    lanes = pl.ds(2 * i * layout.local, 2 * layout.local)
                    target = text.at[2 * i * layout.quarter + c - layout.kv]
                    act(pltpu.make_async_copy(block.at[:, lanes], target, store.at[c % RING, i]))

    return outputs


def pump_scratch(layout, count):
    chunk, m = layout.chunk, layout.m
    return [
        pltpu.VMEM((count, chunk, m), BF),
        pltpu.VMEM((2, layout.window, chunk, m), BF),
        pltpu.VMEM((2, RING, chunk, m), BF),
        pltpu.VMEM((RING, chunk, m), BF),
        pltpu.SemaphoreType.DMA((2, RING)),
        pltpu.SemaphoreType.DMA((2, layout.window)),
        pltpu.SemaphoreType.DMA((RING, 4)),
    ]


def group_ring():
    g, n = lax.axis_index("group"), lax.axis_size("group")
    return [{"group": (g + 1) % n}, {"group": (g + n - 1) % n}]


def enter_kernel(
    frames, gains, qkv, text, kv, o_rows, o_triple, o_memory,
    v_frames, v_gains, v_qkv, v_text, v_kv, rows, triple, memory, load, store, send, recv,
):
    t, x, y, d = neighbours()
    loads = [
        pltpu.make_async_copy(a, b, load.at[i])
        for i, (a, b) in enumerate(
            (
                (frames, v_frames), (gains, v_gains), (text, v_text), (kv, v_kv),
                *((qkv.at[i], v_qkv.at[:, pl.ds(i * qkv.shape[2], qkv.shape[2])]) for i in range(3)),
            )
        )
    ]
    for copy in loads:
        copy.start()
    greet([{"tensor": x}, {"tensor": y}])
    for copy in loads[:2]:
        copy.wait()
    count, width = v_qkv.shape
    block = 384

    def norm_block(i, carry):
        here = rows_at(i, 64)
        hat, _ = normed_rows(v_frames[here].astype(F32))
        rows[t, here] = (hat * v_gains[4:5] + v_gains[5:6]).astype(BF)
        return carry

    lax.fori_loop(0, v_frames.shape[0] // 64, norm_block, 0)
    gather = Gather(rows.at[t], rows, send, recv, 0)
    gather.start()
    texts = Gather(memory.at[t], memory, send, recv, 6)

    def project(place):
        def step(j, carry):
            triple[place, :, cols(j, block)] = dot(rows[place], v_qkv[:, cols(j, block)]).astype(BF)
            return carry

        lax.fori_loop(0, width // block, step, 0)

    def put(k, place):
        a = pltpu.make_async_copy(rows.at[place], o_rows.at[place], store.at[2 * k])
        b = pltpu.make_async_copy(triple.at[place], o_triple.at[place], store.at[2 * k + 1])
        a.start()
        b.start()
        return [a, b]

    loads[2].wait()
    loads[3].wait()

    def texts_step(j, carry):
        memory[t, :, cols(j, block)] = dot(v_text[...], v_kv[:, cols(j, block)]).astype(BF)
        return carry

    lax.fori_loop(0, v_kv.shape[1] // block, texts_step, 0)
    texts.start()
    for copy in loads[4:]:
        copy.wait()
    project(t)
    stores = put(0, t)
    gather.relay_x()
    gather.relay_y()
    gather.have_x()
    project(x)
    stores += put(1, x)
    gather.have_y()
    project(y)
    stores += put(2, y)
    texts.relay_x()
    texts.relay_y()
    texts.have_x()
    texts.have_y()
    gather.have_d()
    project(d)
    stores += put(3, d)
    texts.have_d()
    last = pltpu.make_async_copy(memory, o_memory, store.at[8])
    last.start()
    gather.drain()
    texts.drain()
    for copy in stores:
        copy.wait()
    last.wait()


def enter(frames, gains, qkv, text, kv):
    n, m = frames.shape
    width, texts, kvw = 3 * qkv.shape[2], text.shape[0], kv.shape[1]
    return pl.pallas_call(
        enter_kernel,
        name="enter",
        out_shape=[shape(4, n, m), shape(4, n, width), shape(4, texts, kvw)],
        in_specs=[ANY] * 5,
        out_specs=[ANY] * 3,
        scratch_shapes=[
            pltpu.VMEM((n, m), frames.dtype), pltpu.VMEM(gains.shape, F32),
            pltpu.VMEM((m, width), BF), pltpu.VMEM(text.shape, BF), pltpu.VMEM(kv.shape, BF),
            pltpu.VMEM((4, n, m), BF), pltpu.VMEM((4, n, width), BF), pltpu.VMEM((4, texts, kvw), BF),
            dma(7), dma(9), dma(12), dma(12),
        ],
        compiler_params=params(1),
    )(frames, gains, qkv, text, kv)


def head_lanes(rows):
    return lax.broadcasted_iota(jnp.int32, (rows, 128), 1)


def attend_rows(triple, place, blocks, heads, flat, sums):
    n = triple.shape[1]
    width = heads * HEAD
    scale = HEAD ** (-0.5) * LOG2E
    lanes = head_lanes(n)

    def pair(p, stats):
        here = pl.ds(pl.multiple_of(p * 128, 128), 128)
        key_cols = pl.ds(pl.multiple_of(width + p * 128, 128), 128)
        value_cols = pl.ds(pl.multiple_of(2 * width + p * 128, 128), 128)
        query = triple[place, :, here]
        keys = triple[0:blocks, :, key_cols].reshape(blocks * n, 128)
        values = triple[0:blocks, :, value_cols].reshape(blocks * n, 128)
        outs = []
        for h in range(2):
            mine = (lanes < HEAD) if h == 0 else (lanes >= HEAD)
            scores = dot_t(jnp.where(mine, query, jnp.zeros_like(query)), keys)
            row = lax.broadcasted_iota(jnp.int32, scores.shape, 0)
            col = lax.broadcasted_iota(jnp.int32, scores.shape, 1)
            scores = jnp.where(col <= row + (blocks - 1) * n, scores, NEG_BIG)
            peak = jnp.max(scores, -1, keepdims=True) * scale
            exponent = jnp.exp2(scores * scale - peak)
            total = jnp.sum(exponent, -1, keepdims=True)
            outs.append(dot(exponent.astype(BF), values) / total)
            stats = jnp.where(lanes == 2 * p + h, peak + jnp.log2(total), stats)
        flat[place, :, here] = jnp.where(lanes < HEAD, outs[0], outs[1]).astype(BF)
        return stats

    sums[place] = lax.fori_loop(0, heads // 2, pair, jnp.zeros((n, 128), F32))


def attend_kernel(
    triple_in, out_in, frames_in, wq, wo, o_flat, o_sums, o_after, o_wq, o_wo,
    triple, v_out, v_frames, flat, sums, after, part, land, stage, v_wq, v_wo, load, store, send, recv, side,
):
    t, x, y, d = neighbours()
    s = lax.axis_index("sub")
    subs = lax.axis_size("sub")
    g, groups = lax.axis_index("group"), lax.axis_size("group")
    n = triple.shape[1]
    m = v_out.shape[1]
    heads = v_out.shape[0] // HEAD
    loads = [
        pltpu.make_async_copy(a, b, load.at[i])
        for i, (a, b) in enumerate(
            ((triple_in, triple), (out_in, v_out), (frames_in, v_frames), (wq, v_wq), (wo, v_wo))
        )
    ]
    for copy in loads:
        copy.start()
    greet(
        [{"tensor": x}, {"tensor": y}]
        + [{"sub": (s + k) % subs} for k in range(1, subs)]
        + [{"group": (g + k) % groups} for k in range(1, groups)]
    )
    scatter = Scatter(part, land, stage, send, recv, 0)
    gathers = []
    for i, (weight, full) in enumerate(((wq, o_wq), (wo, o_wo))):
        piece = weight.shape[0] // subs
        strips = groups if i == 0 and piece % (32 * groups) == 0 else 1
        strip = piece // strips
        first, second = split(strip)
        offset = pl.multiple_of(s * piece, piece)
        begin = pl.multiple_of(offset + (g * strip if strips > 1 else 0), strip)
        halves = (
            pl.ds(begin, first.size),
            pl.ds(pl.multiple_of(begin + first.size, 16), second.size),
        )
        gathers.append((Gather(weight, full, send, recv, 6 + 6 * i, halves), full, pl.ds(offset, piece)))
        if i == 0:
            mine = pl.ds(begin, strip)
            spread = [(j, k) for j in range(3) for k in range(1, groups)] if strips > 1 else []

    def shared(i, j, k):
        _, full, piece = gathers[i]
        place = (x, y, d)[j]
        slot = (i * 3 + j) * (subs - 1) + k - 1
        return pltpu.make_async_remote_copy(
            full.at[place, piece], full.at[place, piece],
            send.at[18 + slot], recv.at[18 + slot],
            device_id={"sub": (s + k) % subs}, device_id_type=MESH,
        )

    def stripped(j, k):
        place = (x, y, d)[j]
        slot = 18 + 6 * (subs - 1) + j * (groups - 1) + k - 1
        return pltpu.make_async_remote_copy(
            o_wq.at[place, mine], o_wq.at[place, mine], send.at[slot], recv.at[slot],
            device_id={"group": (g + k) % groups}, device_id_type=MESH,
        )

    (query_gather, _, _), (out_gather, _, _) = gathers
    query_gather.start()
    for copy in loads[:2]:
        copy.wait()

    def one(i, carry):
        far_y = 1 - i // 2
        far_x = 1 - i % 2
        place = (t // 2 + far_y - 2 * (t // 2) * far_y) * 2 + (t % 2 + far_x - 2 * (t % 2) * far_x)

        @pl.when(i == 1)
        def _():
            query_gather.relay_x()
            query_gather.relay_y()
            query_gather.have_x()
            query_gather.have_y()
            for j, k in spread:
                if j < 2:
                    stripped(j, k).start()
            out_gather.start()

        @pl.when(i == 2)
        def _():
            query_gather.have_d()
            for j, k in spread:
                if j == 2:
                    stripped(j, k).start()

        for blocks in range(1, 5):

            @pl.when(place == blocks - 1)
            def _(blocks=blocks):
                attend_rows(triple, blocks - 1, blocks, heads, flat, sums)

        def out_step(j, carry):
            part[place, :, cols(j, 512)] = dot(flat[place], v_out[:, cols(j, 512)]).astype(BF)
            return carry

        lax.fori_loop(0, m // 512, out_step, 0)

        @pl.when(i == 0)
        def _():
            scatter.diagonal()

        @pl.when(i == 1)
        def _():
            scatter.along_y()

        @pl.when(i == 2)
        def _():
            scatter.along_x()

        return carry

    lax.fori_loop(0, 4, one, 0)
    out_gather.relay_x()
    out_gather.relay_y()
    stores = [
        pltpu.make_async_copy(flat, o_flat, store.at[0]),
        pltpu.make_async_copy(sums, o_sums, store.at[1]),
    ]
    loads[3].wait()
    loads[4].wait()
    stores += [
        pltpu.make_async_copy(v_wq, o_wq.at[t], store.at[2]),
        pltpu.make_async_copy(v_wo, o_wo.at[t], store.at[3]),
    ]
    for copy in stores:
        copy.start()
    scatter.relay()
    loads[2].wait()

    def take(rows, total):
        after[rows] = v_frames[rows].astype(F32) + total

    scatter.finish(take, 64)
    last = pltpu.make_async_copy(after, o_after, store.at[4])
    last.start()
    out_gather.have_x()
    out_gather.have_y()
    out_gather.have_d()
    for j in range(3):
        for k in range(1, subs):
            shared(1, j, k).start()
    for j, k in spread:
        stripped(j, k).wait_recv()
    for j in range(3):
        for k in range(1, subs):
            shared(0, j, k).start()
    scatter.drain()
    for j, k in spread:
        stripped(j, k).wait_send()
    for i, (gather, _, _) in enumerate(gathers):
        gather.drain()
        for j in range(3):
            for k in range(1, subs):
                shared(i, j, k).wait()
    for copy in stores:
        copy.wait()
    last.wait()


def attend(triple, out, frames, wq, wo, subs, groups):
    _, n, width = triple.shape
    local, m = out.shape
    extra = 18 + 6 * (subs - 1) + 3 * (groups - 1)
    return pl.pallas_call(
        attend_kernel,
        name="attend",
        out_shape=[
            shape(4, n, local), shape(4, n, 128, kind=F32), shape(n, m, kind=F32),
            shape(4, *wq.shape), shape(4, *wo.shape),
        ],
        in_specs=[ANY] * 5,
        out_specs=[ANY] * 5,
        scratch_shapes=[
            pltpu.VMEM((4, n, width), BF), pltpu.VMEM((local, m), BF), pltpu.VMEM((n, m), frames.dtype),
            pltpu.VMEM((4, n, local), BF), pltpu.VMEM((4, n, 128), F32), pltpu.VMEM((n, m), F32),
            pltpu.VMEM((4, n, m), BF), pltpu.VMEM((6, n // 2, m), BF), pltpu.VMEM((2, n // 2, m), BF),
            pltpu.VMEM(wq.shape, BF), pltpu.VMEM(wo.shape, BF),
            dma(5), dma(5), dma(extra), dma(extra), dma(1),
        ],
        compiler_params=params(2),
    )(triple, out, frames, wq, wo)


def stack_pair(block, rows):
    lanes = head_lanes(rows)
    zero = jnp.zeros_like(block)
    return jnp.concatenate([jnp.where(lanes < HEAD, block, zero), jnp.where(lanes >= HEAD, block, zero)], 0)


def pair_softmax(query, keys):
    scale = HEAD ** (-0.5) * LOG2E
    scores = dot_t(query, keys)
    left = head_lanes(scores.shape[0]) < HEAD
    low = jnp.max(jnp.where(left, scores, -jnp.inf), -1, keepdims=True)
    high = jnp.max(jnp.where(left, -jnp.inf, scores), -1, keepdims=True)
    exponent = jnp.exp2((scores - jnp.where(left, low, high)) * scale)
    total = pair_sum(exponent, left)
    return exponent / total, left


def pair_sum(values, left):
    low = jnp.sum(jnp.where(left, values, 0.0), -1, keepdims=True)
    high = jnp.sum(jnp.where(left, 0.0, values), -1, keepdims=True)
    return jnp.where(left, low, high)


def cross_kernel(
    after_in, gains_in, wq_in, wo_in, memory_in, cot_in,
    o_query, o_flat, o_after, o_rows, o_grads,
    after, gains, wq, wo, memory, cot, rows, query, flat, result, feed, grads, load, store, send, recv,
):
    t, x, y, d = neighbours()
    loads = [
        pltpu.make_async_copy(a, b, load.at[i])
        for i, (a, b) in enumerate(
            ((cot_in, cot), (after_in, after), (gains_in, gains), (wq_in, wq), (memory_in, memory), (wo_in, wo))
        )
    ]
    for copy in loads:
        copy.start()
    greet([{"tensor": x}, {"tensor": y}])
    n, m = after.shape
    width = wq.shape[2]
    texts = memory.shape[1]
    loads[0].wait()

    def round_block(i, carry):
        here = rows_at(i, 64)
        grads[t, here] = cot[here].astype(BF)
        return carry

    lax.fori_loop(0, n // 64, round_block, 0)
    gather = Gather(grads.at[t], grads, send, recv, 0)
    gather.start()
    loads[1].wait()
    loads[2].wait()

    def norm_block(i, carry):
        here = rows_at(i, 64)
        hat, _ = normed_rows(after[here])
        rows[here] = (hat * gains[0:1] + gains[1:2]).astype(BF)
        return carry

    lax.fori_loop(0, n // 64, norm_block, 0)
    loads[3].wait()
    loads[4].wait()

    def quarter(q, carry):
        query[:, cols(q, width)] = dot(rows[...], wq[q]).astype(BF)

        def pair(p, carry):
            keys = stack_pair(memory[q, :, cols(p, 128)], texts)
            values = stack_pair(memory[q, :, pl.ds(pl.multiple_of(width + p * 128, 128), 128)], texts)
            here = pl.ds(pl.multiple_of(q * width + p * 128, 128), 128)
            probs, _ = pair_softmax(query[:, here], keys)
            flat[:, here] = dot(probs.astype(BF), values).astype(BF)
            return carry

        lax.fori_loop(0, width // 128, pair, 0)
        return carry

    lax.fori_loop(0, 4, quarter, 0)
    gather.relay_x()
    gather.relay_y()
    stores = [pltpu.make_async_copy(query, o_query, store.at[0]), pltpu.make_async_copy(flat, o_flat, store.at[1])]
    loads[5].wait()

    def out_step(j, carry):
        result[:, cols(j, 512)] = after[:, cols(j, 512)] + dot(flat[...], wo[:, cols(j, 512)])
        return carry

    lax.fori_loop(0, m // 512, out_step, 0)

    def feed_block(i, carry):
        here = rows_at(i, 64)
        hat, _ = normed_rows(result[here])
        feed[here] = (hat * gains[2:3] + gains[3:4]).astype(BF)
        return carry

    lax.fori_loop(0, n // 64, feed_block, 0)
    stores += [pltpu.make_async_copy(result, o_after, store.at[2]), pltpu.make_async_copy(feed, o_rows, store.at[3])]
    for copy in stores:
        copy.start()
    gather.have_x()
    gather.have_y()
    gather.have_d()
    last = pltpu.make_async_copy(grads, o_grads, store.at[4])
    last.start()
    gather.drain()
    for copy in stores:
        copy.wait()
    last.wait()


def cross(after, gains, wq, wo, memory, cot):
    n, m = after.shape
    return pl.pallas_call(
        cross_kernel,
        name="cross",
        out_shape=[shape(n, m), shape(n, m), shape(n, m, kind=F32), shape(n, m), shape(4, n, m)],
        in_specs=[ANY] * 6,
        out_specs=[ANY] * 5,
        scratch_shapes=[
            pltpu.VMEM((n, m), F32), pltpu.VMEM(gains.shape, F32), pltpu.VMEM(wq.shape, BF), pltpu.VMEM(wo.shape, BF),
            pltpu.VMEM(memory.shape, BF), pltpu.VMEM((n, m), F32), pltpu.VMEM((n, m), BF), pltpu.VMEM((n, m), BF),
            pltpu.VMEM((n, m), BF), pltpu.VMEM((n, m), F32), pltpu.VMEM((n, m), BF), pltpu.VMEM((4, n, m), BF),
            dma(6), dma(5), dma(6), dma(6),
        ],
        compiler_params=params(3),
    )(after, gains, wq, wo, memory, cot)


def gelu_both(pre):
    size = jnp.abs(pre) * 0.7071067811865476
    rate = 1.0 / (1.0 + 0.3275911 * size)
    bell = jnp.exp2(pre * pre * (-0.5 * LOG2E))
    series = rate * (
        0.254829592
        + rate * (-0.284496736 + rate * (1.421413741 + rate * (-1.453152027 + rate * 1.061405429)))
    )
    tail = 0.5 * series * bell
    gate = jnp.where(pre >= 0, 1.0 - tail, tail)
    return pre * gate, gate + pre * (0.3989422804014327 * bell)


class Halves:
    def __init__(self, whole, land, send, recv, base):
        self.whole, self.land, self.send, self.recv, self.base = whole, land, send, recv, base
        self.subs = lax.axis_size("sub")
        self.piece = whole.shape[1] // self.subs

    def copies(self, w):
        s = lax.axis_index("sub")
        made = []
        for k in range(1, self.subs):
            target = (s + k) % self.subs
            slot = w * (self.subs - 1) + k - 1
            made.append(
                pltpu.make_async_remote_copy(
                    self.whole.at[w, rows_at(target, self.piece)],
                    self.land.at[w, k - 1],
                    self.send.at[self.base + slot],
                    self.recv.at[self.base + slot],
                    device_id={"sub": target},
                    device_id_type=MESH,
                )
            )
        return made

    def start(self, w):
        for copy in self.copies(w):
            copy.start()

    def total(self, w, take, step):
        s = lax.axis_index("sub")
        for copy in self.copies(w):
            copy.wait_recv()

        def block(i, carry):
            here = rows_at(i, step)
            value = self.whole[w, pl.ds(pl.multiple_of(s * self.piece + i * step, step), step)].astype(F32)
            for k in range(1, self.subs):
                value = value + self.land[w, k - 1, here].astype(F32)
            take(here, value)
            return carry

        lax.fori_loop(0, self.piece // step, block, 0)

    def drain(self, w):
        for copy in self.copies(w):
            copy.wait_send()


def weight_grad(left, right, whole, w, halves, block):
    s = lax.axis_index("sub")
    subs = lax.axis_size("sub")
    total_rows = left.shape[0] * left.shape[1]
    count = whole.shape[1] // block
    begin = ((s + 1) % subs) * halves.piece // block

    def one(j, carry):
        b = (begin + j) % count
        turned = left[:, :, cols(b, block)].reshape(total_rows, block)

        def inner(i, carry):
            other = right[:, :, cols(i, 512)].reshape(total_rows, 512)
            whole[w, rows_at(b, block), cols(i, 512)] = dot_c(turned, other).astype(BF)
            return carry

        lax.fori_loop(0, whole.shape[2] // 512, inner, 0)
        return carry

    if subs == 2:
        lax.fori_loop(0, count // 2, one, 0)
        halves.start(w)
        lax.fori_loop(count // 2, count, one, 0)
    else:
        lax.fori_loop(0, count, one, 0)
        halves.start(w)


def feed_kernel(
    rows_in, grads_in, up_in, down_in, o_part, o_norm, o_pieces,
    rows, grads, up, down, act, pre_grad, part_out, part_norm, land_norm, stage_norm,
    whole, land_whole, load, store, send, recv,
):
    t, x, y, d = neighbours()
    s = lax.axis_index("sub")
    subs = lax.axis_size("sub")
    loads = [
        pltpu.make_async_copy(a, b, load.at[i])
        for i, (a, b) in enumerate(
            ((rows_in, rows.at[t]), (up_in, up), (grads_in, grads), (down_in, down))
        )
    ]
    for copy in loads:
        copy.start()
    greet([{"tensor": x}, {"tensor": y}] + [{"sub": (s + k) % subs} for k in range(1, subs)])
    _, n, m = rows.shape
    hidden = up.shape[1]
    loads[0].wait()
    gather = Gather(rows.at[t], rows, send, recv, 0)
    gather.start()
    back = Scatter(part_norm, land_norm, stage_norm, send, recv, 6)
    halves = Halves(whole, land_whole, send, recv, 12)
    for copy in loads[1:4]:
        copy.wait()

    def work(place):
        def step(j, carry):
            here = cols(j, 256)
            value, slope = gelu_both(dot(rows[place], up[:, here]))
            act[place, :, here] = value.astype(BF)
            pre_grad[place, :, here] = (dot_t(grads[place], down[here]) * slope).astype(BF)
            return carry

        lax.fori_loop(0, hidden // 256, step, 0)

        def out_step(j, carry):
            part_norm[place, :, cols(j, 512)] = dot_t(pre_grad[place], up[rows_at(j, 512)]).astype(BF)
            part_out[place, :, cols(j, 512)] = dot(act[place], down[:, cols(j, 512)]).astype(BF)
            return carry

        lax.fori_loop(0, m // 512, out_step, 0)

    def turn(i, carry):
        far_y = i // 2
        far_x = i % 2
        place = (t // 2 + far_y - 2 * (t // 2) * far_y) * 2 + (t % 2 + far_x - 2 * (t % 2) * far_x)

        @pl.when(i == 1)
        def _():
            gather.relay_x()
            gather.relay_y()
            gather.have_x()

        @pl.when(i == 2)
        def _():
            gather.have_y()

        @pl.when(i == 3)
        def _():
            gather.have_d()

        work(place)

        @pl.when(i == 1)
        def _():
            back.along_x()

        @pl.when(i == 2)
        def _():
            back.along_y()

        @pl.when(i == 3)
        def _():
            back.diagonal()

        return carry

    lax.fori_loop(0, 4, turn, 0)
    stores = [pltpu.make_async_copy(part_out, o_part, store.at[1])]
    stores[0].start()
    weight_grad(act, grads, whole, 0, halves, 256)
    back.relay()
    weight_grad(rows, pre_grad, whole, 1, halves, 256)
    pieces = land_whole
    for w in range(2):

        def take(here, value, w=w):
            pieces[w, 0, here] = value.astype(BF)

        halves.total(w, take, 64)
    stores.append(pltpu.make_async_copy(pieces.at[:, 0], o_pieces, store.at[0]))
    stores[1].start()
    norm_total = part_norm


    def take_norm(here, total):
        norm_total[t, here] = total.astype(BF)

    back.finish(take_norm, 64)
    stores.append(pltpu.make_async_copy(norm_total.at[t], o_norm, store.at[2]))
    stores[2].start()
    gather.drain()
    back.drain()
    for w in range(2):
        halves.drain(w)
    for copy in stores:
        copy.wait()


def feed(rows, grads, up, down, subs):
    n, m = rows.shape
    hidden = up.shape[1]
    count = 12 + 2 * (subs - 1)
    return pl.pallas_call(
        feed_kernel,
        name="feed",
        out_shape=[shape(4, n, m), shape(n, m), shape(2, m // subs, hidden)],
        in_specs=[ANY] * 4,
        out_specs=[ANY] * 3,
        scratch_shapes=[
            pltpu.VMEM((4, n, m), BF), pltpu.VMEM((4, n, m), BF), pltpu.VMEM((m, hidden), BF), pltpu.VMEM((hidden, m), BF),
            pltpu.VMEM((4, n, hidden), BF), pltpu.VMEM((4, n, hidden), BF),
            pltpu.VMEM((4, n, m), BF), pltpu.VMEM((4, n, m), BF),
            pltpu.VMEM((6, n // 2, m), BF), pltpu.VMEM((2, n // 2, m), BF),
            pltpu.VMEM((2, m, hidden), BF), pltpu.VMEM((2, subs - 1, m // subs, hidden), BF),
            dma(4), dma(3), dma(count), dma(count),
        ],
        compiler_params=params(4),
    )(rows, grads, up, down)


def norm_back_block(grad, source, gain):
    hat, inverse = normed_rows(source)
    scaled = grad * gain
    inner = scaled - jnp.mean(scaled, -1, keepdims=True) - hat * jnp.mean(scaled * hat, -1, keepdims=True)
    return inverse * inner, grad * hat


def fold(block):
    total = block[0:8]
    for i in range(1, block.shape[0] // 8):
        total = total + block[8 * i : 8 * i + 8]
    return total


def unstack(block):
    lanes = head_lanes(block.shape[0] // 2)
    return jnp.where(lanes < HEAD, block[: block.shape[0] // 2], block[block.shape[0] // 2 :])


def cross_back_kernel(
    layout,
    cot_in, norm_in, cross_in, self_in, gains_in, query_in, flat_in, memory_in, wq_in, wo_in, own_in,
    o_out, o_branch, o_sums, o_memory, o_wq, o_wo, o_down, o_land,
    cot, norm, after_cross, after_self, gains, query, flat, memory, wq, wo,
    branch, rows, query_grad, memory_grad, sums, whole_q, whole_o, land_q, land_o, piece_q, piece_o,
    norm_self, own, land, ring, result, ring_send, ring_recv, ring_store,
    load, store, send, recv,
):
    s = lax.axis_index("sub")
    subs = lax.axis_size("sub")
    loads = [
        pltpu.make_async_copy(a, b, load.at[i])
        for i, (a, b) in enumerate(
            (
                (cot_in, cot), (norm_in, norm), (cross_in, after_cross), (gains_in, gains), (wo_in, wo),
                (query_in, query), (flat_in, flat), (memory_in, memory), (self_in, after_self), (wq_in, wq),
                (own_in.at[pl.ds(0, layout.middle)], own),
            )
        )
    ]
    for copy in loads[10:] + loads[:10]:
        copy.start()
    greet([{"sub": (s + k) % subs} for k in range(1, subs)] + group_ring())
    pump = Pump(
        own, land, ring, result, ring_send, ring_recv, ring_store, 0, layout.middle, layout.count,
        sum_outputs(layout, (o_down,)),
    )
    n, m = cot.shape
    width = wq.shape[2]
    texts = memory.shape[1]
    loads[10].wait()
    pump.step(jnp.int32(0))
    for copy in loads[:4]:
        copy.wait()
    scale = HEAD ** (-0.5)

    def feed_block(i, carry):
        here = rows_at(i, 64)
        grad = norm[here].astype(F32)
        inner, terms = norm_back_block(grad, after_cross[here], gains[2:3])
        total = cot[here] + inner
        cot[here] = total
        branch[here] = total.astype(BF)
        return carry[0] + fold(terms), carry[1] + fold(grad)

    zero = jnp.zeros((8, m), F32)
    gain_sum, bias_sum = lax.fori_loop(0, n // 64, feed_block, (zero, zero))
    sums[0:8] = gain_sum
    sums[8:16] = bias_sum
    loads[8].wait()

    def norm_block(i, carry):
        here = rows_at(i, 64)
        hat, _ = normed_rows(after_self[here])
        rows[here] = (hat * gains[0:1] + gains[1:2]).astype(BF)
        return carry

    lax.fori_loop(0, n // 64, norm_block, 0)
    for copy in loads[4:8]:
        copy.wait()
    middle = layout.middle

    def tick(k):
        @pl.when(k < middle)
        def _():
            pump.step(jnp.int32(k))

    tick(jnp.int32(1))

    def quarter(q, carry):
        @pl.when(q % 2 == 1)
        def _():
            tick(2 + q // 2)

        grad_heads = dot_t(branch[...], wo[rows_at(q, width)]).astype(BF)
        whole_q_cols = cols(q, width)
        query_grad_block = []
        for p in range(width // 128):
            lane = slice(p * 128, p * 128 + 128)
            keys = stack_pair(memory[q, :, lane], texts)
            values = stack_pair(memory[q, :, width + p * 128 : width + p * 128 + 128], texts)
            here = pl.ds(pl.multiple_of(q * width + p * 128, 128), 128)
            grad = grad_heads[:, lane]
            ask = query[:, here]
            probs, left = pair_softmax(ask, keys)
            grad_probs = dot_t(grad, values)
            centred = pair_sum(grad_probs * probs, left)
            grad_scores = (probs * (grad_probs - centred)).astype(BF)
            query_grad[:, here] = (dot(grad_scores, keys) * scale).astype(BF)
            memory_grad[q, :, lane] = unstack(dot_c(grad_scores, ask) * scale).astype(BF)
            memory_grad[q, :, width + p * 128 : width + p * 128 + 128] = unstack(
                dot_c(probs.astype(BF), grad)
            ).astype(BF)
        return carry

    lax.fori_loop(0, 4, quarter, 0)
    stores = [pltpu.make_async_copy(memory_grad, o_memory, store.at[0])]
    stores[0].start()
    halves_q = Halves(whole_q, land_q, send, recv, 0)
    halves_o = Halves(whole_o, land_o, send, recv, 4 * (subs - 1))

    def weights(q, carry):

        def grad_o(j, carry):
            whole_o[q, :, cols(j, 512)] = dot_c(flat[:, cols(q, width)], branch[:, cols(j, 512)]).astype(BF)
            return carry

        lax.fori_loop(0, m // 512, grad_o, 0)

        def grad_q(j, carry):
            whole_q[q, rows_at(j, 256)] = dot_c(rows[:, cols(j, 256)], query_grad[:, cols(q, width)]).astype(BF)
            return carry

        lax.fori_loop(0, m // 256, grad_q, 0)
        return carry

    lax.fori_loop(0, 4, weights, 0)
    for q in range(4):
        halves_q.start(q)
        halves_o.start(q)
    loads[9].wait()

    tick(4)

    def norm_grad(j, carry):
        here = rows_at(j, 256)
        total = jnp.zeros((n, 256), F32)
        for q in range(4):
            total = total + dot_t(query_grad[:, q * width : (q + 1) * width], wq[q, here])
        norm_self[:, cols(j, 256)] = total
        return carry

    lax.fori_loop(0, m // 256, norm_grad, 0)

    def self_block(i, carry):
        here = rows_at(i, 64)
        grad = norm_self[here]
        inner, terms = norm_back_block(grad, after_self[here], gains[0:1])
        total = cot[here] + inner
        cot[here] = total
        branch[here] = total.astype(BF)
        return carry[0] + fold(terms), carry[1] + fold(grad)

    gain_sum, bias_sum = lax.fori_loop(0, n // 64, self_block, (zero, zero))
    sums[16:24] = gain_sum
    sums[24:32] = bias_sum
    stores += [
        pltpu.make_async_copy(cot, o_out, store.at[1]),
        pltpu.make_async_copy(branch, o_branch, store.at[2]),
        pltpu.make_async_copy(sums, o_sums, store.at[3]),
    ]
    for copy in stores[1:]:
        copy.start()

    tick(5)
    for halves, piece in ((halves_q, piece_q), (halves_o, piece_o)):
        for q in range(4):

            def take(here, value, q=q, piece=piece):
                piece[q, here] = value.astype(BF)

            halves.total(q, take, 16)
    stores += [pltpu.make_async_copy(piece_q, o_wq, store.at[4]), pltpu.make_async_copy(piece_o, o_wo, store.at[5])]
    for copy in stores[4:]:
        copy.start()
    pump.drain()
    stores.append(pltpu.make_async_copy(land, o_land, store.at[6]))
    stores[-1].start()
    for q in range(4):
        halves_q.drain(q)
        halves_o.drain(q)
    for copy in stores:
        copy.wait()


def cross_back(layout, cot, norm, after_cross, after_self, gains, query, flat, memory, wq, wo, own, subs):
    n, m = cot.shape
    width = wq.shape[2]
    count = 8 * (subs - 1)
    held = (2, layout.window, layout.chunk, m)
    part_q, part_o = (4, m // subs, width), (4, width // subs, m)
    return pl.pallas_call(
        partial(cross_back_kernel, layout),
        name="cross_back",
        out_shape=[
            shape(n, m, kind=F32), shape(n, m), shape(32, m, kind=F32), shape(*memory.shape), shape(*part_q), shape(*part_o),
            shape(layout.feed_count // 2, layout.chunk, m), shape(*held),
        ],
        in_specs=[ANY] * 11,
        out_specs=[ANY] * 8,
        scratch_shapes=[
            pltpu.VMEM((n, m), F32), pltpu.VMEM((n, m), BF), pltpu.VMEM((n, m), F32), pltpu.VMEM((n, m), F32),
            pltpu.VMEM(gains.shape, F32), pltpu.VMEM((n, m), BF), pltpu.VMEM((n, m), BF), pltpu.VMEM(memory.shape, BF),
            pltpu.VMEM(wq.shape, BF), pltpu.VMEM(wo.shape, BF),
            pltpu.VMEM((n, m), BF), pltpu.VMEM((n, m), BF), pltpu.VMEM((n, m), BF), pltpu.VMEM(memory.shape, BF),
            pltpu.VMEM((32, m), F32), pltpu.VMEM((4, m, width), BF), pltpu.VMEM((4, width, m), BF),
            pltpu.VMEM((4, subs - 1, m // subs, width), BF), pltpu.VMEM((4, subs - 1, width // subs, m), BF),
            pltpu.VMEM(part_q, BF), pltpu.VMEM(part_o, BF),
            pltpu.VMEM((n, m), F32),
            *pump_scratch(layout, layout.middle),
            dma(11), dma(7), dma(count), dma(count),
        ],
        compiler_params=params(5),
    )(cot, norm, after_cross, after_self, gains, query, flat, memory, wq, wo, own)


def attend_pair_back(p, triple, place, blocks, heads, grad_heads, deltas, sums, grads, grad_keys, grad_values):
    n = triple.shape[1]
    width = heads * HEAD
    scale = HEAD ** (-0.5)
    lanes = head_lanes(n)
    key_lanes = head_lanes(blocks * n)

    here = pl.ds(pl.multiple_of(p * 128, 128), 128)
    key_cols = pl.ds(pl.multiple_of(width + p * 128, 128), 128)
    value_cols = pl.ds(pl.multiple_of(2 * width + p * 128, 128), 128)
    query = triple[place, :, here]
    grad = grad_heads[place, :, here]
    keys = triple[0:blocks, :, key_cols].reshape(blocks * n, 128)
    values = triple[0:blocks, :, value_cols].reshape(blocks * n, 128)
    stats = sums[place]
    means = deltas[place]
    found = []
    for h in range(2):
        mine = (lanes < HEAD) if h == 0 else (lanes >= HEAD)
        log_sum = jnp.sum(jnp.where(lanes == 2 * p + h, stats, 0.0), -1, keepdims=True)
        delta = jnp.sum(jnp.where(lanes == 2 * p + h, means, 0.0), -1, keepdims=True)
        scores = dot_t(jnp.where(mine, query, jnp.zeros_like(query)), keys)
        row = lax.broadcasted_iota(jnp.int32, scores.shape, 0)
        col = lax.broadcasted_iota(jnp.int32, scores.shape, 1)
        probs = jnp.where(
            col <= row + (blocks - 1) * n, jnp.exp2(scores * (scale * LOG2E) - log_sum), 0.0
        )
        grad_probs = dot_t(jnp.where(mine, grad, jnp.zeros_like(grad)), values)
        grad_scores = (probs * (grad_probs - delta)).astype(BF)
        found.append((dot(grad_scores, keys), dot_c(grad_scores, query), dot_c(probs.astype(BF), grad)))
    grads[place, :, here] = (jnp.where(lanes < HEAD, found[0][0], found[1][0]) * scale).astype(BF)
    grad_keys[0 : blocks * n, here] += jnp.where(key_lanes < HEAD, found[0][1], found[1][1]) * scale
    grad_values[0 : blocks * n, here] += jnp.where(key_lanes < HEAD, found[0][2], found[1][2])


def attend_back_kernel(
    layout,
    branch_in, triple_in, flat_in, sums_in, out_in, qkv_in, rows_in, frames_in, gains_in, grad_in, memory_in, text_in, kv_in,
    own_in, land_in, down_in,
    o_frames, o_sums, o_text, o_qkv, o_more, o_down, o_up, o_kv, o_land,
    branch, triple, flat, sums, out, qkv, rows, frames, gains, grad_out, memory, text, kv,
    land_m, stage_m,
    grad_heads, deltas, grads, grad_keys, grad_values, part, land, stage, whole_qkv, land_qkv, whole_out, land_out,
    whole_kv, land_kv, text_grad, sums_out, sum_m, own, held, ring, result, ring_send, ring_recv, ring_store,
    load, store, send, recv,
):
    t, x, y, d = neighbours()
    s = lax.axis_index("sub")
    subs = lax.axis_size("sub")
    names = (
        (branch_in, branch.at[t]), (out_in, out), (flat_in, flat), (triple_in, triple), (sums_in, sums),
        (memory_in, memory), (own_in, own.at[pl.ds(0, layout.feed_count)]), (land_in, held),
        *((qkv_in.at[i], qkv.at[:, pl.ds(i * qkv_in.shape[2], qkv_in.shape[2])]) for i in range(3)), (rows_in, rows),
        (text_in, text), (kv_in, kv), (frames_in, frames), (gains_in, gains), (grad_in, grad_out),
    )
    loads = [pltpu.make_async_copy(a, b, load.at[i]) for i, (a, b) in enumerate(names)]
    loads[7].start()
    for copy in loads[:7] + loads[8:]:
        copy.start()
    loads[7].wait()
    greet([{"tensor": x}, {"tensor": y}] + [{"sub": (s + k) % subs} for k in range(1, subs)] + group_ring())
    first, last = layout.middle, layout.later
    pump = Pump(
        own, held, ring, result, ring_send, ring_recv, ring_store, first, last, layout.count,
        sum_outputs(layout, (o_down, o_up), o_kv),
    )

    def tick(k):
        @pl.when(k + first < last)
        def _():
            pump.step(jnp.int32(k + first))

    n, m = grad_out.shape
    width = triple.shape[2]
    local = out.shape[0]
    heads = local // HEAD
    gather = Gather(branch.at[t], branch, send, recv, 0)
    scatter = Scatter(part, land, stage, send, recv, 6)
    scatter_m = Scatter(memory, land_m, stage_m, send, recv, 12)
    halves_qkv = Halves(whole_qkv, land_qkv, send, recv, 18)
    halves_out = Halves(whole_out, land_out, send, recv, 18 + subs - 1)
    halves_kv = Halves(whole_kv, land_kv, send, recv, 18 + 2 * (subs - 1))
    loads[0].wait()
    gather.start()
    for copy in loads[5:7]:
        copy.wait()
    scatter_m.diagonal()
    scatter_m.along_x()
    scatter_m.along_y()
    for copy in loads[1:5]:
        copy.wait()
    grad_keys[...] = jnp.zeros_like(grad_keys)
    grad_values[...] = jnp.zeros_like(grad_values)
    lanes = head_lanes(n)

    def turn(i, carry):
        far_y = i // 2
        far_x = i % 2
        place = (t // 2 + far_y - 2 * (t // 2) * far_y) * 2 + (t % 2 + far_x - 2 * (t % 2) * far_x)

        @pl.when(i == 1)
        def _():
            gather.relay_x()
            gather.relay_y()
            gather.have_x()

        @pl.when(i == 2)
        def _():
            gather.have_y()
            scatter_m.relay()

        @pl.when(i == 3)
        def _():
            gather.have_d()

        grad_heads[place] = dot_t(branch[place], out[...]).astype(BF)

        def delta(p, stats):
            here = pl.ds(pl.multiple_of(p * 128, 128), 128)
            product = grad_heads[place, :, here].astype(F32) * flat[place, :, here].astype(F32)
            low = jnp.sum(jnp.where(lanes < HEAD, product, 0.0), -1, keepdims=True)
            high = jnp.sum(jnp.where(lanes < HEAD, 0.0, product), -1, keepdims=True)
            return jnp.where(lanes == 2 * p, low, jnp.where(lanes == 2 * p + 1, high, stats))

        deltas[place] = lax.fori_loop(0, heads // 2, delta, jnp.zeros((n, 128), F32))

        def pair(p, carry):
            turns = i * (heads // 2) + p

            @pl.when(turns % 2 == 0)
            def _():
                tick(turns // 2)

            for blocks in range(1, 5):

                @pl.when(place == blocks - 1)
                def _(blocks=blocks):
                    attend_pair_back(
                        p, triple, blocks - 1, blocks, heads, grad_heads, deltas, sums, grads, grad_keys, grad_values
                    )

            return carry

        lax.fori_loop(0, heads // 2, pair, 0)
        return carry

    lax.fori_loop(0, 4, turn, 0)
    for copy in loads[8:14]:
        copy.wait()

    def finish_grads(i, carry):
        grads[i, :, local : 2 * local] = grad_keys[rows_at(i, n)].astype(BF)
        grads[i, :, 2 * local :] = grad_values[rows_at(i, n)].astype(BF)
        return carry

    lax.fori_loop(0, 4, finish_grads, 0)

    def back(i, carry):
        far_y = 1 - i // 2
        far_x = 1 - i % 2
        place = (t // 2 + far_y - 2 * (t // 2) * far_y) * 2 + (t % 2 + far_x - 2 * (t % 2) * far_x)

        def step(j, carry):
            part[place, :, cols(j, 512)] = dot_t(grads[place], qkv[rows_at(j, 512)]).astype(BF)
            return carry

        lax.fori_loop(0, m // 512, step, 0)

        @pl.when(i % 2 == 0)
        def _():
            tick(6 + i // 2)

        @pl.when(i == 0)
        def _():
            scatter.diagonal()

        @pl.when(i == 1)
        def _():
            scatter.along_y()

        @pl.when(i == 2)
        def _():
            scatter.along_x()

        return carry

    lax.fori_loop(0, 4, back, 0)
    tick(8)

    def take_m(here, total):
        sum_m[here] = total.astype(BF)

    scatter_m.finish(take_m, 16)
    text_grad[...] = dot_t(sum_m[...], kv[...])
    stores = [pltpu.make_async_copy(text_grad, o_text, store.at[0])]
    stores[0].start()

    def grad_kv(j, carry):
        whole_kv[0, rows_at(j, 384)] = dot_c(text[:, cols(j, 384)], sum_m[...]).astype(BF)
        return carry

    lax.fori_loop(0, m // 384, grad_kv, 0)
    halves_kv.start(0)

    def grad_wout(j, carry):
        whole_out[0, :, cols(j, 512)] = dot_c(
            flat[...].reshape(4 * n, local), branch[:, :, cols(j, 512)].reshape(4 * n, 512)
        ).astype(BF)
        return carry

    lax.fori_loop(0, m // 512, grad_wout, 0)
    halves_out.start(0)
    tick(9)
    chunk, half = layout.chunk, 2 * layout.quarter

    def take_kv(here, total):
        c = here.start // chunk
        own[layout.kv + c % half, :, cols(c // half, 2 * local)] = total.astype(BF)

    halves_kv.total(0, take_kv, chunk)
    scatter.relay()

    def grad_wqkv(j, carry):
        @pl.when(j % 2 == 0)
        def _():
            tick(10 + j // 2)

        turned = rows[:, :, cols(j, 256)].reshape(4 * n, 256)

        def inner(i, carry):
            whole_qkv[0, rows_at(j, 256), cols(i, 384)] = dot_c(
                turned, grads[:, :, cols(i, 384)].reshape(4 * n, 384)
            ).astype(BF)
            return carry

        lax.fori_loop(0, width // 384, inner, 0)
        return carry

    lax.fori_loop(0, m // 256, grad_wqkv, 0)
    halves_qkv.start(0)
    tick(13)

    def take_out(here, total):
        own[layout.out + here.start // chunk] = total.astype(BF)

    halves_out.total(0, take_out, chunk)

    def take(here, total):
        land_qkv[0, 0, here] = total.astype(BF)

    halves_qkv.total(0, take, 16)
    stores.append(pltpu.make_async_copy(land_qkv.at[0, 0], o_qkv, store.at[1]))
    stores.append(pltpu.make_async_copy(own.at[pl.ds(layout.kv, layout.qkv - layout.kv)], o_more, store.at[2]))
    for copy in stores[-2:]:
        copy.start()
    tick(14)
    tick(15)
    for copy in loads[14:]:
        copy.wait()

    def take_norm(here, total):
        part[t, here] = total.astype(BF)

    scatter.finish(take_norm, 64)

    def frame_block(i, carry):
        here = rows_at(i, 64)
        grad = part[t, here].astype(F32)
        inner, terms = norm_back_block(grad, frames[here].astype(F32), gains[4:5])
        grad_out[here] = grad_out[here] + inner
        return carry[0] + fold(terms), carry[1] + fold(grad)

    zero = jnp.zeros((8, m), F32)
    gain_sum, bias_sum = lax.fori_loop(0, n // 64, frame_block, (zero, zero))
    sums_out[0:8] = gain_sum
    sums_out[8:16] = bias_sum
    stores += [pltpu.make_async_copy(grad_out, o_frames, store.at[3]), pltpu.make_async_copy(sums_out, o_sums, store.at[4])]
    for copy in stores[-2:]:
        copy.start()
    pump.drain()
    stores.append(pltpu.make_async_copy(held, o_land, store.at[5]))
    stores[-1].start()
    gather.drain()
    for each in (scatter, scatter_m):
        each.drain()
    for each in (halves_qkv, halves_out, halves_kv):
        each.drain(0)
    for copy in stores:
        copy.wait()


def attend_back(
    layout, branch, triple, flat, sums, out, qkv, rows, frames, gains, grad, memory, text, kv, own, land, down, subs
):
    n, m = grad.shape
    width = triple.shape[2]
    local = out.shape[0]
    texts, kvw = text.shape[0], kv.shape[1]
    count = 18 + 3 * (subs - 1)
    v = pltpu.VMEM
    return pl.pallas_call(
        partial(attend_back_kernel, layout),
        name="attend_back",
        out_shape=[
            shape(n, m, kind=F32), shape(16, m, kind=F32), shape(texts, m, kind=F32), shape(m // subs, width),
            shape(layout.qkv - layout.kv, layout.chunk, m), shape(*down.shape), shape(*down.shape),
            shape(4 * layout.quarter, layout.chunk, kvw), shape(*land.shape),
        ],
        in_specs=[ANY] * 16,
        out_specs=[ANY] * 9,
        input_output_aliases={15: 5},
        scratch_shapes=[
            v((4, n, m), BF), v(triple.shape, BF), v(flat.shape, BF), v(sums.shape, F32), v(out.shape, BF), v((m, width), BF),
            v(rows.shape, BF), v(frames.shape, frames.dtype), v(gains.shape, F32), v((n, m), F32), v(memory.shape, BF),
            v(text.shape, BF), v(kv.shape, BF),
            v((6, texts // 2, kvw), BF), v((2, texts // 2, kvw), BF),
            v((4, n, local), BF), v((4, n, 128), F32), v((4, n, width), BF), v((4 * n, local), F32), v((4 * n, local), F32),
            v((4, n, m), BF), v((6, n // 2, m), BF), v((2, n // 2, m), BF),
            v((1, m, width), BF), v((1, subs - 1, m // subs, width), BF),
            v((1, local, m), BF), v((1, subs - 1, local // subs, m), BF),
            v((1, m, kvw), BF), v((1, subs - 1, m // subs, kvw), BF),
            v((texts, m), F32), v((16, m), F32), v((texts, kvw), BF),
            *pump_scratch(layout, layout.qkv),
            dma(17), dma(6), dma(count), dma(count),
        ],
        compiler_params=params(6),
    )(branch, triple, flat, sums, out, qkv, rows, frames, gains, grad, memory, text, kv, own, land, down)


def total_kernel(
    layout,
    feed_in, qkv_in, more_in, cross_q_in, cross_o_in, sums_a_in, sums_b_in, text_in, land_in, part_in, after_in,
    down_in, up_in, kv_in,
    o_qkv, o_cq, o_out, o_co, o_text, o_vectors, o_layer, o_down, o_up, o_kv,
    own, held, ring, result, ring_send, ring_recv, ring_store,
    cross_q, cross_o, land_q, land_o, stage_q, stage_o, part, land_p, stage_p, after,
    sums_a, sums_b, text, text_land, text_full, vectors, vectors_land, share, share_land, load, store, send, recv,
):
    t, x, y, d = neighbours()
    s, subs = lax.axis_index("sub"), lax.axis_size("sub")
    g, groups = lax.axis_index("group"), lax.axis_size("group")
    chunk, m, local = layout.chunk, layout.m, layout.local
    width, quarter = 3 * local, layout.quarter
    at_kv, at_out, at_qkv, at_cq, at_co = layout.kv, layout.out, layout.qkv, layout.cq, layout.co
    def outputs(c, block, slots, act):
        slot = c % RING

        def region(begin, end, copies):
            @pl.when(jnp.logical_and(c >= begin, c < end))
            def _():
                for i, (source, target) in enumerate(copies(c - begin)):
                    act(pltpu.make_async_copy(source, target, slots.at[slot, i]))

        def whole(output):
            return lambda r: [(block, output.at[r])]

        region(0, at_kv // 2, whole(o_down))
        region(at_kv // 2, at_kv, whole(o_up))
        region(
            at_qkv, at_cq,
            lambda r: [
                *((block.at[:, pl.ds(i * local, local)], o_qkv.at[i, r]) for i in range(3)),
                (block.at[:, pl.ds(width, local)], o_qkv.at[r // quarter, 3 * quarter + r % quarter]),
            ],
        )
        region(
            at_kv, at_out,
            lambda r: [
                (block.at[:, pl.ds(2 * i * local, 2 * local)], o_kv.at[2 * i * quarter + r]) for i in range(2)
            ],
        )
        region(at_out, at_qkv, whole(o_out))
        region(
            at_cq, at_co,
            lambda r: [(block.at[:, pl.ds(i * local, local)], o_cq.at[i * quarter + r]) for i in range(4)],
        )
        region(at_co, layout.count, whole(o_co))

    fresh = max(0, layout.later - LAG * (groups - 1))
    newer = max(fresh, at_kv)
    pairs = [
        (land_in, held),
        (more_in.at[pl.ds(newer - at_kv, at_qkv - newer)], own.at[pl.ds(newer, at_qkv - newer)]),
        (qkv_in.at[pl.ds(0, 3 * quarter)], own.at[pl.ds(at_qkv, 3 * quarter), :, pl.ds(0, width)]),
    ]
    for i in range(3):
        pairs.append(
            (
                qkv_in.at[pl.ds(3 * quarter, quarter), :, pl.ds(i * local, local)],
                own.at[pl.ds(at_qkv + i * quarter, quarter), :, pl.ds(width, local)],
            )
        )
    if fresh < at_kv:
        pairs.append((feed_in.at[pl.ds(fresh, at_kv - fresh)], own.at[pl.ds(fresh, at_kv - fresh)]))
    early = len(pairs)
    pairs += [
        (cross_q_in, cross_q), (cross_o_in, cross_o), (sums_a_in, sums_a), (sums_b_in, sums_b), (text_in, text),
        (part_in, part), (after_in, after),
    ]
    loads = [pltpu.make_async_copy(a, b, load.at[i]) for i, (a, b) in enumerate(pairs)]
    for copy in loads:
        copy.start()
    loads[0].wait()
    greet(
        [{"tensor": x}, {"tensor": y}, {"tensor": d}]
        + [{"sub": (s + k) % subs} for k in range(1, subs)]
        + [{"group": (g + k) % groups} for k in range(1, groups)]
    )
    begin, end = layout.later, layout.end
    pump = Pump(own, held, ring, result, ring_send, ring_recv, ring_store, begin, end, layout.count, outputs)

    def run(a, b):
        def step(k, carry):
            pump.step(k)
            return carry

        lax.fori_loop(a, b, step, 0)

    for copy in loads[1:early]:
        copy.wait()
    run(begin, begin + 1)
    for copy in loads[early:-2]:
        copy.wait()
    share_width = m // subs
    for i in range(6):
        source, at = (sums_a, i) if i < 4 else (sums_b, i - 4)
        row = jnp.sum(source[8 * at : 8 * at + 8], 0, keepdims=True)
        for j in range(subs):
            vectors[j, i : i + 1] = row[:, j * share_width : (j + 1) * share_width]
    strip = text.shape[0] // 4

    def remote(source, target, k, device):
        return pltpu.make_async_remote_copy(
            source, target, send.at[k], recv.at[k], device_id=device, device_id_type=MESH
        )

    square = (x, y, d)
    first = [remote(vectors, vectors_land.at[k], k, {"tensor": square[k]}) for k in range(3)]
    first += [
        remote(text.at[rows_at(square[k], strip)], text_land.at[k], 3 + k, {"tensor": square[k]}) for k in range(3)
    ]
    second = [
        remote(share.at[0, (s + k) % subs], share_land.at[k - 1], 5 + k, {"sub": (s + k) % subs}) for k in range(1, subs)
    ]
    base = 5 + subs
    second += [
        remote(text_full.at[rows_at(t, strip)], text_full.at[rows_at(t, strip)], base + k, {"tensor": square[k]}) for k in range(3)
    ]
    base += 3
    third = [
        remote(share.at[1, 0], share_land.at[subs - 2 + k], base + k - 1, {"group": (g + k) % groups})
        for k in range(1, groups)
    ]
    base += groups - 1
    scatter_q = Scatter(cross_q, land_q, stage_q, send, recv, base)
    scatter_o = Scatter(cross_o, land_o, stage_o, send, recv, base + 6)
    for copy in first:
        copy.start()
    scatter_p = Scatter(part, land_p, stage_p, send, recv, base + 12)
    for each in (scatter_q, scatter_o):
        each.diagonal()
        each.along_x()
        each.along_y()

    run(begin + 1, begin + 2)
    for copy in first:
        copy.wait_recv()
    for j in range(subs):
        share[0, j] = vectors[j] + vectors_land[0, j] + vectors_land[1, j] + vectors_land[2, j]
    text_full[rows_at(t, strip)] = text[rows_at(t, strip)] + text_land[0] + text_land[1] + text_land[2]
    for copy in first:
        copy.wait_send()
    for copy in second:
        copy.start()
    run(begin + 2, begin + 3)
    scatter_q.relay()
    scatter_o.relay()
    loads[-2].wait()
    loads[-1].wait()
    scatter_p.diagonal()
    scatter_p.along_x()
    scatter_p.along_y()
    run(begin + 3, at_cq)

    def take_q(rows, value):
        row = rows.start
        c = row // chunk
        own[at_cq + c % quarter, :, cols(c // quarter, local)] = value.astype(BF)

    scatter_q.finish(take_q, chunk)
    run(at_cq, at_co)
    step = min(chunk, scatter_o.half)

    def take_o(rows, value):
        own[at_co + rows.start // chunk, rows_at(rows.start % chunk // step, step)] = value.astype(BF)

    scatter_o.finish(take_o, step)
    for copy in second:
        copy.wait_recv()
    total = share[0, s]
    for k in range(1, subs):
        total = total + share_land[k - 1]
    share[1, 0] = total
    text_store = pltpu.make_async_copy(text_full, o_text, store.at[0])
    text_store.start()
    for copy in third:
        copy.start()
    run(at_co, layout.count)
    scatter_p.relay()
    run(layout.count, end)

    def take_layer(rows, value):
        after[rows] = after[rows] + value

    scatter_p.finish(take_layer, 64)
    layer_store = pltpu.make_async_copy(after, o_layer, store.at[2])
    layer_store.start()
    for copy in third:
        copy.wait_recv()
    total = share[1, 0]
    for k in range(1, groups):
        total = total + share_land[subs - 2 + k]
    share[2, 0] = total
    vector_store = pltpu.make_async_copy(share.at[2, 0], o_vectors, store.at[1])
    vector_store.start()
    for copy in second + third:
        copy.wait_send()
    for each in (scatter_q, scatter_o, scatter_p):
        each.drain()
    pump.drain()
    layer_store.wait()
    text_store.wait()
    vector_store.wait()


def total(layout, pieces, qkv, more, cross_q, cross_o, sums_a, sums_b, text, land, part, after, down, up, kv, subs, groups):
    m, chunk = layout.m, layout.chunk
    n = after.shape[0]
    v = pltpu.VMEM
    sems = 7 + subs + groups + 18
    qkv = qkv.reshape(-1, chunk, qkv.shape[1])
    piece_q, piece_o = cross_q.shape[1:], cross_o.shape[1:]
    out_shape = shape(layout.qkv - layout.out, chunk, m)
    return pl.pallas_call(
        partial(total_kernel, layout),
        name="total",
        out_shape=[
            shape(3, *qkv.shape[:2], layout.local), shape(layout.piece // chunk, chunk, layout.local), out_shape, out_shape,
            shape(*text.shape, kind=F32), shape(8, m // subs, kind=F32), shape(n, m, kind=F32),
            shape(*down.shape), shape(*up.shape), shape(*kv.shape),
        ],
        in_specs=[ANY] * 14,
        out_specs=[ANY] * 10,
        input_output_aliases={11: 7, 12: 8, 13: 9},
        scratch_shapes=[
            *pump_scratch(layout, layout.count),
            v(cross_q.shape, BF), v(cross_o.shape, BF),
            v((6, piece_q[0] // 2, piece_q[1]), BF), v((6, piece_o[0] // 2, piece_o[1]), BF),
            v((2, piece_q[0] // 2, piece_q[1]), BF), v((2, piece_o[0] // 2, piece_o[1]), BF),
            v((4, n, m), BF), v((6, n // 2, m), BF), v((2, n // 2, m), BF), v((n, m), F32),
            v(sums_a.shape, F32), v(sums_b.shape, F32), v(text.shape, F32),
            v((3, text.shape[0] // 4, m), F32), v(text.shape, F32), v((subs, 8, m // subs), F32), v((3, subs, 8, m // subs), F32),
            v((3, subs, 8, m // subs), F32), v((subs - 1 + groups - 1, 8, m // subs), F32),
            dma(14), dma(3), dma(sems), dma(sems),
        ],
        compiler_params=params(7),
    )(pieces, qkv, more, cross_q, cross_o, sums_a, sums_b, text, land, part, after, down, up, kv)


def local(
    frames, text_states, selfgain, selfbias, selfqkv, selfout, crossgain, crossbias, crossquery, crosskv, crossout,
    feedgain, feedbias, feedup, feeddown, cotangent,
):
    subs, groups = lax.axis_size("sub"), lax.axis_size("group")
    m = frames.shape[2]
    width = selfout.shape[0]
    qkv = selfqkv.transpose(1, 0, 2)
    kv = crosskv.reshape(m, 2 * width)
    gains = jnp.concatenate([crossgain, crossbias, feedgain, feedbias, selfgain, selfbias]).reshape(6, m)
    rows, triple, memory = enter(frames[0], gains, qkv, text_states[0], kv)
    flat, sums, after_self, wq, wo = attend(triple, selfout, frames[0], crossquery, crossout, subs, groups)
    wo = wo.reshape(4 * width, m)
    query, cross_flat, after_cross, feed_rows, grads = cross(after_self, gains, wq, wo, memory, cotangent[0])
    layout = Layout(m, width, subs, groups)
    part, norm_grad, pieces = feed(feed_rows, grads, feedup, feeddown, subs)
    pieces = pieces.reshape(-1, layout.chunk, m)
    grad_out, branch, sums_a, memory_grad, piece_q, piece_o, down, land = cross_back(
        layout, cotangent[0], norm_grad, after_cross, after_self, gains, query, cross_flat, memory, wq, wo, pieces, subs
    )
    frame_grad, sums_b, text_part, grad_qkv, more, down, up, full_kv, land = attend_back(
        layout, branch, triple, flat, sums, selfout, qkv, rows, frames[0], gains, grad_out, memory_grad,
        text_states[0], kv, pieces, land, down, subs,
    )
    full_qkv, full_cq, full_out, full_co, text_grad, vectors, layer_output, down, up, full_kv = total(
        layout, pieces, grad_qkv, more, piece_q, piece_o, sums_a, sums_b, text_part, land, part, after_cross,
        down, up, full_kv, subs, groups,
    )
    return (
        layer_output[None],
        frame_grad[None],
        text_grad[None],
        vectors[4],
        vectors[5],
        full_qkv.astype(F32).reshape(3, -1, width).transpose(1, 0, 2),
        full_out.astype(F32).reshape(-1, m),
        vectors[2],
        vectors[3],
        full_cq.astype(F32).reshape(-1, width),
        full_kv.astype(F32).reshape(-1, 2, width),
        full_co.astype(F32).reshape(-1, m),
        vectors[0],
        vectors[1],
        up.astype(F32).reshape(-1, m),
        down.astype(F32).reshape(-1, m),
    )


def solution(mesh):
    clips = P(("sub", "group"), "tensor", None)
    whole = P(("sub", "group"), None, None)
    narrow, wide = P("tensor", None), P(None, "tensor")
    third = P(None, None, "tensor")
    vector = P("sub")
    return jax.shard_map(
        local,
        mesh=mesh,
        in_specs=(
            clips, whole, P(), P(), third, narrow, P(), P(), wide, third, narrow, P(), P(), wide, narrow, clips,
        ),
        out_specs=(
            clips, clips, whole, vector, vector, P("sub", None, "tensor"), P(("tensor", "sub"), None), vector, vector,
            P("sub", "tensor"), P("sub", None, "tensor"), P(("tensor", "sub"), None), vector, vector,
            P("sub", "tensor"), P(("tensor", "sub"), None),
        ),
        check_vma=False,
    )
```
